32 devices in a mesh: dp: 8 (over z, x), seq: 4 (over y, core).
Axes of the slice: x: 2, y: 2, z: 4, core: 2. Of those that a mesh axis runs over, the one named last changes fastest.
Arguments:
- tokens: bfloat16 [12288, 1024], P(('dp', 'seq')), may hold values from -6 to 6
- lengths: int32 [8], P('dp'), may hold values from 193 to 1536, as said below
- cotangent: bfloat16 [12288, 1024], P(('dp', 'seq')), may hold values from -12 to 12
- ln1_gain: bfloat16 [1024], P(('dp', 'seq')), may hold values from 0.25 to 1.75
- ln1_shift: bfloat16 [1024], P(('dp', 'seq')), may hold values from -1.75 to 1.75
- w_qkv: bfloat16 [1024, 3, 1024], P('dp', None, 'seq'), may hold values from -0.1875 to 0.1875
- b_qv: bfloat16 [2048], P(('dp', 'seq')), may hold values from -1.75 to 1.75
- w_out: bfloat16 [1024, 1024], P('seq', 'dp'), may hold values from -0.5 to 0.5
- b_out: bfloat16 [1024], P(('dp', 'seq')), may hold values from -1.75 to 1.75
- ln2_gain: bfloat16 [1024], P(('dp', 'seq')), may hold values from 0.25 to 1.75
- ln2_shift: bfloat16 [1024], P(('dp', 'seq')), may hold values from -1.75 to 1.75
- w_fc1: bfloat16 [1024, 4096], P('dp', 'seq'), may hold values from -0.1875 to 0.1875
- b_fc1: bfloat16 [4096], P(('dp', 'seq')), may hold values from -3 to 3
- w_fc2: bfloat16 [4096, 1024], P('seq', 'dp'), may hold values from -0.125 to 0.125
- b_fc2: bfloat16 [1024], P(('dp', 'seq')), may hold values from -1.75 to 1.75
Outputs:
- output: bfloat16 [12288, 1024], P(('dp', 'seq'))
- grad_tokens: bfloat16 [12288, 1024], P(('dp', 'seq'))
- grad_ln1_gain: float32 [1024], P(('dp', 'seq'))
- grad_ln1_shift: float32 [1024], P(('dp', 'seq'))
- grad_w_qkv: float32 [1024, 3, 1024], P('dp', None, 'seq')
- grad_b_qv: float32 [2048], P(('dp', 'seq'))
- grad_w_out: float32 [1024, 1024], P('seq', 'dp')
- grad_b_out: float32 [1024], P(('dp', 'seq'))
- grad_ln2_gain: float32 [1024], P(('dp', 'seq'))
- grad_ln2_shift: float32 [1024], P(('dp', 'seq'))
- grad_w_fc1: float32 [1024, 4096], P('dp', 'seq')
- grad_b_fc1: float32 [4096], P(('dp', 'seq'))
- grad_w_fc2: float32 [4096, 1024], P('seq', 'dp')
- grad_b_fc2: float32 [1024], P(('dp', 'seq'))
The draws below stay inside these ranges and needn't reach their ends.
Inputs may be any that keep to these rules, and one draw needn't show every extreme that they name: `lengths`: some sequence has length 1536 and some has length 193.
All inputs are finite; a program needn't handle non-finite values.
Results may differ from the reference program's by a relative error of at most 0.014.
Values may be sent and summed in bfloat16 or wider, within the bound.
A program may use at most 192 MiB of HBM per device.

```python
import math
import jax
import jax.numpy as jnp
from jax import lax

D = 1024
HEAD_DIM = 64
FF = 4096
SEQ_LEN = 1536
SEQS = 8
TOKENS = 12288


def draw_lengths(key, part):
    key_vals, key_order = jax.random.split(jax.random.fold_in(key, 17))
    least = SEQ_LEN // 8 + 1
    values = jax.random.randint(key_vals, (SEQS,), least, SEQ_LEN + 1)
    order = jax.random.permutation(key_order, SEQS)
    values = values.at[order[0]].set(SEQ_LEN).at[order[1]].set(least)
    return values.astype(jnp.int32)


def with_spikes(drawn, own_key, source, target, shards_of, factor):
    def block_of(position):
        return (jnp.arange(drawn.shape[position]) // (drawn.shape[position] // shards_of)).reshape((-1,) + (1,) * (drawn.ndim - 1 - position))

    one_side = jax.random.permutation(own_key, shards_of)[block_of(target)]
    other_side = (block_of(target) + shards_of // 2) % shards_of
    return jnp.where((block_of(source) == one_side) | (block_of(source) == other_side), factor * drawn, drawn)


def shard_levels(rng, extent, cuts, low, top_value):
    level = 1.0
    for dim, blocks in cuts:
        heights = jax.random.uniform(jax.random.fold_in(jax.random.fold_in(rng, 6), dim), (blocks,), jnp.float32, low / len(cuts), top_value / len(cuts))
        level = level * jnp.repeat(jnp.exp(heights), extent[dim] // blocks).reshape((-1,) + (1,) * (len(extent) - 1 - dim))
    return level


def noise(stream_key, shape, spread, reach, shards=(), held_as=jnp.bfloat16):
    array = spread * jax.random.normal(stream_key, shape, jnp.float32)
    if shards:
        array = array * shard_levels(stream_key, shape, shards, -0.22, 0.18)
    return jnp.clip(array, -reach, reach).astype(held_as)


def noise_with(key, shape, deviation, reach, cuts, heavy, held_as=jnp.bfloat16):
    values = deviation * jax.random.normal(key, shape, jnp.float32)
    if cuts:
        values = values * shard_levels(key, shape, cuts, -0.22, 0.18)
    return jnp.clip(with_spikes(values, jax.random.fold_in(key, 3), *heavy), -reach, reach).astype(held_as)


def setup_inputs(seed: int = 0) -> dict:
    key_of = jax.random.split(jax.random.key(seed), 16)
    tokens = noise(key_of[0], (TOKENS, D), 1.0, 6.0, ((0, 32),))
    lengths = draw_lengths(jax.random.fold_in(key_of[15], 71), 0)
    cotangent = noise_with(key_of[2], (TOKENS, D), 1.0, 12.0, ((0, 32),), (0, 1, 32, 2.75))
    ln1_gain = jnp.clip(1.0 + 0.15 * jax.random.normal(key_of[3], (D,), jnp.float32), 0.25, 1.75).astype(jnp.bfloat16)
    ln1_shift = noise(key_of[4], (D,), 0.3, 1.75, ((0, 32),))
    w_qkv = noise(key_of[5], (D, 3, D), D ** -0.5, 0.1875, ((0, 8), (2, 4)))
    b_qv = noise(key_of[6], (2 * D,), 0.3, 1.75, ((0, 32),))
    w_out = noise(key_of[7], (D, D), (D // 8) ** -0.5, 0.5, ((0, 4), (1, 8)))
    b_out = noise(key_of[8], (D,), 0.3, 1.75, ((0, 32),))
    ln2_gain = jnp.clip(1.0 + 0.15 * jax.random.normal(key_of[9], (D,), jnp.float32), 0.25, 1.75).astype(jnp.bfloat16)
    ln2_shift = noise(key_of[10], (D,), 0.3, 1.75, ((0, 32),))
    w_fc1 = noise(key_of[11], (D, FF), D ** -0.5, 0.1875, ((0, 8), (1, 4)))
    b_fc1 = noise(key_of[12], (FF,), 0.5, 3.0, ((0, 32),))
    w_fc2 = noise(key_of[13], (FF, D), (FF // 2) ** -0.5, 0.125, ((0, 4), (1, 8)))
    b_fc2 = noise(key_of[14], (D,), 0.3, 1.75, ((0, 32),))
    return {"tokens": tokens, "lengths": lengths, "cotangent": cotangent, "ln1_gain": ln1_gain, "ln1_shift": ln1_shift, "w_qkv": w_qkv, "b_qv": b_qv, "w_out": w_out, "b_out": b_out, "ln2_gain": ln2_gain, "ln2_shift": ln2_shift, "w_fc1": w_fc1, "b_fc1": b_fc1, "w_fc2": w_fc2, "b_fc2": b_fc2}


eps = 1e-05
gelu_coef = 0.044715
precise = lax.Precision.HIGHEST

@jax.custom_vjp
def low(v):
    return lax.optimization_barrier(v.astype(jnp.bfloat16)).astype(jnp.float32)

@jax.custom_vjp
def low_back(v):
    return v

def low_keep(v):
    return (low(v), None)

def low_pass(kept, grad):
    return (grad,)

def back_keep(v):
    return (v, None)

def back_low(kept, grad):
    return (low(grad),)
low.defvjp(low_keep, low_pass)
low_back.defvjp(back_keep, back_low)

def normalize(stream, gain, shift):
    row_mean = lax.optimization_barrier(jnp.mean(stream, axis=-1, keepdims=True))
    centred = stream - row_mean
    variance = lax.optimization_barrier(jnp.mean(centred * centred, axis=-1, keepdims=True))
    return centred * lax.rsqrt(variance + eps) * gain + shift

def gelu_tanh(pre_act):
    inner = math.sqrt(2.0 / math.pi) * (pre_act + gelu_coef * pre_act * pre_act * pre_act)
    return 0.5 * pre_act * (1.0 + jnp.tanh(inner))

def block_forward(stream, params, length):
    gain_one, shift_one, proj_qkv, bias_qv, proj_out, bias_out, gain_two, shift_two, proj_up, bias_up, proj_down, bias_down = params
    seq_len, width = stream.shape
    heads = width // HEAD_DIM
    normed = low(normalize(stream, gain_one, shift_one))
    merged = jnp.dot(normed, proj_qkv.reshape(width, 3 * width), precision=precise)
    queries = low_back(low(merged[:, :width] + bias_qv[:width]))
    keys = low_back(low(merged[:, width:2 * width]))
    values = low_back(low(merged[:, 2 * width:] + bias_qv[width:]))
    queries = queries.reshape(seq_len, heads, HEAD_DIM)
    keys = keys.reshape(seq_len, heads, HEAD_DIM)
    values = values.reshape(seq_len, heads, HEAD_DIM)
    positions = jnp.arange(seq_len, dtype=jnp.int32)
    offset = (positions[None, :] - positions[:, None]).astype(jnp.float32)
    allowed = (positions[None, :] <= positions[:, None]) & (positions[None, :] < length)
    slopes = 2.0 ** (-8.0 * (jnp.arange(heads) + 1).astype(jnp.float32) / heads)
    scores = jnp.einsum('qhd,khd->hqk', queries, keys, precision=precise) * HEAD_DIM ** (-0.5)
    scores = scores + slopes[:, None, None] * offset[None]
    scores = low_back(jnp.where(allowed[None], scores, -1e+30))
    top = lax.optimization_barrier(jnp.max(scores, axis=-1, keepdims=True))
    expo = jnp.exp(scores - top)
    probs = low(expo / lax.optimization_barrier(jnp.sum(expo, axis=-1, keepdims=True)))
    mixed = jnp.einsum('hqk,khd->qhd', probs, values, precision=precise).reshape(seq_len, width)
    mixed = low_back(low(mixed))
    branch = low_back(jnp.dot(mixed, proj_out, precision=precise) + bias_out)
    middle = stream + branch
    normed_two = low(normalize(middle, gain_two, shift_two))
    hidden_pre = low_back(jnp.dot(normed_two, proj_up, precision=precise) + bias_up)
    hidden = low(gelu_tanh(hidden_pre))
    return middle + jnp.dot(hidden, proj_down, precision=precise) + bias_down

def reference(tokens, lengths, cotangent, ln1_gain, ln1_shift, w_qkv, b_qv, w_out, b_out, ln2_gain, ln2_shift, w_fc1, b_fc1, w_fc2, b_fc2):
    params = (ln1_gain, ln1_shift, w_qkv, b_qv, w_out, b_out, ln2_gain, ln2_shift, w_fc1, b_fc1, w_fc2, b_fc2)
    params = tuple((p.astype(jnp.float32) for p in params))
    width = tokens.shape[1]
    inputs = tokens.astype(jnp.float32).reshape(SEQS, SEQ_LEN, width)
    cotans = cotangent.astype(jnp.float32).reshape(SEQS, SEQ_LEN, width)

    def one_sequence(totals, item):
        stream, cotan, length = item
        is_valid = jnp.arange(SEQ_LEN, dtype=jnp.int32) < length
        result, pull = jax.vjp(lambda inp, par: block_forward(inp, par, length), stream, params)
        grad_in, grad_par = pull(jnp.where(is_valid[:, None], cotan, jnp.zeros_like(cotan)))
        totals = jax.tree.map(lambda acc, new: acc + new, totals, grad_par)
        return (totals, (result.astype(jnp.bfloat16), grad_in.astype(jnp.bfloat16)))
    zeros = jax.tree.map(jnp.zeros_like, params)
    grads, (results, grad_ins) = lax.scan(one_sequence, zeros, (inputs, cotans, lengths))
    return (results.reshape(TOKENS, width), grad_ins.reshape(TOKENS, width), grads[0], grads[1], grads[2], grads[3], grads[4], grads[5], grads[6], grads[7], grads[8], grads[9], grads[10], grads[11])
```

```python
import functools
import math

import jax
import jax.numpy as jnp
from jax import lax
from jax.experimental import pallas as pl
from jax.experimental.pallas import tpu as pltpu
from jax.sharding import PartitionSpec as P

HEAD_DIM = 64
EPS = 1e-05
GELU_COEF = 0.044715
NEG = -1e30
LANES = 128
VMEM_BYTES = 60 * 1024 * 1024

f32 = jnp.float32
bf16 = jnp.bfloat16
WHOLE = pl.BlockSpec(memory_space=pltpu.VMEM)
SCALAR = pl.BlockSpec(memory_space=pltpu.SMEM)


def mm(a, b):
    return jnp.dot(a, b, preferred_element_type=f32)


def mm_t(a, b):
    return lax.dot_general(a, b, (((1,), (1,)), ((), ())), preferred_element_type=f32)


def params(**kw):
    return pltpu.CompilerParams(vmem_limit_bytes=VMEM_BYTES, **kw)


def normalize(v):
    width = v.shape[-1]
    centred = v - jnp.sum(v, axis=-1, keepdims=True) * (1.0 / width)
    inv = lax.rsqrt(jnp.sum(centred * centred, axis=-1, keepdims=True) * (1.0 / width) + EPS)
    return centred * inv, inv


def norm_back(grad_out, gain, unit, inv):
    width = unit.shape[-1]
    scaled = grad_out * gain
    mean_one = jnp.sum(scaled, axis=-1, keepdims=True) * (1.0 / width)
    mean_two = jnp.sum(scaled * unit, axis=-1, keepdims=True) * (1.0 / width)
    return inv * (scaled - mean_one - unit * mean_two)


def device_of(index, seq_n):
    return (index // seq_n, index % seq_n)


def greet_all(me, count, seq_n):
    barrier = pltpu.get_barrier_semaphore()

    def hello(i, carry):
        peer = (me + i) % count
        pl.semaphore_signal(
            barrier, inc=1, device_id=device_of(peer, seq_n), device_id_type=pl.DeviceIdType.MESH
        )
        return carry

    lax.fori_loop(1, count, hello, 0)
    pl.semaphore_wait(barrier, count - 1)


def small_gather_body(count, seq_n, x_ref, out_ref, send_sem, recv_sem):
    me = lax.axis_index("dp") * seq_n + lax.axis_index("seq")
    greet_all(me, count, seq_n)

    def copy_to(i):
        peer = (me + i) % count
        return pltpu.make_async_remote_copy(
            src_ref=x_ref,
            dst_ref=out_ref.at[pl.ds(me, 1)],
            send_sem=send_sem.at[i],
            recv_sem=recv_sem.at[i],
            device_id=device_of(peer, seq_n),
            device_id_type=pl.DeviceIdType.MESH,
        )

    def begin(i, carry):
        copy_to(i).start()
        return carry

    def finish(i, carry):
        copy_to(i).wait()
        return carry

    lax.fori_loop(1, count, begin, 0)
    out_ref[pl.ds(me, 1)] = x_ref[...]
    lax.fori_loop(1, count, finish, 0)


def small_gather(x, count, seq_n):
    width = x.shape[-1]
    return pl.pallas_call(
        functools.partial(small_gather_body, count, seq_n),
        out_shape=jax.ShapeDtypeStruct((count, 1, width), f32),
        in_specs=[WHOLE],
        out_specs=WHOLE,
        scratch_shapes=[pltpu.SemaphoreType.DMA((count,)), pltpu.SemaphoreType.DMA((count,))],
        compiler_params=pltpu.CompilerParams(collective_id=1, has_side_effects=True),
        name="small_gather",
    )(x.reshape(1, 1, width))


def small_scatter_body(count, seq_n, v_ref, out_ref, land, send_sem, recv_sem):
    me = lax.axis_index("dp") * seq_n + lax.axis_index("seq")
    greet_all(me, count, seq_n)

    def copy_to(i):
        peer = (me + i) % count
        return pltpu.make_async_remote_copy(
            src_ref=v_ref.at[pl.ds(peer, 1)],
            dst_ref=land.at[pl.ds(i, 1)],
            send_sem=send_sem.at[i],
            recv_sem=recv_sem.at[i],
            device_id=device_of(peer, seq_n),
            device_id_type=pl.DeviceIdType.MESH,
        )

    def begin(i, carry):
        copy_to(i).start()
        return carry

    def finish(i, total):
        copy_to(i).wait()
        return total + land[pl.ds(i, 1)]

    lax.fori_loop(1, count, begin, 0)
    out_ref[...] = lax.fori_loop(1, count, finish, v_ref[pl.ds(me, 1)])


def small_scatter(v, count, seq_n):
    width = v.shape[-1]
    return pl.pallas_call(
        functools.partial(small_scatter_body, count, seq_n),
        out_shape=jax.ShapeDtypeStruct((1, 1, width), f32),
        in_specs=[WHOLE],
        out_specs=WHOLE,
        scratch_shapes=[
            pltpu.VMEM((count, 1, width), f32),
            pltpu.SemaphoreType.DMA((count,)),
            pltpu.SemaphoreType.DMA((count,)),
        ],
        compiler_params=pltpu.CompilerParams(collective_id=2, has_side_effects=True),
        name="small_scatter",
    )(v.reshape(count, 1, width))


def swap(x, bit):
    return lax.ppermute(x, "seq", [(i, i ^ bit) for i in range(4)])


def spread(own):
    far = swap(own, 2)
    return own, swap(own, 1), far, swap(far, 1)


def reduce_rows(near, far):
    got = swap(near, 1)
    across = swap(far[0] + got[1], 2)
    return got, across


def pick(step, refs, dest):
    for k, ref in enumerate(refs):

        @pl.when(step == k)
        def _(ref=ref):
            dest[...] = ref[...]


ORDER = (1, 3, 2, 0)


def rel_of(t):
    return jnp.where(t == 0, 1, jnp.where(t == 1, 3, jnp.where(t == 2, 2, 0)))


def qkv_body(scal, x0, x1, x2, x3, w, gain, shift, bias, h1, qkv, rows):
    pick(pl.program_id(0), (x0, x1, x2, x3), rows)
    unit, _ = normalize(rows[...].astype(f32))
    low = (unit * gain[...] + shift[...]).astype(bf16)
    h1[...] = low
    qkv[...] = (mm(low, w[...]) + bias[...]).astype(bf16)


def qkv_call(scal, pieces, w, gain, shift, bias):
    rows, width = pieces[0].shape
    cols = w.shape[1]
    out = lambda r, sc: (lax.bitwise_xor(sc[0], r), 0)
    return pl.pallas_call(
        qkv_body,
        out_shape=(
            jax.ShapeDtypeStruct((4 * rows, width), bf16),
            jax.ShapeDtypeStruct((4 * rows, cols), bf16),
        ),
        grid_spec=pltpu.PrefetchScalarGridSpec(
            num_scalar_prefetch=1,
            grid=(4,),
            in_specs=[WHOLE] * 8,
            out_specs=(pl.BlockSpec((rows, width), out), pl.BlockSpec((rows, cols), out)),
            scratch_shapes=[pltpu.VMEM((rows, width), bf16)],
        ),
        compiler_params=params(),
        name="qkv",
    )(scal, *pieces, w, gain, shift, bias)


def make_bias(scal, slopes, pair, bias, keys):
    pos = lax.broadcasted_iota(jnp.int32, (keys, LANES), 0)
    inside = pos < scal[1]
    ramp = pos.astype(f32)
    for h in range(2):
        bias[h] = jnp.where(inside, ramp * slopes[2 * pair + h], NEG)


def head_only(x, h):
    lane = lax.broadcasted_iota(jnp.int32, x.shape, 1)
    return jnp.where((lane >= h * HEAD_DIM) & (lane < (h + 1) * HEAD_DIM), x, jnp.zeros_like(x))


def score_t(k_ref, qm, bias, h, length):
    block = qm.shape[0]
    s = mm_t(k_ref[0:length, :], qm)
    b = bias[h, 0:length, :]
    s = s + jnp.concatenate([b] * (block // LANES), axis=1)
    key = lax.broadcasted_iota(jnp.int32, (block, block), 0)
    query = lax.broadcasted_iota(jnp.int32, (block, block), 1)
    last = jnp.where(key <= query, s[length - block :], NEG)
    if length == block:
        return last
    return jnp.concatenate([s[: length - block], last], axis=0)


def attend_body(scal, q, k, v, slopes, o, lse, bias, vt):
    pair, step = pl.program_id(0), pl.program_id(1)
    block = q.shape[0]
    keys = k.shape[0]

    @pl.when(step == 0)
    def _():
        make_bias(scal, slopes, pair, bias, keys)
        vt[...] = v[...].T

    for c in range(keys // block):

        @pl.when(step == c)
        def _(c=c):
            length = (c + 1) * block
            scaled = q[...] * bf16(HEAD_DIM**-0.5)
            outs, logs = [], []
            for h in range(2):
                s = score_t(k, head_only(scaled, h), bias, h, length)
                top = jnp.max(s, axis=0, keepdims=True)
                e = jnp.exp(s - top)
                total = jnp.sum(e, axis=0, keepdims=True)
                mixed = mm(vt[h * HEAD_DIM : (h + 1) * HEAD_DIM, 0:length], e.astype(bf16))
                outs.append(mixed / total)
                logs.append(top + jnp.log(total))
            o[...] = jnp.concatenate(outs, axis=0).T.astype(bf16)
            lse[0, 0:2, :] = jnp.concatenate(logs, axis=0)


def attend_call(scal, slopes, qkv, block):
    keys, cols = qkv.shape
    width = cols // 3
    pairs = width // LANES
    return pl.pallas_call(
        attend_body,
        out_shape=(
            jax.ShapeDtypeStruct((keys, width), bf16),
            jax.ShapeDtypeStruct((pairs, 8, keys), f32),
        ),
        grid_spec=pltpu.PrefetchScalarGridSpec(
            num_scalar_prefetch=1,
            grid=(pairs, keys // block),
            in_specs=[
                pl.BlockSpec((block, LANES), lambda p, c, sc: (c, p)),
                pl.BlockSpec((keys, LANES), lambda p, c, sc: (0, pairs + p)),
                pl.BlockSpec((keys, LANES), lambda p, c, sc: (0, 2 * pairs + p)),
                SCALAR,
            ],
            out_specs=(
                pl.BlockSpec((block, LANES), lambda p, c, sc: (c, p)),
                pl.BlockSpec((1, 8, block), lambda p, c, sc: (p, 0, c)),
            ),
            scratch_shapes=[
                pltpu.VMEM((2, keys, LANES), f32),
                pltpu.VMEM((LANES, keys), bf16),
            ],
        ),
        compiler_params=params(),
        name="attend",
    )(scal, qkv, qkv, qkv, slopes)


def attend_back_body(scal, q, k, v, o, do, lse, slopes, dq, dk, dv, bias, kt, dk_sum, dv_sum):
    pair, step = pl.program_id(0), pl.program_id(1)
    block = q.shape[0]
    keys = k.shape[0]
    scale = HEAD_DIM**-0.5

    @pl.when(step == 0)
    def _():
        make_bias(scal, slopes, pair, bias, keys)
        kt[...] = k[...].T
        dk_sum[...] = jnp.zeros_like(dk_sum)
        dv_sum[...] = jnp.zeros_like(dv_sum)

    for c in range(keys // block):

        @pl.when(step == c)
        def _(c=c):
            length = (c + 1) * block
            scaled = q[...] * bf16(scale)
            both = (do[...].astype(f32) * o[...].astype(f32)).T
            outs = []
            for h in range(2):
                qm = head_only(scaled, h)
                dom = head_only(do[...], h)
                dot_row = jnp.sum(both[h * HEAD_DIM : (h + 1) * HEAD_DIM], axis=0, keepdims=True)
                p = jnp.exp(score_t(k, qm, bias, h, length) - lse[0, h : h + 1, :])
                dp = mm_t(v[0:length, :], dom)
                ds = (p * (dp - dot_row)).astype(bf16)
                dv_sum[0:length, :] += mm(p.astype(bf16), dom)
                dk_sum[0:length, :] += mm(ds, qm)
                outs.append(mm(kt[h * HEAD_DIM : (h + 1) * HEAD_DIM, 0:length], ds))
            dq[...] = (jnp.concatenate(outs, axis=0).T * scale).astype(bf16)

    @pl.when(step == keys // block - 1)
    def _():
        dk[...] = dk_sum[...].astype(bf16)
        dv[...] = dv_sum[...].astype(bf16)


def attend_back_call(scal, slopes, qkv, o, do, lse, block):
    keys, cols = qkv.shape
    width = cols // 3
    pairs = width // LANES
    some = pl.BlockSpec((block, LANES), lambda p, c, sc: (c, p))
    full = pl.BlockSpec((keys, LANES), lambda p, c, sc: (0, p))
    return pl.pallas_call(
        attend_back_body,
        out_shape=(jax.ShapeDtypeStruct((keys, width), bf16),) * 3,
        grid_spec=pltpu.PrefetchScalarGridSpec(
            num_scalar_prefetch=1,
            grid=(pairs, keys // block),
            in_specs=[
                some,
                pl.BlockSpec((keys, LANES), lambda p, c, sc: (0, pairs + p)),
                pl.BlockSpec((keys, LANES), lambda p, c, sc: (0, 2 * pairs + p)),
                some,
                some,
                pl.BlockSpec((1, 8, block), lambda p, c, sc: (p, 0, c)),
                SCALAR,
            ],
            out_specs=(some, full, full),
            scratch_shapes=[
                pltpu.VMEM((2, keys, LANES), f32),
                pltpu.VMEM((LANES, keys), bf16),
                pltpu.VMEM((keys, LANES), f32),
                pltpu.VMEM((keys, LANES), f32),
            ],
        ),
        compiler_params=params(),
        name="attend_back",
    )(scal, qkv, qkv, qkv, o, do, lse, slopes)


def lay_columns(w_ref, first, dest):
    width = w_ref.shape[2]
    for d in range(w_ref.shape[0]):
        dest[:, d * width : (d + 1) * width] = w_ref[d, first : first + dest.shape[0], :]


def out_body(scal, o, w, near, far, flat, *, first):
    t = pl.program_id(0)

    @pl.when(t == 0)
    def _():
        lay_columns(w, first, flat)

    part = mm(o[...], flat[...]).astype(bf16)

    @pl.when(t < 2)
    def _():
        near[0] = part

    @pl.when(t >= 2)
    def _():
        far[0] = part


def near_map(t, *_):
    return (jnp.minimum(t, 1), 0, 0)


def far_map(t, *_):
    return (jnp.maximum(t - 2, 0), 0, 0)


def out_call(scal, o, w, first):
    keys, inner = o.shape
    rows = keys // 4
    width = w.shape[0] * w.shape[2]
    return pl.pallas_call(
        functools.partial(out_body, first=first),
        out_shape=(jax.ShapeDtypeStruct((2, rows, width), bf16),) * 2,
        grid_spec=pltpu.PrefetchScalarGridSpec(
            num_scalar_prefetch=1,
            grid=(4,),
            in_specs=[
                pl.BlockSpec((rows, inner), lambda t, sc: (lax.bitwise_xor(sc[0], rel_of(t)), 0)),
                WHOLE,
            ],
            out_specs=(
                pl.BlockSpec((1, rows, width), near_map),
                pl.BlockSpec((1, rows, width), far_map),
            ),
            scratch_shapes=[pltpu.VMEM((inner, width), bf16)],
        ),
        compiler_params=params(),
        name="out_proj",
    )(scal, o, w)


def mid_body(x, a, b, c, bias, gain, shift, mid, h2):
    value = x[...].astype(f32) + (
        (a[0].astype(f32) + b[0].astype(f32)) + c[...].astype(f32) + bias[...]
    )
    mid[...] = value
    unit, _ = normalize(value)
    h2[...] = (unit * gain[...] + shift[...]).astype(bf16)


def mid_call(x, a, b, c, bias, gain, shift):
    rows, width = x.shape
    one = pl.BlockSpec((rows // 2, width), lambda i: (i, 0))
    first = pl.BlockSpec((1, rows // 2, width), lambda i: (0, i, 0))
    second = pl.BlockSpec((1, rows // 2, width), lambda i: (1, i, 0))
    row = pl.BlockSpec((1, width), lambda i: (0, 0))
    return pl.pallas_call(
        mid_body,
        out_shape=(
            jax.ShapeDtypeStruct((rows, width), f32),
            jax.ShapeDtypeStruct((rows, width), bf16),
        ),
        grid=(2,),
        in_specs=[one, second, first, one, row, row, row],
        out_specs=(one, one),
        compiler_params=params(),
        name="mid_norm",
    )(x, a, b, c, bias, gain, shift)


def gelu_parts(u):
    root = math.sqrt(2.0 / math.pi)
    sq = u * u
    t = jnp.tanh(root * (u + GELU_COEF * (sq * u)))
    half = 0.5 * (1.0 + t)
    slope = half + 0.5 * u * (1.0 - t * t) * (root * (1.0 + 3.0 * GELU_COEF * sq))
    return u * half, slope


def mlp_body(
    h0, h1, h2, h3, g0, g1, g2, g3, w1, w2, b1,
    y_near, y_far, d_near, d_far, a_all, du_all, h_all, g_all, bias_sum,
    flat, hb, gb,
):
    t = pl.program_id(0)

    @pl.when(t == 0)
    def _():
        lay_columns(w2, 0, flat)
        bias_sum[...] = jnp.zeros_like(bias_sum)

    pick(rel_of(t), (h0, h1, h2, h3), hb)
    pick(rel_of(t), (g0, g1, g2, g3), gb)
    h_all[...] = hb[...]
    g_all[...] = gb[...]
    inner = w1.shape[1]
    chunk = 256
    for c in range(inner // chunk):
        cols = slice(c * chunk, (c + 1) * chunk)
        u = mm(hb[...], w1[:, cols]) + b1[:, cols]
        value, slope = gelu_parts(u)
        a_all[:, cols] = value.astype(bf16)
        du = (mm_t(gb[...], flat[cols, :]) * slope).astype(bf16)
        du_all[:, cols] = du
        bias_sum[:, cols] += jnp.sum(du.astype(f32), axis=0, keepdims=True)
    y = mm(a_all[...], flat[...]).astype(bf16)
    d = mm_t(du_all[...], w1[...]).astype(bf16)

    @pl.when(t < 2)
    def _():
        y_near[0] = y
        d_near[0] = d

    @pl.when(t >= 2)
    def _():
        y_far[0] = y
        d_far[0] = d


def mlp_call(h_pieces, g_pieces, w1, w2, b1):
    rows, width = h_pieces[0].shape
    inner = w1.shape[1]
    pair = jax.ShapeDtypeStruct((2, rows, width), bf16)
    near = pl.BlockSpec((1, rows, width), near_map)
    far = pl.BlockSpec((1, rows, width), far_map)
    block = lambda n: pl.BlockSpec((rows, n), lambda t: (t, 0))
    return pl.pallas_call(
        mlp_body,
        out_shape=(
            pair,
            pair,
            pair,
            pair,
            jax.ShapeDtypeStruct((4 * rows, inner), bf16),
            jax.ShapeDtypeStruct((4 * rows, inner), bf16),
            jax.ShapeDtypeStruct((4 * rows, width), bf16),
            jax.ShapeDtypeStruct((4 * rows, width), bf16),
            jax.ShapeDtypeStruct((1, inner), f32),
        ),
        grid=(4,),
        in_specs=[WHOLE] * 11,
        out_specs=(
            near, far, near, far, block(inner), block(inner), block(width), block(width),
            pl.BlockSpec((1, inner), lambda t: (0, 0)),
        ),
        scratch_shapes=[
            pltpu.VMEM((inner, width), bf16),
            pltpu.VMEM((rows, width), bf16),
            pltpu.VMEM((rows, width), bf16),
        ],
        compiler_params=params(),
        name="mlp",
    )(*h_pieces, *g_pieces, w1, w2, b1)


def outer_body(left, right, out, turned, *, blocks):
    @pl.when(pl.program_id(0) == 0)
    def _():
        turned[...] = left[...].T

    part = mm(turned[...], right[...]).astype(bf16)
    if blocks:
        width = out.shape[2]
        for d in range(out.shape[0]):
            out[d] = part[:, d * width : (d + 1) * width]
    else:
        out[...] = part


def outer_call(left, right, parts, name):
    rows, m = left.shape
    n = right.shape[1]
    step = 256
    if parts > 1:
        width = n // parts
        out_shape = jax.ShapeDtypeStruct((parts, m, width), bf16)
        out_spec = pl.BlockSpec((step // width, m, width), lambda j: (j, 0, 0))
    else:
        out_shape = jax.ShapeDtypeStruct((m, n), bf16)
        out_spec = pl.BlockSpec((m, step), lambda j: (0, j))
    return pl.pallas_call(
        functools.partial(outer_body, blocks=parts > 1),
        out_shape=out_shape,
        grid=(n // step,),
        in_specs=[WHOLE, pl.BlockSpec((rows, step), lambda j: (0, j))],
        out_specs=out_spec,
        scratch_shapes=[pltpu.VMEM((m, rows), bf16)],
        compiler_params=params(),
        name=name,
    )(left, right)


def mid_back_body(mid, a, b, c, g, gain, dmid, dbr, sums):
    @pl.when(pl.program_id(0) == 0)
    def _():
        sums[...] = jnp.zeros_like(sums)

    unit, inv = normalize(mid[...])
    e = (a[0].astype(f32) + b[0].astype(f32)) + c[...].astype(f32)
    grad = g[...].astype(f32)
    value = grad + norm_back(e, gain[...], unit, inv)
    dmid[...] = value
    low = value.astype(bf16)
    dbr[...] = low
    sums[0:1, :] += jnp.sum(e * unit, axis=0, keepdims=True)
    sums[1:2, :] += jnp.sum(e, axis=0, keepdims=True)
    sums[2:3, :] += jnp.sum(low.astype(f32), axis=0, keepdims=True)
    sums[3:4, :] += jnp.sum(grad, axis=0, keepdims=True)


def mid_back_call(mid, a, b, c, g, gain):
    rows, width = mid.shape
    one = pl.BlockSpec((rows // 2, width), lambda i: (i, 0))
    first = pl.BlockSpec((1, rows // 2, width), lambda i: (0, i, 0))
    second = pl.BlockSpec((1, rows // 2, width), lambda i: (1, i, 0))
    row = pl.BlockSpec((1, width), lambda i: (0, 0))
    return pl.pallas_call(
        mid_back_body,
        out_shape=(
            jax.ShapeDtypeStruct((rows, width), f32),
            jax.ShapeDtypeStruct((rows, width), bf16),
            jax.ShapeDtypeStruct((8, width), f32),
        ),
        grid=(2,),
        in_specs=[one, second, first, one, one, row],
        out_specs=(one, one, pl.BlockSpec((8, width), lambda i: (0, 0))),
        compiler_params=params(),
        name="mid_back",
    )(mid, a, b, c, g, gain)


def out_back_body(scal, b0, b1, b2, b3, o, w, do, grad, flat, rows, total, *, first):
    r = pl.program_id(0)

    @pl.when(r == 0)
    def _():
        lay_columns(w, first, flat)
        total[...] = jnp.zeros_like(total)

    pick(r, (b0, b1, b2, b3), rows)
    do[...] = mm_t(rows[...], flat[...]).astype(bf16)
    total[...] += mm(o[...].T, rows[...])

    @pl.when(r == 3)
    def _():
        width = grad.shape[2]
        for d in range(grad.shape[0]):
            grad[d] = total[:, d * width : (d + 1) * width].astype(bf16)


def out_back_call(scal, pieces, o, w, first):
    rows, width = pieces[0].shape
    inner = o.shape[1]
    at = pl.BlockSpec((rows, inner), lambda r, sc: (lax.bitwise_xor(sc[0], r), 0))
    grad = (w.shape[0], inner, w.shape[2])
    return pl.pallas_call(
        functools.partial(out_back_body, first=first),
        out_shape=(jax.ShapeDtypeStruct(o.shape, bf16), jax.ShapeDtypeStruct(grad, bf16)),
        grid_spec=pltpu.PrefetchScalarGridSpec(
            num_scalar_prefetch=1,
            grid=(4,),
            in_specs=[WHOLE] * 4 + [at, WHOLE],
            out_specs=(at, pl.BlockSpec(grad, lambda r, sc: (0, 0, 0))),
            scratch_shapes=[
                pltpu.VMEM((inner, width), bf16),
                pltpu.VMEM((rows, width), bf16),
                pltpu.VMEM((inner, width), f32),
            ],
        ),
        compiler_params=params(),
        name="out_back",
    )(scal, *pieces, o, w)


def qkv_back_body(scal, dq, dk, dv, w, near, far, merged, sums):
    t = pl.program_id(0)

    @pl.when(t == 0)
    def _():
        sums[...] = jnp.zeros_like(sums)

    low = jnp.concatenate([dq[...], dk[...], dv[...]], axis=1)
    merged[...] = low
    part = mm_t(low, w[...]).astype(bf16)
    sums[...] += jnp.sum(low.astype(f32), axis=0, keepdims=True)

    @pl.when(t < 2)
    def _():
        near[0] = part

    @pl.when(t >= 2)
    def _():
        far[0] = part


def qkv_back_call(scal, dq, dk, dv, w):
    keys, inner = dq.shape
    rows = keys // 4
    width = w.shape[0]
    where = lambda t, sc: (lax.bitwise_xor(sc[0], rel_of(t)), 0)
    at = pl.BlockSpec((rows, inner), where)
    return pl.pallas_call(
        qkv_back_body,
        out_shape=(
            jax.ShapeDtypeStruct((2, rows, width), bf16),
            jax.ShapeDtypeStruct((2, rows, width), bf16),
            jax.ShapeDtypeStruct((keys, 3 * inner), bf16),
            jax.ShapeDtypeStruct((1, 3 * inner), f32),
        ),
        grid_spec=pltpu.PrefetchScalarGridSpec(
            num_scalar_prefetch=1,
            grid=(4,),
            in_specs=[at, at, at, WHOLE],
            out_specs=(
                pl.BlockSpec((1, rows, width), near_map),
                pl.BlockSpec((1, rows, width), far_map),
                pl.BlockSpec((rows, 3 * inner), where),
                pl.BlockSpec((1, 3 * inner), lambda t, sc: (0, 0)),
            ),
        ),
        compiler_params=params(),
        name="qkv_back",
    )(scal, dq, dk, dv, w)


def in_back_body(x, a, b, c, dmid, gain, grad, sums):
    @pl.when(pl.program_id(0) == 0)
    def _():
        sums[...] = jnp.zeros_like(sums)

    unit, inv = normalize(x[...].astype(f32))
    e = (a[0].astype(f32) + b[0].astype(f32)) + c[...].astype(f32)
    grad[...] = (dmid[...] + norm_back(e, gain[...], unit, inv)).astype(bf16)
    sums[0:1, :] += jnp.sum(e * unit, axis=0, keepdims=True)
    sums[1:2, :] += jnp.sum(e, axis=0, keepdims=True)


def in_back_call(x, a, b, c, dmid, gain):
    rows, width = x.shape
    one = pl.BlockSpec((rows // 2, width), lambda i: (i, 0))
    first = pl.BlockSpec((1, rows // 2, width), lambda i: (0, i, 0))
    second = pl.BlockSpec((1, rows // 2, width), lambda i: (1, i, 0))
    row = pl.BlockSpec((1, width), lambda i: (0, 0))
    return pl.pallas_call(
        in_back_body,
        out_shape=(
            jax.ShapeDtypeStruct((rows, width), bf16),
            jax.ShapeDtypeStruct((8, width), f32),
        ),
        grid=(2,),
        in_specs=[one, second, first, one, one, row],
        out_specs=(one, pl.BlockSpec((8, width), lambda i: (0, 0))),
        compiler_params=params(),
        name="in_back",
    )(x, a, b, c, dmid, gain)


def after(value, *others):
    return lax.optimization_barrier((value, *others))[0]


def on_device(
    dp_n,
    seq_n,
    tokens,
    lengths,
    cotangent,
    ln1_gain,
    ln1_shift,
    w_qkv,
    b_qv,
    w_out,
    b_out,
    ln2_gain,
    ln2_shift,
    w_fc1,
    b_fc1,
    w_fc2,
    b_fc2,
):
    count = dp_n * seq_n
    rows, width = tokens.shape
    heads = width // HEAD_DIM
    inner = w_out.shape[0]
    ff = w_fc1.shape[1]
    s = lax.axis_index("seq")
    length = lengths[0]

    wq = lax.all_gather(
        jnp.concatenate([w_qkv[:, c, :] for c in range(3)], axis=1), "dp", axis=0, tiled=True
    )
    col = w_fc2.shape[1]
    both = jnp.concatenate([w_fc2, w_out], axis=0)
    if col % LANES == 0:
        parts = dp_n
        w_cols = lax.all_gather(both, "dp", axis=0, tiled=False)
    else:
        parts = 1
        w_cols = lax.all_gather(both, "dp", axis=1, tiled=True)[None]
    w1 = lax.all_gather(w_fc1, "dp", axis=0, tiled=True)

    small = (ln1_gain, ln1_shift, b_qv, b_out, ln2_gain, ln2_shift, b_fc1, b_fc2)
    sizes = [v.shape[0] for v in small]
    ends = [sum(sizes[: i + 1]) for i in range(len(sizes))]
    packed = small_gather(jnp.concatenate([v.astype(f32) for v in small]), count, seq_n)
    packed = packed.reshape(count, ends[-1])
    gain1, shift1, bias_qv, bias_out, gain2, shift2, bias_up, bias_down = (
        packed[:, e - n : e].reshape(1, count * n) for e, n in zip(ends, sizes)
    )

    scal = jnp.stack([s.astype(jnp.int32), length])
    slopes = 2.0 ** (-8.0 * (jnp.arange(heads, dtype=jnp.int32) + 1).astype(f32) / heads)
    slopes = lax.dynamic_slice(slopes, (s * (heads // seq_n),), (heads // seq_n,))
    own_bias = lambda v, n: lax.dynamic_slice(v, (0, s * n), (1, n))
    qkv_bias = jnp.concatenate(
        [
            own_bias(bias_qv[:, :width], inner),
            jnp.zeros((1, inner), f32),
            own_bias(bias_qv[:, width:], inner),
        ],
        axis=1,
    )

    x_pieces = spread(tokens)
    valid = s * rows + jnp.arange(rows, dtype=jnp.int32) < length
    grad_low = jnp.where(valid[:, None], cotangent, jnp.zeros_like(cotangent))
    g_pieces = spread(after(grad_low, x_pieces[3]))

    block = 256
    h1, qkv = qkv_call(scal, x_pieces, wq, gain1, shift1, qkv_bias)
    o, lse = attend_call(scal, slopes, qkv, block)
    near, far = out_call(scal, o, w_cols, ff)
    got, across = reduce_rows(near, far)
    mid, h2 = mid_call(tokens, far, got, across, bias_out, gain2, shift2)
    h_pieces = spread(h2)
    y_near, y_far, d_near, d_far, a_all, du_all, h_all, g_all, up_sum = mlp_call(
        h_pieces, g_pieces, w1, w_cols, own_bias(bias_up, ff)
    )
    got, across = reduce_rows(d_near, d_far)
    grad_down = outer_call(a_all, g_all, parts, "grad_fc2")
    grad_up = outer_call(h_all, du_all, 1, "grad_fc1")
    dmid, dbr, mid_sums = mid_back_call(mid, d_far, got, across, grad_low, gain2)
    b_pieces = spread(dbr)

    y_near = after(y_near, b_pieces[3])
    got, across = reduce_rows(y_near, y_far)
    output = (
        mid + ((y_far[1].astype(f32) + got[0].astype(f32)) + across.astype(f32) + bias_down)
    ).astype(bf16)

    do, grad_out = out_back_call(scal, b_pieces, o, w_cols, ff)
    dq, dk, dv = attend_back_call(scal, slopes, qkv, o, do, lse, block)
    near, far, merged, qkv_sums = qkv_back_call(scal, dq, dk, dv, wq)
    got, across = reduce_rows(near, far)
    grad_qkv = outer_call(h1, merged, 1, "grad_qkv")
    grad_tokens, in_sums = in_back_call(tokens, far, got, across, dmid, gain1)

    def shared(part):
        if parts > 1:
            return lax.psum_scatter(part, "dp", scatter_dimension=0, tiled=False).astype(f32)
        return lax.psum_scatter(part, "dp", scatter_dimension=1, tiled=True).astype(f32)

    grad_down = shared(grad_down if parts > 1 else grad_down)
    grad_up = lax.psum_scatter(grad_up, "dp", scatter_dimension=0, tiled=True).astype(f32)
    grad_out = shared(grad_out if parts > 1 else grad_out[0])
    grad_qkv = lax.psum_scatter(grad_qkv, "dp", scatter_dimension=0, tiled=True)
    grad_qkv = grad_qkv.astype(f32).reshape(w_qkv.shape)

    def own_slot(v, total):
        return lax.dynamic_update_slice(jnp.zeros((1, total), f32), v, (0, s * v.shape[1]))

    sums = (
        in_sums[0:1],
        in_sums[1:2],
        jnp.concatenate(
            [own_slot(qkv_sums[:, :inner], width), own_slot(qkv_sums[:, 2 * inner :], width)], axis=1
        ),
        mid_sums[2:3],
        mid_sums[0:1],
        mid_sums[1:2],
        own_slot(up_sum, seq_n * ff),
        mid_sums[3:4],
    )
    grads = jnp.concatenate([v.reshape(count, n) for v, n in zip(sums, sizes)], axis=1)
    grads = small_scatter(grads, count, seq_n).reshape(ends[-1])
    g_gain1, g_shift1, g_qv, g_bout, g_gain2, g_shift2, g_up, g_down = (
        grads[e - n : e] for e, n in zip(ends, sizes)
    )
    return (
        output,
        grad_tokens,
        g_gain1,
        g_shift1,
        grad_qkv,
        g_qv,
        grad_out,
        g_bout,
        g_gain2,
        g_shift2,
        grad_up,
        g_up,
        grad_down,
        g_down,
    )


def solution(mesh):
    rows = P(("dp", "seq"), None)
    vec = P(("dp", "seq"))
    merged = P("dp", None, "seq")
    return jax.shard_map(
        functools.partial(on_device, mesh.shape["dp"], mesh.shape["seq"]),
        mesh=mesh,
        in_specs=(
            rows, P("dp"), rows, vec, vec, merged, vec, P("seq", "dp"), vec, vec, vec,
            P("dp", "seq"), vec, P("seq", "dp"), vec,
        ),
        out_specs=(
            rows, rows, vec, vec, merged, vec, P("seq", "dp"), vec, vec, vec,
            P("dp", "seq"), vec, P("seq", "dp"), vec,
        ),
        check_vma=False,
    )
```

```python
import functools
import math

import jax
import jax.numpy as jnp
from jax import lax
from jax.experimental import pallas as pl
from jax.experimental.pallas import tpu as pltpu
from jax.sharding import PartitionSpec as P

HEAD_DIM = 64
EPS = 1e-05
GELU_COEF = 0.044715
NEG = -1e30
LANES = 128
VMEM_BYTES = 60 * 1024 * 1024

f32 = jnp.float32
bf16 = jnp.bfloat16
WHOLE = pl.BlockSpec(memory_space=pltpu.VMEM)
SCALAR = pl.BlockSpec(memory_space=pltpu.SMEM)


def mm(a, b):
    return jnp.dot(a, b, preferred_element_type=f32)


def mm_t(a, b):
    return lax.dot_general(a, b, (((1,), (1,)), ((), ())), preferred_element_type=f32)


def params(**kw):
    return pltpu.CompilerParams(vmem_limit_bytes=VMEM_BYTES, **kw)


def normalize(v):
    width = v.shape[-1]
    centred = v - jnp.sum(v, axis=-1, keepdims=True) * (1.0 / width)
    inv = lax.rsqrt(jnp.sum(centred * centred, axis=-1, keepdims=True) * (1.0 / width) + EPS)
    return centred * inv, inv


def norm_back(grad_out, gain, unit, inv):
    width = unit.shape[-1]
    scaled = grad_out * gain
    mean_one = jnp.sum(scaled, axis=-1, keepdims=True) * (1.0 / width)
    mean_two = jnp.sum(scaled * unit, axis=-1, keepdims=True) * (1.0 / width)
    return inv * (scaled - mean_one - unit * mean_two)


def device_of(index, seq_n):
    return (index // seq_n, index % seq_n)


def greet_all(me, count, seq_n):
    barrier = pltpu.get_barrier_semaphore()

    def hello(i, carry):
        peer = (me + i) % count
        pl.semaphore_signal(
            barrier, inc=1, device_id=device_of(peer, seq_n), device_id_type=pl.DeviceIdType.MESH
        )
        return carry

    lax.fori_loop(1, count, hello, 0)
    pl.semaphore_wait(barrier, count - 1)


def small_gather_body(count, seq_n, x_ref, out_ref, send_sem, recv_sem):
    me = lax.axis_index("dp") * seq_n + lax.axis_index("seq")
    greet_all(me, count, seq_n)

    def copy_to(i):
        peer = (me + i) % count
        return pltpu.make_async_remote_copy(
            src_ref=x_ref,
            dst_ref=out_ref.at[pl.ds(me, 1)],
            send_sem=send_sem.at[i],
            recv_sem=recv_sem.at[i],
            device_id=device_of(peer, seq_n),
            device_id_type=pl.DeviceIdType.MESH,
        )

    def begin(i, carry):
        copy_to(i).start()
        return carry

    def finish(i, carry):
        copy_to(i).wait()
        return carry

    lax.fori_loop(1, count, begin, 0)
    out_ref[pl.ds(me, 1)] = x_ref[...]
    lax.fori_loop(1, count, finish, 0)


def small_gather(x, count, seq_n):
    width = x.shape[-1]
    return pl.pallas_call(
        functools.partial(small_gather_body, count, seq_n),
        out_shape=jax.ShapeDtypeStruct((count, 1, width), f32),
        in_specs=[WHOLE],
        out_specs=WHOLE,
        scratch_shapes=[pltpu.SemaphoreType.DMA((count,)), pltpu.SemaphoreType.DMA((count,))],
        compiler_params=pltpu.CompilerParams(collective_id=1, has_side_effects=True),
        name="small_gather",
    )(x.reshape(1, 1, width))


def small_scatter_body(count, seq_n, v_ref, out_ref, land, send_sem, recv_sem):
    me = lax.axis_index("dp") * seq_n + lax.axis_index("seq")
    greet_all(me, count, seq_n)

    def copy_to(i):
        peer = (me + i) % count
        return pltpu.make_async_remote_copy(
            src_ref=v_ref.at[pl.ds(peer, 1)],
            dst_ref=land.at[pl.ds(i, 1)],
            send_sem=send_sem.at[i],
            recv_sem=recv_sem.at[i],
            device_id=device_of(peer, seq_n),
            device_id_type=pl.DeviceIdType.MESH,
        )

    def begin(i, carry):
        copy_to(i).start()
        return carry

    def finish(i, total):
        copy_to(i).wait()
        return total + land[pl.ds(i, 1)]

    lax.fori_loop(1, count, begin, 0)
    out_ref[...] = lax.fori_loop(1, count, finish, v_ref[pl.ds(me, 1)])


def small_scatter(v, count, seq_n):
    width = v.shape[-1]
    return pl.pallas_call(
        functools.partial(small_scatter_body, count, seq_n),
        out_shape=jax.ShapeDtypeStruct((1, 1, width), f32),
        in_specs=[WHOLE],
        out_specs=WHOLE,
        scratch_shapes=[
            pltpu.VMEM((count, 1, width), f32),
            pltpu.SemaphoreType.DMA((count,)),
            pltpu.SemaphoreType.DMA((count,)),
        ],
        compiler_params=pltpu.CompilerParams(collective_id=2, has_side_effects=True),
        name="small_scatter",
    )(v.reshape(count, 1, width))


def swap(x, bit):
    return lax.ppermute(x, "seq", [(i, i ^ bit) for i in range(4)])


def spread(own):
    far = swap(own, 2)
    return own, swap(own, 1), far, swap(far, 1)


def reduce_rows(near, far):
    got = swap(near, 1)
    across = swap(far[0] + got[1], 2)
    return got, across


def pick(step, refs, dest):
    for k, ref in enumerate(refs):

        @pl.when(step == k)
        def _(ref=ref):
            dest[...] = ref[...]


ORDER = (1, 3, 2, 0)


def rel_of(t):
    return jnp.where(t == 0, 1, jnp.where(t == 1, 3, jnp.where(t == 2, 2, 0)))


def qkv_body(scal, x0, x1, x2, x3, w, gain, shift, bias, h1, qkv, rows):
    pick(pl.program_id(0), (x0, x1, x2, x3), rows)
    unit, _ = normalize(rows[...].astype(f32))
    low = (unit * gain[...] + shift[...]).astype(bf16)
    h1[...] = low
    qkv[...] = (mm(low, w[...]) + bias[...]).astype(bf16)


def qkv_call(scal, pieces, w, gain, shift, bias):
    rows, width = pieces[0].shape
    cols = w.shape[1]
    out = lambda r, sc: (lax.bitwise_xor(sc[0], r), 0)
    return pl.pallas_call(
        qkv_body,
        out_shape=(
            jax.ShapeDtypeStruct((4 * rows, width), bf16),
            jax.ShapeDtypeStruct((4 * rows, cols), bf16),
        ),
        grid_spec=pltpu.PrefetchScalarGridSpec(
            num_scalar_prefetch=1,
            grid=(4,),
            in_specs=[WHOLE] * 8,
            out_specs=(pl.BlockSpec((rows, width), out), pl.BlockSpec((rows, cols), out)),
            scratch_shapes=[pltpu.VMEM((rows, width), bf16)],
        ),
        compiler_params=params(),
        name="qkv",
    )(scal, *pieces, w, gain, shift, bias)


def make_bias(scal, slopes, pair, bias, keys):
    pos = lax.broadcasted_iota(jnp.int32, (keys, LANES), 0)
    inside = pos < scal[1]
    ramp = pos.astype(f32)
    for h in range(2):
        bias[h] = jnp.where(inside, ramp * slopes[2 * pair + h], NEG)


def head_only(x, h):
    lane = lax.broadcasted_iota(jnp.int32, x.shape, 1)
    return jnp.where((lane >= h * HEAD_DIM) & (lane < (h + 1) * HEAD_DIM), x, jnp.zeros_like(x))


def score_t(k_ref, qm, bias, h, length):
    block = qm.shape[0]
    s = mm_t(k_ref[0:length, :], qm)
    b = bias[h, 0:length, :]
    s = s + jnp.concatenate([b] * (block // LANES), axis=1)
    key = lax.broadcasted_iota(jnp.int32, (block, block), 0)
    query = lax.broadcasted_iota(jnp.int32, (block, block), 1)
    last = jnp.where(key <= query, s[length - block :], NEG)
    if length == block:
        return last
    return jnp.concatenate([s[: length - block], last], axis=0)


def attend_body(scal, q, k, v, slopes, o, lse, bias, vt):
    pair, step = pl.program_id(0), pl.program_id(1)
    block = q.shape[0]
    keys = k.shape[0]

    @pl.when(step == 0)
    def _():
        make_bias(scal, slopes, pair, bias, keys)
        vt[...] = v[...].T

    for c in range(keys // block):

        @pl.when(step == c)
        def _(c=c):
            length = (c + 1) * block
            scaled = q[...] * bf16(HEAD_DIM**-0.5)
            outs, logs = [], []
            for h in range(2):
                s = score_t(k, head_only(scaled, h), bias, h, length)
                top = jnp.max(s, axis=0, keepdims=True)
                e = jnp.exp(s - top)
                total = jnp.sum(e, axis=0, keepdims=True)
                mixed = mm(vt[h * HEAD_DIM : (h + 1) * HEAD_DIM, 0:length], e.astype(bf16))
                outs.append(mixed / total)
                logs.append(top + jnp.log(total))
            o[...] = jnp.concatenate(outs, axis=0).T.astype(bf16)
            lse[0, 0:2, :] = jnp.concatenate(logs, axis=0)


def attend_call(scal, slopes, qkv, block):
    keys, cols = qkv.shape
    width = cols // 3
    pairs = width // LANES
    return pl.pallas_call(
        attend_body,
        out_shape=(
            jax.ShapeDtypeStruct((keys, width), bf16),
            jax.ShapeDtypeStruct((pairs, 8, keys), f32),
        ),
        grid_spec=pltpu.PrefetchScalarGridSpec(
            num_scalar_prefetch=1,
            grid=(pairs, keys // block),
            in_specs=[
                pl.BlockSpec((block, LANES), lambda p, c, sc: (c, p)),
                pl.BlockSpec((keys, LANES), lambda p, c, sc: (0, pairs + p)),
                pl.BlockSpec((keys, LANES), lambda p, c, sc: (0, 2 * pairs + p)),
                SCALAR,
            ],
            out_specs=(
                pl.BlockSpec((block, LANES), lambda p, c, sc: (c, p)),
                pl.BlockSpec((1, 8, block), lambda p, c, sc: (p, 0, c)),
            ),
            scratch_shapes=[
                pltpu.VMEM((2, keys, LANES), f32),
                pltpu.VMEM((LANES, keys), bf16),
            ],
        ),
        compiler_params=params(),
        name="attend",
    )(scal, qkv, qkv, qkv, slopes)


def attend_back_body(scal, q, k, v, o, do, lse, slopes, dq, dk, dv, bias, kt, dk_sum, dv_sum):
    pair, step = pl.program_id(0), pl.program_id(1)
    block = q.shape[0]
    keys = k.shape[0]
    scale = HEAD_DIM**-0.5

    @pl.when(step == 0)
    def _():
        make_bias(scal, slopes, pair, bias, keys)
        kt[...] = k[...].T
        dk_sum[...] = jnp.zeros_like(dk_sum)
        dv_sum[...] = jnp.zeros_like(dv_sum)

    for c in range(keys // block):

        @pl.when(step == c)
        def _(c=c):
            length = (c + 1) * block
            scaled = q[...] * bf16(scale)
            both = (do[...].astype(f32) * o[...].astype(f32)).T
            outs = []
            for h in range(2):
                qm = head_only(scaled, h)
                dom = head_only(do[...], h)
                dot_row = jnp.sum(both[h * HEAD_DIM : (h + 1) * HEAD_DIM], axis=0, keepdims=True)
                p = jnp.exp(score_t(k, qm, bias, h, length) - lse[0, h : h + 1, :])
                dp = mm_t(v[0:length, :], dom)
                ds = (p * (dp - dot_row)).astype(bf16)
                dv_sum[0:length, :] += mm(p.astype(bf16), dom)
                dk_sum[0:length, :] += mm(ds, qm)
                outs.append(mm(kt[h * HEAD_DIM : (h + 1) * HEAD_DIM, 0:length], ds))
            dq[...] = (jnp.concatenate(outs, axis=0).T * scale).astype(bf16)

    @pl.when(step == keys // block - 1)
    def _():
        dk[...] = dk_sum[...].astype(bf16)
        dv[...] = dv_sum[...].astype(bf16)


def attend_back_call(scal, slopes, qkv, o, do, lse, block):
    keys, cols = qkv.shape
    width = cols // 3
    pairs = width // LANES
    some = pl.BlockSpec((block, LANES), lambda p, c, sc: (c, p))
    full = pl.BlockSpec((keys, LANES), lambda p, c, sc: (0, p))
    return pl.pallas_call(
        attend_back_body,
        out_shape=(jax.ShapeDtypeStruct((keys, width), bf16),) * 3,
        grid_spec=pltpu.PrefetchScalarGridSpec(
            num_scalar_prefetch=1,
            grid=(pairs, keys // block),
            in_specs=[
                some,
                pl.BlockSpec((keys, LANES), lambda p, c, sc: (0, pairs + p)),
                pl.BlockSpec((keys, LANES), lambda p, c, sc: (0, 2 * pairs + p)),
                some,
                some,
                pl.BlockSpec((1, 8, block), lambda p, c, sc: (p, 0, c)),
                SCALAR,
            ],
            out_specs=(some, full, full),
            scratch_shapes=[
                pltpu.VMEM((2, keys, LANES), f32),
                pltpu.VMEM((LANES, keys), bf16),
                pltpu.VMEM((keys, LANES), f32),
                pltpu.VMEM((keys, LANES), f32),
            ],
        ),
        compiler_params=params(),
        name="attend_back",
    )(scal, qkv, qkv, qkv, o, do, lse, slopes)


def lay_columns(w_ref, first, dest):
    width = w_ref.shape[2]
    for d in range(w_ref.shape[0]):
        dest[:, d * width : (d + 1) * width] = w_ref[d, first : first + dest.shape[0], :]


def out_body(scal, o, w, near, far, flat, *, first):
    t = pl.program_id(0)

    @pl.when(t == 0)
    def _():
        lay_columns(w, first, flat)

    part = mm(o[...], flat[...]).astype(bf16)

    @pl.when(t < 2)
    def _():
        near[0] = part

    @pl.when(t >= 2)
    def _():
        far[0] = part


def near_map(t, *_):
    return (jnp.minimum(t, 1), 0, 0)


def far_map(t, *_):
    return (jnp.maximum(t - 2, 0), 0, 0)


def out_call(scal, o, w, first):
    keys, inner = o.shape
    rows = keys // 4
    width = w.shape[0] * w.shape[2]
    return pl.pallas_call(
        functools.partial(out_body, first=first),
        out_shape=(jax.ShapeDtypeStruct((2, rows, width), bf16),) * 2,
        grid_spec=pltpu.PrefetchScalarGridSpec(
            num_scalar_prefetch=1,
            grid=(4,),
            in_specs=[
                pl.BlockSpec((rows, inner), lambda t, sc: (lax.bitwise_xor(sc[0], rel_of(t)), 0)),
                WHOLE,
            ],
            out_specs=(
                pl.BlockSpec((1, rows, width), near_map),
                pl.BlockSpec((1, rows, width), far_map),
            ),
            scratch_shapes=[pltpu.VMEM((inner, width), bf16)],
        ),
        compiler_params=params(),
        name="out_proj",
    )(scal, o, w)


def mid_body(x, a, b, c, bias, gain, shift, mid, h2):
    value = x[...].astype(f32) + (
        (a[0].astype(f32) + b[0].astype(f32)) + c[...].astype(f32) + bias[...]
    )
    mid[...] = value
    unit, _ = normalize(value)
    h2[...] = (unit * gain[...] + shift[...]).astype(bf16)


def mid_call(x, a, b, c, bias, gain, shift):
    rows, width = x.shape
    one = pl.BlockSpec((rows // 2, width), lambda i: (i, 0))
    first = pl.BlockSpec((1, rows // 2, width), lambda i: (0, i, 0))
    second = pl.BlockSpec((1, rows // 2, width), lambda i: (1, i, 0))
    row = pl.BlockSpec((1, width), lambda i: (0, 0))
    return pl.pallas_call(
        mid_body,
        out_shape=(
            jax.ShapeDtypeStruct((rows, width), f32),
            jax.ShapeDtypeStruct((rows, width), bf16),
        ),
        grid=(2,),
        in_specs=[one, second, first, one, row, row, row],
        out_specs=(one, one),
        compiler_params=params(),
        name="mid_norm",
    )(x, a, b, c, bias, gain, shift)


def gelu_parts(u):
    root = math.sqrt(2.0 / math.pi)
    sq = u * u
    t = jnp.tanh(root * (u + GELU_COEF * (sq * u)))
    half = 0.5 * (1.0 + t)
    slope = half + 0.5 * u * (1.0 - t * t) * (root * (1.0 + 3.0 * GELU_COEF * sq))
    return u * half, slope


def mlp_body(
    h0, h1, h2, h3, g0, g1, g2, g3, w1, w2, b1,
    y_near, y_far, d_near, d_far, a_all, du_all, h_all, g_all, bias_sum,
    flat, hb, gb,
):
    t = pl.program_id(0)

    @pl.when(t == 0)
    def _():
        lay_columns(w2, 0, flat)
        bias_sum[...] = jnp.zeros_like(bias_sum)

    pick(rel_of(t), (h0, h1, h2, h3), hb)
    pick(rel_of(t), (g0, g1, g2, g3), gb)
    h_all[...] = hb[...]
    g_all[...] = gb[...]
    inner = w1.shape[1]
    chunk = 256
    for c in range(inner // chunk):
        cols = slice(c * chunk, (c + 1) * chunk)
        u = mm(hb[...], w1[:, cols]) + b1[:, cols]
        value, slope = gelu_parts(u)
        a_all[:, cols] = value.astype(bf16)
        du = (mm_t(gb[...], flat[cols, :]) * slope).astype(bf16)
        du_all[:, cols] = du
        bias_sum[:, cols] += jnp.sum(du.astype(f32), axis=0, keepdims=True)
    y = mm(a_all[...], flat[...]).astype(bf16)
    d = mm_t(du_all[...], w1[...]).astype(bf16)

    @pl.when(t < 2)
    def _():
        y_near[0] = y
        d_near[0] = d

    @pl.when(t >= 2)
    def _():
        y_far[0] = y
        d_far[0] = d


def mlp_call(h_pieces, g_pieces, w1, w2, b1):
    rows, width = h_pieces[0].shape
    inner = w1.shape[1]
    pair = jax.ShapeDtypeStruct((2, rows, width), bf16)
    near = pl.BlockSpec((1, rows, width), near_map)
    far = pl.BlockSpec((1, rows, width), far_map)
    block = lambda n: pl.BlockSpec((rows, n), lambda t: (t, 0))
    return pl.pallas_call(
        mlp_body,
        out_shape=(
            pair,
            pair,
            pair,
            pair,
            jax.ShapeDtypeStruct((4 * rows, inner), bf16),
            jax.ShapeDtypeStruct((4 * rows, inner), bf16),
            jax.ShapeDtypeStruct((4 * rows, width), bf16),
            jax.ShapeDtypeStruct((4 * rows, width), bf16),
            jax.ShapeDtypeStruct((1, inner), f32),
        ),
        grid=(4,),
        in_specs=[WHOLE] * 11,
        out_specs=(
            near, far, near, far, block(inner), block(inner), block(width), block(width),
            pl.BlockSpec((1, inner), lambda t: (0, 0)),
        ),
        scratch_shapes=[
            pltpu.VMEM((inner, width), bf16),
            pltpu.VMEM((rows, width), bf16),
            pltpu.VMEM((rows, width), bf16),
        ],
        compiler_params=params(),
        name="mlp",
    )(*h_pieces, *g_pieces, w1, w2, b1)


def outer_body(left, right, out, turned, *, blocks):
    @pl.when(pl.program_id(0) == 0)
    def _():
        turned[...] = left[...].T

    part = mm(turned[...], right[...]).astype(bf16)
    if blocks:
        width = out.shape[2]
        for d in range(out.shape[0]):
            out[d] = part[:, d * width : (d + 1) * width]
    else:
        out[...] = part


def outer_call(left, right, parts, name):
    rows, m = left.shape
    n = right.shape[1]
    step = 256
    if parts > 1:
        width = n // parts
        out_shape = jax.ShapeDtypeStruct((parts, m, width), bf16)
        out_spec = pl.BlockSpec((step // width, m, width), lambda j: (j, 0, 0))
    else:
        out_shape = jax.ShapeDtypeStruct((m, n), bf16)
        out_spec = pl.BlockSpec((m, step), lambda j: (0, j))
    return pl.pallas_call(
        functools.partial(outer_body, blocks=parts > 1),
        out_shape=out_shape,
        grid=(n // step,),
        in_specs=[WHOLE, pl.BlockSpec((rows, step), lambda j: (0, j))],
        out_specs=out_spec,
        scratch_shapes=[pltpu.VMEM((m, rows), bf16)],
        compiler_params=params(),
        name=name,
    )(left, right)


def mid_back_body(mid, a, b, c, g, gain, dmid, dbr, sums):
    @pl.when(pl.program_id(0) == 0)
    def _():
        sums[...] = jnp.zeros_like(sums)

    unit, inv = normalize(mid[...])
    e = (a[0].astype(f32) + b[0].astype(f32)) + c[...].astype(f32)
    grad = g[...].astype(f32)
    value = grad + norm_back(e, gain[...], unit, inv)
    dmid[...] = value
    low = value.astype(bf16)
    dbr[...] = low
    sums[0:1, :] += jnp.sum(e * unit, axis=0, keepdims=True)
    sums[1:2, :] += jnp.sum(e, axis=0, keepdims=True)
    sums[2:3, :] += jnp.sum(low.astype(f32), axis=0, keepdims=True)
    sums[3:4, :] += jnp.sum(grad, axis=0, keepdims=True)


def mid_back_call(mid, a, b, c, g, gain):
    rows, width = mid.shape
    one = pl.BlockSpec((rows // 2, width), lambda i: (i, 0))
    first = pl.BlockSpec((1, rows // 2, width), lambda i: (0, i, 0))
    second = pl.BlockSpec((1, rows // 2, width), lambda i: (1, i, 0))
    row = pl.BlockSpec((1, width), lambda i: (0, 0))
    return pl.pallas_call(
        mid_back_body,
        out_shape=(
            jax.ShapeDtypeStruct((rows, width), f32),
            jax.ShapeDtypeStruct((rows, width), bf16),
            jax.ShapeDtypeStruct((8, width), f32),
        ),
        grid=(2,),
        in_specs=[one, second, first, one, one, row],
        out_specs=(one, one, pl.BlockSpec((8, width), lambda i: (0, 0))),
        compiler_params=params(),
        name="mid_back",
    )(mid, a, b, c, g, gain)


def out_back_body(scal, b0, b1, b2, b3, o, w, do, grad, flat, rows, total, *, first):
    r = pl.program_id(0)

    @pl.when(r == 0)
    def _():
        lay_columns(w, first, flat)
        total[...] = jnp.zeros_like(total)

    pick(r, (b0, b1, b2, b3), rows)
    do[...] = mm_t(rows[...], flat[...]).astype(bf16)
    total[...] += mm(o[...].T, rows[...])

    @pl.when(r == 3)
    def _():
        width = grad.shape[2]
        for d in range(grad.shape[0]):
            grad[d] = total[:, d * width : (d + 1) * width].astype(bf16)


def out_back_call(scal, pieces, o, w, first):
    rows, width = pieces[0].shape
    inner = o.shape[1]
    at = pl.BlockSpec((rows, inner), lambda r, sc: (lax.bitwise_xor(sc[0], r), 0))
    grad = (w.shape[0], inner, w.shape[2])
    return pl.pallas_call(
        functools.partial(out_back_body, first=first),
        out_shape=(jax.ShapeDtypeStruct(o.shape, bf16), jax.ShapeDtypeStruct(grad, bf16)),
        grid_spec=pltpu.PrefetchScalarGridSpec(
            num_scalar_prefetch=1,
            grid=(4,),
            in_specs=[WHOLE] * 4 + [at, WHOLE],
            out_specs=(at, pl.BlockSpec(grad, lambda r, sc: (0, 0, 0))),
            scratch_shapes=[
                pltpu.VMEM((inner, width), bf16),
                pltpu.VMEM((rows, width), bf16),
                pltpu.VMEM((inner, width), f32),
            ],
        ),
        compiler_params=params(),
        name="out_back",
    )(scal, *pieces, o, w)


def qkv_back_body(scal, dq, dk, dv, w, near, far, merged, sums):
    t = pl.program_id(0)

    @pl.when(t == 0)
    def _():
        sums[...] = jnp.zeros_like(sums)

    low = jnp.concatenate([dq[...], dk[...], dv[...]], axis=1)
    merged[...] = low
    part = mm_t(low, w[...]).astype(bf16)
    sums[...] += jnp.sum(low.astype(f32), axis=0, keepdims=True)

    @pl.when(t < 2)
    def _():
        near[0] = part

    @pl.when(t >= 2)
    def _():
        far[0] = part


def qkv_back_call(scal, dq, dk, dv, w):
    keys, inner = dq.shape
    rows = keys // 4
    width = w.shape[0]
    where = lambda t, sc: (lax.bitwise_xor(sc[0], rel_of(t)), 0)
    at = pl.BlockSpec((rows, inner), where)
    return pl.pallas_call(
        qkv_back_body,
        out_shape=(
            jax.ShapeDtypeStruct((2, rows, width), bf16),
            jax.ShapeDtypeStruct((2, rows, width), bf16),
            jax.ShapeDtypeStruct((keys, 3 * inner), bf16),
            jax.ShapeDtypeStruct((1, 3 * inner), f32),
        ),
        grid_spec=pltpu.PrefetchScalarGridSpec(
            num_scalar_prefetch=1,
            grid=(4,),
            in_specs=[at, at, at, WHOLE],
            out_specs=(
                pl.BlockSpec((1, rows, width), near_map),
                pl.BlockSpec((1, rows, width), far_map),
                pl.BlockSpec((rows, 3 * inner), where),
                pl.BlockSpec((1, 3 * inner), lambda t, sc: (0, 0)),
            ),
        ),
        compiler_params=params(),
        name="qkv_back",
    )(scal, dq, dk, dv, w)


def in_back_body(x, a, b, c, dmid, gain, grad, sums):
    @pl.when(pl.program_id(0) == 0)
    def _():
        sums[...] = jnp.zeros_like(sums)

    unit, inv = normalize(x[...].astype(f32))
    e = (a[0].astype(f32) + b[0].astype(f32)) + c[...].astype(f32)
    grad[...] = (dmid[...] + norm_back(e, gain[...], unit, inv)).astype(bf16)
    sums[0:1, :] += jnp.sum(e * unit, axis=0, keepdims=True)
    sums[1:2, :] += jnp.sum(e, axis=0, keepdims=True)


def in_back_call(x, a, b, c, dmid, gain):
    rows, width = x.shape
    one = pl.BlockSpec((rows // 2, width), lambda i: (i, 0))
    first = pl.BlockSpec((1, rows // 2, width), lambda i: (0, i, 0))
    second = pl.BlockSpec((1, rows // 2, width), lambda i: (1, i, 0))
    row = pl.BlockSpec((1, width), lambda i: (0, 0))
    return pl.pallas_call(
        in_back_body,
        out_shape=(
            jax.ShapeDtypeStruct((rows, width), bf16),
            jax.ShapeDtypeStruct((8, width), f32),
        ),
        grid=(2,),
        in_specs=[one, second, first, one, one, row],
        out_specs=(one, pl.BlockSpec((8, width), lambda i: (0, 0))),
        compiler_params=params(),
        name="in_back",
    )(x, a, b, c, dmid, gain)


def remote(src, dst, send, recv, dp, seq):
    return pltpu.make_async_remote_copy(
        src_ref=src,
        dst_ref=dst,
        send_sem=send,
        recv_sem=recv,
        device_id=(dp, seq),
        device_id_type=pl.DeviceIdType.MESH,
    )


def greet(peers):
    barrier = pltpu.get_barrier_semaphore()
    for dp, seq in peers:
        pl.semaphore_signal(
            barrier, inc=1, device_id=(dp, seq), device_id_type=pl.DeviceIdType.MESH
        )
    pl.semaphore_wait(barrier, len(peers))


class GradSum:
    def __init__(self, part, acc, landx, landr, landl, sems, dp, seq):
        self.part, self.acc = part, acc
        self.landx, self.landr, self.landl = landx, landr, landl
        self.sems, self.dp, self.seq = sems, dp, seq
        self.z, self.x = dp // 2, dp % 2

    def cross(self, k):
        return remote(
            self.part.at[2 * k + (1 - self.x)],
            self.landx.at[k],
            self.sems.at[0, k],
            self.sems.at[1, k],
            2 * self.z + (1 - self.x),
            self.seq,
        )

    def right(self, b, src):
        return remote(
            src.at[b],
            self.landr.at[b],
            self.sems.at[2, b],
            self.sems.at[3, b],
            2 * ((self.z + 1) % 4) + self.x,
            self.seq,
        )

    def left(self, b, src):
        return remote(
            src.at[b],
            self.landl.at[b],
            self.sems.at[4, b],
            self.sems.at[5, b],
            2 * ((self.z + 3) % 4) + self.x,
            self.seq,
        )

    def start(self):
        for k in (3, 0, 2, 1):
            self.cross(k).start()

    def add_cross(self):
        for k in (3, 0, 2, 1):
            self.cross(k).wait_recv()
            own = self.part[2 * k + self.x].astype(f32)
            self.acc[k] = (own + self.landx[k].astype(f32)).astype(bf16)

    def stage(self, k):
        @pl.when(self.z == k)
        def _():
            for b in range(3, k, -1):
                src = self.acc
                if k > 0:
                    src = self.landr
                    self.right(b, src).wait_recv()
                    src[b] = (src[b].astype(f32) + self.acc[b].astype(f32)).astype(bf16)
                self.right(b, src).start()

        @pl.when(self.z == 3 - k)
        def _():
            for b in range(0, 3 - k):
                src = self.acc
                if k > 0:
                    src = self.landl
                    self.left(b, src).wait_recv()
                    src[b] = (src[b].astype(f32) + self.acc[b].astype(f32)).astype(bf16)
                self.left(b, src).start()

    def finish(self, out):
        z = self.z
        out[...] = self.acc[z].astype(f32)

        @pl.when(z > 0)
        def _():
            self.right(z, self.landr).wait_recv()
            out[...] += self.landr[z].astype(f32)

        @pl.when(z < 3)
        def _():
            self.left(z, self.landl).wait_recv()
            out[...] += self.landl[z].astype(f32)

    def drain(self):
        for k in range(4):
            self.cross(k).wait_send()
        for k in range(3):

            @pl.when(self.z == k)
            def _(k=k):
                for b in range(3, k, -1):
                    self.right(b, self.landr).wait_send()

            @pl.when(self.z == 3 - k)
            def _(k=k):
                for b in range(0, 3 - k):
                    self.left(b, self.landl).wait_send()

    @staticmethod
    def scratch(m, n):
        return [pltpu.VMEM((4, m, n), bf16)] * 4 + [pltpu.SemaphoreType.DMA((6, 4))]


SMALL_ROWS = 16


def tail_body(
    near, far, x, dmid, gain, gq, go, mid_sums, up_sum, qkv_sums,
    grad, gq_out, go_out, small_out,
    q_acc, q_x, q_r, q_l, q_sem, o_acc, o_x, o_r, o_l, o_sem,
    land_c, sum_y, land_y, row_sems, small, small_land, own, seq_land, small_sems, seq_sems,
):
    dp, seq = lax.axis_index("dp"), lax.axis_index("seq")
    mate, across = seq + 1 - 2 * (seq % 2), (seq + 2) % 4
    far_mate = (mate + 2) % 4
    greet([((dp + i) % 8, seq) for i in range(1, 8)] + [(dp, mate), (dp, across), (dp, far_mate)])
    rows, width = x.shape

    cores = [
        remote(near.at[k], land_c.at[k], row_sems.at[0, k], row_sems.at[1, k], dp, mate)
        for k in range(2)
    ]
    cores[1].start()
    cores[0].start()
    sum_q = GradSum(gq, q_acc, q_x, q_r, q_l, q_sem, dp, seq)
    sum_o = GradSum(go, o_acc, o_x, o_r, o_l, o_sem, dp, seq)
    sum_o.start()
    sum_q.start()

    cores[1].wait_recv()
    chunk = 128
    for i in range(rows // chunk):
        at = slice(i * chunk, (i + 1) * chunk)
        sum_y[at, :] = (far[0, at, :].astype(f32) + land_c[1, at, :].astype(f32)).astype(bf16)
    over = remote(sum_y, land_y, row_sems.at[0, 2], row_sems.at[1, 2], dp, across)
    over.start()

    small[...] = jnp.zeros_like(small)
    for d in range(8):
        at = slice(d * LANES, (d + 1) * LANES)
        for row, src in ((4, mid_sums[2:3, at]), (5, mid_sums[0:1, at]), (6, mid_sums[1:2, at])):
            small[d, row : row + 1, :] = src
        small[d, 11:12, :] = mid_sums[3:4, at]
    for i in range(2):
        at = slice(i * LANES, (i + 1) * LANES)
        small[pl.ds(seq, 1), 2 + i, :] = qkv_sums[:, at]
        at = slice((4 + i) * LANES, (5 + i) * LANES)
        small[pl.ds(4 + seq, 1), 2 + i, :] = qkv_sums[:, at]
    for i in range(8):
        at = slice(i * LANES, (i + 1) * LANES)
        small[pl.ds(2 * seq + i // 4, 1), 7 + i % 4, :] = up_sum[:, at]

    sum_o.add_cross()
    sum_o.stage(0)
    sum_o.stage(1)
    sum_q.add_cross()
    sum_q.stage(0)
    sum_o.stage(2)

    cores[0].wait_recv()
    over.wait_recv()
    gain_sum = jnp.zeros((1, width), f32)
    shift_sum = jnp.zeros((1, width), f32)
    for i in range(rows // chunk):
        at = slice(i * chunk, (i + 1) * chunk)
        unit, inv = normalize(x[at, :].astype(f32))
        e = (far[1, at, :].astype(f32) + land_c[0, at, :].astype(f32)) + land_y[at, :].astype(f32)
        grad[at, :] = (dmid[at, :] + norm_back(e, gain[...], unit, inv)).astype(bf16)
        gain_sum += jnp.sum(e * unit, axis=0, keepdims=True)
        shift_sum += jnp.sum(e, axis=0, keepdims=True)
    for d in range(8):
        at = slice(d * LANES, (d + 1) * LANES)
        small[d, 0:1, :] = gain_sum[:, at]
        small[d, 1:2, :] = shift_sum[:, at]

    def small_to(i):
        peer = (dp + i) % 8
        return remote(
            small.at[peer], small_land.at[i], small_sems.at[0, i], small_sems.at[1, i], peer, seq
        )

    for i in range(1, 8):
        small_to(i).start()
    sum_q.stage(1)
    sum_q.stage(2)
    sum_o.finish(go_out)
    total = small[dp]
    for i in range(1, 8):
        small_to(i).wait_recv()
        total = total + small_land[i]
    own[...] = total

    def seq_to(i, peer):
        return remote(own, seq_land.at[i], seq_sems.at[0, i], seq_sems.at[1, i], dp, peer)

    group = [seq_to(0, mate), seq_to(1, across), seq_to(2, far_mate)]
    for copy in group:
        copy.start()
    sum_q.finish(gq_out)
    for copy in group:
        copy.wait_recv()
    small_out[...] = (own[...] + seq_land[0]) + (seq_land[1] + seq_land[2])

    for copy in group + cores + [over]:
        copy.wait_send()
    for i in range(1, 8):
        small_to(i).wait_send()
    sum_o.drain()
    sum_q.drain()


def tail_call(near, far, x, dmid, gain, gq, go, mid_sums, up_sum, qkv_sums):
    rows, width = x.shape
    sem = pltpu.SemaphoreType.DMA
    return pl.pallas_call(
        tail_body,
        out_shape=(
            jax.ShapeDtypeStruct((rows, width), bf16),
            jax.ShapeDtypeStruct(gq.shape[1:], f32),
            jax.ShapeDtypeStruct(go.shape[1:], f32),
            jax.ShapeDtypeStruct((SMALL_ROWS, LANES), f32),
        ),
        in_specs=[WHOLE] * 10,
        out_specs=(WHOLE,) * 4,
        scratch_shapes=GradSum.scratch(*gq.shape[1:])
        + GradSum.scratch(*go.shape[1:])
        + [
            pltpu.VMEM((2, rows, width), bf16),
            pltpu.VMEM((rows, width), bf16),
            pltpu.VMEM((rows, width), bf16),
            sem((2, 3)),
            pltpu.VMEM((8, SMALL_ROWS, LANES), f32),
            pltpu.VMEM((8, SMALL_ROWS, LANES), f32),
            pltpu.VMEM((SMALL_ROWS, LANES), f32),
            pltpu.VMEM((3, SMALL_ROWS, LANES), f32),
            sem((2, 8)),
            sem((2, 3)),
        ],
        compiler_params=params(collective_id=3, has_side_effects=True),
        name="tail",
    )(near, far, x, dmid, gain, gq, go, mid_sums, up_sum, qkv_sums)


def finish_body(
    scal, grad, gq, go, small,
    grad_out, gq_out, go_out, gain1, shift1, qv, bout, gain2, shift2, up, down,
):
    seq = scal[0]
    grad_out[...] = grad[...]
    go_out[...] = go[...]
    cols = gq_out.shape[2]
    for c in range(3):
        gq_out[:, c, :] = gq[:, c * cols : (c + 1) * cols]
    for ref, row in ((gain1, 0), (shift1, 1), (bout, 4), (gain2, 5), (shift2, 6), (down, 11)):
        n = ref.shape[1]
        value = small[row : row + 1, 0:n]
        for i in range(1, 4):
            value = jnp.where(seq == i, small[row : row + 1, i * n : (i + 1) * n], value)
        ref[...] = value
    value = small[2:3, 0:64]
    for i in range(1, 4):
        at = 64 * (i % 2)
        value = jnp.where(seq == i, small[2 + i // 2 : 3 + i // 2, at : at + 64], value)
    qv[...] = value
    up[...] = small[pl.ds(7 + seq, 1), :]


def finish_call(scal, grad, gq, go, small):
    one = lambda n: jax.ShapeDtypeStruct((1, n), f32)
    return pl.pallas_call(
        finish_body,
        out_shape=(
            jax.ShapeDtypeStruct(grad.shape, bf16),
            jax.ShapeDtypeStruct((gq.shape[0], 3, gq.shape[1] // 3), f32),
            jax.ShapeDtypeStruct(go.shape, f32),
            one(32), one(32), one(64), one(32), one(32), one(32), one(LANES), one(32),
        ),
        in_specs=[SCALAR] + [WHOLE] * 4,
        out_specs=(WHOLE,) * 11,
        compiler_params=params(),
        name="finish",
    )(scal, grad, gq, go, small)


def after(value, *others):
    return lax.optimization_barrier((value, *others))[0]


def on_device(
    dp_n,
    seq_n,
    tokens,
    lengths,
    cotangent,
    ln1_gain,
    ln1_shift,
    w_qkv,
    b_qv,
    w_out,
    b_out,
    ln2_gain,
    ln2_shift,
    w_fc1,
    b_fc1,
    w_fc2,
    b_fc2,
):
    count = dp_n * seq_n
    rows, width = tokens.shape
    heads = width // HEAD_DIM
    inner = w_out.shape[0]
    ff = w_fc1.shape[1]
    s = lax.axis_index("seq")
    length = lengths[0]

    wq = lax.all_gather(
        jnp.concatenate([w_qkv[:, c, :] for c in range(3)], axis=1), "dp", axis=0, tiled=True
    )
    col = w_fc2.shape[1]
    both = jnp.concatenate([w_fc2, w_out], axis=0)
    if col % LANES == 0:
        parts = dp_n
        w_cols = lax.all_gather(both, "dp", axis=0, tiled=False)
    else:
        parts = 1
        w_cols = lax.all_gather(both, "dp", axis=1, tiled=True)[None]
    w1 = lax.all_gather(w_fc1, "dp", axis=0, tiled=True)

    small = (ln1_gain, ln1_shift, b_qv, b_out, ln2_gain, ln2_shift, b_fc1, b_fc2)
    sizes = [v.shape[0] for v in small]
    ends = [sum(sizes[: i + 1]) for i in range(len(sizes))]
    packed = small_gather(jnp.concatenate([v.astype(f32) for v in small]), count, seq_n)
    packed = packed.reshape(count, ends[-1])
    gain1, shift1, bias_qv, bias_out, gain2, shift2, bias_up, bias_down = (
        packed[:, e - n : e].reshape(1, count * n) for e, n in zip(ends, sizes)
    )

    scal = jnp.stack([s.astype(jnp.int32), length])
    slopes = 2.0 ** (-8.0 * (jnp.arange(heads, dtype=jnp.int32) + 1).astype(f32) / heads)
    slopes = lax.dynamic_slice(slopes, (s * (heads // seq_n),), (heads // seq_n,))
    own_bias = lambda v, n: lax.dynamic_slice(v, (0, s * n), (1, n))
    qkv_bias = jnp.concatenate(
        [
            own_bias(bias_qv[:, :width], inner),
            jnp.zeros((1, inner), f32),
            own_bias(bias_qv[:, width:], inner),
        ],
        axis=1,
    )

    x_pieces = spread(tokens)
    valid = s * rows + jnp.arange(rows, dtype=jnp.int32) < length
    grad_low = jnp.where(valid[:, None], cotangent, jnp.zeros_like(cotangent))
    g_pieces = spread(after(grad_low, x_pieces[3]))

    block = 384
    h1, qkv = qkv_call(scal, x_pieces, wq, gain1, shift1, qkv_bias)
    o, lse = attend_call(scal, slopes, qkv, block)
    o = after(o, g_pieces[2], g_pieces[3])
    near, far = out_call(scal, o, w_cols, ff)
    got, across = reduce_rows(near, far)
    mid, h2 = mid_call(tokens, far, got, across, bias_out, gain2, shift2)
    h_pieces = spread(h2)
    y_near, y_far, d_near, d_far, a_all, du_all, h_all, g_all, up_sum = mlp_call(
        h_pieces, g_pieces, w1, w_cols, own_bias(bias_up, ff)
    )
    got, across = reduce_rows(d_near, d_far)
    grad_down = outer_call(a_all, g_all, parts, "grad_fc2")
    grad_up = outer_call(h_all, du_all, 1, "grad_fc1")
    dmid, dbr, mid_sums = mid_back_call(mid, d_far, got, across, grad_low, gain2)
    b_pieces = spread(dbr)

    y_near = after(y_near, b_pieces[3])
    got, across = reduce_rows(y_near, y_far)
    output = (
        mid + ((y_far[1].astype(f32) + got[0].astype(f32)) + across.astype(f32) + bias_down)
    ).astype(bf16)

    do, grad_out = out_back_call(scal, b_pieces, o, w_cols, ff)
    dq, dk, dv = attend_back_call(scal, slopes, qkv, o, do, lse, block)
    near, far, merged, qkv_sums = qkv_back_call(scal, dq, dk, dv, wq)
    grad_qkv = outer_call(h1, merged, 1, "grad_qkv")

    def shared(part):
        if parts > 1:
            return lax.psum_scatter(part, "dp", scatter_dimension=0, tiled=False).astype(f32)
        return lax.psum_scatter(part, "dp", scatter_dimension=1, tiled=True).astype(f32)

    grad_down = shared(grad_down if parts > 1 else grad_down)
    grad_up = lax.psum_scatter(grad_up, "dp", scatter_dimension=0, tiled=True).astype(f32)
    if dp_n == 8 and seq_n == 4 and width == 8 * LANES and ff == width and inner == 2 * LANES:
        tail = tail_call(
            near, far, tokens, dmid, gain1, grad_qkv.reshape(8, -1, 3 * inner), grad_out,
            mid_sums, up_sum, qkv_sums,
        )
        grad_tokens, grad_qkv, grad_out, *vectors = finish_call(scal, *tail)
        g_gain1, g_shift1, g_qv, g_bout, g_gain2, g_shift2, g_up, g_down = (
            v.reshape(n) for v, n in zip(vectors, sizes)
        )
        return (
            output, grad_tokens, g_gain1, g_shift1, grad_qkv, g_qv, grad_out, g_bout,
            g_gain2, g_shift2, grad_up, g_up, grad_down, g_down,
        )

    got, across = reduce_rows(near, far)
    grad_tokens, in_sums = in_back_call(tokens, far, got, across, dmid, gain1)
    grad_out = shared(grad_out if parts > 1 else grad_out[0])
    grad_qkv = lax.psum_scatter(grad_qkv, "dp", scatter_dimension=0, tiled=True)
    grad_qkv = grad_qkv.astype(f32).reshape(w_qkv.shape)

    def own_slot(v, total):
        return lax.dynamic_update_slice(jnp.zeros((1, total), f32), v, (0, s * v.shape[1]))

    sums = (
        in_sums[0:1],
        in_sums[1:2],
        jnp.concatenate(
            [own_slot(qkv_sums[:, :inner], width), own_slot(qkv_sums[:, 2 * inner :], width)], axis=1
        ),
        mid_sums[2:3],
        mid_sums[0:1],
        mid_sums[1:2],
        own_slot(up_sum, seq_n * ff),
        mid_sums[3:4],
    )
    grads = jnp.concatenate([v.reshape(count, n) for v, n in zip(sums, sizes)], axis=1)
    grads = small_scatter(grads, count, seq_n).reshape(ends[-1])
    g_gain1, g_shift1, g_qv, g_bout, g_gain2, g_shift2, g_up, g_down = (
        grads[e - n : e] for e, n in zip(ends, sizes)
    )
    return (
        output,
        grad_tokens,
        g_gain1,
        g_shift1,
        grad_qkv,
        g_qv,
        grad_out,
        g_bout,
        g_gain2,
        g_shift2,
        grad_up,
        g_up,
        grad_down,
        g_down,
    )


def solution(mesh):
    rows = P(("dp", "seq"), None)
    vec = P(("dp", "seq"))
    merged = P("dp", None, "seq")
    return jax.shard_map(
        functools.partial(on_device, mesh.shape["dp"], mesh.shape["seq"]),
        mesh=mesh,
        in_specs=(
            rows, P("dp"), rows, vec, vec, merged, vec, P("seq", "dp"), vec, vec, vec,
            P("dp", "seq"), vec, P("seq", "dp"), vec,
        ),
        out_specs=(
            rows, rows, vec, vec, merged, vec, P("seq", "dp"), vec, vec, vec,
            P("dp", "seq"), vec, P("seq", "dp"), vec,
        ),
        check_vma=False,
    )
```

```python
import functools
import math

import jax
import jax.numpy as jnp
from jax import lax
from jax.experimental import pallas as pl
from jax.experimental.pallas import tpu as pltpu
from jax.sharding import PartitionSpec as P

HEAD_DIM = 64
EPS = 1e-05
GELU_COEF = 0.044715
NEG = -1e30
LANES = 128
VMEM_BYTES = 60 * 1024 * 1024

f32 = jnp.float32
bf16 = jnp.bfloat16
WHOLE = pl.BlockSpec(memory_space=pltpu.VMEM)
SCALAR = pl.BlockSpec(memory_space=pltpu.SMEM)


def mm(a, b):
    return jnp.dot(a, b, preferred_element_type=f32)


def mm_t(a, b):
    return lax.dot_general(a, b, (((1,), (1,)), ((), ())), preferred_element_type=f32)


def params(**kw):
    return pltpu.CompilerParams(vmem_limit_bytes=VMEM_BYTES, **kw)


def normalize(v):
    width = v.shape[-1]
    centred = v - jnp.sum(v, axis=-1, keepdims=True) * (1.0 / width)
    inv = lax.rsqrt(jnp.sum(centred * centred, axis=-1, keepdims=True) * (1.0 / width) + EPS)
    return centred * inv, inv


def norm_back(grad_out, gain, unit, inv):
    width = unit.shape[-1]
    scaled = grad_out * gain
    mean_one = jnp.sum(scaled, axis=-1, keepdims=True) * (1.0 / width)
    mean_two = jnp.sum(scaled * unit, axis=-1, keepdims=True) * (1.0 / width)
    return inv * (scaled - mean_one - unit * mean_two)


def device_of(index, seq_n):
    return (index // seq_n, index % seq_n)


def greet_all(me, count, seq_n):
    barrier = pltpu.get_barrier_semaphore()

    def hello(i, carry):
        peer = (me + i) % count
        pl.semaphore_signal(
            barrier, inc=1, device_id=device_of(peer, seq_n), device_id_type=pl.DeviceIdType.MESH
        )
        return carry

    lax.fori_loop(1, count, hello, 0)
    pl.semaphore_wait(barrier, count - 1)


def small_gather_body(count, seq_n, x_ref, out_ref, send_sem, recv_sem):
    me = lax.axis_index("dp") * seq_n + lax.axis_index("seq")
    greet_all(me, count, seq_n)

    def copy_to(i):
        peer = (me + i) % count
        return pltpu.make_async_remote_copy(
            src_ref=x_ref,
            dst_ref=out_ref.at[pl.ds(me, 1)],
            send_sem=send_sem.at[i],
            recv_sem=recv_sem.at[i],
            device_id=device_of(peer, seq_n),
            device_id_type=pl.DeviceIdType.MESH,
        )

    def begin(i, carry):
        copy_to(i).start()
        return carry

    def finish(i, carry):
        copy_to(i).wait()
        return carry

    lax.fori_loop(1, count, begin, 0)
    out_ref[pl.ds(me, 1)] = x_ref[...]
    lax.fori_loop(1, count, finish, 0)


def small_gather(x, count, seq_n):
    width = x.shape[-1]
    return pl.pallas_call(
        functools.partial(small_gather_body, count, seq_n),
        out_shape=jax.ShapeDtypeStruct((count, 1, width), f32),
        in_specs=[WHOLE],
        out_specs=WHOLE,
        scratch_shapes=[pltpu.SemaphoreType.DMA((count,)), pltpu.SemaphoreType.DMA((count,))],
        compiler_params=pltpu.CompilerParams(collective_id=1, has_side_effects=True),
        name="small_gather",
    )(x.reshape(1, 1, width))


def small_scatter_body(count, seq_n, v_ref, out_ref, land, send_sem, recv_sem):
    me = lax.axis_index("dp") * seq_n + lax.axis_index("seq")
    greet_all(me, count, seq_n)

    def copy_to(i):
        peer = (me + i) % count
        return pltpu.make_async_remote_copy(
            src_ref=v_ref.at[pl.ds(peer, 1)],
            dst_ref=land.at[pl.ds(i, 1)],
            send_sem=send_sem.at[i],
            recv_sem=recv_sem.at[i],
            device_id=device_of(peer, seq_n),
            device_id_type=pl.DeviceIdType.MESH,
        )

    def begin(i, carry):
        copy_to(i).start()
        return carry

    def finish(i, total):
        copy_to(i).wait()
        return total + land[pl.ds(i, 1)]

    lax.fori_loop(1, count, begin, 0)
    out_ref[...] = lax.fori_loop(1, count, finish, v_ref[pl.ds(me, 1)])


def small_scatter(v, count, seq_n):
    width = v.shape[-1]
    return pl.pallas_call(
        functools.partial(small_scatter_body, count, seq_n),
        out_shape=jax.ShapeDtypeStruct((1, 1, width), f32),
        in_specs=[WHOLE],
        out_specs=WHOLE,
        scratch_shapes=[
            pltpu.VMEM((count, 1, width), f32),
            pltpu.SemaphoreType.DMA((count,)),
            pltpu.SemaphoreType.DMA((count,)),
        ],
        compiler_params=pltpu.CompilerParams(collective_id=2, has_side_effects=True),
        name="small_scatter",
    )(v.reshape(count, 1, width))


def swap(x, bit):
    return lax.ppermute(x, "seq", [(i, i ^ bit) for i in range(4)])


def spread(own):
    far = swap(own, 2)
    return own, swap(own, 1), far, swap(far, 1)


def reduce_rows(near, far):
    got = swap(near, 1)
    across = swap(far[0] + got[1], 2)
    return got, across


def pick(step, refs, dest):
    for k, ref in enumerate(refs):

        @pl.when(step == k)
        def _(ref=ref):
            dest[...] = ref[...]


ORDER = (1, 3, 2, 0)


def rel_of(t):
    return jnp.where(t == 0, 1, jnp.where(t == 1, 3, jnp.where(t == 2, 2, 0)))


def qkv_body(scal, x0, x1, x2, x3, w, gain, shift, bias, h1, qkv, rows):
    pick(pl.program_id(0), (x0, x1, x2, x3), rows)
    unit, _ = normalize(rows[...].astype(f32))
    low = (unit * gain[...] + shift[...]).astype(bf16)
    h1[...] = low
    qkv[...] = (mm(low, w[...]) + bias[...]).astype(bf16)


def qkv_call(scal, pieces, w, gain, shift, bias):
    rows, width = pieces[0].shape
    cols = w.shape[1]
    out = lambda r, sc: (lax.bitwise_xor(sc[0], r), 0)
    return pl.pallas_call(
        qkv_body,
        out_shape=(
            jax.ShapeDtypeStruct((4 * rows, width), bf16),
            jax.ShapeDtypeStruct((4 * rows, cols), bf16),
        ),
        grid_spec=pltpu.PrefetchScalarGridSpec(
            num_scalar_prefetch=1,
            grid=(4,),
            in_specs=[WHOLE] * 8,
            out_specs=(pl.BlockSpec((rows, width), out), pl.BlockSpec((rows, cols), out)),
            scratch_shapes=[pltpu.VMEM((rows, width), bf16)],
        ),
        compiler_params=params(),
        name="qkv",
    )(scal, *pieces, w, gain, shift, bias)


def make_bias(scal, slopes, pair, bias, keys):
    pos = lax.broadcasted_iota(jnp.int32, (keys, LANES), 0)
    inside = pos < scal[1]
    ramp = pos.astype(f32)
    for h in range(2):
        bias[h] = jnp.where(inside, ramp * slopes[2 * pair + h], NEG)


def head_only(x, h):
    lane = lax.broadcasted_iota(jnp.int32, x.shape, 1)
    return jnp.where((lane >= h * HEAD_DIM) & (lane < (h + 1) * HEAD_DIM), x, jnp.zeros_like(x))


def score_t(k_ref, qm, bias, h, length):
    block = qm.shape[0]
    s = mm_t(k_ref[0:length, :], qm)
    b = bias[h, 0:length, :]
    s = s + jnp.concatenate([b] * (block // LANES), axis=1)
    key = lax.broadcasted_iota(jnp.int32, (block, block), 0)
    query = lax.broadcasted_iota(jnp.int32, (block, block), 1)
    last = jnp.where(key <= query, s[length - block :], NEG)
    if length == block:
        return last
    return jnp.concatenate([s[: length - block], last], axis=0)


def attend_body(scal, q, k, v, slopes, o, lse, bias, vt):
    pair, step = pl.program_id(0), pl.program_id(1)
    block = q.shape[0]
    keys = k.shape[0]

    @pl.when(step == 0)
    def _():
        make_bias(scal, slopes, pair, bias, keys)
        vt[...] = v[...].T

    for c in range(keys // block):

        @pl.when(step == c)
        def _(c=c):
            length = (c + 1) * block
            scaled = q[...] * bf16(HEAD_DIM**-0.5)
            outs, logs = [], []
            for h in range(2):
                s = score_t(k, head_only(scaled, h), bias, h, length)
                top = jnp.max(s, axis=0, keepdims=True)
                e = jnp.exp(s - top)
                total = jnp.sum(e, axis=0, keepdims=True)
                mixed = mm(vt[h * HEAD_DIM : (h + 1) * HEAD_DIM, 0:length], e.astype(bf16))
                outs.append(mixed / total)
                logs.append(top + jnp.log(total))
            o[...] = jnp.concatenate(outs, axis=0).T.astype(bf16)
            lse[0, 0:2, :] = jnp.concatenate(logs, axis=0)


def attend_call(scal, slopes, qkv, block):
    keys, cols = qkv.shape
    width = cols // 3
    pairs = width // LANES
    return pl.pallas_call(
        attend_body,
        out_shape=(
            jax.ShapeDtypeStruct((keys, width), bf16),
            jax.ShapeDtypeStruct((pairs, 8, keys), f32),
        ),
        grid_spec=pltpu.PrefetchScalarGridSpec(
            num_scalar_prefetch=1,
            grid=(pairs, keys // block),
            in_specs=[
                pl.BlockSpec((block, LANES), lambda p, c, sc: (c, p)),
                pl.BlockSpec((keys, LANES), lambda p, c, sc: (0, pairs + p)),
                pl.BlockSpec((keys, LANES), lambda p, c, sc: (0, 2 * pairs + p)),
                SCALAR,
            ],
            out_specs=(
                pl.BlockSpec((block, LANES), lambda p, c, sc: (c, p)),
                pl.BlockSpec((1, 8, block), lambda p, c, sc: (p, 0, c)),
            ),
            scratch_shapes=[
                pltpu.VMEM((2, keys, LANES), f32),
                pltpu.VMEM((LANES, keys), bf16),
            ],
        ),
        compiler_params=params(),
        name="attend",
    )(scal, qkv, qkv, qkv, slopes)


def attend_back_body(scal, q, k, v, o, do, lse, slopes, dq, dk, dv, bias, kt, dk_sum, dv_sum):
    pair, step = pl.program_id(0), pl.program_id(1)
    block = q.shape[0]
    keys = k.shape[0]
    scale = HEAD_DIM**-0.5

    @pl.when(step == 0)
    def _():
        make_bias(scal, slopes, pair, bias, keys)
        kt[...] = k[...].T
        dk_sum[...] = jnp.zeros_like(dk_sum)
        dv_sum[...] = jnp.zeros_like(dv_sum)

    for c in range(keys // block):

        @pl.when(step == c)
        def _(c=c):
            length = (c + 1) * block
            scaled = q[...] * bf16(scale)
            both = (do[...].astype(f32) * o[...].astype(f32)).T
            outs = []
            for h in range(2):
                qm = head_only(scaled, h)
                dom = head_only(do[...], h)
                dot_row = jnp.sum(both[h * HEAD_DIM : (h + 1) * HEAD_DIM], axis=0, keepdims=True)
                p = jnp.exp(score_t(k, qm, bias, h, length) - lse[0, h : h + 1, :])
                dp = mm_t(v[0:length, :], dom)
                ds = (p * (dp - dot_row)).astype(bf16)
                dv_sum[0:length, :] += mm(p.astype(bf16), dom)
                dk_sum[0:length, :] += mm(ds, qm)
                outs.append(mm(kt[h * HEAD_DIM : (h + 1) * HEAD_DIM, 0:length], ds))
            dq[...] = (jnp.concatenate(outs, axis=0).T * scale).astype(bf16)

    @pl.when(step == keys // block - 1)
    def _():
        dk[...] = dk_sum[...].astype(bf16)
        dv[...] = dv_sum[...].astype(bf16)


def attend_back_call(scal, slopes, qkv, o, do, lse, block):
    keys, cols = qkv.shape
    width = cols // 3
    pairs = width // LANES
    some = pl.BlockSpec((block, LANES), lambda p, c, sc: (c, p))
    full = pl.BlockSpec((keys, LANES), lambda p, c, sc: (0, p))
    return pl.pallas_call(
        attend_back_body,
        out_shape=(jax.ShapeDtypeStruct((keys, width), bf16),) * 3,
        grid_spec=pltpu.PrefetchScalarGridSpec(
            num_scalar_prefetch=1,
            grid=(pairs, keys // block),
            in_specs=[
                some,
                pl.BlockSpec((keys, LANES), lambda p, c, sc: (0, pairs + p)),
                pl.BlockSpec((keys, LANES), lambda p, c, sc: (0, 2 * pairs + p)),
                some,
                some,
                pl.BlockSpec((1, 8, block), lambda p, c, sc: (p, 0, c)),
                SCALAR,
            ],
            out_specs=(some, full, full),
            scratch_shapes=[
                pltpu.VMEM((2, keys, LANES), f32),
                pltpu.VMEM((LANES, keys), bf16),
                pltpu.VMEM((keys, LANES), f32),
                pltpu.VMEM((keys, LANES), f32),
            ],
        ),
        compiler_params=params(),
        name="attend_back",
    )(scal, qkv, qkv, qkv, o, do, lse, slopes)


def lay_columns(w_ref, first, dest):
    width = w_ref.shape[2]
    for d in range(w_ref.shape[0]):
        dest[:, d * width : (d + 1) * width] = w_ref[d, first : first + dest.shape[0], :]


def out_body(scal, o, w, near, far, flat, *, first):
    t = pl.program_id(0)

    @pl.when(t == 0)
    def _():
        lay_columns(w, first, flat)

    part = mm(o[...], flat[...]).astype(bf16)

    @pl.when(t < 2)
    def _():
        near[0] = part

    @pl.when(t >= 2)
    def _():
        far[0] = part


def near_map(t, *_):
    return (jnp.minimum(t, 1), 0, 0)


def far_map(t, *_):
    return (jnp.maximum(t - 2, 0), 0, 0)


def out_call(scal, o, w, first):
    keys, inner = o.shape
    rows = keys // 4
    width = w.shape[0] * w.shape[2]
    return pl.pallas_call(
        functools.partial(out_body, first=first),
        out_shape=(jax.ShapeDtypeStruct((2, rows, width), bf16),) * 2,
        grid_spec=pltpu.PrefetchScalarGridSpec(
            num_scalar_prefetch=1,
            grid=(4,),
            in_specs=[
                pl.BlockSpec((rows, inner), lambda t, sc: (lax.bitwise_xor(sc[0], rel_of(t)), 0)),
                WHOLE,
            ],
            out_specs=(
                pl.BlockSpec((1, rows, width), near_map),
                pl.BlockSpec((1, rows, width), far_map),
            ),
            scratch_shapes=[pltpu.VMEM((inner, width), bf16)],
        ),
        compiler_params=params(),
        name="out_proj",
    )(scal, o, w)


def mid_body(x, a, b, c, bias, gain, shift, mid, h2):
    value = x[...].astype(f32) + (
        (a[0].astype(f32) + b[0].astype(f32)) + c[...].astype(f32) + bias[...]
    )
    mid[...] = value
    unit, _ = normalize(value)
    h2[...] = (unit * gain[...] + shift[...]).astype(bf16)


def mid_call(x, a, b, c, bias, gain, shift):
    rows, width = x.shape
    one = pl.BlockSpec((rows // 2, width), lambda i: (i, 0))
    first = pl.BlockSpec((1, rows // 2, width), lambda i: (0, i, 0))
    second = pl.BlockSpec((1, rows // 2, width), lambda i: (1, i, 0))
    row = pl.BlockSpec((1, width), lambda i: (0, 0))
    return pl.pallas_call(
        mid_body,
        out_shape=(
            jax.ShapeDtypeStruct((rows, width), f32),
            jax.ShapeDtypeStruct((rows, width), bf16),
        ),
        grid=(2,),
        in_specs=[one, second, first, one, row, row, row],
        out_specs=(one, one),
        compiler_params=params(),
        name="mid_norm",
    )(x, a, b, c, bias, gain, shift)


def gelu_parts(u):
    root = math.sqrt(2.0 / math.pi)
    sq = u * u
    t = jnp.tanh(root * (u + GELU_COEF * (sq * u)))
    half = 0.5 * (1.0 + t)
    slope = half + 0.5 * u * (1.0 - t * t) * (root * (1.0 + 3.0 * GELU_COEF * sq))
    return u * half, slope


def mlp_body(
    h0, h1, h2, h3, g_rows, w1, w2, b1,
    y_near, y_far, d_near, d_far, a_all, du_all, h_all, g_all, bias_sum,
    flat, hb, gb,
):
    t = pl.program_id(0)

    @pl.when(t == 0)
    def _():
        lay_columns(w2, 0, flat)
        bias_sum[...] = jnp.zeros_like(bias_sum)

    pick(rel_of(t), (h0, h1, h2, h3), hb)
    gb[...] = g_rows[rel_of(t)]
    h_all[...] = hb[...]
    g_all[...] = gb[...]
    inner = w1.shape[1]
    chunk = 256
    for c in range(inner // chunk):
        cols = slice(c * chunk, (c + 1) * chunk)
        u = mm(hb[...], w1[:, cols]) + b1[:, cols]
        value, slope = gelu_parts(u)
        a_all[:, cols] = value.astype(bf16)
        du = (mm_t(gb[...], flat[cols, :]) * slope).astype(bf16)
        du_all[:, cols] = du
        bias_sum[:, cols] += jnp.sum(du.astype(f32), axis=0, keepdims=True)
    y = mm(a_all[...], flat[...]).astype(bf16)
    d = mm_t(du_all[...], w1[...]).astype(bf16)

    @pl.when(t < 2)
    def _():
        y_near[0] = y
        d_near[0] = d

    @pl.when(t >= 2)
    def _():
        y_far[0] = y
        d_far[0] = d


def mlp_call(h_pieces, g_rows, w1, w2, b1):
    rows, width = h_pieces[0].shape
    inner = w1.shape[1]
    pair = jax.ShapeDtypeStruct((2, rows, width), bf16)
    near = pl.BlockSpec((1, rows, width), near_map)
    far = pl.BlockSpec((1, rows, width), far_map)
    block = lambda n: pl.BlockSpec((rows, n), lambda t: (t, 0))
    return pl.pallas_call(
        mlp_body,
        out_shape=(
            pair,
            pair,
            pair,
            pair,
            jax.ShapeDtypeStruct((4 * rows, inner), bf16),
            jax.ShapeDtypeStruct((4 * rows, inner), bf16),
            jax.ShapeDtypeStruct((4 * rows, width), bf16),
            jax.ShapeDtypeStruct((4 * rows, width), bf16),
            jax.ShapeDtypeStruct((1, inner), f32),
        ),
        grid=(4,),
        in_specs=[WHOLE] * 8,
        out_specs=(
            near, far, near, far, block(inner), block(inner), block(width), block(width),
            pl.BlockSpec((1, inner), lambda t: (0, 0)),
        ),
        scratch_shapes=[
            pltpu.VMEM((inner, width), bf16),
            pltpu.VMEM((rows, width), bf16),
            pltpu.VMEM((rows, width), bf16),
        ],
        compiler_params=params(),
        name="mlp",
    )(*h_pieces, g_rows, w1, w2, b1)


def outer_body(left, right, out, turned, *, blocks):
    @pl.when(pl.program_id(0) == 0)
    def _():
        turned[...] = left[...].T

    part = mm(turned[...], right[...]).astype(bf16)
    if blocks:
        width = out.shape[2]
        for d in range(out.shape[0]):
            out[d] = part[:, d * width : (d + 1) * width]
    else:
        out[...] = part


def outer_call(left, right, parts, name):
    rows, m = left.shape
    n = right.shape[1]
    step = 256
    if parts > 1:
        width = n // parts
        out_shape = jax.ShapeDtypeStruct((parts, m, width), bf16)
        out_spec = pl.BlockSpec((step // width, m, width), lambda j: (j, 0, 0))
    else:
        out_shape = jax.ShapeDtypeStruct((m, n), bf16)
        out_spec = pl.BlockSpec((m, step), lambda j: (0, j))
    return pl.pallas_call(
        functools.partial(outer_body, blocks=parts > 1),
        out_shape=out_shape,
        grid=(n // step,),
        in_specs=[WHOLE, pl.BlockSpec((rows, step), lambda j: (0, j))],
        out_specs=out_spec,
        scratch_shapes=[pltpu.VMEM((m, rows), bf16)],
        compiler_params=params(),
        name=name,
    )(left, right)


def mid_back_body(mid, a, b, c, g, gain, dmid, dbr, sums):
    @pl.when(pl.program_id(0) == 0)
    def _():
        sums[...] = jnp.zeros_like(sums)

    unit, inv = normalize(mid[...])
    e = (a[0].astype(f32) + b[0].astype(f32)) + c[...].astype(f32)
    grad = g[...].astype(f32)
    value = grad + norm_back(e, gain[...], unit, inv)
    dmid[...] = value
    low = value.astype(bf16)
    dbr[...] = low
    sums[0:1, :] += jnp.sum(e * unit, axis=0, keepdims=True)
    sums[1:2, :] += jnp.sum(e, axis=0, keepdims=True)
    sums[2:3, :] += jnp.sum(low.astype(f32), axis=0, keepdims=True)
    sums[3:4, :] += jnp.sum(grad, axis=0, keepdims=True)


def mid_back_call(mid, a, b, c, g, gain):
    rows, width = mid.shape
    one = pl.BlockSpec((rows // 2, width), lambda i: (i, 0))
    first = pl.BlockSpec((1, rows // 2, width), lambda i: (0, i, 0))
    second = pl.BlockSpec((1, rows // 2, width), lambda i: (1, i, 0))
    row = pl.BlockSpec((1, width), lambda i: (0, 0))
    return pl.pallas_call(
        mid_back_body,
        out_shape=(
            jax.ShapeDtypeStruct((rows, width), f32),
            jax.ShapeDtypeStruct((rows, width), bf16),
            jax.ShapeDtypeStruct((8, width), f32),
        ),
        grid=(2,),
        in_specs=[one, second, first, one, one, row],
        out_specs=(one, one, pl.BlockSpec((8, width), lambda i: (0, 0))),
        compiler_params=params(),
        name="mid_back",
    )(mid, a, b, c, g, gain)


def out_back_body(scal, b0, b1, b2, b3, o, w, do, grad, flat, rows, total, *, first):
    r = pl.program_id(0)

    @pl.when(r == 0)
    def _():
        lay_columns(w, first, flat)
        total[...] = jnp.zeros_like(total)

    pick(r, (b0, b1, b2, b3), rows)
    do[...] = mm_t(rows[...], flat[...]).astype(bf16)
    total[...] += mm(o[...].T, rows[...])

    @pl.when(r == 3)
    def _():
        width = grad.shape[2]
        for d in range(grad.shape[0]):
            grad[d] = total[:, d * width : (d + 1) * width].astype(bf16)


def out_back_call(scal, pieces, o, w, first):
    rows, width = pieces[0].shape
    inner = o.shape[1]
    at = pl.BlockSpec((rows, inner), lambda r, sc: (lax.bitwise_xor(sc[0], r), 0))
    grad = (w.shape[0], inner, w.shape[2])
    return pl.pallas_call(
        functools.partial(out_back_body, first=first),
        out_shape=(jax.ShapeDtypeStruct(o.shape, bf16), jax.ShapeDtypeStruct(grad, bf16)),
        grid_spec=pltpu.PrefetchScalarGridSpec(
            num_scalar_prefetch=1,
            grid=(4,),
            in_specs=[WHOLE] * 4 + [at, WHOLE],
            out_specs=(at, pl.BlockSpec(grad, lambda r, sc: (0, 0, 0))),
            scratch_shapes=[
                pltpu.VMEM((inner, width), bf16),
                pltpu.VMEM((rows, width), bf16),
                pltpu.VMEM((inner, width), f32),
            ],
        ),
        compiler_params=params(),
        name="out_back",
    )(scal, *pieces, o, w)


def qkv_back_body(scal, dq, dk, dv, w, near, far, merged, sums):
    t = pl.program_id(0)

    @pl.when(t == 0)
    def _():
        sums[...] = jnp.zeros_like(sums)

    low = jnp.concatenate([dq[...], dk[...], dv[...]], axis=1)
    merged[...] = low
    part = mm_t(low, w[...]).astype(bf16)
    sums[...] += jnp.sum(low.astype(f32), axis=0, keepdims=True)

    @pl.when(t < 2)
    def _():
        near[0] = part

    @pl.when(t >= 2)
    def _():
        far[0] = part


def qkv_back_call(scal, dq, dk, dv, w):
    keys, inner = dq.shape
    rows = keys // 4
    width = w.shape[0]
    where = lambda t, sc: (lax.bitwise_xor(sc[0], rel_of(t)), 0)
    at = pl.BlockSpec((rows, inner), where)
    return pl.pallas_call(
        qkv_back_body,
        out_shape=(
            jax.ShapeDtypeStruct((2, rows, width), bf16),
            jax.ShapeDtypeStruct((2, rows, width), bf16),
            jax.ShapeDtypeStruct((keys, 3 * inner), bf16),
            jax.ShapeDtypeStruct((1, 3 * inner), f32),
        ),
        grid_spec=pltpu.PrefetchScalarGridSpec(
            num_scalar_prefetch=1,
            grid=(4,),
            in_specs=[at, at, at, WHOLE],
            out_specs=(
                pl.BlockSpec((1, rows, width), near_map),
                pl.BlockSpec((1, rows, width), far_map),
                pl.BlockSpec((rows, 3 * inner), where),
                pl.BlockSpec((1, 3 * inner), lambda t, sc: (0, 0)),
            ),
        ),
        compiler_params=params(),
        name="qkv_back",
    )(scal, dq, dk, dv, w)


def in_back_body(x, a, b, c, dmid, gain, grad, sums):
    @pl.when(pl.program_id(0) == 0)
    def _():
        sums[...] = jnp.zeros_like(sums)

    unit, inv = normalize(x[...].astype(f32))
    e = (a[0].astype(f32) + b[0].astype(f32)) + c[...].astype(f32)
    grad[...] = (dmid[...] + norm_back(e, gain[...], unit, inv)).astype(bf16)
    sums[0:1, :] += jnp.sum(e * unit, axis=0, keepdims=True)
    sums[1:2, :] += jnp.sum(e, axis=0, keepdims=True)


def in_back_call(x, a, b, c, dmid, gain):
    rows, width = x.shape
    one = pl.BlockSpec((rows // 2, width), lambda i: (i, 0))
    first = pl.BlockSpec((1, rows // 2, width), lambda i: (0, i, 0))
    second = pl.BlockSpec((1, rows // 2, width), lambda i: (1, i, 0))
    row = pl.BlockSpec((1, width), lambda i: (0, 0))
    return pl.pallas_call(
        in_back_body,
        out_shape=(
            jax.ShapeDtypeStruct((rows, width), bf16),
            jax.ShapeDtypeStruct((8, width), f32),
        ),
        grid=(2,),
        in_specs=[one, second, first, one, one, row],
        out_specs=(one, pl.BlockSpec((8, width), lambda i: (0, 0))),
        compiler_params=params(),
        name="in_back",
    )(x, a, b, c, dmid, gain)


def remote(src, dst, send, recv, dp, seq):
    return pltpu.make_async_remote_copy(
        src_ref=src,
        dst_ref=dst,
        send_sem=send,
        recv_sem=recv,
        device_id=(dp, seq),
        device_id_type=pl.DeviceIdType.MESH,
    )


def greet(peers):
    barrier = pltpu.get_barrier_semaphore()
    for dp, seq in peers:
        pl.semaphore_signal(
            barrier, inc=1, device_id=(dp, seq), device_id_type=pl.DeviceIdType.MESH
        )
    pl.semaphore_wait(barrier, len(peers))


class GradSum:
    def __init__(self, part, acc, landx, landr, landl, sems, dp, seq):
        self.part, self.acc = part, acc
        self.landx, self.landr, self.landl = landx, landr, landl
        self.sems, self.dp, self.seq = sems, dp, seq
        self.z, self.x = dp // 2, dp % 2

    def cross(self, k):
        return remote(
            self.part.at[2 * k + (1 - self.x)],
            self.landx.at[k],
            self.sems.at[0, k],
            self.sems.at[1, k],
            2 * self.z + (1 - self.x),
            self.seq,
        )

    def right(self, b, src):
        return remote(
            src.at[b],
            self.landr.at[b],
            self.sems.at[2, b],
            self.sems.at[3, b],
            2 * ((self.z + 1) % 4) + self.x,
            self.seq,
        )

    def left(self, b, src):
        return remote(
            src.at[b],
            self.landl.at[b],
            self.sems.at[4, b],
            self.sems.at[5, b],
            2 * ((self.z + 3) % 4) + self.x,
            self.seq,
        )

    def start(self):
        for k in (3, 0, 2, 1):
            self.cross(k).start()

    def add_cross(self):
        for k in (3, 0, 2, 1):
            self.cross(k).wait_recv()
            own = self.part[2 * k + self.x].astype(f32)
            self.acc[k] = (own + self.landx[k].astype(f32)).astype(bf16)

    def stage(self, k):
        @pl.when(self.z == k)
        def _():
            for b in range(3, k, -1):
                src = self.acc
                if k > 0:
                    src = self.landr
                    self.right(b, src).wait_recv()
                    src[b] = (src[b].astype(f32) + self.acc[b].astype(f32)).astype(bf16)
                self.right(b, src).start()

        @pl.when(self.z == 3 - k)
        def _():
            for b in range(0, 3 - k):
                src = self.acc
                if k > 0:
                    src = self.landl
                    self.left(b, src).wait_recv()
                    src[b] = (src[b].astype(f32) + self.acc[b].astype(f32)).astype(bf16)
                self.left(b, src).start()

    def finish(self, out):
        z = self.z
        out[...] = self.acc[z].astype(f32)

        @pl.when(z > 0)
        def _():
            self.right(z, self.landr).wait_recv()
            out[...] += self.landr[z].astype(f32)

        @pl.when(z < 3)
        def _():
            self.left(z, self.landl).wait_recv()
            out[...] += self.landl[z].astype(f32)

    def drain(self):
        for k in range(4):
            self.cross(k).wait_send()
        for k in range(3):

            @pl.when(self.z == k)
            def _(k=k):
                for b in range(3, k, -1):
                    self.right(b, self.landr).wait_send()

            @pl.when(self.z == 3 - k)
            def _(k=k):
                for b in range(0, 3 - k):
                    self.left(b, self.landl).wait_send()

    @staticmethod
    def scratch(m, n):
        return [pltpu.VMEM((4, m, n), bf16)] * 4 + [pltpu.SemaphoreType.DMA((6, 4))]


SMALL_ROWS = 16


def tail_body(
    near, far, x, dmid, gain, gq, go, mid_sums, up_sum, qkv_sums,
    grad, gq_out, go_out, small_out,
    q_acc, q_x, q_r, q_l, q_sem, o_acc, o_x, o_r, o_l, o_sem,
    land_c, sum_y, land_y, row_sems, small, small_land, own, seq_land, small_sems, seq_sems,
):
    dp, seq = lax.axis_index("dp"), lax.axis_index("seq")
    mate, across = seq + 1 - 2 * (seq % 2), (seq + 2) % 4
    far_mate = (mate + 2) % 4
    greet([((dp + i) % 8, seq) for i in range(1, 8)] + [(dp, mate), (dp, across), (dp, far_mate)])
    rows, width = x.shape

    cores = [
        remote(near.at[k], land_c.at[k], row_sems.at[0, k], row_sems.at[1, k], dp, mate)
        for k in range(2)
    ]
    cores[1].start()
    cores[0].start()
    sum_q = GradSum(gq, q_acc, q_x, q_r, q_l, q_sem, dp, seq)
    sum_o = GradSum(go, o_acc, o_x, o_r, o_l, o_sem, dp, seq)
    sum_o.start()
    sum_q.start()

    cores[1].wait_recv()
    chunk = 128
    for i in range(rows // chunk):
        at = slice(i * chunk, (i + 1) * chunk)
        sum_y[at, :] = (far[0, at, :].astype(f32) + land_c[1, at, :].astype(f32)).astype(bf16)
    over = remote(sum_y, land_y, row_sems.at[0, 2], row_sems.at[1, 2], dp, across)
    over.start()

    small[...] = jnp.zeros_like(small)
    for d in range(8):
        at = slice(d * LANES, (d + 1) * LANES)
        for row, src in ((4, mid_sums[2:3, at]), (5, mid_sums[0:1, at]), (6, mid_sums[1:2, at])):
            small[d, row : row + 1, :] = src
        small[d, 11:12, :] = mid_sums[3:4, at]
    for i in range(2):
        at = slice(i * LANES, (i + 1) * LANES)
        small[pl.ds(seq, 1), 2 + i, :] = qkv_sums[:, at]
        at = slice((4 + i) * LANES, (5 + i) * LANES)
        small[pl.ds(4 + seq, 1), 2 + i, :] = qkv_sums[:, at]
    for i in range(8):
        at = slice(i * LANES, (i + 1) * LANES)
        small[pl.ds(2 * seq + i // 4, 1), 7 + i % 4, :] = up_sum[:, at]

    sum_o.add_cross()
    sum_o.stage(0)
    sum_o.stage(1)
    sum_q.add_cross()
    sum_q.stage(0)
    sum_o.stage(2)

    cores[0].wait_recv()
    over.wait_recv()
    gain_sum = jnp.zeros((1, width), f32)
    shift_sum = jnp.zeros((1, width), f32)
    for i in range(rows // chunk):
        at = slice(i * chunk, (i + 1) * chunk)
        unit, inv = normalize(x[at, :].astype(f32))
        e = (far[1, at, :].astype(f32) + land_c[0, at, :].astype(f32)) + land_y[at, :].astype(f32)
        grad[at, :] = (dmid[at, :] + norm_back(e, gain[...], unit, inv)).astype(bf16)
        gain_sum += jnp.sum(e * unit, axis=0, keepdims=True)
        shift_sum += jnp.sum(e, axis=0, keepdims=True)
    for d in range(8):
        at = slice(d * LANES, (d + 1) * LANES)
        small[d, 0:1, :] = gain_sum[:, at]
        small[d, 1:2, :] = shift_sum[:, at]

    def small_to(i):
        peer = (dp + i) % 8
        return remote(
            small.at[peer], small_land.at[i], small_sems.at[0, i], small_sems.at[1, i], peer, seq
        )

    for i in range(1, 8):
        small_to(i).start()
    sum_q.stage(1)
    sum_q.stage(2)
    sum_o.finish(go_out)
    total = small[dp]
    for i in range(1, 8):
        small_to(i).wait_recv()
        total = total + small_land[i]
    own[...] = total

    def seq_to(i, peer):
        return remote(own, seq_land.at[i], seq_sems.at[0, i], seq_sems.at[1, i], dp, peer)

    group = [seq_to(0, mate), seq_to(1, across), seq_to(2, far_mate)]
    for copy in group:
        copy.start()
    sum_q.finish(gq_out)
    for copy in group:
        copy.wait_recv()
    small_out[...] = (own[...] + seq_land[0]) + (seq_land[1] + seq_land[2])

    for copy in group + cores + [over]:
        copy.wait_send()
    for i in range(1, 8):
        small_to(i).wait_send()
    sum_o.drain()
    sum_q.drain()


def tail_call(near, far, x, dmid, gain, gq, go, mid_sums, up_sum, qkv_sums):
    rows, width = x.shape
    sem = pltpu.SemaphoreType.DMA
    return pl.pallas_call(
        tail_body,
        out_shape=(
            jax.ShapeDtypeStruct((rows, width), bf16),
            jax.ShapeDtypeStruct(gq.shape[1:], f32),
            jax.ShapeDtypeStruct(go.shape[1:], f32),
            jax.ShapeDtypeStruct((SMALL_ROWS, LANES), f32),
        ),
        in_specs=[WHOLE] * 10,
        out_specs=(WHOLE,) * 4,
        scratch_shapes=GradSum.scratch(*gq.shape[1:])
        + GradSum.scratch(*go.shape[1:])
        + [
            pltpu.VMEM((2, rows, width), bf16),
            pltpu.VMEM((rows, width), bf16),
            pltpu.VMEM((rows, width), bf16),
            sem((2, 3)),
            pltpu.VMEM((8, SMALL_ROWS, LANES), f32),
            pltpu.VMEM((8, SMALL_ROWS, LANES), f32),
            pltpu.VMEM((SMALL_ROWS, LANES), f32),
            pltpu.VMEM((3, SMALL_ROWS, LANES), f32),
            sem((2, 8)),
            sem((2, 3)),
        ],
        compiler_params=params(collective_id=3, has_side_effects=True),
        name="tail",
    )(near, far, x, dmid, gain, gq, go, mid_sums, up_sum, qkv_sums)


class Gather:
    def __init__(self, own, out, sems, dp, seq):
        self.own, self.out, self.sems = own, out, sems
        self.seq, self.z, self.x = seq, dp // 2, dp % 2

    def along(self, k, step, src=None):
        slot = self.out.at[2 * k + self.x]
        return remote(
            slot if src is None else src,
            slot,
            self.sems.at[0 if step > 0 else 1, k],
            self.sems.at[3, k],
            2 * ((self.z + step + 4) % 4) + self.x,
            self.seq,
        )

    def over(self, k, src=None):
        slot = self.out.at[2 * k + self.x]
        return remote(
            slot if src is None else src,
            slot,
            self.sems.at[2, k],
            self.sems.at[4, k],
            2 * self.z + (1 - self.x),
            self.seq,
        )

    def keep(self):
        return pltpu.make_async_copy(
            self.own, self.out.at[2 * self.z + self.x], self.sems.at[5, 0]
        )

    def start(self):
        z = self.z

        @pl.when(z < 3)
        def _():
            self.along(z, 1, self.own).start()

        @pl.when(z > 0)
        def _():
            self.along(z, -1, self.own).start()

        self.over(z, self.own).start()
        self.keep().start()

    def hop(self, dist):
        z = self.z

        @pl.when(z - dist >= 0)
        def _():
            k = z - dist
            self.along(k, 1).wait_recv()

            @pl.when(z < 3)
            def _():
                self.along(k, 1).start()

            self.over(k).start()

        @pl.when(z + dist <= 3)
        def _():
            k = z + dist
            self.along(k, -1).wait_recv()

            @pl.when(z > 0)
            def _():
                self.along(k, -1).start()

            self.over(k).start()

    def finish(self):
        z = self.z
        self.keep().wait()
        for k in range(4):
            self.over(k).wait_recv()
            self.over(k).wait_send()

            @pl.when((z < 3) & (z >= k))
            def _(k=k):
                self.along(k, 1).wait_send()

            @pl.when((z > 0) & (z <= k))
            def _(k=k):
                self.along(k, -1).wait_send()

    @staticmethod
    def scratch():
        return pltpu.SemaphoreType.DMA((6, 4))


class Spread:
    def __init__(self, own, rows, sems, dp, seq):
        mate, across = seq + 1 - 2 * (seq % 2), (seq + 2) % 4
        to = lambda src, r, peer: remote(src, rows.at[r], sems.at[0, r], sems.at[1, r], dp, peer)
        self.near, self.far = to(own, 1, mate), to(own, 2, across)
        self.last = to(rows.at[2], 3, mate)

    def start(self):
        self.far.start()
        self.near.start()

    def forward(self):
        self.far.wait_recv()
        self.last.start()

    def drain(self):
        for copy in (self.near, self.far, self.last):
            copy.wait_send()


def neighbours(seq):
    mate = seq + 1 - 2 * (seq % 2)
    return mate, (seq + 2) % 4, (mate + 2) % 4


def block_at(seq, rel):
    return 2 * ((seq // 2 + rel // 2) % 2) + (seq + rel) % 2


def front_body(
    wq, wo, x, small,
    wq_all, wo_all, x_rows, gain1, shift1, bias_qkv, bias_out, gain2, shift2, bias_up, bias_down,
    vectors, q_sem, o_sem, x_sem, seq_sem, dp_sem, keep_sem,
):
    dp, seq = lax.axis_index("dp"), lax.axis_index("seq")
    greet([((dp + i) % 8, seq) for i in range(1, 8)] + [(dp, p) for p in neighbours(seq)])
    gather_q = Gather(wq, wq_all, q_sem, dp, seq)
    gather_o = Gather(wo, wo_all, o_sem, dp, seq)
    rows = Spread(x, x_rows, x_sem, dp, seq)
    rows.start()
    gather_q.start()
    keep_x = pltpu.make_async_copy(x, x_rows.at[0], keep_sem.at[0])
    keep_x.start()
    keep_v = pltpu.make_async_copy(small, vectors.at[dp, seq], keep_sem.at[1])
    keep_v.start()
    group = [
        remote(small, vectors.at[dp, seq], seq_sem.at[0, i], seq_sem.at[1, i], dp, peer)
        for i, peer in enumerate(neighbours(seq))
    ]
    for copy in group:
        copy.start()
    gather_o.start()
    keep_v.wait()
    for copy in group:
        copy.wait_recv()

    def to_dp(i):
        return remote(
            vectors.at[dp], vectors.at[dp], dp_sem.at[0, i], dp_sem.at[1, i], (dp + i) % 8, seq
        )

    for i in range(1, 8):
        to_dp(i).start()
    gather_q.hop(1)
    gather_o.hop(1)
    for i in range(1, 8):
        to_dp(i).wait_recv()
    for ref, at in (
        (gain1, 192), (shift1, 224), (bias_out, 256), (gain2, 288), (shift2, 320), (bias_down, 352),
    ):
        for d in range(8):
            ref[:, d * LANES : (d + 1) * LANES] = jnp.concatenate(
                [vectors[d, i, :, at : at + 32] for i in range(4)], axis=1
            )
    for part in range(2):
        for half in range(2):
            lane = part * 512 + half * LANES
            bias_qkv[:, lane : lane + LANES] = jnp.concatenate(
                [vectors[4 * part + seq, 2 * half + i, :, 128:192] for i in range(2)], axis=1
            )
    bias_qkv[:, 256:512] = jnp.zeros((1, 256), f32)
    for i in range(8):
        bias_up[:, i * LANES : (i + 1) * LANES] = vectors[2 * seq + i // 4, i % 4, :, 0:LANES]
    gather_q.hop(2)
    gather_o.hop(2)
    rows.forward()
    gather_q.hop(3)
    gather_o.hop(3)
    gather_q.finish()
    gather_o.finish()
    rows.near.wait_recv()
    rows.last.wait_recv()
    rows.drain()
    keep_x.wait()
    for copy in group:
        copy.wait_send()
    for i in range(1, 8):
        to_dp(i).wait_send()


def front_call(wq, wo, x, small):
    rows, width = x.shape
    one = lambda n: jax.ShapeDtypeStruct((1, n), f32)
    sem = pltpu.SemaphoreType.DMA
    return pl.pallas_call(
        front_body,
        out_shape=(
            jax.ShapeDtypeStruct((8, *wq.shape), bf16),
            jax.ShapeDtypeStruct((8, *wo.shape), bf16),
            jax.ShapeDtypeStruct((4, rows, width), bf16),
            one(width), one(width), one(wq.shape[1]), one(width), one(width), one(width),
            one(width), one(width),
        ),
        in_specs=[WHOLE] * 4,
        out_specs=(WHOLE,) * 11,
        scratch_shapes=[
            pltpu.VMEM((8, 4, 1, small.shape[-1]), f32),
            Gather.scratch(),
            Gather.scratch(),
            sem((2, 4)),
            sem((2, 3)),
            sem((2, 8)),
            sem((2,)),
        ],
        compiler_params=params(collective_id=4, has_side_effects=True),
        name="front",
    )(wq, wo, x, small.reshape(1, -1))


def attention_body(
    scal, slopes, x_rows, g, wq, wo, gain1, shift1, bias_qkv, bias_out, gain2, shift2,
    h1, qkv, o, lse, mid, h2, g_rows,
    bias, vt, flat, part, land_c, sum_y, land_y, g_sem, row_sems, keep_sem,
):
    dp, seq = lax.axis_index("dp"), lax.axis_index("seq")
    mate, across, _ = neighbours(seq)
    greet([(dp, mate), (dp, across)])
    rows, width = g.shape
    keys = qkv.shape[0]
    inner = o.shape[1]
    pairs = inner // LANES
    spread_g = Spread(g, g_rows, g_sem, dp, seq)
    spread_g.start()
    keep = pltpu.make_async_copy(g, g_rows.at[0], keep_sem.at[0])
    keep.start()
    lay_columns(wo, 0, flat)

    def project(r, carry):
        at = pl.ds(pl.multiple_of(block_at(seq, r) * rows, rows), rows)
        unit, _ = normalize(x_rows[r].astype(f32))
        low = (unit * gain1[...] + shift1[...]).astype(bf16)
        h1[at, :] = low
        qkv[at, :] = (mm(low, wq[...]) + bias_qkv[...]).astype(bf16)
        return carry

    lax.fori_loop(0, 4, project, 0)

    def prepare(p, carry):
        pos = lax.broadcasted_iota(jnp.int32, (keys, LANES), 0)
        ramp = pos.astype(f32)
        inside = pos < scal[1]
        for h in range(2):
            bias[2 * p + h] = jnp.where(inside, ramp * slopes[2 * p + h], NEG)
        lane = pl.ds(pl.multiple_of(2 * inner + p * LANES, LANES), LANES)
        vt[p] = qkv[:, lane].T
        return carry

    lax.fori_loop(0, pairs, prepare, 0)
    spread_g.forward()

    cores = [
        remote(part.at[r], land_c.at[k], row_sems.at[0, k], row_sems.at[1, k], dp, mate)
        for k, r in ((0, 1), (1, 3))
    ]
    over = remote(sum_y, land_y, row_sems.at[0, 2], row_sems.at[1, 2], dp, across)
    chunk = 128

    def attend(t, carry):
        rel = 3 - t
        c_now = block_at(seq, rel)
        at = pl.ds(pl.multiple_of(c_now * rows, rows), rows)
        for c in range(keys // rows):

            @pl.when(c_now == c)
            def _(c=c):
                length = (c + 1) * rows

                def one_pair(p, carry):
                    lane = pl.ds(pl.multiple_of(p * LANES, LANES), LANES)
                    k_lane = pl.ds(pl.multiple_of(inner + p * LANES, LANES), LANES)
                    scaled = qkv[c * rows : length, lane] * bf16(HEAD_DIM**-0.5)
                    k = qkv[0:length, k_lane]
                    outs, logs = [], []
                    for h in range(2):
                        s = scores(k, head_only(scaled, h), bias[2 * p + h, 0:length, :])
                        top = jnp.max(s, axis=0, keepdims=True)
                        e = jnp.exp(s - top)
                        total = jnp.sum(e, axis=0, keepdims=True)
                        half = vt[p, h * HEAD_DIM : (h + 1) * HEAD_DIM, 0:length]
                        outs.append(mm(half, e.astype(bf16)) / total)
                        logs.append(top + jnp.log(total))
                    o[c * rows : length, lane] = jnp.concatenate(outs, axis=0).T.astype(bf16)
                    lse[p, 0:2, c * rows : length] = jnp.concatenate(logs, axis=0)
                    return carry

                lax.fori_loop(0, pairs, one_pair, 0)

        part[rel] = mm(o[at, :], flat[...]).astype(bf16)

        @pl.when(t == 0)
        def _():
            cores[1].start()

        @pl.when(t == 1)
        def _():
            cores[1].wait_recv()
            for i in range(rows // chunk):
                at = slice(i * chunk, (i + 1) * chunk)
                total = part[2, at, :].astype(f32) + land_c[1, at, :].astype(f32)
                sum_y[at, :] = total.astype(bf16)
            over.start()

        @pl.when(t == 2)
        def _():
            cores[0].start()

        return carry

    lax.fori_loop(0, 4, attend, 0)
    cores[0].wait_recv()
    over.wait_recv()

    def second_norm(i, carry):
        at = pl.ds(pl.multiple_of(i * chunk, chunk), chunk)
        total = (part[0, at, :].astype(f32) + land_c[0, at, :].astype(f32)) + land_y[
            at, :
        ].astype(f32)
        value = x_rows[0, at, :].astype(f32) + (total + bias_out[...])
        mid[at, :] = value
        unit, _ = normalize(value)
        h2[at, :] = (unit * gain2[...] + shift2[...]).astype(bf16)
        return carry

    lax.fori_loop(0, rows // chunk, second_norm, 0)
    spread_g.near.wait_recv()
    spread_g.last.wait_recv()
    spread_g.drain()
    keep.wait()
    for copy in cores + [over]:
        copy.wait_send()


def scores(k, qm, ramp):
    block = qm.shape[0]
    length = k.shape[0]
    s = mm_t(k, qm) + jnp.concatenate([ramp] * (block // LANES), axis=1)
    key = lax.broadcasted_iota(jnp.int32, (block, block), 0)
    query = lax.broadcasted_iota(jnp.int32, (block, block), 1)
    last = jnp.where(key <= query, s[length - block :], NEG)
    if length == block:
        return last
    return jnp.concatenate([s[: length - block], last], axis=0)


def attention_call(scal, slopes, x_rows, g, wq, wo, *vectors):
    rows, width = g.shape
    keys = 4 * rows
    inner = wo.shape[1]
    pairs = inner // LANES
    sem = pltpu.SemaphoreType.DMA
    return pl.pallas_call(
        attention_body,
        out_shape=(
            jax.ShapeDtypeStruct((keys, width), bf16),
            jax.ShapeDtypeStruct((keys, 3 * inner), bf16),
            jax.ShapeDtypeStruct((keys, inner), bf16),
            jax.ShapeDtypeStruct((pairs, 8, keys), f32),
            jax.ShapeDtypeStruct((rows, width), f32),
            jax.ShapeDtypeStruct((rows, width), bf16),
            jax.ShapeDtypeStruct((4, rows, width), bf16),
        ),
        in_specs=[SCALAR, SCALAR] + [WHOLE] * (4 + len(vectors)),
        out_specs=(WHOLE,) * 7,
        scratch_shapes=[
            pltpu.VMEM((2 * pairs, keys, LANES), f32),
            pltpu.VMEM((pairs, LANES, keys), bf16),
            pltpu.VMEM((inner, width), bf16),
            pltpu.VMEM((4, rows, width), bf16),
            pltpu.VMEM((2, rows, width), bf16),
            pltpu.VMEM((rows, width), bf16),
            pltpu.VMEM((rows, width), bf16),
            sem((2, 4)),
            sem((2, 3)),
            sem((1,)),
        ],
        compiler_params=params(collective_id=5, has_side_effects=True),
        name="attention",
    )(scal, slopes, x_rows, g, wq, wo, *vectors)


def finish_body(
    scal, grad, gq, go, small,
    grad_out, gq_out, go_out, gain1, shift1, qv, bout, gain2, shift2, up, down,
):
    seq = scal[0]
    grad_out[...] = grad[...]
    go_out[...] = go[...]
    cols = gq_out.shape[2]
    for c in range(3):
        gq_out[:, c, :] = gq[:, c * cols : (c + 1) * cols]
    for ref, row in ((gain1, 0), (shift1, 1), (bout, 4), (gain2, 5), (shift2, 6), (down, 11)):
        n = ref.shape[1]
        value = small[row : row + 1, 0:n]
        for i in range(1, 4):
            value = jnp.where(seq == i, small[row : row + 1, i * n : (i + 1) * n], value)
        ref[...] = value
    value = small[2:3, 0:64]
    for i in range(1, 4):
        at = 64 * (i % 2)
        value = jnp.where(seq == i, small[2 + i // 2 : 3 + i // 2, at : at + 64], value)
    qv[...] = value
    up[...] = small[pl.ds(7 + seq, 1), :]


def finish_call(scal, grad, gq, go, small):
    one = lambda n: jax.ShapeDtypeStruct((1, n), f32)
    return pl.pallas_call(
        finish_body,
        out_shape=(
            jax.ShapeDtypeStruct(grad.shape, bf16),
            jax.ShapeDtypeStruct((gq.shape[0], 3, gq.shape[1] // 3), f32),
            jax.ShapeDtypeStruct(go.shape, f32),
            one(32), one(32), one(64), one(32), one(32), one(32), one(LANES), one(32),
        ),
        in_specs=[SCALAR] + [WHOLE] * 4,
        out_specs=(WHOLE,) * 11,
        compiler_params=params(),
        name="finish",
    )(scal, grad, gq, go, small)


def after(value, *others):
    return lax.optimization_barrier((value, *others))[0]


def on_device(
    dp_n,
    seq_n,
    tokens,
    lengths,
    cotangent,
    ln1_gain,
    ln1_shift,
    w_qkv,
    b_qv,
    w_out,
    b_out,
    ln2_gain,
    ln2_shift,
    w_fc1,
    b_fc1,
    w_fc2,
    b_fc2,
):
    count = dp_n * seq_n
    rows, width = tokens.shape
    heads = width // HEAD_DIM
    inner = w_out.shape[0]
    ff = w_fc1.shape[1]
    s = lax.axis_index("seq")
    length = lengths[0]

    scal = jnp.stack([s.astype(jnp.int32), length])
    slopes = 2.0 ** (-8.0 * (jnp.arange(heads, dtype=jnp.int32) + 1).astype(f32) / heads)
    slopes = lax.dynamic_slice(slopes, (s * (heads // seq_n),), (heads // seq_n,))
    valid = s * rows + jnp.arange(rows, dtype=jnp.int32) < length
    grad_low = jnp.where(valid[:, None], cotangent, jnp.zeros_like(cotangent))
    wq_own = jnp.concatenate([w_qkv[:, c, :] for c in range(3)], axis=1)
    small = (ln1_gain, ln1_shift, b_qv, b_out, ln2_gain, ln2_shift, b_fc1, b_fc2)
    sizes = [v.shape[0] for v in small]
    ends = [sum(sizes[: i + 1]) for i in range(len(sizes))]
    block = 384
    fast = dp_n == 8 and seq_n == 4 and width == 8 * LANES and ff == width and inner == 2 * LANES
    if fast:
        parts = dp_n
        w1 = lax.all_gather(w_fc1, "dp", axis=0, tiled=True)
        w_cols = lax.all_gather(w_fc2, "dp", axis=0, tiled=False)
        order = (b_fc1, b_qv, ln1_gain, ln1_shift, b_out, ln2_gain, ln2_shift, b_fc2)
        wq, w_o, x_rows, gain1, shift1, qkv_bias, bias_out, gain2, shift2, own_up, bias_down = (
            front_call(
                wq_own, w_out, tokens, jnp.concatenate([v.astype(f32) for v in order])
            )
        )
        wq = wq.reshape(width, 3 * inner)
        h1, qkv, o, lse, mid, h2, g_rows = attention_call(
            scal, slopes, x_rows, grad_low, wq, w_o,
            gain1, shift1, qkv_bias, bias_out, gain2, shift2,
        )
        out_first = 0
    else:
        wq = lax.all_gather(wq_own, "dp", axis=0, tiled=True)
        col = w_fc2.shape[1]
        both = jnp.concatenate([w_fc2, w_out], axis=0)
        if col % LANES == 0:
            parts = dp_n
            w_cols = lax.all_gather(both, "dp", axis=0, tiled=False)
        else:
            parts = 1
            w_cols = lax.all_gather(both, "dp", axis=1, tiled=True)[None]
        w_o = w_cols
        out_first = ff
        w1 = lax.all_gather(w_fc1, "dp", axis=0, tiled=True)
        packed = small_gather(jnp.concatenate([v.astype(f32) for v in small]), count, seq_n)
        packed = packed.reshape(count, ends[-1])
        gain1, shift1, bias_qv, bias_out, gain2, shift2, bias_up, bias_down = (
            packed[:, e - n : e].reshape(1, count * n) for e, n in zip(ends, sizes)
        )
        own_bias = lambda v, n: lax.dynamic_slice(v, (0, s * n), (1, n))
        own_up = own_bias(bias_up, ff)
        qkv_bias = jnp.concatenate(
            [
                own_bias(bias_qv[:, :width], inner),
                jnp.zeros((1, inner), f32),
                own_bias(bias_qv[:, width:], inner),
            ],
            axis=1,
        )
        x_pieces = spread(tokens)
        g_rows = jnp.stack(spread(after(grad_low, x_pieces[3])))
        h1, qkv = qkv_call(scal, x_pieces, wq, gain1, shift1, qkv_bias)
        o, lse = attend_call(scal, slopes, qkv, block)
        near, far = out_call(scal, o, w_o, out_first)
        got, across = reduce_rows(near, far)
        mid, h2 = mid_call(tokens, far, got, across, bias_out, gain2, shift2)

    h_pieces = spread(h2)
    y_near, y_far, d_near, d_far, a_all, du_all, h_all, g_all, up_sum = mlp_call(
        h_pieces, g_rows, w1, w_cols, own_up
    )
    got, across = reduce_rows(d_near, d_far)
    grad_down = outer_call(a_all, g_all, parts, "grad_fc2")
    grad_up = outer_call(h_all, du_all, 1, "grad_fc1")
    dmid, dbr, mid_sums = mid_back_call(mid, d_far, got, across, grad_low, gain2)
    b_pieces = spread(dbr)

    y_near = after(y_near, b_pieces[3])
    got, across = reduce_rows(y_near, y_far)
    output = (
        mid + ((y_far[1].astype(f32) + got[0].astype(f32)) + across.astype(f32) + bias_down)
    ).astype(bf16)

    do, grad_out = out_back_call(scal, b_pieces, o, w_o, out_first)
    dq, dk, dv = attend_back_call(scal, slopes, qkv, o, do, lse, block)
    near, far, merged, qkv_sums = qkv_back_call(scal, dq, dk, dv, wq)
    grad_qkv = outer_call(h1, merged, 1, "grad_qkv")

    def shared(part):
        if parts > 1:
            return lax.psum_scatter(part, "dp", scatter_dimension=0, tiled=False).astype(f32)
        return lax.psum_scatter(part, "dp", scatter_dimension=1, tiled=True).astype(f32)

    grad_down = shared(grad_down if parts > 1 else grad_down)
    grad_up = lax.psum_scatter(grad_up, "dp", scatter_dimension=0, tiled=True).astype(f32)
    if fast:
        tail = tail_call(
            near, far, tokens, dmid, gain1, grad_qkv.reshape(8, -1, 3 * inner), grad_out,
            mid_sums, up_sum, qkv_sums,
        )
        grad_tokens, grad_qkv, grad_out, *vectors = finish_call(scal, *tail)
        g_gain1, g_shift1, g_qv, g_bout, g_gain2, g_shift2, g_up, g_down = (
            v.reshape(n) for v, n in zip(vectors, sizes)
        )
        return (
            output, grad_tokens, g_gain1, g_shift1, grad_qkv, g_qv, grad_out, g_bout,
            g_gain2, g_shift2, grad_up, g_up, grad_down, g_down,
        )

    got, across = reduce_rows(near, far)
    grad_tokens, in_sums = in_back_call(tokens, far, got, across, dmid, gain1)
    grad_out = shared(grad_out if parts > 1 else grad_out[0])
    grad_qkv = lax.psum_scatter(grad_qkv, "dp", scatter_dimension=0, tiled=True)
    grad_qkv = grad_qkv.astype(f32).reshape(w_qkv.shape)

    def own_slot(v, total):
        return lax.dynamic_update_slice(jnp.zeros((1, total), f32), v, (0, s * v.shape[1]))

    sums = (
        in_sums[0:1],
        in_sums[1:2],
        jnp.concatenate(
            [own_slot(qkv_sums[:, :inner], width), own_slot(qkv_sums[:, 2 * inner :], width)], axis=1
        ),
        mid_sums[2:3],
        mid_sums[0:1],
        mid_sums[1:2],
        own_slot(up_sum, seq_n * ff),
        mid_sums[3:4],
    )
    grads = jnp.concatenate([v.reshape(count, n) for v, n in zip(sums, sizes)], axis=1)
    grads = small_scatter(grads, count, seq_n).reshape(ends[-1])
    g_gain1, g_shift1, g_qv, g_bout, g_gain2, g_shift2, g_up, g_down = (
        grads[e - n : e] for e, n in zip(ends, sizes)
    )
    return (
        output,
        grad_tokens,
        g_gain1,
        g_shift1,
        grad_qkv,
        g_qv,
        grad_out,
        g_bout,
        g_gain2,
        g_shift2,
        grad_up,
        g_up,
        grad_down,
        g_down,
    )


def solution(mesh):
    rows = P(("dp", "seq"), None)
    vec = P(("dp", "seq"))
    merged = P("dp", None, "seq")
    return jax.shard_map(
        functools.partial(on_device, mesh.shape["dp"], mesh.shape["seq"]),
        mesh=mesh,
        in_specs=(
            rows, P("dp"), rows, vec, vec, merged, vec, P("seq", "dp"), vec, vec, vec,
            P("dp", "seq"), vec, P("seq", "dp"), vec,
        ),
        out_specs=(
            rows, rows, vec, vec, merged, vec, P("seq", "dp"), vec, vec, vec,
            P("dp", "seq"), vec, P("seq", "dp"), vec,
        ),
        check_vma=False,
    )
```

```python
import functools
import math

import jax
import jax.numpy as jnp
from jax import lax
from jax.experimental import pallas as pl
from jax.experimental.pallas import tpu as pltpu
from jax.sharding import PartitionSpec as P

HEAD_DIM = 64
EPS = 1e-05
GELU_COEF = 0.044715
NEG = -1e30
LANES = 128
VMEM_BYTES = 60 * 1024 * 1024

f32 = jnp.float32
bf16 = jnp.bfloat16
WHOLE = pl.BlockSpec(memory_space=pltpu.VMEM)
SCALAR = pl.BlockSpec(memory_space=pltpu.SMEM)


def mm(a, b):
    return jnp.dot(a, b, preferred_element_type=f32)


def mm_t(a, b):
    return lax.dot_general(a, b, (((1,), (1,)), ((), ())), preferred_element_type=f32)


def params(**kw):
    return pltpu.CompilerParams(vmem_limit_bytes=VMEM_BYTES, **kw)


def normalize(v):
    width = v.shape[-1]
    centred = v - jnp.sum(v, axis=-1, keepdims=True) * (1.0 / width)
    inv = lax.rsqrt(jnp.sum(centred * centred, axis=-1, keepdims=True) * (1.0 / width) + EPS)
    return centred * inv, inv


def norm_back(grad_out, gain, unit, inv):
    width = unit.shape[-1]
    scaled = grad_out * gain
    mean_one = jnp.sum(scaled, axis=-1, keepdims=True) * (1.0 / width)
    mean_two = jnp.sum(scaled * unit, axis=-1, keepdims=True) * (1.0 / width)
    return inv * (scaled - mean_one - unit * mean_two)


def device_of(index, seq_n):
    return (index // seq_n, index % seq_n)


def greet_all(me, count, seq_n):
    barrier = pltpu.get_barrier_semaphore()

    def hello(i, carry):
        peer = (me + i) % count
        pl.semaphore_signal(
            barrier, inc=1, device_id=device_of(peer, seq_n), device_id_type=pl.DeviceIdType.MESH
        )
        return carry

    lax.fori_loop(1, count, hello, 0)
    pl.semaphore_wait(barrier, count - 1)


def small_gather_body(count, seq_n, x_ref, out_ref, send_sem, recv_sem):
    me = lax.axis_index("dp") * seq_n + lax.axis_index("seq")
    greet_all(me, count, seq_n)

    def copy_to(i):
        peer = (me + i) % count
        return pltpu.make_async_remote_copy(
            src_ref=x_ref,
            dst_ref=out_ref.at[pl.ds(me, 1)],
            send_sem=send_sem.at[i],
            recv_sem=recv_sem.at[i],
            device_id=device_of(peer, seq_n),
            device_id_type=pl.DeviceIdType.MESH,
        )

    def begin(i, carry):
        copy_to(i).start()
        return carry

    def finish(i, carry):
        copy_to(i).wait()
        return carry

    lax.fori_loop(1, count, begin, 0)
    out_ref[pl.ds(me, 1)] = x_ref[...]
    lax.fori_loop(1, count, finish, 0)


def small_gather(x, count, seq_n):
    width = x.shape[-1]
    return pl.pallas_call(
        functools.partial(small_gather_body, count, seq_n),
        out_shape=jax.ShapeDtypeStruct((count, 1, width), f32),
        in_specs=[WHOLE],
        out_specs=WHOLE,
        scratch_shapes=[pltpu.SemaphoreType.DMA((count,)), pltpu.SemaphoreType.DMA((count,))],
        compiler_params=pltpu.CompilerParams(collective_id=1, has_side_effects=True),
        name="small_gather",
    )(x.reshape(1, 1, width))


def small_scatter_body(count, seq_n, v_ref, out_ref, land, send_sem, recv_sem):
    me = lax.axis_index("dp") * seq_n + lax.axis_index("seq")
    greet_all(me, count, seq_n)

    def copy_to(i):
        peer = (me + i) % count
        return pltpu.make_async_remote_copy(
            src_ref=v_ref.at[pl.ds(peer, 1)],
            dst_ref=land.at[pl.ds(i, 1)],
            send_sem=send_sem.at[i],
            recv_sem=recv_sem.at[i],
            device_id=device_of(peer, seq_n),
            device_id_type=pl.DeviceIdType.MESH,
        )

    def begin(i, carry):
        copy_to(i).start()
        return carry

    def finish(i, total):
        copy_to(i).wait()
        return total + land[pl.ds(i, 1)]

    lax.fori_loop(1, count, begin, 0)
    out_ref[...] = lax.fori_loop(1, count, finish, v_ref[pl.ds(me, 1)])


def small_scatter(v, count, seq_n):
    width = v.shape[-1]
    return pl.pallas_call(
        functools.partial(small_scatter_body, count, seq_n),
        out_shape=jax.ShapeDtypeStruct((1, 1, width), f32),
        in_specs=[WHOLE],
        out_specs=WHOLE,
        scratch_shapes=[
            pltpu.VMEM((count, 1, width), f32),
            pltpu.SemaphoreType.DMA((count,)),
            pltpu.SemaphoreType.DMA((count,)),
        ],
        compiler_params=pltpu.CompilerParams(collective_id=2, has_side_effects=True),
        name="small_scatter",
    )(v.reshape(count, 1, width))


def swap(x, bit):
    return lax.ppermute(x, "seq", [(i, i ^ bit) for i in range(4)])


def spread(own):
    far = swap(own, 2)
    return own, swap(own, 1), far, swap(far, 1)


def reduce_rows(near, far):
    got = swap(near, 1)
    across = swap(far[0] + got[1], 2)
    return got, across


def pick(step, refs, dest):
    for k, ref in enumerate(refs):

        @pl.when(step == k)
        def _(ref=ref):
            dest[...] = ref[...]


ORDER = (1, 3, 2, 0)


def rel_of(t):
    return jnp.where(t == 0, 1, jnp.where(t == 1, 3, jnp.where(t == 2, 2, 0)))


def qkv_body(scal, x0, x1, x2, x3, w, gain, shift, bias, h1, qkv, rows):
    pick(pl.program_id(0), (x0, x1, x2, x3), rows)
    unit, _ = normalize(rows[...].astype(f32))
    low = (unit * gain[...] + shift[...]).astype(bf16)
    h1[...] = low
    qkv[...] = (mm(low, w[...]) + bias[...]).astype(bf16)


def qkv_call(scal, pieces, w, gain, shift, bias):
    rows, width = pieces[0].shape
    cols = w.shape[1]
    out = lambda r, sc: (lax.bitwise_xor(sc[0], r), 0)
    return pl.pallas_call(
        qkv_body,
        out_shape=(
            jax.ShapeDtypeStruct((4 * rows, width), bf16),
            jax.ShapeDtypeStruct((4 * rows, cols), bf16),
        ),
        grid_spec=pltpu.PrefetchScalarGridSpec(
            num_scalar_prefetch=1,
            grid=(4,),
            in_specs=[WHOLE] * 8,
            out_specs=(pl.BlockSpec((rows, width), out), pl.BlockSpec((rows, cols), out)),
            scratch_shapes=[pltpu.VMEM((rows, width), bf16)],
        ),
        compiler_params=params(),
        name="qkv",
    )(scal, *pieces, w, gain, shift, bias)


def make_bias(scal, slopes, pair, bias, keys):
    pos = lax.broadcasted_iota(jnp.int32, (keys, LANES), 0)
    inside = pos < scal[1]
    ramp = pos.astype(f32)
    for h in range(2):
        bias[h] = jnp.where(inside, ramp * slopes[2 * pair + h], NEG)


def head_only(x, h):
    lane = lax.broadcasted_iota(jnp.int32, x.shape, 1)
    return jnp.where((lane >= h * HEAD_DIM) & (lane < (h + 1) * HEAD_DIM), x, jnp.zeros_like(x))


def score_t(k_ref, qm, bias, h, length):
    block = qm.shape[0]
    s = mm_t(k_ref[0:length, :], qm)
    b = bias[h, 0:length, :]
    s = s + jnp.concatenate([b] * (block // LANES), axis=1)
    key = lax.broadcasted_iota(jnp.int32, (block, block), 0)
    query = lax.broadcasted_iota(jnp.int32, (block, block), 1)
    last = jnp.where(key <= query, s[length - block :], NEG)
    if length == block:
        return last
    return jnp.concatenate([s[: length - block], last], axis=0)


def attend_body(scal, q, k, v, slopes, o, lse, bias, vt):
    pair, step = pl.program_id(0), pl.program_id(1)
    block = q.shape[0]
    keys = k.shape[0]

    @pl.when(step == 0)
    def _():
        make_bias(scal, slopes, pair, bias, keys)
        vt[...] = v[...].T

    for c in range(keys // block):

        @pl.when(step == c)
        def _(c=c):
            length = (c + 1) * block
            scaled = q[...] * bf16(HEAD_DIM**-0.5)
            outs, logs = [], []
            for h in range(2):
                s = score_t(k, head_only(scaled, h), bias, h, length)
                top = jnp.max(s, axis=0, keepdims=True)
                e = jnp.exp(s - top)
                total = jnp.sum(e, axis=0, keepdims=True)
                mixed = mm(vt[h * HEAD_DIM : (h + 1) * HEAD_DIM, 0:length], e.astype(bf16))
                outs.append(mixed / total)
                logs.append(top + jnp.log(total))
            o[...] = jnp.concatenate(outs, axis=0).T.astype(bf16)
            lse[0, 0:2, :] = jnp.concatenate(logs, axis=0)


def attend_call(scal, slopes, qkv, block):
    keys, cols = qkv.shape
    width = cols // 3
    pairs = width // LANES
    return pl.pallas_call(
        attend_body,
        out_shape=(
            jax.ShapeDtypeStruct((keys, width), bf16),
            jax.ShapeDtypeStruct((pairs, 8, keys), f32),
        ),
        grid_spec=pltpu.PrefetchScalarGridSpec(
            num_scalar_prefetch=1,
            grid=(pairs, keys // block),
            in_specs=[
                pl.BlockSpec((block, LANES), lambda p, c, sc: (c, p)),
                pl.BlockSpec((keys, LANES), lambda p, c, sc: (0, pairs + p)),
                pl.BlockSpec((keys, LANES), lambda p, c, sc: (0, 2 * pairs + p)),
                SCALAR,
            ],
            out_specs=(
                pl.BlockSpec((block, LANES), lambda p, c, sc: (c, p)),
                pl.BlockSpec((1, 8, block), lambda p, c, sc: (p, 0, c)),
            ),
            scratch_shapes=[
                pltpu.VMEM((2, keys, LANES), f32),
                pltpu.VMEM((LANES, keys), bf16),
            ],
        ),
        compiler_params=params(),
        name="attend",
    )(scal, qkv, qkv, qkv, slopes)


def attend_back_body(scal, q, k, v, o, do, lse, slopes, dq, dk, dv, bias, kt, dk_sum, dv_sum):
    pair, step = pl.program_id(0), pl.program_id(1)
    block = q.shape[0]
    keys = k.shape[0]
    scale = HEAD_DIM**-0.5

    @pl.when(step == 0)
    def _():
        make_bias(scal, slopes, pair, bias, keys)
        kt[...] = k[...].T
        dk_sum[...] = jnp.zeros_like(dk_sum)
        dv_sum[...] = jnp.zeros_like(dv_sum)

    for c in range(keys // block):

        @pl.when(step == c)
        def _(c=c):
            length = (c + 1) * block
            scaled = q[...] * bf16(scale)
            both = (do[...].astype(f32) * o[...].astype(f32)).T
            outs = []
            for h in range(2):
                qm = head_only(scaled, h)
                dom = head_only(do[...], h)
                dot_row = jnp.sum(both[h * HEAD_DIM : (h + 1) * HEAD_DIM], axis=0, keepdims=True)
                p = jnp.exp(score_t(k, qm, bias, h, length) - lse[0, h : h + 1, :])
                dp = mm_t(v[0:length, :], dom)
                ds = (p * (dp - dot_row)).astype(bf16)
                dv_sum[0:length, :] += mm(p.astype(bf16), dom)
                dk_sum[0:length, :] += mm(ds, qm)
                outs.append(mm(kt[h * HEAD_DIM : (h + 1) * HEAD_DIM, 0:length], ds))
            dq[...] = (jnp.concatenate(outs, axis=0).T * scale).astype(bf16)

    @pl.when(step == keys // block - 1)
    def _():
        dk[...] = dk_sum[...].astype(bf16)
        dv[...] = dv_sum[...].astype(bf16)


def attend_back_call(scal, slopes, qkv, o, do, lse, block):
    keys, cols = qkv.shape
    width = cols // 3
    pairs = width // LANES
    some = pl.BlockSpec((block, LANES), lambda p, c, sc: (c, p))
    full = pl.BlockSpec((keys, LANES), lambda p, c, sc: (0, p))
    return pl.pallas_call(
        attend_back_body,
        out_shape=(jax.ShapeDtypeStruct((keys, width), bf16),) * 3,
        grid_spec=pltpu.PrefetchScalarGridSpec(
            num_scalar_prefetch=1,
            grid=(pairs, keys // block),
            in_specs=[
                some,
                pl.BlockSpec((keys, LANES), lambda p, c, sc: (0, pairs + p)),
                pl.BlockSpec((keys, LANES), lambda p, c, sc: (0, 2 * pairs + p)),
                some,
                some,
                pl.BlockSpec((1, 8, block), lambda p, c, sc: (p, 0, c)),
                SCALAR,
            ],
            out_specs=(some, full, full),
            scratch_shapes=[
                pltpu.VMEM((2, keys, LANES), f32),
                pltpu.VMEM((LANES, keys), bf16),
                pltpu.VMEM((keys, LANES), f32),
                pltpu.VMEM((keys, LANES), f32),
            ],
        ),
        compiler_params=params(),
        name="attend_back",
    )(scal, qkv, qkv, qkv, o, do, lse, slopes)


def lay_columns(w_ref, first, dest):
    width = w_ref.shape[2]
    for d in range(w_ref.shape[0]):
        dest[:, d * width : (d + 1) * width] = w_ref[d, first : first + dest.shape[0], :]


def out_body(scal, o, w, near, far, flat, *, first):
    t = pl.program_id(0)

    @pl.when(t == 0)
    def _():
        lay_columns(w, first, flat)

    part = mm(o[...], flat[...]).astype(bf16)

    @pl.when(t < 2)
    def _():
        near[0] = part

    @pl.when(t >= 2)
    def _():
        far[0] = part


def near_map(t, *_):
    return (jnp.minimum(t, 1), 0, 0)


def far_map(t, *_):
    return (jnp.maximum(t - 2, 0), 0, 0)


def out_call(scal, o, w, first):
    keys, inner = o.shape
    rows = keys // 4
    width = w.shape[0] * w.shape[2]
    return pl.pallas_call(
        functools.partial(out_body, first=first),
        out_shape=(jax.ShapeDtypeStruct((2, rows, width), bf16),) * 2,
        grid_spec=pltpu.PrefetchScalarGridSpec(
            num_scalar_prefetch=1,
            grid=(4,),
            in_specs=[
                pl.BlockSpec((rows, inner), lambda t, sc: (lax.bitwise_xor(sc[0], rel_of(t)), 0)),
                WHOLE,
            ],
            out_specs=(
                pl.BlockSpec((1, rows, width), near_map),
                pl.BlockSpec((1, rows, width), far_map),
            ),
            scratch_shapes=[pltpu.VMEM((inner, width), bf16)],
        ),
        compiler_params=params(),
        name="out_proj",
    )(scal, o, w)


def mid_body(x, a, b, c, bias, gain, shift, mid, h2):
    value = x[...].astype(f32) + (
        (a[0].astype(f32) + b[0].astype(f32)) + c[...].astype(f32) + bias[...]
    )
    mid[...] = value
    unit, _ = normalize(value)
    h2[...] = (unit * gain[...] + shift[...]).astype(bf16)


def mid_call(x, a, b, c, bias, gain, shift):
    rows, width = x.shape
    one = pl.BlockSpec((rows // 2, width), lambda i: (i, 0))
    first = pl.BlockSpec((1, rows // 2, width), lambda i: (0, i, 0))
    second = pl.BlockSpec((1, rows // 2, width), lambda i: (1, i, 0))
    row = pl.BlockSpec((1, width), lambda i: (0, 0))
    return pl.pallas_call(
        mid_body,
        out_shape=(
            jax.ShapeDtypeStruct((rows, width), f32),
            jax.ShapeDtypeStruct((rows, width), bf16),
        ),
        grid=(2,),
        in_specs=[one, second, first, one, row, row, row],
        out_specs=(one, one),
        compiler_params=params(),
        name="mid_norm",
    )(x, a, b, c, bias, gain, shift)


def gelu_parts(u):
    root = math.sqrt(2.0 / math.pi)
    sq = u * u
    t = jnp.tanh(root * (u + GELU_COEF * (sq * u)))
    half = 0.5 * (1.0 + t)
    slope = half + 0.5 * u * (1.0 - t * t) * (root * (1.0 + 3.0 * GELU_COEF * sq))
    return u * half, slope


def mlp_body(
    h0, h1, h2, h3, g_rows, w1, w2, b1,
    y_near, y_far, d_near, d_far, a_all, du_all, h_all, g_all, bias_sum,
    flat, hb, gb,
):
    t = pl.program_id(0)

    @pl.when(t == 0)
    def _():
        lay_columns(w2, 0, flat)
        bias_sum[...] = jnp.zeros_like(bias_sum)

    pick(rel_of(t), (h0, h1, h2, h3), hb)
    gb[...] = g_rows[rel_of(t)]
    h_all[...] = hb[...]
    g_all[...] = gb[...]
    inner = w1.shape[1]
    chunk = 256
    for c in range(inner // chunk):
        cols = slice(c * chunk, (c + 1) * chunk)
        u = mm(hb[...], w1[:, cols]) + b1[:, cols]
        value, slope = gelu_parts(u)
        a_all[:, cols] = value.astype(bf16)
        du = (mm_t(gb[...], flat[cols, :]) * slope).astype(bf16)
        du_all[:, cols] = du
        bias_sum[:, cols] += jnp.sum(du.astype(f32), axis=0, keepdims=True)
    y = mm(a_all[...], flat[...]).astype(bf16)
    d = mm_t(du_all[...], w1[...]).astype(bf16)

    @pl.when(t < 2)
    def _():
        y_near[0] = y
        d_near[0] = d

    @pl.when(t >= 2)
    def _():
        y_far[0] = y
        d_far[0] = d


def mlp_call(h_pieces, g_rows, w1, w2, b1):
    rows, width = h_pieces[0].shape
    inner = w1.shape[1]
    pair = jax.ShapeDtypeStruct((2, rows, width), bf16)
    near = pl.BlockSpec((1, rows, width), near_map)
    far = pl.BlockSpec((1, rows, width), far_map)
    block = lambda n: pl.BlockSpec((rows, n), lambda t: (t, 0))
    return pl.pallas_call(
        mlp_body,
        out_shape=(
            pair,
            pair,
            pair,
            pair,
            jax.ShapeDtypeStruct((4 * rows, inner), bf16),
            jax.ShapeDtypeStruct((4 * rows, inner), bf16),
            jax.ShapeDtypeStruct((4 * rows, width), bf16),
            jax.ShapeDtypeStruct((4 * rows, width), bf16),
            jax.ShapeDtypeStruct((1, inner), f32),
        ),
        grid=(4,),
        in_specs=[WHOLE] * 8,
        out_specs=(
            near, far, near, far, block(inner), block(inner), block(width), block(width),
            pl.BlockSpec((1, inner), lambda t: (0, 0)),
        ),
        scratch_shapes=[
            pltpu.VMEM((inner, width), bf16),
            pltpu.VMEM((rows, width), bf16),
            pltpu.VMEM((rows, width), bf16),
        ],
        compiler_params=params(),
        name="mlp",
    )(*h_pieces, g_rows, w1, w2, b1)


def outer_body(left, right, out, turned, *, blocks):
    @pl.when(pl.program_id(0) == 0)
    def _():
        turned[...] = left[...].T

    part = mm(turned[...], right[...]).astype(bf16)
    if blocks:
        width = out.shape[2]
        for d in range(out.shape[0]):
            out[d] = part[:, d * width : (d + 1) * width]
    else:
        out[...] = part


def outer_call(left, right, parts, name):
    rows, m = left.shape
    n = right.shape[1]
    step = 256
    if parts > 1:
        width = n // parts
        out_shape = jax.ShapeDtypeStruct((parts, m, width), bf16)
        out_spec = pl.BlockSpec((step // width, m, width), lambda j: (j, 0, 0))
    else:
        out_shape = jax.ShapeDtypeStruct((m, n), bf16)
        out_spec = pl.BlockSpec((m, step), lambda j: (0, j))
    return pl.pallas_call(
        functools.partial(outer_body, blocks=parts > 1),
        out_shape=out_shape,
        grid=(n // step,),
        in_specs=[WHOLE, pl.BlockSpec((rows, step), lambda j: (0, j))],
        out_specs=out_spec,
        scratch_shapes=[pltpu.VMEM((m, rows), bf16)],
        compiler_params=params(),
        name=name,
    )(left, right)


def mid_back_body(mid, a, b, c, g, gain, dmid, dbr, sums):
    @pl.when(pl.program_id(0) == 0)
    def _():
        sums[...] = jnp.zeros_like(sums)

    unit, inv = normalize(mid[...])
    e = (a[0].astype(f32) + b[0].astype(f32)) + c[...].astype(f32)
    grad = g[...].astype(f32)
    value = grad + norm_back(e, gain[...], unit, inv)
    dmid[...] = value
    low = value.astype(bf16)
    dbr[...] = low
    sums[0:1, :] += jnp.sum(e * unit, axis=0, keepdims=True)
    sums[1:2, :] += jnp.sum(e, axis=0, keepdims=True)
    sums[2:3, :] += jnp.sum(low.astype(f32), axis=0, keepdims=True)
    sums[3:4, :] += jnp.sum(grad, axis=0, keepdims=True)


def mid_back_call(mid, a, b, c, g, gain):
    rows, width = mid.shape
    one = pl.BlockSpec((rows // 2, width), lambda i: (i, 0))
    first = pl.BlockSpec((1, rows // 2, width), lambda i: (0, i, 0))
    second = pl.BlockSpec((1, rows // 2, width), lambda i: (1, i, 0))
    row = pl.BlockSpec((1, width), lambda i: (0, 0))
    return pl.pallas_call(
        mid_back_body,
        out_shape=(
            jax.ShapeDtypeStruct((rows, width), f32),
            jax.ShapeDtypeStruct((rows, width), bf16),
            jax.ShapeDtypeStruct((8, width), f32),
        ),
        grid=(2,),
        in_specs=[one, second, first, one, one, row],
        out_specs=(one, one, pl.BlockSpec((8, width), lambda i: (0, 0))),
        compiler_params=params(),
        name="mid_back",
    )(mid, a, b, c, g, gain)


def out_back_body(scal, b0, b1, b2, b3, o, w, do, grad, flat, rows, total, *, first):
    r = pl.program_id(0)

    @pl.when(r == 0)
    def _():
        lay_columns(w, first, flat)
        total[...] = jnp.zeros_like(total)

    pick(r, (b0, b1, b2, b3), rows)
    do[...] = mm_t(rows[...], flat[...]).astype(bf16)
    total[...] += mm(o[...].T, rows[...])

    @pl.when(r == 3)
    def _():
        width = grad.shape[2]
        for d in range(grad.shape[0]):
            grad[d] = total[:, d * width : (d + 1) * width].astype(bf16)


def out_back_call(scal, pieces, o, w, first):
    rows, width = pieces[0].shape
    inner = o.shape[1]
    at = pl.BlockSpec((rows, inner), lambda r, sc: (lax.bitwise_xor(sc[0], r), 0))
    grad = (w.shape[0], inner, w.shape[2])
    return pl.pallas_call(
        functools.partial(out_back_body, first=first),
        out_shape=(jax.ShapeDtypeStruct(o.shape, bf16), jax.ShapeDtypeStruct(grad, bf16)),
        grid_spec=pltpu.PrefetchScalarGridSpec(
            num_scalar_prefetch=1,
            grid=(4,),
            in_specs=[WHOLE] * 4 + [at, WHOLE],
            out_specs=(at, pl.BlockSpec(grad, lambda r, sc: (0, 0, 0))),
            scratch_shapes=[
                pltpu.VMEM((inner, width), bf16),
                pltpu.VMEM((rows, width), bf16),
                pltpu.VMEM((inner, width), f32),
            ],
        ),
        compiler_params=params(),
        name="out_back",
    )(scal, *pieces, o, w)


def qkv_back_body(scal, dq, dk, dv, w, near, far, merged, sums):
    t = pl.program_id(0)

    @pl.when(t == 0)
    def _():
        sums[...] = jnp.zeros_like(sums)

    low = jnp.concatenate([dq[...], dk[...], dv[...]], axis=1)
    merged[...] = low
    part = mm_t(low, w[...]).astype(bf16)
    sums[...] += jnp.sum(low.astype(f32), axis=0, keepdims=True)

    @pl.when(t < 2)
    def _():
        near[0] = part

    @pl.when(t >= 2)
    def _():
        far[0] = part


def qkv_back_call(scal, dq, dk, dv, w):
    keys, inner = dq.shape
    rows = keys // 4
    width = w.shape[0]
    where = lambda t, sc: (lax.bitwise_xor(sc[0], rel_of(t)), 0)
    at = pl.BlockSpec((rows, inner), where)
    return pl.pallas_call(
        qkv_back_body,
        out_shape=(
            jax.ShapeDtypeStruct((2, rows, width), bf16),
            jax.ShapeDtypeStruct((2, rows, width), bf16),
            jax.ShapeDtypeStruct((keys, 3 * inner), bf16),
            jax.ShapeDtypeStruct((1, 3 * inner), f32),
        ),
        grid_spec=pltpu.PrefetchScalarGridSpec(
            num_scalar_prefetch=1,
            grid=(4,),
            in_specs=[at, at, at, WHOLE],
            out_specs=(
                pl.BlockSpec((1, rows, width), near_map),
                pl.BlockSpec((1, rows, width), far_map),
                pl.BlockSpec((rows, 3 * inner), where),
                pl.BlockSpec((1, 3 * inner), lambda t, sc: (0, 0)),
            ),
        ),
        compiler_params=params(),
        name="qkv_back",
    )(scal, dq, dk, dv, w)


def in_back_body(x, a, b, c, dmid, gain, grad, sums):
    @pl.when(pl.program_id(0) == 0)
    def _():
        sums[...] = jnp.zeros_like(sums)

    unit, inv = normalize(x[...].astype(f32))
    e = (a[0].astype(f32) + b[0].astype(f32)) + c[...].astype(f32)
    grad[...] = (dmid[...] + norm_back(e, gain[...], unit, inv)).astype(bf16)
    sums[0:1, :] += jnp.sum(e * unit, axis=0, keepdims=True)
    sums[1:2, :] += jnp.sum(e, axis=0, keepdims=True)


def in_back_call(x, a, b, c, dmid, gain):
    rows, width = x.shape
    one = pl.BlockSpec((rows // 2, width), lambda i: (i, 0))
    first = pl.BlockSpec((1, rows // 2, width), lambda i: (0, i, 0))
    second = pl.BlockSpec((1, rows // 2, width), lambda i: (1, i, 0))
    row = pl.BlockSpec((1, width), lambda i: (0, 0))
    return pl.pallas_call(
        in_back_body,
        out_shape=(
            jax.ShapeDtypeStruct((rows, width), bf16),
            jax.ShapeDtypeStruct((8, width), f32),
        ),
        grid=(2,),
        in_specs=[one, second, first, one, one, row],
        out_specs=(one, pl.BlockSpec((8, width), lambda i: (0, 0))),
        compiler_params=params(),
        name="in_back",
    )(x, a, b, c, dmid, gain)


def remote(src, dst, send, recv, dp, seq):
    return pltpu.make_async_remote_copy(
        src_ref=src,
        dst_ref=dst,
        send_sem=send,
        recv_sem=recv,
        device_id=(dp, seq),
        device_id_type=pl.DeviceIdType.MESH,
    )


def greet(peers):
    barrier = pltpu.get_barrier_semaphore()
    for dp, seq in peers:
        pl.semaphore_signal(
            barrier, inc=1, device_id=(dp, seq), device_id_type=pl.DeviceIdType.MESH
        )
    pl.semaphore_wait(barrier, len(peers))


class GradSum:
    def __init__(self, part, acc, landx, landr, landl, sems, dp, seq):
        self.part, self.acc = part, acc
        self.landx, self.landr, self.landl = landx, landr, landl
        self.sems, self.dp, self.seq = sems, dp, seq
        self.z, self.x = dp // 2, dp % 2

    def cross(self, k):
        return remote(
            self.part.at[2 * k + (1 - self.x)],
            self.landx.at[k],
            self.sems.at[0, k],
            self.sems.at[1, k],
            2 * self.z + (1 - self.x),
            self.seq,
        )

    def right(self, b, src):
        return remote(
            src.at[b],
            self.landr.at[b],
            self.sems.at[2, b],
            self.sems.at[3, b],
            2 * ((self.z + 1) % 4) + self.x,
            self.seq,
        )

    def left(self, b, src):
        return remote(
            src.at[b],
            self.landl.at[b],
            self.sems.at[4, b],
            self.sems.at[5, b],
            2 * ((self.z + 3) % 4) + self.x,
            self.seq,
        )

    def start(self):
        for k in (3, 0, 2, 1):
            self.cross(k).start()

    def add_cross(self):
        for k in (3, 0, 2, 1):
            self.cross(k).wait_recv()
            own = self.part[2 * k + self.x].astype(f32)
            self.acc[k] = (own + self.landx[k].astype(f32)).astype(bf16)

    def stage(self, k):
        @pl.when(self.z == k)
        def _():
            for b in range(3, k, -1):
                src = self.acc
                if k > 0:
                    src = self.landr
                    self.right(b, src).wait_recv()
                    src[b] = (src[b].astype(f32) + self.acc[b].astype(f32)).astype(bf16)
                self.right(b, src).start()

        @pl.when(self.z == 3 - k)
        def _():
            for b in range(0, 3 - k):
                src = self.acc
                if k > 0:
                    src = self.landl
                    self.left(b, src).wait_recv()
                    src[b] = (src[b].astype(f32) + self.acc[b].astype(f32)).astype(bf16)
                self.left(b, src).start()

    def finish(self, out):
        z = self.z
        out[...] = self.acc[z].astype(f32)

        @pl.when(z > 0)
        def _():
            self.right(z, self.landr).wait_recv()
            out[...] += self.landr[z].astype(f32)

        @pl.when(z < 3)
        def _():
            self.left(z, self.landl).wait_recv()
            out[...] += self.landl[z].astype(f32)

    def drain(self):
        for k in range(4):
            self.cross(k).wait_send()
        for k in range(3):

            @pl.when(self.z == k)
            def _(k=k):
                for b in range(3, k, -1):
                    self.right(b, self.landr).wait_send()

            @pl.when(self.z == 3 - k)
            def _(k=k):
                for b in range(0, 3 - k):
                    self.left(b, self.landl).wait_send()

    @staticmethod
    def scratch(m, n):
        return [pltpu.VMEM((4, m, n), bf16)] * 4 + [pltpu.SemaphoreType.DMA((6, 4))]


SMALL_ROWS = 16


def tail_body(
    near, far, x, dmid, gain, gq, go, mid_sums, up_sum, qkv_sums,
    grad, gq_out, go_out, small_out,
    q_acc, q_x, q_r, q_l, q_sem, o_acc, o_x, o_r, o_l, o_sem,
    land_c, sum_y, land_y, row_sems, small, small_land, own, seq_land, small_sems, seq_sems,
):
    dp, seq = lax.axis_index("dp"), lax.axis_index("seq")
    mate, across = seq + 1 - 2 * (seq % 2), (seq + 2) % 4
    far_mate = (mate + 2) % 4
    greet([((dp + i) % 8, seq) for i in range(1, 8)] + [(dp, mate), (dp, across), (dp, far_mate)])
    rows, width = x.shape

    cores = [
        remote(near.at[k], land_c.at[k], row_sems.at[0, k], row_sems.at[1, k], dp, mate)
        for k in range(2)
    ]
    cores[1].start()
    cores[0].start()
    sum_q = GradSum(gq, q_acc, q_x, q_r, q_l, q_sem, dp, seq)
    sum_o = GradSum(go, o_acc, o_x, o_r, o_l, o_sem, dp, seq)
    sum_o.start()
    sum_q.start()

    cores[1].wait_recv()
    chunk = 128
    for i in range(rows // chunk):
        at = slice(i * chunk, (i + 1) * chunk)
        sum_y[at, :] = (far[0, at, :].astype(f32) + land_c[1, at, :].astype(f32)).astype(bf16)
    over = remote(sum_y, land_y, row_sems.at[0, 2], row_sems.at[1, 2], dp, across)
    over.start()

    small[...] = jnp.zeros_like(small)
    for d in range(8):
        at = slice(d * LANES, (d + 1) * LANES)
        for row, src in ((4, mid_sums[2:3, at]), (5, mid_sums[0:1, at]), (6, mid_sums[1:2, at])):
            small[d, row : row + 1, :] = src
        small[d, 11:12, :] = mid_sums[3:4, at]
    for i in range(2):
        at = slice(i * LANES, (i + 1) * LANES)
        small[pl.ds(seq, 1), 2 + i, :] = qkv_sums[:, at]
        at = slice((4 + i) * LANES, (5 + i) * LANES)
        small[pl.ds(4 + seq, 1), 2 + i, :] = qkv_sums[:, at]
    for i in range(8):
        at = slice(i * LANES, (i + 1) * LANES)
        small[pl.ds(2 * seq + i // 4, 1), 7 + i % 4, :] = up_sum[:, at]

    sum_o.add_cross()
    sum_o.stage(0)
    sum_o.stage(1)
    sum_q.add_cross()
    sum_q.stage(0)
    sum_o.stage(2)

    cores[0].wait_recv()
    over.wait_recv()
    gain_sum = jnp.zeros((1, width), f32)
    shift_sum = jnp.zeros((1, width), f32)
    for i in range(rows // chunk):
        at = slice(i * chunk, (i + 1) * chunk)
        unit, inv = normalize(x[at, :].astype(f32))
        e = (far[1, at, :].astype(f32) + land_c[0, at, :].astype(f32)) + land_y[at, :].astype(f32)
        grad[at, :] = (dmid[at, :] + norm_back(e, gain[...], unit, inv)).astype(bf16)
        gain_sum += jnp.sum(e * unit, axis=0, keepdims=True)
        shift_sum += jnp.sum(e, axis=0, keepdims=True)
    for d in range(8):
        at = slice(d * LANES, (d + 1) * LANES)
        small[d, 0:1, :] = gain_sum[:, at]
        small[d, 1:2, :] = shift_sum[:, at]

    def small_to(i):
        peer = (dp + i) % 8
        return remote(
            small.at[peer], small_land.at[i], small_sems.at[0, i], small_sems.at[1, i], peer, seq
        )

    for i in range(1, 8):
        small_to(i).start()
    sum_q.stage(1)
    sum_q.stage(2)
    sum_o.finish(go_out)
    total = small[dp]
    for i in range(1, 8):
        small_to(i).wait_recv()
        total = total + small_land[i]
    own[...] = total

    def seq_to(i, peer):
        return remote(own, seq_land.at[i], seq_sems.at[0, i], seq_sems.at[1, i], dp, peer)

    group = [seq_to(0, mate), seq_to(1, across), seq_to(2, far_mate)]
    for copy in group:
        copy.start()
    sum_q.finish(gq_out)
    for copy in group:
        copy.wait_recv()
    small_out[...] = (own[...] + seq_land[0]) + (seq_land[1] + seq_land[2])

    for copy in group + cores + [over]:
        copy.wait_send()
    for i in range(1, 8):
        small_to(i).wait_send()
    sum_o.drain()
    sum_q.drain()


def tail_call(near, far, x, dmid, gain, gq, go, mid_sums, up_sum, qkv_sums):
    rows, width = x.shape
    sem = pltpu.SemaphoreType.DMA
    return pl.pallas_call(
        tail_body,
        out_shape=(
            jax.ShapeDtypeStruct((rows, width), bf16),
            jax.ShapeDtypeStruct(gq.shape[1:], f32),
            jax.ShapeDtypeStruct(go.shape[1:], f32),
            jax.ShapeDtypeStruct((SMALL_ROWS, LANES), f32),
        ),
        in_specs=[WHOLE] * 10,
        out_specs=(WHOLE,) * 4,
        scratch_shapes=GradSum.scratch(*gq.shape[1:])
        + GradSum.scratch(*go.shape[1:])
        + [
            pltpu.VMEM((2, rows, width), bf16),
            pltpu.VMEM((rows, width), bf16),
            pltpu.VMEM((rows, width), bf16),
            sem((2, 3)),
            pltpu.VMEM((8, SMALL_ROWS, LANES), f32),
            pltpu.VMEM((8, SMALL_ROWS, LANES), f32),
            pltpu.VMEM((SMALL_ROWS, LANES), f32),
            pltpu.VMEM((3, SMALL_ROWS, LANES), f32),
            sem((2, 8)),
            sem((2, 3)),
        ],
        compiler_params=params(collective_id=3, has_side_effects=True),
        name="tail",
    )(near, far, x, dmid, gain, gq, go, mid_sums, up_sum, qkv_sums)


class Gather:
    def __init__(self, own, out, sems, dp, seq):
        self.own, self.out, self.sems = own, out, sems
        self.seq, self.z, self.x = seq, dp // 2, dp % 2

    def along(self, k, step, src=None):
        slot = self.out.at[2 * k + self.x]
        return remote(
            slot if src is None else src,
            slot,
            self.sems.at[0 if step > 0 else 1, k],
            self.sems.at[3, k],
            2 * ((self.z + step + 4) % 4) + self.x,
            self.seq,
        )

    def over(self, k, src=None):
        slot = self.out.at[2 * k + self.x]
        return remote(
            slot if src is None else src,
            slot,
            self.sems.at[2, k],
            self.sems.at[4, k],
            2 * self.z + (1 - self.x),
            self.seq,
        )

    def keep(self):
        return pltpu.make_async_copy(
            self.own, self.out.at[2 * self.z + self.x], self.sems.at[5, 0]
        )

    def start(self):
        z = self.z

        @pl.when(z < 3)
        def _():
            self.along(z, 1, self.own).start()

        @pl.when(z > 0)
        def _():
            self.along(z, -1, self.own).start()

        self.over(z, self.own).start()
        self.keep().start()

    def hop(self, dist):
        z = self.z

        @pl.when(z - dist >= 0)
        def _():
            k = z - dist
            self.along(k, 1).wait_recv()

            @pl.when(z < 3)
            def _():
                self.along(k, 1).start()

            self.over(k).start()

        @pl.when(z + dist <= 3)
        def _():
            k = z + dist
            self.along(k, -1).wait_recv()

            @pl.when(z > 0)
            def _():
                self.along(k, -1).start()

            self.over(k).start()

    def finish(self):
        z = self.z
        self.keep().wait()
        for k in range(4):
            self.over(k).wait_recv()
            self.over(k).wait_send()

            @pl.when((z < 3) & (z >= k))
            def _(k=k):
                self.along(k, 1).wait_send()

            @pl.when((z > 0) & (z <= k))
            def _(k=k):
                self.along(k, -1).wait_send()

    @staticmethod
    def scratch():
        return pltpu.SemaphoreType.DMA((6, 4))


class Spread:
    def __init__(self, own, rows, sems, dp, seq):
        mate, across = seq + 1 - 2 * (seq % 2), (seq + 2) % 4
        to = lambda src, r, peer: remote(src, rows.at[r], sems.at[0, r], sems.at[1, r], dp, peer)
        self.near, self.far = to(own, 1, mate), to(own, 2, across)
        self.last = to(rows.at[2], 3, mate)

    def start(self):
        self.far.start()
        self.near.start()

    def forward(self):
        self.far.wait_recv()
        self.last.start()

    def drain(self):
        for copy in (self.near, self.far, self.last):
            copy.wait_send()


def neighbours(seq):
    mate = seq + 1 - 2 * (seq % 2)
    return mate, (seq + 2) % 4, (mate + 2) % 4


def block_at(seq, rel):
    return 2 * ((seq // 2 + rel // 2) % 2) + (seq + rel) % 2


def front_body(
    wq, wo, x, v_up, v_qv, v_g1, v_s1, v_out, v_g2, v_s2, v_down,
    wq_all, wo_all, x_rows, gain1, shift1, bias_qkv, bias_out, gain2, shift2, bias_up, bias_down,
    small, vectors, q_sem, o_sem, x_sem, seq_sem, dp_sem, keep_sem,
):
    dp, seq = lax.axis_index("dp"), lax.axis_index("seq")
    greet([((dp + i) % 8, seq) for i in range(1, 8)] + [(dp, p) for p in neighbours(seq)])
    gather_q = Gather(wq, wq_all, q_sem, dp, seq)
    gather_o = Gather(wo, wo_all, o_sem, dp, seq)
    rows = Spread(x, x_rows, x_sem, dp, seq)
    rows.start()
    gather_q.start()
    keep_x = pltpu.make_async_copy(x, x_rows.at[0], keep_sem.at[0])
    keep_x.start()
    at = 0
    for ref in (v_up, v_qv, v_g1, v_s1, v_out, v_g2, v_s2, v_down):
        small[:, at : at + ref.shape[1]] = ref[...].astype(f32)
        at += ref.shape[1]
    keep_v = pltpu.make_async_copy(small, vectors.at[dp, seq], keep_sem.at[1])
    keep_v.start()
    group = [
        remote(small, vectors.at[dp, seq], seq_sem.at[0, i], seq_sem.at[1, i], dp, peer)
        for i, peer in enumerate(neighbours(seq))
    ]
    for copy in group:
        copy.start()
    gather_o.start()
    keep_v.wait()
    for copy in group:
        copy.wait_recv()

    def to_dp(i):
        return remote(
            vectors.at[dp], vectors.at[dp], dp_sem.at[0, i], dp_sem.at[1, i], (dp + i) % 8, seq
        )

    for i in range(1, 8):
        to_dp(i).start()
    gather_q.hop(1)
    gather_o.hop(1)
    for i in range(1, 8):
        to_dp(i).wait_recv()
    for ref, at in (
        (gain1, 192), (shift1, 224), (bias_out, 256), (gain2, 288), (shift2, 320), (bias_down, 352),
    ):
        for d in range(8):
            ref[:, d * LANES : (d + 1) * LANES] = jnp.concatenate(
                [vectors[d, i, :, at : at + 32] for i in range(4)], axis=1
            )
    for part in range(2):
        for half in range(2):
            lane = part * 512 + half * LANES
            bias_qkv[:, lane : lane + LANES] = jnp.concatenate(
                [vectors[4 * part + seq, 2 * half + i, :, 128:192] for i in range(2)], axis=1
            )
    bias_qkv[:, 256:512] = jnp.zeros((1, 256), f32)
    for i in range(8):
        bias_up[:, i * LANES : (i + 1) * LANES] = vectors[2 * seq + i // 4, i % 4, :, 0:LANES]
    gather_q.hop(2)
    gather_o.hop(2)
    rows.forward()
    gather_q.hop(3)
    gather_o.hop(3)
    gather_q.finish()
    gather_o.finish()
    rows.near.wait_recv()
    rows.last.wait_recv()
    rows.drain()
    keep_x.wait()
    for copy in group:
        copy.wait_send()
    for i in range(1, 8):
        to_dp(i).wait_send()


def front_call(wq, wo, x, small):
    count = sum(v.shape[0] for v in small)
    rows, width = x.shape
    one = lambda n: jax.ShapeDtypeStruct((1, n), f32)
    sem = pltpu.SemaphoreType.DMA
    return pl.pallas_call(
        front_body,
        out_shape=(
            jax.ShapeDtypeStruct((8, *wq.shape), bf16),
            jax.ShapeDtypeStruct((8, *wo.shape), bf16),
            jax.ShapeDtypeStruct((4, rows, width), bf16),
            one(width), one(width), one(wq.shape[1]), one(width), one(width), one(width),
            one(width), one(width),
        ),
        in_specs=[WHOLE] * 11,
        out_specs=(WHOLE,) * 11,
        scratch_shapes=[
            pltpu.VMEM((1, count), f32),
            pltpu.VMEM((8, 4, 1, count), f32),
            Gather.scratch(),
            Gather.scratch(),
            sem((2, 4)),
            sem((2, 3)),
            sem((2, 8)),
            sem((2,)),
        ],
        compiler_params=params(collective_id=4, has_side_effects=True),
        name="front",
    )(wq, wo, x, *(v.reshape(1, -1) for v in small))


def attention_body(
    scal, slopes, x_rows, g, wq, wo, w1, w2, gain1, shift1, bias_qkv, bias_out, gain2, shift2,
    h1, qkv, o, lse, mid, h2, g_rows, w1_all, w2_all,
    bias, vt, flat, part, land_c, sum_y, land_y, g_sem, row_sems, keep_sem, w1_sem, w2_sem,
):
    dp, seq = lax.axis_index("dp"), lax.axis_index("seq")
    mate, across, _ = neighbours(seq)
    greet([((dp + i) % 8, seq) for i in range(1, 8)] + [(dp, mate), (dp, across)])
    rows, width = g.shape
    keys = qkv.shape[0]
    inner = o.shape[1]
    pairs = inner // LANES
    gathers = [Gather(w1, w1_all, w1_sem, dp, seq), Gather(w2, w2_all, w2_sem, dp, seq)]
    for gather in gathers:
        gather.start()
    spread_g = Spread(g, g_rows, g_sem, dp, seq)
    spread_g.start()
    keep = pltpu.make_async_copy(g, g_rows.at[0], keep_sem.at[0])
    keep.start()
    lay_columns(wo, 0, flat)

    def project(r, carry):
        at = pl.ds(pl.multiple_of(block_at(seq, r) * rows, rows), rows)
        unit, _ = normalize(x_rows[r].astype(f32))
        low = (unit * gain1[...] + shift1[...]).astype(bf16)
        h1[at, :] = low
        qkv[at, :] = (mm(low, wq[...]) + bias_qkv[...]).astype(bf16)
        return carry

    lax.fori_loop(0, 4, project, 0)

    def prepare(p, carry):
        pos = lax.broadcasted_iota(jnp.int32, (keys, LANES), 0)
        ramp = pos.astype(f32)
        inside = pos < scal[1]
        for h in range(2):
            bias[2 * p + h] = jnp.where(inside, ramp * slopes[2 * p + h], NEG)
        lane = pl.ds(pl.multiple_of(2 * inner + p * LANES, LANES), LANES)
        vt[p] = qkv[:, lane].T
        return carry

    lax.fori_loop(0, pairs, prepare, 0)
    for gather in gathers:
        gather.hop(1)
    spread_g.forward()

    cores = [
        remote(part.at[r], land_c.at[k], row_sems.at[0, k], row_sems.at[1, k], dp, mate)
        for k, r in ((0, 1), (1, 3))
    ]
    over = remote(sum_y, land_y, row_sems.at[0, 2], row_sems.at[1, 2], dp, across)
    chunk = 128

    def attend(t, carry):
        rel = 3 - t
        c_now = block_at(seq, rel)
        at = pl.ds(pl.multiple_of(c_now * rows, rows), rows)
        for c in range(keys // rows):

            @pl.when(c_now == c)
            def _(c=c):
                length = (c + 1) * rows

                def one_pair(p, carry):
                    lane = pl.ds(pl.multiple_of(p * LANES, LANES), LANES)
                    k_lane = pl.ds(pl.multiple_of(inner + p * LANES, LANES), LANES)
                    scaled = qkv[c * rows : length, lane] * bf16(HEAD_DIM**-0.5)
                    k = qkv[0:length, k_lane]
                    outs, logs = [], []
                    for h in range(2):
                        s = scores(k, head_only(scaled, h), bias[2 * p + h, 0:length, :])
                        top = jnp.max(s, axis=0, keepdims=True)
                        e = jnp.exp(s - top)
                        total = jnp.sum(e, axis=0, keepdims=True)
                        half = vt[p, h * HEAD_DIM : (h + 1) * HEAD_DIM, 0:length]
                        outs.append(mm(half, e.astype(bf16)) / total)
                        logs.append(top + jnp.log(total))
                    o[c * rows : length, lane] = jnp.concatenate(outs, axis=0).T.astype(bf16)
                    lse[p, 0:2, c * rows : length] = jnp.concatenate(logs, axis=0)
                    return carry

                lax.fori_loop(0, pairs, one_pair, 0)

        part[rel] = mm(o[at, :], flat[...]).astype(bf16)

        @pl.when(t == 0)
        def _():
            cores[1].start()

        @pl.when(t == 1)
        def _():
            cores[1].wait_recv()
            for i in range(rows // chunk):
                at = slice(i * chunk, (i + 1) * chunk)
                total = part[2, at, :].astype(f32) + land_c[1, at, :].astype(f32)
                sum_y[at, :] = total.astype(bf16)
            over.start()
            for gather in gathers:
                gather.hop(2)

        @pl.when(t == 2)
        def _():
            cores[0].start()
            for gather in gathers:
                gather.hop(3)

        return carry

    lax.fori_loop(0, 4, attend, 0)
    cores[0].wait_recv()
    over.wait_recv()

    def second_norm(i, carry):
        at = pl.ds(pl.multiple_of(i * chunk, chunk), chunk)
        total = (part[0, at, :].astype(f32) + land_c[0, at, :].astype(f32)) + land_y[
            at, :
        ].astype(f32)
        value = x_rows[0, at, :].astype(f32) + (total + bias_out[...])
        mid[at, :] = value
        unit, _ = normalize(value)
        h2[at, :] = (unit * gain2[...] + shift2[...]).astype(bf16)
        return carry

    lax.fori_loop(0, rows // chunk, second_norm, 0)
    for gather in gathers:
        gather.finish()
    spread_g.near.wait_recv()
    spread_g.last.wait_recv()
    spread_g.drain()
    keep.wait()
    for copy in cores + [over]:
        copy.wait_send()


def scores(k, qm, ramp):
    block = qm.shape[0]
    length = k.shape[0]
    s = mm_t(k, qm) + jnp.concatenate([ramp] * (block // LANES), axis=1)
    key = lax.broadcasted_iota(jnp.int32, (block, block), 0)
    query = lax.broadcasted_iota(jnp.int32, (block, block), 1)
    last = jnp.where(key <= query, s[length - block :], NEG)
    if length == block:
        return last
    return jnp.concatenate([s[: length - block], last], axis=0)


def attention_call(scal, slopes, x_rows, g, wq, wo, w1, w2, *vectors):
    rows, width = g.shape
    keys = 4 * rows
    inner = wo.shape[1]
    pairs = inner // LANES
    sem = pltpu.SemaphoreType.DMA
    return pl.pallas_call(
        attention_body,
        out_shape=(
            jax.ShapeDtypeStruct((keys, width), bf16),
            jax.ShapeDtypeStruct((keys, 3 * inner), bf16),
            jax.ShapeDtypeStruct((keys, inner), bf16),
            jax.ShapeDtypeStruct((pairs, 8, keys), f32),
            jax.ShapeDtypeStruct((rows, width), f32),
            jax.ShapeDtypeStruct((rows, width), bf16),
            jax.ShapeDtypeStruct((4, rows, width), bf16),
            jax.ShapeDtypeStruct((8, *w1.shape), bf16),
            jax.ShapeDtypeStruct((8, *w2.shape), bf16),
        ),
        in_specs=[SCALAR, SCALAR] + [WHOLE] * (6 + len(vectors)),
        out_specs=(WHOLE,) * 9,
        scratch_shapes=[
            pltpu.VMEM((2 * pairs, keys, LANES), f32),
            pltpu.VMEM((pairs, LANES, keys), bf16),
            pltpu.VMEM((inner, width), bf16),
            pltpu.VMEM((4, rows, width), bf16),
            pltpu.VMEM((2, rows, width), bf16),
            pltpu.VMEM((rows, width), bf16),
            pltpu.VMEM((rows, width), bf16),
            sem((2, 4)),
            sem((2, 3)),
            sem((1,)),
            Gather.scratch(),
            Gather.scratch(),
        ],
        compiler_params=params(collective_id=5, has_side_effects=True),
        name="attention",
    )(scal, slopes, x_rows, g, wq, wo, w1, w2, *vectors)


def feed_body(
    h2, g_rows, w1, w2, b1, mid, gain2,
    y_near, y_far, gw1, gw2, dmid, dbr, sums, up_sum,
    h_rows, a_all, du_all, flat, part, land_c, sum_y, land_y, turned, h_sem, row_sems, keep_sem,
):
    dp, seq = lax.axis_index("dp"), lax.axis_index("seq")
    mate, across, _ = neighbours(seq)
    greet([(dp, mate), (dp, across)])
    rows, width = h2.shape
    inner = w1.shape[1]
    spread_h = Spread(h2, h_rows, h_sem, dp, seq)
    spread_h.start()
    keep = pltpu.make_async_copy(h2, h_rows.at[0], keep_sem.at[0])
    keep.start()
    lay_columns(w2, 0, flat)
    up_sum[...] = jnp.zeros_like(up_sum)
    sums[...] = jnp.zeros_like(sums)
    keep.wait()
    cores = [
        remote(part.at[r], land_c.at[k], row_sems.at[0, k], row_sems.at[1, k], dp, mate)
        for k, r in ((0, 1), (1, 3))
    ]
    over = remote(sum_y, land_y, row_sems.at[0, 2], row_sems.at[1, 2], dp, across)
    chunk = 256

    def block(t, carry):
        @pl.when(t == 1)
        def _():
            spread_h.near.wait_recv()

        @pl.when(t == 2)
        def _():
            spread_h.forward()

        @pl.when(t == 3)
        def _():
            spread_h.last.wait_recv()

        at = pl.ds(pl.multiple_of(t * rows, rows), rows)
        for c in range(inner // chunk):
            cols = slice(c * chunk, (c + 1) * chunk)
            u = mm(h_rows[t], w1[:, cols]) + b1[:, cols]
            value, slope = gelu_parts(u)
            a_all[at, cols] = value.astype(bf16)
            du = (mm_t(g_rows[t], flat[cols, :]) * slope).astype(bf16)
            du_all[at, cols] = du
            up_sum[:, cols] += jnp.sum(du.astype(f32), axis=0, keepdims=True)
        y = mm(a_all[at, :], flat[...]).astype(bf16)
        part[t] = mm_t(du_all[at, :], w1[...]).astype(bf16)
        for r, (ref, k) in enumerate(((y_far, 1), (y_near, 0), (y_far, 0), (y_near, 1))):

            @pl.when(t == r)
            def _(ref=ref, k=k):
                ref[k] = y

        @pl.when(t == 1)
        def _():
            cores[0].start()

        @pl.when(t == 3)
        def _():
            cores[1].start()

        return carry

    lax.fori_loop(0, 4, block, 0)

    def turn(load):
        def step(i, carry):
            turned[:, pl.ds(pl.multiple_of(i * rows, rows), rows)] = load(i).T
            return carry

        lax.fori_loop(0, 4, step, 0)

    turn(lambda i: h_rows[i])

    def outer_up(j, carry):
        cols = pl.ds(pl.multiple_of(j * chunk, chunk), chunk)
        gw1[:, cols] = mm(turned[...], du_all[:, cols]).astype(bf16)
        return carry

    lax.fori_loop(0, 1, outer_up, 0)
    cores[1].wait_recv()
    small = 128
    for i in range(rows // small):
        at = slice(i * small, (i + 1) * small)
        total = part[2, at, :].astype(f32) + land_c[1, at, :].astype(f32)
        sum_y[at, :] = total.astype(bf16)
    over.start()
    lax.fori_loop(1, inner // chunk, outer_up, 0)
    turn(lambda i: a_all[pl.ds(pl.multiple_of(i * rows, rows), rows), :])

    def outer_down(j, carry):
        cols = pl.ds(pl.multiple_of(j * chunk, chunk), chunk)
        right = g_rows[:, :, cols].reshape(4 * rows, chunk)
        grad = mm(turned[...], right).astype(bf16)
        gw2[2 * j] = grad[:, :LANES]
        gw2[2 * j + 1] = grad[:, LANES:]
        return carry

    lax.fori_loop(0, width // chunk, outer_down, 0)
    cores[0].wait_recv()
    over.wait_recv()

    def norm_step(i, carry):
        at = pl.ds(pl.multiple_of(i * small, small), small)
        unit, inv = normalize(mid[at, :])
        e = (part[0, at, :].astype(f32) + land_c[0, at, :].astype(f32)) + land_y[at, :].astype(f32)
        grad = g_rows[0, at, :].astype(f32)
        value = grad + norm_back(e, gain2[...], unit, inv)
        dmid[at, :] = value
        low = value.astype(bf16)
        dbr[at, :] = low
        sums[0:1, :] += jnp.sum(e * unit, axis=0, keepdims=True)
        sums[1:2, :] += jnp.sum(e, axis=0, keepdims=True)
        sums[2:3, :] += jnp.sum(low.astype(f32), axis=0, keepdims=True)
        sums[3:4, :] += jnp.sum(grad, axis=0, keepdims=True)
        return carry

    lax.fori_loop(0, rows // small, norm_step, 0)
    spread_h.drain()
    for copy in cores + [over]:
        copy.wait_send()


def feed_call(h2, g_rows, w1, w2, b1, mid, gain2):
    rows, width = h2.shape
    inner = w1.shape[1]
    sem = pltpu.SemaphoreType.DMA
    pair = jax.ShapeDtypeStruct((2, rows, width), bf16)
    return pl.pallas_call(
        feed_body,
        out_shape=(
            pair,
            pair,
            jax.ShapeDtypeStruct((width, inner), bf16),
            jax.ShapeDtypeStruct(w2.shape, bf16),
            jax.ShapeDtypeStruct((rows, width), f32),
            jax.ShapeDtypeStruct((rows, width), bf16),
            jax.ShapeDtypeStruct((8, width), f32),
            jax.ShapeDtypeStruct((1, inner), f32),
        ),
        in_specs=[WHOLE] * 7,
        out_specs=(WHOLE,) * 8,
        scratch_shapes=[
            pltpu.VMEM((4, rows, width), bf16),
            pltpu.VMEM((4 * rows, inner), bf16),
            pltpu.VMEM((4 * rows, inner), bf16),
            pltpu.VMEM((inner, width), bf16),
            pltpu.VMEM((4, rows, width), bf16),
            pltpu.VMEM((2, rows, width), bf16),
            pltpu.VMEM((rows, width), bf16),
            pltpu.VMEM((rows, width), bf16),
            pltpu.VMEM((width, 4 * rows), bf16),
            sem((2, 4)),
            sem((2, 3)),
            sem((1,)),
        ],
        compiler_params=params(collective_id=6, has_side_effects=True),
        name="feed_forward",
    )(h2, g_rows, w1, w2, b1, mid, gain2)


def finish_body(
    scal, grad, gq, go, small,
    grad_out, gq_out, go_out, gain1, shift1, qv, bout, gain2, shift2, up, down,
):
    seq = scal[0]
    grad_out[...] = grad[...]
    go_out[...] = go[...]
    cols = gq_out.shape[2]
    for c in range(3):
        gq_out[:, c, :] = gq[:, c * cols : (c + 1) * cols]
    for ref, row in ((gain1, 0), (shift1, 1), (bout, 4), (gain2, 5), (shift2, 6), (down, 11)):
        n = ref.shape[1]
        value = small[row : row + 1, 0:n]
        for i in range(1, 4):
            value = jnp.where(seq == i, small[row : row + 1, i * n : (i + 1) * n], value)
        ref[...] = value
    value = small[2:3, 0:64]
    for i in range(1, 4):
        at = 64 * (i % 2)
        value = jnp.where(seq == i, small[2 + i // 2 : 3 + i // 2, at : at + 64], value)
    qv[...] = value
    up[...] = small[pl.ds(7 + seq, 1), :]


def finish_call(scal, grad, gq, go, small):
    one = lambda n: jax.ShapeDtypeStruct((1, n), f32)
    return pl.pallas_call(
        finish_body,
        out_shape=(
            jax.ShapeDtypeStruct(grad.shape, bf16),
            jax.ShapeDtypeStruct((gq.shape[0], 3, gq.shape[1] // 3), f32),
            jax.ShapeDtypeStruct(go.shape, f32),
            one(32), one(32), one(64), one(32), one(32), one(32), one(LANES), one(32),
        ),
        in_specs=[SCALAR] + [WHOLE] * 4,
        out_specs=(WHOLE,) * 11,
        compiler_params=params(),
        name="finish",
    )(scal, grad, gq, go, small)


def after(value, *others):
    return lax.optimization_barrier((value, *others))[0]


def on_device(
    dp_n,
    seq_n,
    tokens,
    lengths,
    cotangent,
    ln1_gain,
    ln1_shift,
    w_qkv,
    b_qv,
    w_out,
    b_out,
    ln2_gain,
    ln2_shift,
    w_fc1,
    b_fc1,
    w_fc2,
    b_fc2,
):
    count = dp_n * seq_n
    rows, width = tokens.shape
    heads = width // HEAD_DIM
    inner = w_out.shape[0]
    ff = w_fc1.shape[1]
    s = lax.axis_index("seq")
    length = lengths[0]

    scal = jnp.stack([s.astype(jnp.int32), length])
    slopes = 2.0 ** (-8.0 * (jnp.arange(heads, dtype=jnp.int32) + 1).astype(f32) / heads)
    slopes = lax.dynamic_slice(slopes, (s * (heads // seq_n),), (heads // seq_n,))
    valid = s * rows + jnp.arange(rows, dtype=jnp.int32) < length
    grad_low = jnp.where(valid[:, None], cotangent, jnp.zeros_like(cotangent))
    wq_own = jnp.concatenate([w_qkv[:, c, :] for c in range(3)], axis=1)
    small = (ln1_gain, ln1_shift, b_qv, b_out, ln2_gain, ln2_shift, b_fc1, b_fc2)
    sizes = [v.shape[0] for v in small]
    ends = [sum(sizes[: i + 1]) for i in range(len(sizes))]
    block = 384
    fast = dp_n == 8 and seq_n == 4 and width == 8 * LANES and ff == width and inner == 2 * LANES
    if fast:
        parts = dp_n
        order = (b_fc1, b_qv, ln1_gain, ln1_shift, b_out, ln2_gain, ln2_shift, b_fc2)
        wq, w_o, x_rows, gain1, shift1, qkv_bias, bias_out, gain2, shift2, own_up, bias_down = (
            front_call(wq_own, w_out, tokens, order)
        )
        wq = wq.reshape(width, 3 * inner)
        h1, qkv, o, lse, mid, h2, g_rows, w1, w_cols = attention_call(
            scal, slopes, x_rows, grad_low, wq, w_o, w_fc1, w_fc2,
            gain1, shift1, qkv_bias, bias_out, gain2, shift2,
        )
        out_first = 0
        y_near, y_far, grad_up, grad_down, dmid, dbr, mid_sums, up_sum = feed_call(
            h2, g_rows, w1.reshape(width, ff), w_cols, own_up, mid, gain2
        )
    else:
        wq = lax.all_gather(wq_own, "dp", axis=0, tiled=True)
        col = w_fc2.shape[1]
        both = jnp.concatenate([w_fc2, w_out], axis=0)
        if col % LANES == 0:
            parts = dp_n
            w_cols = lax.all_gather(both, "dp", axis=0, tiled=False)
        else:
            parts = 1
            w_cols = lax.all_gather(both, "dp", axis=1, tiled=True)[None]
        w_o = w_cols
        out_first = ff
        w1 = lax.all_gather(w_fc1, "dp", axis=0, tiled=True)
        packed = small_gather(jnp.concatenate([v.astype(f32) for v in small]), count, seq_n)
        packed = packed.reshape(count, ends[-1])
        gain1, shift1, bias_qv, bias_out, gain2, shift2, bias_up, bias_down = (
            packed[:, e - n : e].reshape(1, count * n) for e, n in zip(ends, sizes)
        )
        own_bias = lambda v, n: lax.dynamic_slice(v, (0, s * n), (1, n))
        own_up = own_bias(bias_up, ff)
        qkv_bias = jnp.concatenate(
            [
                own_bias(bias_qv[:, :width], inner),
                jnp.zeros((1, inner), f32),
                own_bias(bias_qv[:, width:], inner),
            ],
            axis=1,
        )
        x_pieces = spread(tokens)
        g_rows = jnp.stack(spread(after(grad_low, x_pieces[3])))
        h1, qkv = qkv_call(scal, x_pieces, wq, gain1, shift1, qkv_bias)
        o, lse = attend_call(scal, slopes, qkv, block)
        near, far = out_call(scal, o, w_o, out_first)
        got, across = reduce_rows(near, far)
        mid, h2 = mid_call(tokens, far, got, across, bias_out, gain2, shift2)
        h_pieces = spread(h2)
        y_near, y_far, d_near, d_far, a_all, du_all, h_all, g_all, up_sum = mlp_call(
            h_pieces, g_rows, w1, w_cols, own_up
        )
        got, across = reduce_rows(d_near, d_far)
        grad_down = outer_call(a_all, g_all, parts, "grad_fc2")
        grad_up = outer_call(h_all, du_all, 1, "grad_fc1")
        dmid, dbr, mid_sums = mid_back_call(mid, d_far, got, across, grad_low, gain2)

    b_pieces = spread(dbr)

    y_near = after(y_near, b_pieces[3])
    got, across = reduce_rows(y_near, y_far)
    output = (
        mid + ((y_far[1].astype(f32) + got[0].astype(f32)) + across.astype(f32) + bias_down)
    ).astype(bf16)

    do, grad_out = out_back_call(scal, b_pieces, o, w_o, out_first)
    dq, dk, dv = attend_back_call(scal, slopes, qkv, o, do, lse, block)
    near, far, merged, qkv_sums = qkv_back_call(scal, dq, dk, dv, wq)
    grad_qkv = outer_call(h1, merged, 1, "grad_qkv")

    def shared(part):
        if parts > 1:
            return lax.psum_scatter(part, "dp", scatter_dimension=0, tiled=False).astype(f32)
        return lax.psum_scatter(part, "dp", scatter_dimension=1, tiled=True).astype(f32)

    grad_down = shared(grad_down if parts > 1 else grad_down)
    grad_up = lax.psum_scatter(grad_up, "dp", scatter_dimension=0, tiled=True).astype(f32)
    if fast:
        tail = tail_call(
            near, far, tokens, dmid, gain1, grad_qkv.reshape(8, -1, 3 * inner), grad_out,
            mid_sums, up_sum, qkv_sums,
        )
        grad_tokens, grad_qkv, grad_out, *vectors = finish_call(scal, *tail)
        g_gain1, g_shift1, g_qv, g_bout, g_gain2, g_shift2, g_up, g_down = (
            v.reshape(n) for v, n in zip(vectors, sizes)
        )
        return (
            output, grad_tokens, g_gain1, g_shift1, grad_qkv, g_qv, grad_out, g_bout,
            g_gain2, g_shift2, grad_up, g_up, grad_down, g_down,
        )

    got, across = reduce_rows(near, far)
    grad_tokens, in_sums = in_back_call(tokens, far, got, across, dmid, gain1)
    grad_out = shared(grad_out if parts > 1 else grad_out[0])
    grad_qkv = lax.psum_scatter(grad_qkv, "dp", scatter_dimension=0, tiled=True)
    grad_qkv = grad_qkv.astype(f32).reshape(w_qkv.shape)

    def own_slot(v, total):
        return lax.dynamic_update_slice(jnp.zeros((1, total), f32), v, (0, s * v.shape[1]))

    sums = (
        in_sums[0:1],
        in_sums[1:2],
        jnp.concatenate(
            [own_slot(qkv_sums[:, :inner], width), own_slot(qkv_sums[:, 2 * inner :], width)], axis=1
        ),
        mid_sums[2:3],
        mid_sums[0:1],
        mid_sums[1:2],
        own_slot(up_sum, seq_n * ff),
        mid_sums[3:4],
    )
    grads = jnp.concatenate([v.reshape(count, n) for v, n in zip(sums, sizes)], axis=1)
    grads = small_scatter(grads, count, seq_n).reshape(ends[-1])
    g_gain1, g_shift1, g_qv, g_bout, g_gain2, g_shift2, g_up, g_down = (
        grads[e - n : e] for e, n in zip(ends, sizes)
    )
    return (
        output,
        grad_tokens,
        g_gain1,
        g_shift1,
        grad_qkv,
        g_qv,
        grad_out,
        g_bout,
        g_gain2,
        g_shift2,
        grad_up,
        g_up,
        grad_down,
        g_down,
    )


def solution(mesh):
    rows = P(("dp", "seq"), None)
    vec = P(("dp", "seq"))
    merged = P("dp", None, "seq")
    return jax.shard_map(
        functools.partial(on_device, mesh.shape["dp"], mesh.shape["seq"]),
        mesh=mesh,
        in_specs=(
            rows, P("dp"), rows, vec, vec, merged, vec, P("seq", "dp"), vec, vec, vec,
            P("dp", "seq"), vec, P("seq", "dp"), vec,
        ),
        out_specs=(
            rows, rows, vec, vec, merged, vec, P("seq", "dp"), vec, vec, vec,
            P("dp", "seq"), vec, P("seq", "dp"), vec,
        ),
        check_vma=False,
    )
```

```python
import functools
import math

import jax
import jax.numpy as jnp
from jax import lax
from jax.experimental import pallas as pl
from jax.experimental.pallas import tpu as pltpu
from jax.sharding import PartitionSpec as P

HEAD_DIM = 64
EPS = 1e-05
GELU_COEF = 0.044715
NEG = -1e30
LANES = 128
VMEM_BYTES = 60 * 1024 * 1024

f32 = jnp.float32
bf16 = jnp.bfloat16
WHOLE = pl.BlockSpec(memory_space=pltpu.VMEM)
SCALAR = pl.BlockSpec(memory_space=pltpu.SMEM)


def mm(a, b):
    return jnp.dot(a, b, preferred_element_type=f32)


def mm_t(a, b):
    return lax.dot_general(a, b, (((1,), (1,)), ((), ())), preferred_element_type=f32)


def params(**kw):
    return pltpu.CompilerParams(vmem_limit_bytes=VMEM_BYTES, **kw)


def normalize(v):
    width = v.shape[-1]
    centred = v - jnp.sum(v, axis=-1, keepdims=True) * (1.0 / width)
    inv = lax.rsqrt(jnp.sum(centred * centred, axis=-1, keepdims=True) * (1.0 / width) + EPS)
    return centred * inv, inv


def norm_back(grad_out, gain, unit, inv):
    width = unit.shape[-1]
    scaled = grad_out * gain
    mean_one = jnp.sum(scaled, axis=-1, keepdims=True) * (1.0 / width)
    mean_two = jnp.sum(scaled * unit, axis=-1, keepdims=True) * (1.0 / width)
    return inv * (scaled - mean_one - unit * mean_two)


def device_of(index, seq_n):
    return (index // seq_n, index % seq_n)


def greet_all(me, count, seq_n):
    barrier = pltpu.get_barrier_semaphore()

    def hello(i, carry):
        peer = (me + i) % count
        pl.semaphore_signal(
            barrier, inc=1, device_id=device_of(peer, seq_n), device_id_type=pl.DeviceIdType.MESH
        )
        return carry

    lax.fori_loop(1, count, hello, 0)
    pl.semaphore_wait(barrier, count - 1)


def small_gather_body(count, seq_n, x_ref, out_ref, send_sem, recv_sem):
    me = lax.axis_index("dp") * seq_n + lax.axis_index("seq")
    greet_all(me, count, seq_n)

    def copy_to(i):
        peer = (me + i) % count
        return pltpu.make_async_remote_copy(
            src_ref=x_ref,
            dst_ref=out_ref.at[pl.ds(me, 1)],
            send_sem=send_sem.at[i],
            recv_sem=recv_sem.at[i],
            device_id=device_of(peer, seq_n),
            device_id_type=pl.DeviceIdType.MESH,
        )

    def begin(i, carry):
        copy_to(i).start()
        return carry

    def finish(i, carry):
        copy_to(i).wait()
        return carry

    lax.fori_loop(1, count, begin, 0)
    out_ref[pl.ds(me, 1)] = x_ref[...]
    lax.fori_loop(1, count, finish, 0)


def small_gather(x, count, seq_n):
    width = x.shape[-1]
    return pl.pallas_call(
        functools.partial(small_gather_body, count, seq_n),
        out_shape=jax.ShapeDtypeStruct((count, 1, width), f32),
        in_specs=[WHOLE],
        out_specs=WHOLE,
        scratch_shapes=[pltpu.SemaphoreType.DMA((count,)), pltpu.SemaphoreType.DMA((count,))],
        compiler_params=pltpu.CompilerParams(collective_id=1, has_side_effects=True),
        name="small_gather",
    )(x.reshape(1, 1, width))


def small_scatter_body(count, seq_n, v_ref, out_ref, land, send_sem, recv_sem):
    me = lax.axis_index("dp") * seq_n + lax.axis_index("seq")
    greet_all(me, count, seq_n)

    def copy_to(i):
        peer = (me + i) % count
        return pltpu.make_async_remote_copy(
            src_ref=v_ref.at[pl.ds(peer, 1)],
            dst_ref=land.at[pl.ds(i, 1)],
            send_sem=send_sem.at[i],
            recv_sem=recv_sem.at[i],
            device_id=device_of(peer, seq_n),
            device_id_type=pl.DeviceIdType.MESH,
        )

    def begin(i, carry):
        copy_to(i).start()
        return carry

    def finish(i, total):
        copy_to(i).wait()
        return total + land[pl.ds(i, 1)]

    lax.fori_loop(1, count, begin, 0)
    out_ref[...] = lax.fori_loop(1, count, finish, v_ref[pl.ds(me, 1)])


def small_scatter(v, count, seq_n):
    width = v.shape[-1]
    return pl.pallas_call(
        functools.partial(small_scatter_body, count, seq_n),
        out_shape=jax.ShapeDtypeStruct((1, 1, width), f32),
        in_specs=[WHOLE],
        out_specs=WHOLE,
        scratch_shapes=[
            pltpu.VMEM((count, 1, width), f32),
            pltpu.SemaphoreType.DMA((count,)),
            pltpu.SemaphoreType.DMA((count,)),
        ],
        compiler_params=pltpu.CompilerParams(collective_id=2, has_side_effects=True),
        name="small_scatter",
    )(v.reshape(count, 1, width))


def swap(x, bit):
    return lax.ppermute(x, "seq", [(i, i ^ bit) for i in range(4)])


def spread(own):
    far = swap(own, 2)
    return own, swap(own, 1), far, swap(far, 1)


def reduce_rows(near, far):
    got = swap(near, 1)
    across = swap(far[0] + got[1], 2)
    return got, across


def pick(step, refs, dest):
    for k, ref in enumerate(refs):

        @pl.when(step == k)
        def _(ref=ref):
            dest[...] = ref[...]


ORDER = (1, 3, 2, 0)


def rel_of(t):
    return jnp.where(t == 0, 1, jnp.where(t == 1, 3, jnp.where(t == 2, 2, 0)))


def qkv_body(scal, x0, x1, x2, x3, w, gain, shift, bias, h1, qkv, rows):
    pick(pl.program_id(0), (x0, x1, x2, x3), rows)
    unit, _ = normalize(rows[...].astype(f32))
    low = (unit * gain[...] + shift[...]).astype(bf16)
    h1[...] = low
    qkv[...] = (mm(low, w[...]) + bias[...]).astype(bf16)


def qkv_call(scal, pieces, w, gain, shift, bias):
    rows, width = pieces[0].shape
    cols = w.shape[1]
    out = lambda r, sc: (lax.bitwise_xor(sc[0], r), 0)
    return pl.pallas_call(
        qkv_body,
        out_shape=(
            jax.ShapeDtypeStruct((4 * rows, width), bf16),
            jax.ShapeDtypeStruct((4 * rows, cols), bf16),
        ),
        grid_spec=pltpu.PrefetchScalarGridSpec(
            num_scalar_prefetch=1,
            grid=(4,),
            in_specs=[WHOLE] * 8,
            out_specs=(pl.BlockSpec((rows, width), out), pl.BlockSpec((rows, cols), out)),
            scratch_shapes=[pltpu.VMEM((rows, width), bf16)],
        ),
        compiler_params=params(),
        name="qkv",
    )(scal, *pieces, w, gain, shift, bias)


def make_bias(scal, slopes, pair, bias, keys):
    pos = lax.broadcasted_iota(jnp.int32, (keys, LANES), 0)
    inside = pos < scal[1]
    ramp = pos.astype(f32)
    for h in range(2):
        bias[h] = jnp.where(inside, ramp * slopes[2 * pair + h], NEG)


def head_only(x, h):
    lane = lax.broadcasted_iota(jnp.int32, x.shape, 1)
    return jnp.where((lane >= h * HEAD_DIM) & (lane < (h + 1) * HEAD_DIM), x, jnp.zeros_like(x))


def score_t(k_ref, qm, bias, h, length):
    block = qm.shape[0]
    s = mm_t(k_ref[0:length, :], qm)
    b = bias[h, 0:length, :]
    s = s + jnp.concatenate([b] * (block // LANES), axis=1)
    key = lax.broadcasted_iota(jnp.int32, (block, block), 0)
    query = lax.broadcasted_iota(jnp.int32, (block, block), 1)
    last = jnp.where(key <= query, s[length - block :], NEG)
    if length == block:
        return last
    return jnp.concatenate([s[: length - block], last], axis=0)


def attend_body(scal, q, k, v, slopes, o, lse, bias, vt):
    pair, step = pl.program_id(0), pl.program_id(1)
    block = q.shape[0]
    keys = k.shape[0]

    @pl.when(step == 0)
    def _():
        make_bias(scal, slopes, pair, bias, keys)
        vt[...] = v[...].T

    for c in range(keys // block):

        @pl.when(step == c)
        def _(c=c):
            length = (c + 1) * block
            scaled = q[...] * bf16(HEAD_DIM**-0.5)
            outs, logs = [], []
            for h in range(2):
                s = score_t(k, head_only(scaled, h), bias, h, length)
                top = jnp.max(s, axis=0, keepdims=True)
                e = jnp.exp(s - top)
                total = jnp.sum(e, axis=0, keepdims=True)
                mixed = mm(vt[h * HEAD_DIM : (h + 1) * HEAD_DIM, 0:length], e.astype(bf16))
                outs.append(mixed / total)
                logs.append(top + jnp.log(total))
            o[...] = jnp.concatenate(outs, axis=0).T.astype(bf16)
            lse[0, 0:2, :] = jnp.concatenate(logs, axis=0)


def attend_call(scal, slopes, qkv, block):
    keys, cols = qkv.shape
    width = cols // 3
    pairs = width // LANES
    return pl.pallas_call(
        attend_body,
        out_shape=(
            jax.ShapeDtypeStruct((keys, width), bf16),
            jax.ShapeDtypeStruct((pairs, 8, keys), f32),
        ),
        grid_spec=pltpu.PrefetchScalarGridSpec(
            num_scalar_prefetch=1,
            grid=(pairs, keys // block),
            in_specs=[
                pl.BlockSpec((block, LANES), lambda p, c, sc: (c, p)),
                pl.BlockSpec((keys, LANES), lambda p, c, sc: (0, pairs + p)),
                pl.BlockSpec((keys, LANES), lambda p, c, sc: (0, 2 * pairs + p)),
                SCALAR,
            ],
            out_specs=(
                pl.BlockSpec((block, LANES), lambda p, c, sc: (c, p)),
                pl.BlockSpec((1, 8, block), lambda p, c, sc: (p, 0, c)),
            ),
            scratch_shapes=[
                pltpu.VMEM((2, keys, LANES), f32),
                pltpu.VMEM((LANES, keys), bf16),
            ],
        ),
        compiler_params=params(),
        name="attend",
    )(scal, qkv, qkv, qkv, slopes)


def attend_back_body(scal, q, k, v, o, do, lse, slopes, dq, dk, dv, bias, kt, dk_sum, dv_sum):
    pair, step = pl.program_id(0), pl.program_id(1)
    block = q.shape[0]
    keys = k.shape[0]
    scale = HEAD_DIM**-0.5

    @pl.when(step == 0)
    def _():
        make_bias(scal, slopes, pair, bias, keys)
        kt[...] = k[...].T
        dk_sum[...] = jnp.zeros_like(dk_sum)
        dv_sum[...] = jnp.zeros_like(dv_sum)

    for c in range(keys // block):

        @pl.when(step == c)
        def _(c=c):
            length = (c + 1) * block
            scaled = q[...] * bf16(scale)
            both = (do[...].astype(f32) * o[...].astype(f32)).T
            outs = []
            for h in range(2):
                qm = head_only(scaled, h)
                dom = head_only(do[...], h)
                dot_row = jnp.sum(both[h * HEAD_DIM : (h + 1) * HEAD_DIM], axis=0, keepdims=True)
                p = jnp.exp(score_t(k, qm, bias, h, length) - lse[0, h : h + 1, :])
                dp = mm_t(v[0:length, :], dom)
                ds = (p * (dp - dot_row)).astype(bf16)
                dv_sum[0:length, :] += mm(p.astype(bf16), dom)
                dk_sum[0:length, :] += mm(ds, qm)
                outs.append(mm(kt[h * HEAD_DIM : (h + 1) * HEAD_DIM, 0:length], ds))
            dq[...] = (jnp.concatenate(outs, axis=0).T * scale).astype(bf16)

    @pl.when(step == keys // block - 1)
    def _():
        dk[...] = dk_sum[...].astype(bf16)
        dv[...] = dv_sum[...].astype(bf16)


def attend_back_call(scal, slopes, qkv, o, do, lse, block):
    keys, cols = qkv.shape
    width = cols // 3
    pairs = width // LANES
    some = pl.BlockSpec((block, LANES), lambda p, c, sc: (c, p))
    full = pl.BlockSpec((keys, LANES), lambda p, c, sc: (0, p))
    return pl.pallas_call(
        attend_back_body,
        out_shape=(jax.ShapeDtypeStruct((keys, width), bf16),) * 3,
        grid_spec=pltpu.PrefetchScalarGridSpec(
            num_scalar_prefetch=1,
            grid=(pairs, keys // block),
            in_specs=[
                some,
                pl.BlockSpec((keys, LANES), lambda p, c, sc: (0, pairs + p)),
                pl.BlockSpec((keys, LANES), lambda p, c, sc: (0, 2 * pairs + p)),
                some,
                some,
                pl.BlockSpec((1, 8, block), lambda p, c, sc: (p, 0, c)),
                SCALAR,
            ],
            out_specs=(some, full, full),
            scratch_shapes=[
                pltpu.VMEM((2, keys, LANES), f32),
                pltpu.VMEM((LANES, keys), bf16),
                pltpu.VMEM((keys, LANES), f32),
                pltpu.VMEM((keys, LANES), f32),
            ],
        ),
        compiler_params=params(),
        name="attend_back",
    )(scal, qkv, qkv, qkv, o, do, lse, slopes)


def lay_columns(w_ref, first, dest):
    width = w_ref.shape[2]
    for d in range(w_ref.shape[0]):
        dest[:, d * width : (d + 1) * width] = w_ref[d, first : first + dest.shape[0], :]


def out_body(scal, o, w, near, far, flat, *, first):
    t = pl.program_id(0)

    @pl.when(t == 0)
    def _():
        lay_columns(w, first, flat)

    part = mm(o[...], flat[...]).astype(bf16)

    @pl.when(t < 2)
    def _():
        near[0] = part

    @pl.when(t >= 2)
    def _():
        far[0] = part


def near_map(t, *_):
    return (jnp.minimum(t, 1), 0, 0)


def far_map(t, *_):
    return (jnp.maximum(t - 2, 0), 0, 0)


def out_call(scal, o, w, first):
    keys, inner = o.shape
    rows = keys // 4
    width = w.shape[0] * w.shape[2]
    return pl.pallas_call(
        functools.partial(out_body, first=first),
        out_shape=(jax.ShapeDtypeStruct((2, rows, width), bf16),) * 2,
        grid_spec=pltpu.PrefetchScalarGridSpec(
            num_scalar_prefetch=1,
            grid=(4,),
            in_specs=[
                pl.BlockSpec((rows, inner), lambda t, sc: (lax.bitwise_xor(sc[0], rel_of(t)), 0)),
                WHOLE,
            ],
            out_specs=(
                pl.BlockSpec((1, rows, width), near_map),
                pl.BlockSpec((1, rows, width), far_map),
            ),
            scratch_shapes=[pltpu.VMEM((inner, width), bf16)],
        ),
        compiler_params=params(),
        name="out_proj",
    )(scal, o, w)


def mid_body(x, a, b, c, bias, gain, shift, mid, h2):
    value = x[...].astype(f32) + (
        (a[0].astype(f32) + b[0].astype(f32)) + c[...].astype(f32) + bias[...]
    )
    mid[...] = value
    unit, _ = normalize(value)
    h2[...] = (unit * gain[...] + shift[...]).astype(bf16)


def mid_call(x, a, b, c, bias, gain, shift):
    rows, width = x.shape
    one = pl.BlockSpec((rows // 2, width), lambda i: (i, 0))
    first = pl.BlockSpec((1, rows // 2, width), lambda i: (0, i, 0))
    second = pl.BlockSpec((1, rows // 2, width), lambda i: (1, i, 0))
    row = pl.BlockSpec((1, width), lambda i: (0, 0))
    return pl.pallas_call(
        mid_body,
        out_shape=(
            jax.ShapeDtypeStruct((rows, width), f32),
            jax.ShapeDtypeStruct((rows, width), bf16),
        ),
        grid=(2,),
        in_specs=[one, second, first, one, row, row, row],
        out_specs=(one, one),
        compiler_params=params(),
        name="mid_norm",
    )(x, a, b, c, bias, gain, shift)


def gelu_parts(u):
    root = math.sqrt(2.0 / math.pi)
    sq = u * u
    t = jnp.tanh(root * (u + GELU_COEF * (sq * u)))
    half = 0.5 * (1.0 + t)
    slope = half + 0.5 * u * (1.0 - t * t) * (root * (1.0 + 3.0 * GELU_COEF * sq))
    return u * half, slope


def mlp_body(
    h0, h1, h2, h3, g_rows, w1, w2, b1,
    y_near, y_far, d_near, d_far, a_all, du_all, h_all, g_all, bias_sum,
    flat, hb, gb,
):
    t = pl.program_id(0)

    @pl.when(t == 0)
    def _():
        lay_columns(w2, 0, flat)
        bias_sum[...] = jnp.zeros_like(bias_sum)

    pick(rel_of(t), (h0, h1, h2, h3), hb)
    gb[...] = g_rows[rel_of(t)]
    h_all[...] = hb[...]
    g_all[...] = gb[...]
    inner = w1.shape[1]
    chunk = 256
    for c in range(inner // chunk):
        cols = slice(c * chunk, (c + 1) * chunk)
        u = mm(hb[...], w1[:, cols]) + b1[:, cols]
        value, slope = gelu_parts(u)
        a_all[:, cols] = value.astype(bf16)
        du = (mm_t(gb[...], flat[cols, :]) * slope).astype(bf16)
        du_all[:, cols] = du
        bias_sum[:, cols] += jnp.sum(du.astype(f32), axis=0, keepdims=True)
    y = mm(a_all[...], flat[...]).astype(bf16)
    d = mm_t(du_all[...], w1[...]).astype(bf16)

    @pl.when(t < 2)
    def _():
        y_near[0] = y
        d_near[0] = d

    @pl.when(t >= 2)
    def _():
        y_far[0] = y
        d_far[0] = d


def mlp_call(h_pieces, g_rows, w1, w2, b1):
    rows, width = h_pieces[0].shape
    inner = w1.shape[1]
    pair = jax.ShapeDtypeStruct((2, rows, width), bf16)
    near = pl.BlockSpec((1, rows, width), near_map)
    far = pl.BlockSpec((1, rows, width), far_map)
    block = lambda n: pl.BlockSpec((rows, n), lambda t: (t, 0))
    return pl.pallas_call(
        mlp_body,
        out_shape=(
            pair,
            pair,
            pair,
            pair,
            jax.ShapeDtypeStruct((4 * rows, inner), bf16),
            jax.ShapeDtypeStruct((4 * rows, inner), bf16),
            jax.ShapeDtypeStruct((4 * rows, width), bf16),
            jax.ShapeDtypeStruct((4 * rows, width), bf16),
            jax.ShapeDtypeStruct((1, inner), f32),
        ),
        grid=(4,),
        in_specs=[WHOLE] * 8,
        out_specs=(
            near, far, near, far, block(inner), block(inner), block(width), block(width),
            pl.BlockSpec((1, inner), lambda t: (0, 0)),
        ),
        scratch_shapes=[
            pltpu.VMEM((inner, width), bf16),
            pltpu.VMEM((rows, width), bf16),
            pltpu.VMEM((rows, width), bf16),
        ],
        compiler_params=params(),
        name="mlp",
    )(*h_pieces, g_rows, w1, w2, b1)


def outer_body(left, right, out, turned, *, blocks):
    @pl.when(pl.program_id(0) == 0)
    def _():
        turned[...] = left[...].T

    part = mm(turned[...], right[...]).astype(bf16)
    if blocks:
        width = out.shape[2]
        for d in range(out.shape[0]):
            out[d] = part[:, d * width : (d + 1) * width]
    else:
        out[...] = part


def outer_call(left, right, parts, name):
    rows, m = left.shape
    n = right.shape[1]
    step = 256
    if parts > 1:
        width = n // parts
        out_shape = jax.ShapeDtypeStruct((parts, m, width), bf16)
        out_spec = pl.BlockSpec((step // width, m, width), lambda j: (j, 0, 0))
    else:
        out_shape = jax.ShapeDtypeStruct((m, n), bf16)
        out_spec = pl.BlockSpec((m, step), lambda j: (0, j))
    return pl.pallas_call(
        functools.partial(outer_body, blocks=parts > 1),
        out_shape=out_shape,
        grid=(n // step,),
        in_specs=[WHOLE, pl.BlockSpec((rows, step), lambda j: (0, j))],
        out_specs=out_spec,
        scratch_shapes=[pltpu.VMEM((m, rows), bf16)],
        compiler_params=params(),
        name=name,
    )(left, right)


def mid_back_body(mid, a, b, c, g, gain, dmid, dbr, sums):
    @pl.when(pl.program_id(0) == 0)
    def _():
        sums[...] = jnp.zeros_like(sums)

    unit, inv = normalize(mid[...])
    e = (a[0].astype(f32) + b[0].astype(f32)) + c[...].astype(f32)
    grad = g[...].astype(f32)
    value = grad + norm_back(e, gain[...], unit, inv)
    dmid[...] = value
    low = value.astype(bf16)
    dbr[...] = low
    sums[0:1, :] += jnp.sum(e * unit, axis=0, keepdims=True)
    sums[1:2, :] += jnp.sum(e, axis=0, keepdims=True)
    sums[2:3, :] += jnp.sum(low.astype(f32), axis=0, keepdims=True)
    sums[3:4, :] += jnp.sum(grad, axis=0, keepdims=True)


def mid_back_call(mid, a, b, c, g, gain):
    rows, width = mid.shape
    one = pl.BlockSpec((rows // 2, width), lambda i: (i, 0))
    first = pl.BlockSpec((1, rows // 2, width), lambda i: (0, i, 0))
    second = pl.BlockSpec((1, rows // 2, width), lambda i: (1, i, 0))
    row = pl.BlockSpec((1, width), lambda i: (0, 0))
    return pl.pallas_call(
        mid_back_body,
        out_shape=(
            jax.ShapeDtypeStruct((rows, width), f32),
            jax.ShapeDtypeStruct((rows, width), bf16),
            jax.ShapeDtypeStruct((8, width), f32),
        ),
        grid=(2,),
        in_specs=[one, second, first, one, one, row],
        out_specs=(one, one, pl.BlockSpec((8, width), lambda i: (0, 0))),
        compiler_params=params(),
        name="mid_back",
    )(mid, a, b, c, g, gain)


def out_back_body(scal, b0, b1, b2, b3, o, w, do, grad, flat, rows, total, *, first):
    r = pl.program_id(0)

    @pl.when(r == 0)
    def _():
        lay_columns(w, first, flat)
        total[...] = jnp.zeros_like(total)

    pick(r, (b0, b1, b2, b3), rows)
    do[...] = mm_t(rows[...], flat[...]).astype(bf16)
    total[...] += mm(o[...].T, rows[...])

    @pl.when(r == 3)
    def _():
        width = grad.shape[2]
        for d in range(grad.shape[0]):
            grad[d] = total[:, d * width : (d + 1) * width].astype(bf16)


def out_back_call(scal, pieces, o, w, first):
    rows, width = pieces[0].shape
    inner = o.shape[1]
    at = pl.BlockSpec((rows, inner), lambda r, sc: (lax.bitwise_xor(sc[0], r), 0))
    grad = (w.shape[0], inner, w.shape[2])
    return pl.pallas_call(
        functools.partial(out_back_body, first=first),
        out_shape=(jax.ShapeDtypeStruct(o.shape, bf16), jax.ShapeDtypeStruct(grad, bf16)),
        grid_spec=pltpu.PrefetchScalarGridSpec(
            num_scalar_prefetch=1,
            grid=(4,),
            in_specs=[WHOLE] * 4 + [at, WHOLE],
            out_specs=(at, pl.BlockSpec(grad, lambda r, sc: (0, 0, 0))),
            scratch_shapes=[
                pltpu.VMEM((inner, width), bf16),
                pltpu.VMEM((rows, width), bf16),
                pltpu.VMEM((inner, width), f32),
            ],
        ),
        compiler_params=params(),
        name="out_back",
    )(scal, *pieces, o, w)


def qkv_back_body(scal, dq, dk, dv, w, near, far, merged, sums):
    t = pl.program_id(0)

    @pl.when(t == 0)
    def _():
        sums[...] = jnp.zeros_like(sums)

    low = jnp.concatenate([dq[...], dk[...], dv[...]], axis=1)
    merged[...] = low
    part = mm_t(low, w[...]).astype(bf16)
    sums[...] += jnp.sum(low.astype(f32), axis=0, keepdims=True)

    @pl.when(t < 2)
    def _():
        near[0] = part

    @pl.when(t >= 2)
    def _():
        far[0] = part


def qkv_back_call(scal, dq, dk, dv, w):
    keys, inner = dq.shape
    rows = keys // 4
    width = w.shape[0]
    where = lambda t, sc: (lax.bitwise_xor(sc[0], rel_of(t)), 0)
    at = pl.BlockSpec((rows, inner), where)
    return pl.pallas_call(
        qkv_back_body,
        out_shape=(
            jax.ShapeDtypeStruct((2, rows, width), bf16),
            jax.ShapeDtypeStruct((2, rows, width), bf16),
            jax.ShapeDtypeStruct((keys, 3 * inner), bf16),
            jax.ShapeDtypeStruct((1, 3 * inner), f32),
        ),
        grid_spec=pltpu.PrefetchScalarGridSpec(
            num_scalar_prefetch=1,
            grid=(4,),
            in_specs=[at, at, at, WHOLE],
            out_specs=(
                pl.BlockSpec((1, rows, width), near_map),
                pl.BlockSpec((1, rows, width), far_map),
                pl.BlockSpec((rows, 3 * inner), where),
                pl.BlockSpec((1, 3 * inner), lambda t, sc: (0, 0)),
            ),
        ),
        compiler_params=params(),
        name="qkv_back",
    )(scal, dq, dk, dv, w)


def in_back_body(x, a, b, c, dmid, gain, grad, sums):
    @pl.when(pl.program_id(0) == 0)
    def _():
        sums[...] = jnp.zeros_like(sums)

    unit, inv = normalize(x[...].astype(f32))
    e = (a[0].astype(f32) + b[0].astype(f32)) + c[...].astype(f32)
    grad[...] = (dmid[...] + norm_back(e, gain[...], unit, inv)).astype(bf16)
    sums[0:1, :] += jnp.sum(e * unit, axis=0, keepdims=True)
    sums[1:2, :] += jnp.sum(e, axis=0, keepdims=True)


def in_back_call(x, a, b, c, dmid, gain):
    rows, width = x.shape
    one = pl.BlockSpec((rows // 2, width), lambda i: (i, 0))
    first = pl.BlockSpec((1, rows // 2, width), lambda i: (0, i, 0))
    second = pl.BlockSpec((1, rows // 2, width), lambda i: (1, i, 0))
    row = pl.BlockSpec((1, width), lambda i: (0, 0))
    return pl.pallas_call(
        in_back_body,
        out_shape=(
            jax.ShapeDtypeStruct((rows, width), bf16),
            jax.ShapeDtypeStruct((8, width), f32),
        ),
        grid=(2,),
        in_specs=[one, second, first, one, one, row],
        out_specs=(one, pl.BlockSpec((8, width), lambda i: (0, 0))),
        compiler_params=params(),
        name="in_back",
    )(x, a, b, c, dmid, gain)


def remote(src, dst, send, recv, dp, seq):
    return pltpu.make_async_remote_copy(
        src_ref=src,
        dst_ref=dst,
        send_sem=send,
        recv_sem=recv,
        device_id=(dp, seq),
        device_id_type=pl.DeviceIdType.MESH,
    )


def greet(peers):
    barrier = pltpu.get_barrier_semaphore()
    for dp, seq in peers:
        pl.semaphore_signal(
            barrier, inc=1, device_id=(dp, seq), device_id_type=pl.DeviceIdType.MESH
        )
    pl.semaphore_wait(barrier, len(peers))


class GradSum:
    def __init__(self, part, acc, landx, land, sems, dp, seq):
        self.part, self.landx, self.land, self.sems = part, landx, land, sems
        self.fetched = acc is not None
        self.acc = acc if self.fetched else landx
        self.seq, self.z, self.x = seq, dp // 2, dp % 2

    def cross(self, k):
        return remote(
            self.part.at[2 * k + (1 - self.x)],
            self.landx.at[k],
            self.sems.at[0, k],
            self.sems.at[1, k],
            2 * self.z + (1 - self.x),
            self.seq,
        )

    def fetch(self, k):
        return pltpu.make_async_copy(
            self.part.at[2 * k + self.x], self.acc.at[k], self.sems.at[6, k]
        )

    def right(self, b, first):
        return remote(
            self.acc.at[b] if first else self.land.at[b + 1],
            self.land.at[b + 1],
            self.sems.at[2, b],
            self.sems.at[3, b],
            2 * ((self.z + 1) % 4) + self.x,
            self.seq,
        )

    def left(self, b, first):
        return remote(
            self.acc.at[b] if first else self.land.at[b],
            self.land.at[b],
            self.sems.at[4, b],
            self.sems.at[5, b],
            2 * ((self.z + 3) % 4) + self.x,
            self.seq,
        )

    def start(self):
        for k in (3, 0, 2, 1):
            self.cross(k).start()
        if self.fetched:
            for k in range(4):
                self.fetch(k).start()

    def add_cross(self):
        for k in (3, 0, 2, 1):
            self.cross(k).wait_recv()
            if self.fetched:
                self.fetch(k).wait()
                own = self.acc[k].astype(f32)
            else:
                own = self.part[2 * k + self.x].astype(f32)
            self.acc[k] = (own + self.landx[k].astype(f32)).astype(bf16)

    def stage(self, k):
        @pl.when(self.z == k)
        def _():
            for b in range(3, k, -1):
                if k > 0:
                    self.right(b, False).wait_recv()
                    total = self.land[b + 1].astype(f32) + self.acc[b].astype(f32)
                    self.land[b + 1] = total.astype(bf16)
                self.right(b, k == 0).start()

        @pl.when(self.z == 3 - k)
        def _():
            for b in range(0, 3 - k):
                if k > 0:
                    self.left(b, False).wait_recv()
                    total = self.land[b].astype(f32) + self.acc[b].astype(f32)
                    self.land[b] = total.astype(bf16)
                self.left(b, k == 0).start()

    def finish(self, out):
        z = self.z
        out[...] = self.acc[z].astype(f32)

        @pl.when(z > 0)
        def _():
            self.right(z, False).wait_recv()
            out[...] += self.land[z + 1].astype(f32)

        @pl.when(z < 3)
        def _():
            self.left(z, False).wait_recv()
            out[...] += self.land[z].astype(f32)

    def drain(self):
        for k in range(4):
            self.cross(k).wait_send()
        for k in range(3):

            @pl.when(self.z == k)
            def _(k=k):
                for b in range(3, k, -1):
                    self.right(b, k == 0).wait_send()

            @pl.when(self.z == 3 - k)
            def _(k=k):
                for b in range(0, 3 - k):
                    self.left(b, k == 0).wait_send()

    @staticmethod
    def scratch(m, n, fetched=False):
        own = [pltpu.VMEM((4, m, n), bf16)] if fetched else []
        return own + [
            pltpu.VMEM((4, m, n), bf16),
            pltpu.VMEM((5, m, n), bf16),
            pltpu.SemaphoreType.DMA((7, 4)),
        ]


SMALL_ROWS = 16


class Gather:
    def __init__(self, own, out, sems, dp, seq):
        self.own, self.out, self.sems = own, out, sems
        self.seq, self.z, self.x = seq, dp // 2, dp % 2

    def along(self, k, step, src=None):
        slot = self.out.at[2 * k + self.x]
        return remote(
            slot if src is None else src,
            slot,
            self.sems.at[0 if step > 0 else 1, k],
            self.sems.at[3, k],
            2 * ((self.z + step + 4) % 4) + self.x,
            self.seq,
        )

    def over(self, k, src=None):
        slot = self.out.at[2 * k + self.x]
        return remote(
            slot if src is None else src,
            slot,
            self.sems.at[2, k],
            self.sems.at[4, k],
            2 * self.z + (1 - self.x),
            self.seq,
        )

    def keep(self):
        return pltpu.make_async_copy(
            self.own, self.out.at[2 * self.z + self.x], self.sems.at[5, 0]
        )

    def start(self):
        z = self.z

        @pl.when(z < 3)
        def _():
            self.along(z, 1, self.own).start()

        @pl.when(z > 0)
        def _():
            self.along(z, -1, self.own).start()

        self.over(z, self.own).start()
        self.keep().start()

    def hop(self, dist):
        z = self.z

        @pl.when(z - dist >= 0)
        def _():
            k = z - dist
            self.along(k, 1).wait_recv()

            @pl.when(z < 3)
            def _():
                self.along(k, 1).start()

            self.over(k).start()

        @pl.when(z + dist <= 3)
        def _():
            k = z + dist
            self.along(k, -1).wait_recv()

            @pl.when(z > 0)
            def _():
                self.along(k, -1).start()

            self.over(k).start()

    def finish(self):
        z = self.z
        self.keep().wait()
        for k in range(4):
            self.over(k).wait_recv()
            self.over(k).wait_send()

            @pl.when((z < 3) & (z >= k))
            def _(k=k):
                self.along(k, 1).wait_send()

            @pl.when((z > 0) & (z <= k))
            def _(k=k):
                self.along(k, -1).wait_send()

    @staticmethod
    def scratch():
        return pltpu.SemaphoreType.DMA((6, 4))


class Spread:
    def __init__(self, own, rows, sems, dp, seq):
        mate, across = seq + 1 - 2 * (seq % 2), (seq + 2) % 4
        to = lambda src, r, peer: remote(src, rows.at[r], sems.at[0, r], sems.at[1, r], dp, peer)
        self.near, self.far = to(own, 1, mate), to(own, 2, across)
        self.last = to(rows.at[2], 3, mate)

    def start(self):
        self.far.start()
        self.near.start()

    def forward(self):
        self.far.wait_recv()
        self.last.start()

    def drain(self):
        for copy in (self.near, self.far, self.last):
            copy.wait_send()


def neighbours(seq):
    mate = seq + 1 - 2 * (seq % 2)
    return mate, (seq + 2) % 4, (mate + 2) % 4


def block_at(seq, rel):
    return 2 * ((seq // 2 + rel // 2) % 2) + (seq + rel) % 2


def front_body(
    wq, wo, x, v_up, v_qv, v_g1, v_s1, v_out, v_g2, v_s2, v_down,
    wq_all, wo_all, x_rows, gain1, shift1, bias_qkv, bias_out, gain2, shift2, bias_up, bias_down,
    small, vectors, q_sem, o_sem, x_sem, seq_sem, dp_sem, keep_sem,
):
    dp, seq = lax.axis_index("dp"), lax.axis_index("seq")
    greet([((dp + i) % 8, seq) for i in range(1, 8)] + [(dp, p) for p in neighbours(seq)])
    gather_q = Gather(wq, wq_all, q_sem, dp, seq)
    gather_o = Gather(wo, wo_all, o_sem, dp, seq)
    rows = Spread(x, x_rows, x_sem, dp, seq)
    rows.start()
    gather_q.start()
    keep_x = pltpu.make_async_copy(x, x_rows.at[0], keep_sem.at[0])
    keep_x.start()
    at = 0
    for ref in (v_up, v_qv, v_g1, v_s1, v_out, v_g2, v_s2, v_down):
        small[:, at : at + ref.shape[1]] = ref[...].astype(f32)
        at += ref.shape[1]
    keep_v = pltpu.make_async_copy(small, vectors.at[dp, seq], keep_sem.at[1])
    keep_v.start()
    group = [
        remote(small, vectors.at[dp, seq], seq_sem.at[0, i], seq_sem.at[1, i], dp, peer)
        for i, peer in enumerate(neighbours(seq))
    ]
    for copy in group:
        copy.start()
    gather_o.start()
    keep_v.wait()
    for copy in group:
        copy.wait_recv()

    def to_dp(i):
        return remote(
            vectors.at[dp], vectors.at[dp], dp_sem.at[0, i], dp_sem.at[1, i], (dp + i) % 8, seq
        )

    for i in range(1, 8):
        to_dp(i).start()
    gather_q.hop(1)
    gather_o.hop(1)
    for i in range(1, 8):
        to_dp(i).wait_recv()
    for ref, at in (
        (gain1, 192), (shift1, 224), (bias_out, 256), (gain2, 288), (shift2, 320), (bias_down, 352),
    ):
        for d in range(8):
            ref[:, d * LANES : (d + 1) * LANES] = jnp.concatenate(
                [vectors[d, i, :, at : at + 32] for i in range(4)], axis=1
            )
    for part in range(2):
        for half in range(2):
            lane = part * 512 + half * LANES
            bias_qkv[:, lane : lane + LANES] = jnp.concatenate(
                [vectors[4 * part + seq, 2 * half + i, :, 128:192] for i in range(2)], axis=1
            )
    bias_qkv[:, 256:512] = jnp.zeros((1, 256), f32)
    for i in range(8):
        bias_up[:, i * LANES : (i + 1) * LANES] = vectors[2 * seq + i // 4, i % 4, :, 0:LANES]
    gather_q.hop(2)
    gather_o.hop(2)
    rows.forward()
    gather_q.hop(3)
    gather_o.hop(3)
    gather_q.finish()
    gather_o.finish()
    rows.near.wait_recv()
    rows.last.wait_recv()
    rows.drain()
    keep_x.wait()
    for copy in group:
        copy.wait_send()
    for i in range(1, 8):
        to_dp(i).wait_send()


def front_call(wq, wo, x, small):
    count = sum(v.shape[0] for v in small)
    rows, width = x.shape
    one = lambda n: jax.ShapeDtypeStruct((1, n), f32)
    sem = pltpu.SemaphoreType.DMA
    return pl.pallas_call(
        front_body,
        out_shape=(
            jax.ShapeDtypeStruct((8, *wq.shape), bf16),
            jax.ShapeDtypeStruct((8, *wo.shape), bf16),
            jax.ShapeDtypeStruct((4, rows, width), bf16),
            one(width), one(width), one(wq.shape[1]), one(width), one(width), one(width),
            one(width), one(width),
        ),
        in_specs=[WHOLE] * 11,
        out_specs=(WHOLE,) * 11,
        scratch_shapes=[
            pltpu.VMEM((1, count), f32),
            pltpu.VMEM((8, 4, 1, count), f32),
            Gather.scratch(),
            Gather.scratch(),
            sem((2, 4)),
            sem((2, 3)),
            sem((2, 8)),
            sem((2,)),
        ],
        compiler_params=params(collective_id=4, has_side_effects=True),
        name="front",
    )(wq, wo, x, *(v.reshape(1, -1) for v in small))


def attention_body(
    scal, slopes, x_rows, g, wq, wo, w1, w2, gain1, shift1, bias_qkv, bias_out, gain2, shift2,
    h1, qkv, o, lse, mid, h2, g_rows, w1_all, w2_all,
    bias, vt, flat, part, land_c, sum_y, land_y, g_sem, row_sems, keep_sem, w1_sem, w2_sem,
):
    dp, seq = lax.axis_index("dp"), lax.axis_index("seq")
    mate, across, _ = neighbours(seq)
    greet([((dp + i) % 8, seq) for i in range(1, 8)] + [(dp, mate), (dp, across)])
    rows, width = g.shape
    keys = qkv.shape[0]
    inner = o.shape[1]
    pairs = inner // LANES
    gathers = [Gather(w1, w1_all, w1_sem, dp, seq), Gather(w2, w2_all, w2_sem, dp, seq)]
    for gather in gathers:
        gather.start()
    spread_g = Spread(g, g_rows, g_sem, dp, seq)
    spread_g.start()
    keep = pltpu.make_async_copy(g, g_rows.at[0], keep_sem.at[0])
    keep.start()
    lay_columns(wo, 0, flat)

    def project(r, carry):
        at = pl.ds(pl.multiple_of(block_at(seq, r) * rows, rows), rows)
        unit, _ = normalize(x_rows[r].astype(f32))
        low = (unit * gain1[...] + shift1[...]).astype(bf16)
        h1[at, :] = low
        qkv[at, :] = (mm(low, wq[...]) + bias_qkv[...]).astype(bf16)
        return carry

    lax.fori_loop(0, 4, project, 0)

    def prepare(p, carry):
        pos = lax.broadcasted_iota(jnp.int32, (keys, LANES), 0)
        ramp = pos.astype(f32)
        inside = pos < scal[1]
        for h in range(2):
            bias[2 * p + h] = jnp.where(inside, ramp * slopes[2 * p + h], NEG)
        lane = pl.ds(pl.multiple_of(2 * inner + p * LANES, LANES), LANES)
        vt[p] = qkv[:, lane].T
        return carry

    lax.fori_loop(0, pairs, prepare, 0)
    for gather in gathers:
        gather.hop(1)
    spread_g.forward()

    cores = [
        remote(part.at[r], land_c.at[k], row_sems.at[0, k], row_sems.at[1, k], dp, mate)
        for k, r in ((0, 1), (1, 3))
    ]
    over = remote(sum_y, land_y, row_sems.at[0, 2], row_sems.at[1, 2], dp, across)
    chunk = 128

    def attend(t, carry):
        rel = 3 - t
        c_now = block_at(seq, rel)
        at = pl.ds(pl.multiple_of(c_now * rows, rows), rows)
        for c in range(keys // rows):

            @pl.when(c_now == c)
            def _(c=c):
                length = (c + 1) * rows

                def one_pair(p, carry):
                    lane = pl.ds(pl.multiple_of(p * LANES, LANES), LANES)
                    k_lane = pl.ds(pl.multiple_of(inner + p * LANES, LANES), LANES)
                    scaled = qkv[c * rows : length, lane] * bf16(HEAD_DIM**-0.5)
                    k = qkv[0:length, k_lane]
                    outs, logs = [], []
                    for h in range(2):
                        s = scores(k, head_only(scaled, h), bias[2 * p + h, 0:length, :])
                        top = jnp.max(s, axis=0, keepdims=True)
                        e = jnp.exp(s - top)
                        total = jnp.sum(e, axis=0, keepdims=True)
                        half = vt[p, h * HEAD_DIM : (h + 1) * HEAD_DIM, 0:length]
                        outs.append(mm(half, e.astype(bf16)) / total)
                        logs.append(top + jnp.log(total))
                    o[c * rows : length, lane] = jnp.concatenate(outs, axis=0).T.astype(bf16)
                    lse[p, 0:2, c * rows : length] = jnp.concatenate(logs, axis=0)
                    return carry

                lax.fori_loop(0, pairs, one_pair, 0)

        part[rel] = mm(o[at, :], flat[...]).astype(bf16)

        @pl.when(t == 0)
        def _():
            cores[1].start()

        @pl.when(t == 1)
        def _():
            cores[1].wait_recv()
            for i in range(rows // chunk):
                at = slice(i * chunk, (i + 1) * chunk)
                total = part[2, at, :].astype(f32) + land_c[1, at, :].astype(f32)
                sum_y[at, :] = total.astype(bf16)
            over.start()
            for gather in gathers:
                gather.hop(2)

        @pl.when(t == 2)
        def _():
            cores[0].start()
            for gather in gathers:
                gather.hop(3)

        return carry

    lax.fori_loop(0, 4, attend, 0)
    cores[0].wait_recv()
    over.wait_recv()

    def second_norm(i, carry):
        at = pl.ds(pl.multiple_of(i * chunk, chunk), chunk)
        total = (part[0, at, :].astype(f32) + land_c[0, at, :].astype(f32)) + land_y[
            at, :
        ].astype(f32)
        value = x_rows[0, at, :].astype(f32) + (total + bias_out[...])
        mid[at, :] = value
        unit, _ = normalize(value)
        h2[at, :] = (unit * gain2[...] + shift2[...]).astype(bf16)
        return carry

    lax.fori_loop(0, rows // chunk, second_norm, 0)
    for gather in gathers:
        gather.finish()
    spread_g.near.wait_recv()
    spread_g.last.wait_recv()
    spread_g.drain()
    keep.wait()
    for copy in cores + [over]:
        copy.wait_send()


def scores(k, qm, ramp):
    block = qm.shape[0]
    length = k.shape[0]
    s = mm_t(k, qm) + jnp.concatenate([ramp] * (block // LANES), axis=1)
    key = lax.broadcasted_iota(jnp.int32, (block, block), 0)
    query = lax.broadcasted_iota(jnp.int32, (block, block), 1)
    last = jnp.where(key <= query, s[length - block :], NEG)
    if length == block:
        return last
    return jnp.concatenate([s[: length - block], last], axis=0)


def attention_call(scal, slopes, x_rows, g, wq, wo, w1, w2, *vectors):
    rows, width = g.shape
    keys = 4 * rows
    inner = wo.shape[1]
    pairs = inner // LANES
    sem = pltpu.SemaphoreType.DMA
    return pl.pallas_call(
        attention_body,
        out_shape=(
            jax.ShapeDtypeStruct((keys, width), bf16),
            jax.ShapeDtypeStruct((keys, 3 * inner), bf16),
            jax.ShapeDtypeStruct((keys, inner), bf16),
            jax.ShapeDtypeStruct((pairs, 8, keys), f32),
            jax.ShapeDtypeStruct((rows, width), f32),
            jax.ShapeDtypeStruct((rows, width), bf16),
            jax.ShapeDtypeStruct((4, rows, width), bf16),
            jax.ShapeDtypeStruct((8, *w1.shape), bf16),
            jax.ShapeDtypeStruct((8, *w2.shape), bf16),
        ),
        in_specs=[SCALAR, SCALAR] + [WHOLE] * (6 + len(vectors)),
        out_specs=(WHOLE,) * 9,
        scratch_shapes=[
            pltpu.VMEM((2 * pairs, keys, LANES), f32),
            pltpu.VMEM((pairs, LANES, keys), bf16),
            pltpu.VMEM((inner, width), bf16),
            pltpu.VMEM((4, rows, width), bf16),
            pltpu.VMEM((2, rows, width), bf16),
            pltpu.VMEM((rows, width), bf16),
            pltpu.VMEM((rows, width), bf16),
            sem((2, 4)),
            sem((2, 3)),
            sem((1,)),
            Gather.scratch(),
            Gather.scratch(),
        ],
        compiler_params=params(collective_id=5, has_side_effects=True),
        name="attention",
    )(scal, slopes, x_rows, g, wq, wo, w1, w2, *vectors)


def feed_body(
    h2, g_rows, w1, w2, b1, mid, gain2,
    y_near, y_far, gw1, gw2, dmid, dbr, sums, up_sum,
    h_rows, a_all, du_all, flat, part, land_c, sum_y, land_y, turned, h_sem, row_sems, keep_sem,
):
    dp, seq = lax.axis_index("dp"), lax.axis_index("seq")
    mate, across, _ = neighbours(seq)
    greet([(dp, mate), (dp, across)])
    rows, width = h2.shape
    inner = w1.shape[1]
    spread_h = Spread(h2, h_rows, h_sem, dp, seq)
    spread_h.start()
    keep = pltpu.make_async_copy(h2, h_rows.at[0], keep_sem.at[0])
    keep.start()
    lay_columns(w2, 0, flat)
    up_sum[...] = jnp.zeros_like(up_sum)
    sums[...] = jnp.zeros_like(sums)
    keep.wait()
    cores = [
        remote(part.at[r], land_c.at[k], row_sems.at[0, k], row_sems.at[1, k], dp, mate)
        for k, r in ((0, 1), (1, 3))
    ]
    over = remote(sum_y, land_y, row_sems.at[0, 2], row_sems.at[1, 2], dp, across)
    chunk = 256

    def block(t, carry):
        @pl.when(t == 1)
        def _():
            spread_h.near.wait_recv()

        @pl.when(t == 2)
        def _():
            spread_h.forward()

        @pl.when(t == 3)
        def _():
            spread_h.last.wait_recv()

        at = pl.ds(pl.multiple_of(t * rows, rows), rows)
        for c in range(inner // chunk):
            cols = slice(c * chunk, (c + 1) * chunk)
            u = mm(h_rows[t], w1[:, cols]) + b1[:, cols]
            value, slope = gelu_parts(u)
            a_all[at, cols] = value.astype(bf16)
            du = (mm_t(g_rows[t], flat[cols, :]) * slope).astype(bf16)
            du_all[at, cols] = du
            up_sum[:, cols] += jnp.sum(du.astype(f32), axis=0, keepdims=True)
        y = mm(a_all[at, :], flat[...]).astype(bf16)
        part[t] = mm_t(du_all[at, :], w1[...]).astype(bf16)
        for r, (ref, k) in enumerate(((y_far, 1), (y_near, 0), (y_far, 0), (y_near, 1))):

            @pl.when(t == r)
            def _(ref=ref, k=k):
                ref[k] = y

        @pl.when(t == 1)
        def _():
            cores[0].start()

        @pl.when(t == 3)
        def _():
            cores[1].start()

        return carry

    lax.fori_loop(0, 4, block, 0)

    def turn(load):
        def step(i, carry):
            turned[:, pl.ds(pl.multiple_of(i * rows, rows), rows)] = load(i).T
            return carry

        lax.fori_loop(0, 4, step, 0)

    turn(lambda i: h_rows[i])

    def outer_up(j, carry):
        cols = pl.ds(pl.multiple_of(j * chunk, chunk), chunk)
        gw1[:, cols] = mm(turned[...], du_all[:, cols]).astype(bf16)
        return carry

    lax.fori_loop(0, 1, outer_up, 0)
    cores[1].wait_recv()
    small = 128
    for i in range(rows // small):
        at = slice(i * small, (i + 1) * small)
        total = part[2, at, :].astype(f32) + land_c[1, at, :].astype(f32)
        sum_y[at, :] = total.astype(bf16)
    over.start()
    lax.fori_loop(1, inner // chunk, outer_up, 0)
    turn(lambda i: a_all[pl.ds(pl.multiple_of(i * rows, rows), rows), :])

    def outer_down(j, carry):
        cols = pl.ds(pl.multiple_of(j * chunk, chunk), chunk)
        right = g_rows[:, :, cols].reshape(4 * rows, chunk)
        grad = mm(turned[...], right).astype(bf16)
        gw2[2 * j] = grad[:, :LANES]
        gw2[2 * j + 1] = grad[:, LANES:]
        return carry

    lax.fori_loop(0, width // chunk, outer_down, 0)
    cores[0].wait_recv()
    over.wait_recv()

    def norm_step(i, carry):
        at = pl.ds(pl.multiple_of(i * small, small), small)
        unit, inv = normalize(mid[at, :])
        e = (part[0, at, :].astype(f32) + land_c[0, at, :].astype(f32)) + land_y[at, :].astype(f32)
        grad = g_rows[0, at, :].astype(f32)
        value = grad + norm_back(e, gain2[...], unit, inv)
        dmid[at, :] = value
        low = value.astype(bf16)
        dbr[at, :] = low
        sums[0:1, :] += jnp.sum(e * unit, axis=0, keepdims=True)
        sums[1:2, :] += jnp.sum(e, axis=0, keepdims=True)
        sums[2:3, :] += jnp.sum(low.astype(f32), axis=0, keepdims=True)
        sums[3:4, :] += jnp.sum(grad, axis=0, keepdims=True)
        return carry

    lax.fori_loop(0, rows // small, norm_step, 0)
    spread_h.drain()
    for copy in cores + [over]:
        copy.wait_send()


def feed_call(h2, g_rows, w1, w2, b1, mid, gain2):
    rows, width = h2.shape
    inner = w1.shape[1]
    sem = pltpu.SemaphoreType.DMA
    pair = jax.ShapeDtypeStruct((2, rows, width), bf16)
    return pl.pallas_call(
        feed_body,
        out_shape=(
            pair,
            pair,
            jax.ShapeDtypeStruct((width, inner), bf16),
            jax.ShapeDtypeStruct(w2.shape, bf16),
            jax.ShapeDtypeStruct((rows, width), f32),
            jax.ShapeDtypeStruct((rows, width), bf16),
            jax.ShapeDtypeStruct((8, width), f32),
            jax.ShapeDtypeStruct((1, inner), f32),
        ),
        in_specs=[WHOLE] * 7,
        out_specs=(WHOLE,) * 8,
        scratch_shapes=[
            pltpu.VMEM((4, rows, width), bf16),
            pltpu.VMEM((4 * rows, inner), bf16),
            pltpu.VMEM((4 * rows, inner), bf16),
            pltpu.VMEM((inner, width), bf16),
            pltpu.VMEM((4, rows, width), bf16),
            pltpu.VMEM((2, rows, width), bf16),
            pltpu.VMEM((rows, width), bf16),
            pltpu.VMEM((rows, width), bf16),
            pltpu.VMEM((width, 4 * rows), bf16),
            sem((2, 4)),
            sem((2, 3)),
            sem((1,)),
        ],
        compiler_params=params(collective_id=6, has_side_effects=True),
        name="feed_forward",
    )(h2, g_rows, w1, w2, b1, mid, gain2)


def back_body(
    scal, slopes, dbr, o, wo, qkv, lse, wq, h1, gw1, gw2, y_near, y_far, mid, bias_down, x, dmid,
    gain1, mid_sums, up_sum,
    output, grad, gq_out, go_out, gw1_out, gw2_out, small_out,
    b_rows, flat, do, go_sum, go_part, bias, kt, dk_sum, dv_sum, merged, qkv_sums, h_buf, turned,
    gq_part, land_c, sum_y, land_y, y_land_c, y_sum, y_land_y,
    a_acc, a_x, a_land, a_sem, b_acc, b_x, b_land, b_sem, o_x, o_land, o_sem,
    q0_x, q0_land, q0_sem, q1_x, q1_land, q1_sem, q2_x, q2_land, q2_sem,
    small, small_land, own, seq_land,
    b_row_sem, row_sems, y_sems, h_sem, small_sems, seq_sems,
):
    dp, seq = lax.axis_index("dp"), lax.axis_index("seq")
    mate, across, far_mate = neighbours(seq)
    greet([((dp + i) % 8, seq) for i in range(1, 8)] + [(dp, p) for p in neighbours(seq)])
    rows, width = dbr.shape
    keys, inner = o.shape
    pairs = inner // LANES
    scale = HEAD_DIM**-0.5
    chunk = 128

    spread_b = Spread(dbr, b_rows, b_row_sem, dp, seq)
    spread_b.start()
    sum_a = GradSum(gw2, a_acc, a_x, a_land, a_sem, dp, seq)
    sum_b = GradSum(gw1, b_acc, b_x, b_land, b_sem, dp, seq)
    sum_o = GradSum(go_part, None, o_x, o_land, o_sem, dp, seq)
    sums_q = [
        GradSum(gq_part.at[0], None, q0_x, q0_land, q0_sem, dp, seq),
        GradSum(gq_part.at[1], None, q1_x, q1_land, q1_sem, dp, seq),
        GradSum(gq_part.at[2], None, q2_x, q2_land, q2_sem, dp, seq),
    ]
    sum_a.start()
    sum_b.start()
    y_cores = [
        remote(y_near.at[k], y_land_c.at[k], y_sems.at[0, k], y_sems.at[1, k], dp, mate)
        for k in range(2)
    ]
    y_over = remote(y_sum, y_land_y, y_sems.at[0, 2], y_sems.at[1, 2], dp, across)
    cores = [
        remote(b_rows.at[r], land_c.at[k], row_sems.at[0, k], row_sems.at[1, k], dp, mate)
        for k, r in ((0, 1), (1, 3))
    ]
    over = remote(sum_y, land_y, row_sems.at[0, 2], row_sems.at[1, 2], dp, across)

    def fetch_h(i):
        at = pl.ds(pl.multiple_of(i * rows, rows), rows)
        return pltpu.make_async_copy(h1.at[at], h_buf.at[i % 2], h_sem.at[i % 2])

    fetch_h(0).start()
    fetch_h(1).start()
    lay_columns(wo, 0, flat)
    go_sum[...] = jnp.zeros_like(go_sum)

    def out_back(r, carry):
        if r >= 2:
            spread_b.forward() if r == 2 else spread_b.last.wait_recv()
        if r == 1:
            spread_b.near.wait_recv()
        at = pl.ds(pl.multiple_of(block_at(seq, r) * rows, rows), rows)
        src = dbr if r == 0 else b_rows.at[r]
        do[at, :] = mm_t(src[...], flat[...]).astype(bf16)
        go_sum[...] += mm(o[at, :].T, src[...])
        return carry

    out_back(0, 0)
    y_cores[1].start()
    y_cores[0].start()
    out_back(1, 0)

    def turn(i, carry):
        fetch_h(i).wait()
        turned[:, pl.ds(pl.multiple_of(i * rows, rows), rows)] = h_buf[i % 2].T

        @pl.when(i < 2)
        def _():
            fetch_h(i + 2).start()

        return carry

    lax.fori_loop(0, 4, turn, 0)
    small[...] = jnp.zeros_like(small)
    for d in range(8):
        at = slice(d * LANES, (d + 1) * LANES)
        for row, src in ((4, 2), (5, 0), (6, 1), (11, 3)):
            small[d, row : row + 1, :] = mid_sums[src : src + 1, at]
    for i in range(8):
        at = slice(i * LANES, (i + 1) * LANES)
        small[pl.ds(2 * seq + i // 4, 1), 7 + i % 4, :] = up_sum[:, at]
    out_back(2, 0)
    y_cores[1].wait_recv()
    for i in range(rows // chunk):
        at = slice(i * chunk, (i + 1) * chunk)
        total = y_far[0, at, :].astype(f32) + y_land_c[1, at, :].astype(f32)
        y_sum[at, :] = total.astype(bf16)
    y_over.start()
    out_back(3, 0)
    for d in range(8):
        go_part[d] = go_sum[:, d * LANES : (d + 1) * LANES].astype(bf16)
    sum_o.start()
    sum_a.add_cross()
    sum_a.stage(0)

    def one_pair(p, carry):
        lane = pl.ds(pl.multiple_of(p * LANES, LANES), LANES)
        k_lane = pl.ds(pl.multiple_of(inner + p * LANES, LANES), LANES)
        v_lane = pl.ds(pl.multiple_of(2 * inner + p * LANES, LANES), LANES)
        pos = lax.broadcasted_iota(jnp.int32, (keys, LANES), 0)
        ramp = pos.astype(f32)
        inside = pos < scal[1]
        for h in range(2):
            bias[h] = jnp.where(inside, ramp * slopes[2 * p + h], NEG)
        kt[...] = qkv[:, k_lane].T
        dk_sum[...] = jnp.zeros_like(dk_sum)
        dv_sum[...] = jnp.zeros_like(dv_sum)
        for c in range(keys // rows):
            length = (c + 1) * rows
            at = slice(c * rows, length)
            scaled = qkv[at, lane] * bf16(scale)
            g = do[at, lane]
            both = (g.astype(f32) * o[at, lane].astype(f32)).T
            k = qkv[0:length, k_lane]
            v = qkv[0:length, v_lane]
            outs = []
            for h in range(2):
                half = slice(h * HEAD_DIM, (h + 1) * HEAD_DIM)
                qm = head_only(scaled, h)
                gm = head_only(g, h)
                dot_row = jnp.sum(both[half], axis=0, keepdims=True)
                log = lse[p, h : h + 1, at]
                e = jnp.exp(scores(k, qm, bias[h, 0:length, :]) - log)
                ds = (e * (mm_t(v, gm) - dot_row)).astype(bf16)
                dv_sum[0:length, :] += mm(e.astype(bf16), gm)
                dk_sum[0:length, :] += mm(ds, qm)
                outs.append(mm(kt[half, 0:length], ds))
            merged[at, lane] = (jnp.concatenate(outs, axis=0).T * scale).astype(bf16)
            if c == 2:

                @pl.when(p == 1)
                def _():
                    sum_a.stage(2)

        merged[:, k_lane] = dk_sum[...].astype(bf16)
        merged[:, v_lane] = dv_sum[...].astype(bf16)

        @pl.when(p == 0)
        def _():
            sum_a.stage(1)

        return carry

    lax.fori_loop(0, pairs, one_pair, 0)
    spread_b.drain()
    sum_b.add_cross()
    sum_b.stage(0)
    qkv_sums[...] = jnp.zeros_like(qkv_sums)

    def qkv_back(t, carry):
        rel = 3 - t
        at = pl.ds(pl.multiple_of(block_at(seq, rel) * rows, rows), rows)
        low = merged[at, :]
        b_rows[rel] = mm_t(low, wq[...]).astype(bf16)
        qkv_sums[...] += jnp.sum(low.astype(f32), axis=0, keepdims=True)

        @pl.when(t == 0)
        def _():
            cores[1].start()

        @pl.when(t == 1)
        def _():
            cores[1].wait_recv()
            for i in range(rows // chunk):
                at = slice(i * chunk, (i + 1) * chunk)
                total = b_rows[2, at, :].astype(f32) + land_c[1, at, :].astype(f32)
                sum_y[at, :] = total.astype(bf16)
            over.start()

        @pl.when(t == 2)
        def _():
            cores[0].start()

        return carry

    lax.fori_loop(0, 4, qkv_back, 0)
    for j in range(3):
        cols = slice(j * inner, (j + 1) * inner)
        value = mm(turned[...], merged[:, cols]).astype(bf16)
        gq_part[j] = value.reshape(8, width // 8, inner)
        sums_q[j].start()
        if j == 0:
            sum_o.add_cross()
            sum_o.stage(0)
            sum_b.stage(1)
    for i in range(2):
        at = slice(i * LANES, (i + 1) * LANES)
        small[pl.ds(seq, 1), 2 + i, :] = qkv_sums[:, at]
        at = slice((4 + i) * LANES, (5 + i) * LANES)
        small[pl.ds(4 + seq, 1), 2 + i, :] = qkv_sums[:, at]
    sum_a.finish(gw2_out)
    y_cores[0].wait_recv()
    y_over.wait_recv()

    def out_step(i, carry):
        at = pl.ds(pl.multiple_of(i * chunk, chunk), chunk)
        total = y_far[1, at, :].astype(f32) + y_land_c[0, at, :].astype(f32)
        total = total + y_land_y[at, :].astype(f32)
        output[at, :] = (mid[at, :] + (total + bias_down[...])).astype(bf16)
        return carry

    lax.fori_loop(0, rows // chunk, out_step, 0)
    sums_q[0].add_cross()
    sums_q[0].stage(0)
    sum_b.stage(2)
    sum_o.stage(1)
    cores[0].wait_recv()
    over.wait_recv()
    own[...] = jnp.zeros_like(own)
    qkv_gain = [jnp.zeros((1, width), f32), jnp.zeros((1, width), f32)]
    for i in range(rows // chunk):
        at = slice(i * chunk, (i + 1) * chunk)
        unit, inv = normalize(x[at, :].astype(f32))
        e = (b_rows[0, at, :].astype(f32) + land_c[0, at, :].astype(f32)) + land_y[
            at, :
        ].astype(f32)
        grad[at, :] = (dmid[at, :] + norm_back(e, gain1[...], unit, inv)).astype(bf16)
        qkv_gain[0] += jnp.sum(e * unit, axis=0, keepdims=True)
        qkv_gain[1] += jnp.sum(e, axis=0, keepdims=True)
    for d in range(8):
        at = slice(d * LANES, (d + 1) * LANES)
        small[d, 0:1, :] = qkv_gain[0][:, at]
        small[d, 1:2, :] = qkv_gain[1][:, at]

    def small_to(i):
        peer = (dp + i) % 8
        return remote(
            small.at[peer], small_land.at[i], small_sems.at[0, i], small_sems.at[1, i], peer, seq
        )

    for i in range(1, 8):
        small_to(i).start()
    sums_q[1].add_cross()
    sums_q[1].stage(0)
    sums_q[0].stage(1)
    sum_o.stage(2)
    sums_q[2].add_cross()
    sums_q[2].stage(0)
    sums_q[1].stage(1)
    sums_q[0].stage(2)
    total = small[dp]
    for i in range(1, 8):
        small_to(i).wait_recv()
        total = total + small_land[i]
    own[...] = total

    def seq_to(i, peer):
        return remote(own, seq_land.at[i], seq_sems.at[0, i], seq_sems.at[1, i], dp, peer)

    group = [seq_to(i, peer) for i, peer in enumerate(neighbours(seq))]
    for copy in group:
        copy.start()
    sums_q[2].stage(1)
    sums_q[1].stage(2)
    sums_q[2].stage(2)
    sum_b.finish(gw1_out)
    sum_o.finish(go_out)
    for copy in group:
        copy.wait_recv()
    small_out[...] = (own[...] + seq_land[0]) + (seq_land[1] + seq_land[2])
    for j in range(3):
        sums_q[j].finish(gq_out.at[:, j * inner : (j + 1) * inner])
    for copy in group + cores + y_cores + [over, y_over]:
        copy.wait_send()
    for i in range(1, 8):
        small_to(i).wait_send()
    for part in [sum_a, sum_b, sum_o] + sums_q:
        part.drain()


def back_call(*args):
    dbr, o, wo, qkv, lse, wq, h1, gw1, gw2 = args[2:11]
    rows, width = dbr.shape
    keys, inner = o.shape
    sem = pltpu.SemaphoreType.DMA
    block = lambda dtype: pltpu.VMEM((rows, width), dtype)
    pair_rows = pltpu.VMEM((2, rows, width), bf16)
    any_space = pl.BlockSpec(memory_space=pl.ANY)
    specs = [SCALAR, SCALAR] + [WHOLE] * (len(args) - 2)
    for at in (8, 9, 10, 11):
        specs[at] = any_space
    shape = jax.ShapeDtypeStruct
    return pl.pallas_call(
        back_body,
        out_shape=(
            shape((rows, width), bf16),
            shape((rows, width), bf16),
            shape((width // 8, 3 * inner), f32),
            shape((inner, LANES), f32),
            shape(gw1.shape[1:], f32),
            shape(gw2.shape[1:], f32),
            shape((SMALL_ROWS, LANES), f32),
        ),
        in_specs=specs,
        out_specs=(WHOLE,) * 7,
        scratch_shapes=[
            pltpu.VMEM((4, rows, width), bf16),
            pltpu.VMEM((inner, width), bf16),
            pltpu.VMEM((keys, inner), bf16),
            pltpu.VMEM((inner, width), f32),
            pltpu.VMEM((8, inner, LANES), bf16),
            pltpu.VMEM((2, keys, LANES), f32),
            pltpu.VMEM((LANES, keys), bf16),
            pltpu.VMEM((keys, LANES), f32),
            pltpu.VMEM((keys, LANES), f32),
            pltpu.VMEM((keys, 3 * inner), bf16),
            pltpu.VMEM((1, 3 * inner), f32),
            pair_rows,
            pltpu.VMEM((width, keys), bf16),
            pltpu.VMEM((3, 8, width // 8, inner), bf16),
            pair_rows, block(bf16), block(bf16),
            pair_rows, block(bf16), block(bf16),
            *GradSum.scratch(*gw2.shape[1:], fetched=True),
            *GradSum.scratch(*gw1.shape[1:], fetched=True),
            *GradSum.scratch(inner, LANES),
            *(GradSum.scratch(width // 8, inner) * 3),
            pltpu.VMEM((8, SMALL_ROWS, LANES), f32),
            pltpu.VMEM((8, SMALL_ROWS, LANES), f32),
            pltpu.VMEM((SMALL_ROWS, LANES), f32),
            pltpu.VMEM((3, SMALL_ROWS, LANES), f32),
            sem((2, 4)), sem((2, 3)), sem((2, 3)), sem((2,)), sem((2, 8)), sem((2, 3)),
        ],
        compiler_params=pltpu.CompilerParams(
            vmem_limit_bytes=67043328, collective_id=3, has_side_effects=True
        ),
        name="back",
    )(*args)


def finish_body(
    scal, output, grad, gq, go, gw1, gw2, small,
    output_out, grad_out, gq_out, go_out, gw1_out, gw2_out,
    gain1, shift1, qv, bout, gain2, shift2, up, down,
):
    seq = scal[0]
    output_out[...] = output[...]
    grad_out[...] = grad[...]
    go_out[...] = go[...]
    gw1_out[...] = gw1[...]
    gw2_out[...] = gw2[...]
    cols = gq_out.shape[2]
    for c in range(3):
        gq_out[:, c, :] = gq[:, c * cols : (c + 1) * cols]
    for ref, row in ((gain1, 0), (shift1, 1), (bout, 4), (gain2, 5), (shift2, 6), (down, 11)):
        n = ref.shape[1]
        value = small[row : row + 1, 0:n]
        for i in range(1, 4):
            value = jnp.where(seq == i, small[row : row + 1, i * n : (i + 1) * n], value)
        ref[...] = value
    value = small[2:3, 0:64]
    for i in range(1, 4):
        at = 64 * (i % 2)
        value = jnp.where(seq == i, small[2 + i // 2 : 3 + i // 2, at : at + 64], value)
    qv[...] = value
    up[...] = small[pl.ds(7 + seq, 1), :]


def finish_call(scal, output, grad, gq, go, gw1, gw2, small):
    one = lambda n: jax.ShapeDtypeStruct((1, n), f32)
    like = lambda v: jax.ShapeDtypeStruct(v.shape, v.dtype)
    return pl.pallas_call(
        finish_body,
        out_shape=(
            like(output), like(grad),
            jax.ShapeDtypeStruct((gq.shape[0], 3, gq.shape[1] // 3), f32),
            like(go), like(gw1), like(gw2),
            one(32), one(32), one(64), one(32), one(32), one(32), one(LANES), one(32),
        ),
        in_specs=[SCALAR] + [WHOLE] * 7,
        out_specs=(WHOLE,) * 14,
        compiler_params=params(),
        name="finish",
    )(scal, output, grad, gq, go, gw1, gw2, small)


def after(value, *others):
    return lax.optimization_barrier((value, *others))[0]


def on_device(
    dp_n,
    seq_n,
    tokens,
    lengths,
    cotangent,
    ln1_gain,
    ln1_shift,
    w_qkv,
    b_qv,
    w_out,
    b_out,
    ln2_gain,
    ln2_shift,
    w_fc1,
    b_fc1,
    w_fc2,
    b_fc2,
):
    count = dp_n * seq_n
    rows, width = tokens.shape
    heads = width // HEAD_DIM
    inner = w_out.shape[0]
    ff = w_fc1.shape[1]
    s = lax.axis_index("seq")
    length = lengths[0]

    scal = jnp.stack([s.astype(jnp.int32), length])
    slopes = 2.0 ** (-8.0 * (jnp.arange(heads, dtype=jnp.int32) + 1).astype(f32) / heads)
    slopes = lax.dynamic_slice(slopes, (s * (heads // seq_n),), (heads // seq_n,))
    valid = s * rows + jnp.arange(rows, dtype=jnp.int32) < length
    grad_low = jnp.where(valid[:, None], cotangent, jnp.zeros_like(cotangent))
    wq_own = jnp.concatenate([w_qkv[:, c, :] for c in range(3)], axis=1)
    small = (ln1_gain, ln1_shift, b_qv, b_out, ln2_gain, ln2_shift, b_fc1, b_fc2)
    sizes = [v.shape[0] for v in small]
    ends = [sum(sizes[: i + 1]) for i in range(len(sizes))]
    block = 384
    fast = dp_n == 8 and seq_n == 4 and width == 8 * LANES and ff == width and inner == 2 * LANES
    if fast:
        parts = dp_n
        order = (b_fc1, b_qv, ln1_gain, ln1_shift, b_out, ln2_gain, ln2_shift, b_fc2)
        wq, w_o, x_rows, gain1, shift1, qkv_bias, bias_out, gain2, shift2, own_up, bias_down = (
            front_call(wq_own, w_out, tokens, order)
        )
        wq = wq.reshape(width, 3 * inner)
        h1, qkv, o, lse, mid, h2, g_rows, w1, w_cols = attention_call(
            scal, slopes, x_rows, grad_low, wq, w_o, w_fc1, w_fc2,
            gain1, shift1, qkv_bias, bias_out, gain2, shift2,
        )
        y_near, y_far, grad_up, grad_down, dmid, dbr, mid_sums, up_sum = feed_call(
            h2, g_rows, w1.reshape(width, ff), w_cols, own_up, mid, gain2
        )
        results = back_call(
            scal, slopes, dbr, o, w_o, qkv, lse, wq, h1, grad_up.reshape(8, -1, ff), grad_down,
            y_near, y_far, mid, bias_down, tokens, dmid, gain1, mid_sums, up_sum,
        )
        output, grad_tokens, grad_qkv, grad_out, grad_up, grad_down, *vectors = finish_call(
            scal, *results
        )
        g_gain1, g_shift1, g_qv, g_bout, g_gain2, g_shift2, g_up, g_down = (
            v.reshape(n) for v, n in zip(vectors, sizes)
        )
        return (
            output, grad_tokens, g_gain1, g_shift1, grad_qkv, g_qv, grad_out, g_bout,
            g_gain2, g_shift2, grad_up, g_up, grad_down, g_down,
        )

    wq = lax.all_gather(wq_own, "dp", axis=0, tiled=True)
    col = w_fc2.shape[1]
    both = jnp.concatenate([w_fc2, w_out], axis=0)
    if col % LANES == 0:
        parts = dp_n
        w_cols = lax.all_gather(both, "dp", axis=0, tiled=False)
    else:
        parts = 1
        w_cols = lax.all_gather(both, "dp", axis=1, tiled=True)[None]
    w_o = w_cols
    out_first = ff
    w1 = lax.all_gather(w_fc1, "dp", axis=0, tiled=True)
    packed = small_gather(jnp.concatenate([v.astype(f32) for v in small]), count, seq_n)
    packed = packed.reshape(count, ends[-1])
    gain1, shift1, bias_qv, bias_out, gain2, shift2, bias_up, bias_down = (
        packed[:, e - n : e].reshape(1, count * n) for e, n in zip(ends, sizes)
    )
    own_bias = lambda v, n: lax.dynamic_slice(v, (0, s * n), (1, n))
    own_up = own_bias(bias_up, ff)
    qkv_bias = jnp.concatenate(
        [
            own_bias(bias_qv[:, :width], inner),
            jnp.zeros((1, inner), f32),
            own_bias(bias_qv[:, width:], inner),
        ],
        axis=1,
    )
    x_pieces = spread(tokens)
    g_rows = jnp.stack(spread(after(grad_low, x_pieces[3])))
    h1, qkv = qkv_call(scal, x_pieces, wq, gain1, shift1, qkv_bias)
    o, lse = attend_call(scal, slopes, qkv, block)
    near, far = out_call(scal, o, w_o, out_first)
    got, across = reduce_rows(near, far)
    mid, h2 = mid_call(tokens, far, got, across, bias_out, gain2, shift2)
    h_pieces = spread(h2)
    y_near, y_far, d_near, d_far, a_all, du_all, h_all, g_all, up_sum = mlp_call(
        h_pieces, g_rows, w1, w_cols, own_up
    )
    got, across = reduce_rows(d_near, d_far)
    grad_down = outer_call(a_all, g_all, parts, "grad_fc2")
    grad_up = outer_call(h_all, du_all, 1, "grad_fc1")
    dmid, dbr, mid_sums = mid_back_call(mid, d_far, got, across, grad_low, gain2)

    b_pieces = spread(dbr)

    y_near = after(y_near, b_pieces[3])
    got, across = reduce_rows(y_near, y_far)
    output = (
        mid + ((y_far[1].astype(f32) + got[0].astype(f32)) + across.astype(f32) + bias_down)
    ).astype(bf16)

    do, grad_out = out_back_call(scal, b_pieces, o, w_o, out_first)
    dq, dk, dv = attend_back_call(scal, slopes, qkv, o, do, lse, block)
    near, far, merged, qkv_sums = qkv_back_call(scal, dq, dk, dv, wq)
    grad_qkv = outer_call(h1, merged, 1, "grad_qkv")

    def shared(part):
        if parts > 1:
            return lax.psum_scatter(part, "dp", scatter_dimension=0, tiled=False).astype(f32)
        return lax.psum_scatter(part, "dp", scatter_dimension=1, tiled=True).astype(f32)

    grad_down = shared(grad_down if parts > 1 else grad_down)
    grad_up = lax.psum_scatter(grad_up, "dp", scatter_dimension=0, tiled=True).astype(f32)
    got, across = reduce_rows(near, far)
    grad_tokens, in_sums = in_back_call(tokens, far, got, across, dmid, gain1)
    grad_out = shared(grad_out if parts > 1 else grad_out[0])
    grad_qkv = lax.psum_scatter(grad_qkv, "dp", scatter_dimension=0, tiled=True)
    grad_qkv = grad_qkv.astype(f32).reshape(w_qkv.shape)

    def own_slot(v, total):
        return lax.dynamic_update_slice(jnp.zeros((1, total), f32), v, (0, s * v.shape[1]))

    sums = (
        in_sums[0:1],
        in_sums[1:2],
        jnp.concatenate(
            [own_slot(qkv_sums[:, :inner], width), own_slot(qkv_sums[:, 2 * inner :], width)], axis=1
        ),
        mid_sums[2:3],
        mid_sums[0:1],
        mid_sums[1:2],
        own_slot(up_sum, seq_n * ff),
        mid_sums[3:4],
    )
    grads = jnp.concatenate([v.reshape(count, n) for v, n in zip(sums, sizes)], axis=1)
    grads = small_scatter(grads, count, seq_n).reshape(ends[-1])
    g_gain1, g_shift1, g_qv, g_bout, g_gain2, g_shift2, g_up, g_down = (
        grads[e - n : e] for e, n in zip(ends, sizes)
    )
    return (
        output,
        grad_tokens,
        g_gain1,
        g_shift1,
        grad_qkv,
        g_qv,
        grad_out,
        g_bout,
        g_gain2,
        g_shift2,
        grad_up,
        g_up,
        grad_down,
        g_down,
    )


def solution(mesh):
    rows = P(("dp", "seq"), None)
    vec = P(("dp", "seq"))
    merged = P("dp", None, "seq")
    return jax.shard_map(
        functools.partial(on_device, mesh.shape["dp"], mesh.shape["seq"]),
        mesh=mesh,
        in_specs=(
            rows, P("dp"), rows, vec, vec, merged, vec, P("seq", "dp"), vec, vec, vec,
            P("dp", "seq"), vec, P("seq", "dp"), vec,
        ),
        out_specs=(
            rows, rows, vec, vec, merged, vec, P("seq", "dp"), vec, vec, vec,
            P("dp", "seq"), vec, P("seq", "dp"), vec,
        ),
        check_vma=False,
    )
```

```python
import functools
import math

import jax
import jax.numpy as jnp
from jax import lax
from jax.experimental import pallas as pl
from jax.experimental.pallas import tpu as pltpu
from jax.sharding import PartitionSpec as P

HEAD_DIM = 64
EPS = 1e-05
GELU_COEF = 0.044715
NEG = -1e30
LANES = 128
VMEM_BYTES = 60 * 1024 * 1024

f32 = jnp.float32
bf16 = jnp.bfloat16
WHOLE = pl.BlockSpec(memory_space=pltpu.VMEM)
SCALAR = pl.BlockSpec(memory_space=pltpu.SMEM)


def mm(a, b):
    return jnp.dot(a, b, preferred_element_type=f32)


def mm_t(a, b):
    return lax.dot_general(a, b, (((1,), (1,)), ((), ())), preferred_element_type=f32)


def params(**kw):
    return pltpu.CompilerParams(vmem_limit_bytes=VMEM_BYTES, **kw)


def normalize(v):
    width = v.shape[-1]
    centred = v - jnp.sum(v, axis=-1, keepdims=True) * (1.0 / width)
    inv = lax.rsqrt(jnp.sum(centred * centred, axis=-1, keepdims=True) * (1.0 / width) + EPS)
    return centred * inv, inv


def norm_back(grad_out, gain, unit, inv):
    width = unit.shape[-1]
    scaled = grad_out * gain
    mean_one = jnp.sum(scaled, axis=-1, keepdims=True) * (1.0 / width)
    mean_two = jnp.sum(scaled * unit, axis=-1, keepdims=True) * (1.0 / width)
    return inv * (scaled - mean_one - unit * mean_two)


def device_of(index, seq_n):
    return (index // seq_n, index % seq_n)


def greet_all(me, count, seq_n):
    barrier = pltpu.get_barrier_semaphore()

    def hello(i, carry):
        peer = (me + i) % count
        pl.semaphore_signal(
            barrier, inc=1, device_id=device_of(peer, seq_n), device_id_type=pl.DeviceIdType.MESH
        )
        return carry

    lax.fori_loop(1, count, hello, 0)
    pl.semaphore_wait(barrier, count - 1)


def small_gather_body(count, seq_n, x_ref, out_ref, send_sem, recv_sem):
    me = lax.axis_index("dp") * seq_n + lax.axis_index("seq")
    greet_all(me, count, seq_n)

    def copy_to(i):
        peer = (me + i) % count
        return pltpu.make_async_remote_copy(
            src_ref=x_ref,
            dst_ref=out_ref.at[pl.ds(me, 1)],
            send_sem=send_sem.at[i],
            recv_sem=recv_sem.at[i],
            device_id=device_of(peer, seq_n),
            device_id_type=pl.DeviceIdType.MESH,
        )

    def begin(i, carry):
        copy_to(i).start()
        return carry

    def finish(i, carry):
        copy_to(i).wait()
        return carry

    lax.fori_loop(1, count, begin, 0)
    out_ref[pl.ds(me, 1)] = x_ref[...]
    lax.fori_loop(1, count, finish, 0)


def small_gather(x, count, seq_n):
    width = x.shape[-1]
    return pl.pallas_call(
        functools.partial(small_gather_body, count, seq_n),
        out_shape=jax.ShapeDtypeStruct((count, 1, width), f32),
        in_specs=[WHOLE],
        out_specs=WHOLE,
        scratch_shapes=[pltpu.SemaphoreType.DMA((count,)), pltpu.SemaphoreType.DMA((count,))],
        compiler_params=pltpu.CompilerParams(collective_id=1, has_side_effects=True),
        name="small_gather",
    )(x.reshape(1, 1, width))


def small_scatter_body(count, seq_n, v_ref, out_ref, land, send_sem, recv_sem):
    me = lax.axis_index("dp") * seq_n + lax.axis_index("seq")
    greet_all(me, count, seq_n)

    def copy_to(i):
        peer = (me + i) % count
        return pltpu.make_async_remote_copy(
            src_ref=v_ref.at[pl.ds(peer, 1)],
            dst_ref=land.at[pl.ds(i, 1)],
            send_sem=send_sem.at[i],
            recv_sem=recv_sem.at[i],
            device_id=device_of(peer, seq_n),
            device_id_type=pl.DeviceIdType.MESH,
        )

    def begin(i, carry):
        copy_to(i).start()
        return carry

    def finish(i, total):
        copy_to(i).wait()
        return total + land[pl.ds(i, 1)]

    lax.fori_loop(1, count, begin, 0)
    out_ref[...] = lax.fori_loop(1, count, finish, v_ref[pl.ds(me, 1)])


def small_scatter(v, count, seq_n):
    width = v.shape[-1]
    return pl.pallas_call(
        functools.partial(small_scatter_body, count, seq_n),
        out_shape=jax.ShapeDtypeStruct((1, 1, width), f32),
        in_specs=[WHOLE],
        out_specs=WHOLE,
        scratch_shapes=[
            pltpu.VMEM((count, 1, width), f32),
            pltpu.SemaphoreType.DMA((count,)),
            pltpu.SemaphoreType.DMA((count,)),
        ],
        compiler_params=pltpu.CompilerParams(collective_id=2, has_side_effects=True),
        name="small_scatter",
    )(v.reshape(count, 1, width))


def swap(x, bit):
    return lax.ppermute(x, "seq", [(i, i ^ bit) for i in range(4)])


def spread(own):
    far = swap(own, 2)
    return own, swap(own, 1), far, swap(far, 1)


def reduce_rows(near, far):
    got = swap(near, 1)
    across = swap(far[0] + got[1], 2)
    return got, across


def pick(step, refs, dest):
    for k, ref in enumerate(refs):

        @pl.when(step == k)
        def _(ref=ref):
            dest[...] = ref[...]


ORDER = (1, 3, 2, 0)


def rel_of(t):
    return jnp.where(t == 0, 1, jnp.where(t == 1, 3, jnp.where(t == 2, 2, 0)))


def qkv_body(scal, x0, x1, x2, x3, w, gain, shift, bias, h1, qkv, rows):
    pick(pl.program_id(0), (x0, x1, x2, x3), rows)
    unit, _ = normalize(rows[...].astype(f32))
    low = (unit * gain[...] + shift[...]).astype(bf16)
    h1[...] = low
    qkv[...] = (mm(low, w[...]) + bias[...]).astype(bf16)


def qkv_call(scal, pieces, w, gain, shift, bias):
    rows, width = pieces[0].shape
    cols = w.shape[1]
    out = lambda r, sc: (lax.bitwise_xor(sc[0], r), 0)
    return pl.pallas_call(
        qkv_body,
        out_shape=(
            jax.ShapeDtypeStruct((4 * rows, width), bf16),
            jax.ShapeDtypeStruct((4 * rows, cols), bf16),
        ),
        grid_spec=pltpu.PrefetchScalarGridSpec(
            num_scalar_prefetch=1,
            grid=(4,),
            in_specs=[WHOLE] * 8,
            out_specs=(pl.BlockSpec((rows, width), out), pl.BlockSpec((rows, cols), out)),
            scratch_shapes=[pltpu.VMEM((rows, width), bf16)],
        ),
        compiler_params=params(),
        name="qkv",
    )(scal, *pieces, w, gain, shift, bias)


def make_bias(scal, slopes, pair, bias, keys):
    pos = lax.broadcasted_iota(jnp.int32, (keys, LANES), 0)
    inside = pos < scal[1]
    ramp = pos.astype(f32)
    for h in range(2):
        bias[h] = jnp.where(inside, ramp * slopes[2 * pair + h], NEG)


def head_only(x, h):
    lane = lax.broadcasted_iota(jnp.int32, x.shape, 1)
    return jnp.where((lane >= h * HEAD_DIM) & (lane < (h + 1) * HEAD_DIM), x, jnp.zeros_like(x))


def score_t(k_ref, qm, bias, h, length):
    block = qm.shape[0]
    s = mm_t(k_ref[0:length, :], qm)
    b = bias[h, 0:length, :]
    s = s + jnp.concatenate([b] * (block // LANES), axis=1)
    key = lax.broadcasted_iota(jnp.int32, (block, block), 0)
    query = lax.broadcasted_iota(jnp.int32, (block, block), 1)
    last = jnp.where(key <= query, s[length - block :], NEG)
    if length == block:
        return last
    return jnp.concatenate([s[: length - block], last], axis=0)


def attend_body(scal, q, k, v, slopes, o, lse, bias, vt):
    pair, step = pl.program_id(0), pl.program_id(1)
    block = q.shape[0]
    keys = k.shape[0]

    @pl.when(step == 0)
    def _():
        make_bias(scal, slopes, pair, bias, keys)
        vt[...] = v[...].T

    for c in range(keys // block):

        @pl.when(step == c)
        def _(c=c):
            length = (c + 1) * block
            scaled = q[...] * bf16(HEAD_DIM**-0.5)
            outs, logs = [], []
            for h in range(2):
                s = score_t(k, head_only(scaled, h), bias, h, length)
                top = jnp.max(s, axis=0, keepdims=True)
                e = jnp.exp(s - top)
                total = jnp.sum(e, axis=0, keepdims=True)
                mixed = mm(vt[h * HEAD_DIM : (h + 1) * HEAD_DIM, 0:length], e.astype(bf16))
                outs.append(mixed / total)
                logs.append(top + jnp.log(total))
            o[...] = jnp.concatenate(outs, axis=0).T.astype(bf16)
            lse[0, 0:2, :] = jnp.concatenate(logs, axis=0)


def attend_call(scal, slopes, qkv, block):
    keys, cols = qkv.shape
    width = cols // 3
    pairs = width // LANES
    return pl.pallas_call(
        attend_body,
        out_shape=(
            jax.ShapeDtypeStruct((keys, width), bf16),
            jax.ShapeDtypeStruct((pairs, 8, keys), f32),
        ),
        grid_spec=pltpu.PrefetchScalarGridSpec(
            num_scalar_prefetch=1,
            grid=(pairs, keys // block),
            in_specs=[
                pl.BlockSpec((block, LANES), lambda p, c, sc: (c, p)),
                pl.BlockSpec((keys, LANES), lambda p, c, sc: (0, pairs + p)),
                pl.BlockSpec((keys, LANES), lambda p, c, sc: (0, 2 * pairs + p)),
                SCALAR,
            ],
            out_specs=(
                pl.BlockSpec((block, LANES), lambda p, c, sc: (c, p)),
                pl.BlockSpec((1, 8, block), lambda p, c, sc: (p, 0, c)),
            ),
            scratch_shapes=[
                pltpu.VMEM((2, keys, LANES), f32),
                pltpu.VMEM((LANES, keys), bf16),
            ],
        ),
        compiler_params=params(),
        name="attend",
    )(scal, qkv, qkv, qkv, slopes)


def attend_back_body(scal, q, k, v, o, do, lse, slopes, dq, dk, dv, bias, kt, dk_sum, dv_sum):
    pair, step = pl.program_id(0), pl.program_id(1)
    block = q.shape[0]
    keys = k.shape[0]
    scale = HEAD_DIM**-0.5

    @pl.when(step == 0)
    def _():
        make_bias(scal, slopes, pair, bias, keys)
        kt[...] = k[...].T
        dk_sum[...] = jnp.zeros_like(dk_sum)
        dv_sum[...] = jnp.zeros_like(dv_sum)

    for c in range(keys // block):

        @pl.when(step == c)
        def _(c=c):
            length = (c + 1) * block
            scaled = q[...] * bf16(scale)
            both = (do[...].astype(f32) * o[...].astype(f32)).T
            outs = []
            for h in range(2):
                qm = head_only(scaled, h)
                dom = head_only(do[...], h)
                dot_row = jnp.sum(both[h * HEAD_DIM : (h + 1) * HEAD_DIM], axis=0, keepdims=True)
                p = jnp.exp(score_t(k, qm, bias, h, length) - lse[0, h : h + 1, :])
                dp = mm_t(v[0:length, :], dom)
                ds = (p * (dp - dot_row)).astype(bf16)
                dv_sum[0:length, :] += mm(p.astype(bf16), dom)
                dk_sum[0:length, :] += mm(ds, qm)
                outs.append(mm(kt[h * HEAD_DIM : (h + 1) * HEAD_DIM, 0:length], ds))
            dq[...] = (jnp.concatenate(outs, axis=0).T * scale).astype(bf16)

    @pl.when(step == keys // block - 1)
    def _():
        dk[...] = dk_sum[...].astype(bf16)
        dv[...] = dv_sum[...].astype(bf16)


def attend_back_call(scal, slopes, qkv, o, do, lse, block):
    keys, cols = qkv.shape
    width = cols // 3
    pairs = width // LANES
    some = pl.BlockSpec((block, LANES), lambda p, c, sc: (c, p))
    full = pl.BlockSpec((keys, LANES), lambda p, c, sc: (0, p))
    return pl.pallas_call(
        attend_back_body,
        out_shape=(jax.ShapeDtypeStruct((keys, width), bf16),) * 3,
        grid_spec=pltpu.PrefetchScalarGridSpec(
            num_scalar_prefetch=1,
            grid=(pairs, keys // block),
            in_specs=[
                some,
                pl.BlockSpec((keys, LANES), lambda p, c, sc: (0, pairs + p)),
                pl.BlockSpec((keys, LANES), lambda p, c, sc: (0, 2 * pairs + p)),
                some,
                some,
                pl.BlockSpec((1, 8, block), lambda p, c, sc: (p, 0, c)),
                SCALAR,
            ],
            out_specs=(some, full, full),
            scratch_shapes=[
                pltpu.VMEM((2, keys, LANES), f32),
                pltpu.VMEM((LANES, keys), bf16),
                pltpu.VMEM((keys, LANES), f32),
                pltpu.VMEM((keys, LANES), f32),
            ],
        ),
        compiler_params=params(),
        name="attend_back",
    )(scal, qkv, qkv, qkv, o, do, lse, slopes)


def lay_columns(w_ref, first, dest):
    width = w_ref.shape[2]
    for d in range(w_ref.shape[0]):
        dest[:, d * width : (d + 1) * width] = w_ref[d, first : first + dest.shape[0], :]


def out_body(scal, o, w, near, far, flat, *, first):
    t = pl.program_id(0)

    @pl.when(t == 0)
    def _():
        lay_columns(w, first, flat)

    part = mm(o[...], flat[...]).astype(bf16)

    @pl.when(t < 2)
    def _():
        near[0] = part

    @pl.when(t >= 2)
    def _():
        far[0] = part


def near_map(t, *_):
    return (jnp.minimum(t, 1), 0, 0)


def far_map(t, *_):
    return (jnp.maximum(t - 2, 0), 0, 0)


def out_call(scal, o, w, first):
    keys, inner = o.shape
    rows = keys // 4
    width = w.shape[0] * w.shape[2]
    return pl.pallas_call(
        functools.partial(out_body, first=first),
        out_shape=(jax.ShapeDtypeStruct((2, rows, width), bf16),) * 2,
        grid_spec=pltpu.PrefetchScalarGridSpec(
            num_scalar_prefetch=1,
            grid=(4,),
            in_specs=[
                pl.BlockSpec((rows, inner), lambda t, sc: (lax.bitwise_xor(sc[0], rel_of(t)), 0)),
                WHOLE,
            ],
            out_specs=(
                pl.BlockSpec((1, rows, width), near_map),
                pl.BlockSpec((1, rows, width), far_map),
            ),
            scratch_shapes=[pltpu.VMEM((inner, width), bf16)],
        ),
        compiler_params=params(),
        name="out_proj",
    )(scal, o, w)


def mid_body(x, a, b, c, bias, gain, shift, mid, h2):
    value = x[...].astype(f32) + (
        (a[0].astype(f32) + b[0].astype(f32)) + c[...].astype(f32) + bias[...]
    )
    mid[...] = value
    unit, _ = normalize(value)
    h2[...] = (unit * gain[...] + shift[...]).astype(bf16)


def mid_call(x, a, b, c, bias, gain, shift):
    rows, width = x.shape
    one = pl.BlockSpec((rows // 2, width), lambda i: (i, 0))
    first = pl.BlockSpec((1, rows // 2, width), lambda i: (0, i, 0))
    second = pl.BlockSpec((1, rows // 2, width), lambda i: (1, i, 0))
    row = pl.BlockSpec((1, width), lambda i: (0, 0))
    return pl.pallas_call(
        mid_body,
        out_shape=(
            jax.ShapeDtypeStruct((rows, width), f32),
            jax.ShapeDtypeStruct((rows, width), bf16),
        ),
        grid=(2,),
        in_specs=[one, second, first, one, row, row, row],
        out_specs=(one, one),
        compiler_params=params(),
        name="mid_norm",
    )(x, a, b, c, bias, gain, shift)


def gelu_parts(u):
    root = math.sqrt(2.0 / math.pi)
    sq = u * u
    t = jnp.tanh(root * (u + GELU_COEF * (sq * u)))
    half = 0.5 * (1.0 + t)
    slope = half + 0.5 * u * (1.0 - t * t) * (root * (1.0 + 3.0 * GELU_COEF * sq))
    return u * half, slope


def mlp_body(
    h0, h1, h2, h3, g_rows, w1, w2, b1,
    y_near, y_far, d_near, d_far, a_all, du_all, h_all, g_all, bias_sum,
    flat, hb, gb,
):
    t = pl.program_id(0)

    @pl.when(t == 0)
    def _():
        lay_columns(w2, 0, flat)
        bias_sum[...] = jnp.zeros_like(bias_sum)

    pick(rel_of(t), (h0, h1, h2, h3), hb)
    gb[...] = g_rows[rel_of(t)]
    h_all[...] = hb[...]
    g_all[...] = gb[...]
    inner = w1.shape[1]
    chunk = 256
    for c in range(inner // chunk):
        cols = slice(c * chunk, (c + 1) * chunk)
        u = mm(hb[...], w1[:, cols]) + b1[:, cols]
        value, slope = gelu_parts(u)
        a_all[:, cols] = value.astype(bf16)
        du = (mm_t(gb[...], flat[cols, :]) * slope).astype(bf16)
        du_all[:, cols] = du
        bias_sum[:, cols] += jnp.sum(du.astype(f32), axis=0, keepdims=True)
    y = mm(a_all[...], flat[...]).astype(bf16)
    d = mm_t(du_all[...], w1[...]).astype(bf16)

    @pl.when(t < 2)
    def _():
        y_near[0] = y
        d_near[0] = d

    @pl.when(t >= 2)
    def _():
        y_far[0] = y
        d_far[0] = d


def mlp_call(h_pieces, g_rows, w1, w2, b1):
    rows, width = h_pieces[0].shape
    inner = w1.shape[1]
    pair = jax.ShapeDtypeStruct((2, rows, width), bf16)
    near = pl.BlockSpec((1, rows, width), near_map)
    far = pl.BlockSpec((1, rows, width), far_map)
    block = lambda n: pl.BlockSpec((rows, n), lambda t: (t, 0))
    return pl.pallas_call(
        mlp_body,
        out_shape=(
            pair,
            pair,
            pair,
            pair,
            jax.ShapeDtypeStruct((4 * rows, inner), bf16),
            jax.ShapeDtypeStruct((4 * rows, inner), bf16),
            jax.ShapeDtypeStruct((4 * rows, width), bf16),
            jax.ShapeDtypeStruct((4 * rows, width), bf16),
            jax.ShapeDtypeStruct((1, inner), f32),
        ),
        grid=(4,),
        in_specs=[WHOLE] * 8,
        out_specs=(
            near, far, near, far, block(inner), block(inner), block(width), block(width),
            pl.BlockSpec((1, inner), lambda t: (0, 0)),
        ),
        scratch_shapes=[
            pltpu.VMEM((inner, width), bf16),
            pltpu.VMEM((rows, width), bf16),
            pltpu.VMEM((rows, width), bf16),
        ],
        compiler_params=params(),
        name="mlp",
    )(*h_pieces, g_rows, w1, w2, b1)


def outer_body(left, right, out, turned, *, blocks):
    @pl.when(pl.program_id(0) == 0)
    def _():
        turned[...] = left[...].T

    part = mm(turned[...], right[...]).astype(bf16)
    if blocks:
        width = out.shape[2]
        for d in range(out.shape[0]):
            out[d] = part[:, d * width : (d + 1) * width]
    else:
        out[...] = part


def outer_call(left, right, parts, name):
    rows, m = left.shape
    n = right.shape[1]
    step = 256
    if parts > 1:
        width = n // parts
        out_shape = jax.ShapeDtypeStruct((parts, m, width), bf16)
        out_spec = pl.BlockSpec((step // width, m, width), lambda j: (j, 0, 0))
    else:
        out_shape = jax.ShapeDtypeStruct((m, n), bf16)
        out_spec = pl.BlockSpec((m, step), lambda j: (0, j))
    return pl.pallas_call(
        functools.partial(outer_body, blocks=parts > 1),
        out_shape=out_shape,
        grid=(n // step,),
        in_specs=[WHOLE, pl.BlockSpec((rows, step), lambda j: (0, j))],
        out_specs=out_spec,
        scratch_shapes=[pltpu.VMEM((m, rows), bf16)],
        compiler_params=params(),
        name=name,
    )(left, right)


def mid_back_body(mid, a, b, c, g, gain, dmid, dbr, sums):
    @pl.when(pl.program_id(0) == 0)
    def _():
        sums[...] = jnp.zeros_like(sums)

    unit, inv = normalize(mid[...])
    e = (a[0].astype(f32) + b[0].astype(f32)) + c[...].astype(f32)
    grad = g[...].astype(f32)
    value = grad + norm_back(e, gain[...], unit, inv)
    dmid[...] = value
    low = value.astype(bf16)
    dbr[...] = low
    sums[0:1, :] += jnp.sum(e * unit, axis=0, keepdims=True)
    sums[1:2, :] += jnp.sum(e, axis=0, keepdims=True)
    sums[2:3, :] += jnp.sum(low.astype(f32), axis=0, keepdims=True)
    sums[3:4, :] += jnp.sum(grad, axis=0, keepdims=True)


def mid_back_call(mid, a, b, c, g, gain):
    rows, width = mid.shape
    one = pl.BlockSpec((rows // 2, width), lambda i: (i, 0))
    first = pl.BlockSpec((1, rows // 2, width), lambda i: (0, i, 0))
    second = pl.BlockSpec((1, rows // 2, width), lambda i: (1, i, 0))
    row = pl.BlockSpec((1, width), lambda i: (0, 0))
    return pl.pallas_call(
        mid_back_body,
        out_shape=(
            jax.ShapeDtypeStruct((rows, width), f32),
            jax.ShapeDtypeStruct((rows, width), bf16),
            jax.ShapeDtypeStruct((8, width), f32),
        ),
        grid=(2,),
        in_specs=[one, second, first, one, one, row],
        out_specs=(one, one, pl.BlockSpec((8, width), lambda i: (0, 0))),
        compiler_params=params(),
        name="mid_back",
    )(mid, a, b, c, g, gain)


def out_back_body(scal, b0, b1, b2, b3, o, w, do, grad, flat, rows, total, *, first):
    r = pl.program_id(0)

    @pl.when(r == 0)
    def _():
        lay_columns(w, first, flat)
        total[...] = jnp.zeros_like(total)

    pick(r, (b0, b1, b2, b3), rows)
    do[...] = mm_t(rows[...], flat[...]).astype(bf16)
    total[...] += mm(o[...].T, rows[...])

    @pl.when(r == 3)
    def _():
        width = grad.shape[2]
        for d in range(grad.shape[0]):
            grad[d] = total[:, d * width : (d + 1) * width].astype(bf16)


def out_back_call(scal, pieces, o, w, first):
    rows, width = pieces[0].shape
    inner = o.shape[1]
    at = pl.BlockSpec((rows, inner), lambda r, sc: (lax.bitwise_xor(sc[0], r), 0))
    grad = (w.shape[0], inner, w.shape[2])
    return pl.pallas_call(
        functools.partial(out_back_body, first=first),
        out_shape=(jax.ShapeDtypeStruct(o.shape, bf16), jax.ShapeDtypeStruct(grad, bf16)),
        grid_spec=pltpu.PrefetchScalarGridSpec(
            num_scalar_prefetch=1,
            grid=(4,),
            in_specs=[WHOLE] * 4 + [at, WHOLE],
            out_specs=(at, pl.BlockSpec(grad, lambda r, sc: (0, 0, 0))),
            scratch_shapes=[
                pltpu.VMEM((inner, width), bf16),
                pltpu.VMEM((rows, width), bf16),
                pltpu.VMEM((inner, width), f32),
            ],
        ),
        compiler_params=params(),
        name="out_back",
    )(scal, *pieces, o, w)


def qkv_back_body(scal, dq, dk, dv, w, near, far, merged, sums):
    t = pl.program_id(0)

    @pl.when(t == 0)
    def _():
        sums[...] = jnp.zeros_like(sums)

    low = jnp.concatenate([dq[...], dk[...], dv[...]], axis=1)
    merged[...] = low
    part = mm_t(low, w[...]).astype(bf16)
    sums[...] += jnp.sum(low.astype(f32), axis=0, keepdims=True)

    @pl.when(t < 2)
    def _():
        near[0] = part

    @pl.when(t >= 2)
    def _():
        far[0] = part


def qkv_back_call(scal, dq, dk, dv, w):
    keys, inner = dq.shape
    rows = keys // 4
    width = w.shape[0]
    where = lambda t, sc: (lax.bitwise_xor(sc[0], rel_of(t)), 0)
    at = pl.BlockSpec((rows, inner), where)
    return pl.pallas_call(
        qkv_back_body,
        out_shape=(
            jax.ShapeDtypeStruct((2, rows, width), bf16),
            jax.ShapeDtypeStruct((2, rows, width), bf16),
            jax.ShapeDtypeStruct((keys, 3 * inner), bf16),
            jax.ShapeDtypeStruct((1, 3 * inner), f32),
        ),
        grid_spec=pltpu.PrefetchScalarGridSpec(
            num_scalar_prefetch=1,
            grid=(4,),
            in_specs=[at, at, at, WHOLE],
            out_specs=(
                pl.BlockSpec((1, rows, width), near_map),
                pl.BlockSpec((1, rows, width), far_map),
                pl.BlockSpec((rows, 3 * inner), where),
                pl.BlockSpec((1, 3 * inner), lambda t, sc: (0, 0)),
            ),
        ),
        compiler_params=params(),
        name="qkv_back",
    )(scal, dq, dk, dv, w)


def in_back_body(x, a, b, c, dmid, gain, grad, sums):
    @pl.when(pl.program_id(0) == 0)
    def _():
        sums[...] = jnp.zeros_like(sums)

    unit, inv = normalize(x[...].astype(f32))
    e = (a[0].astype(f32) + b[0].astype(f32)) + c[...].astype(f32)
    grad[...] = (dmid[...] + norm_back(e, gain[...], unit, inv)).astype(bf16)
    sums[0:1, :] += jnp.sum(e * unit, axis=0, keepdims=True)
    sums[1:2, :] += jnp.sum(e, axis=0, keepdims=True)


def in_back_call(x, a, b, c, dmid, gain):
    rows, width = x.shape
    one = pl.BlockSpec((rows // 2, width), lambda i: (i, 0))
    first = pl.BlockSpec((1, rows // 2, width), lambda i: (0, i, 0))
    second = pl.BlockSpec((1, rows // 2, width), lambda i: (1, i, 0))
    row = pl.BlockSpec((1, width), lambda i: (0, 0))
    return pl.pallas_call(
        in_back_body,
        out_shape=(
            jax.ShapeDtypeStruct((rows, width), bf16),
            jax.ShapeDtypeStruct((8, width), f32),
        ),
        grid=(2,),
        in_specs=[one, second, first, one, one, row],
        out_specs=(one, pl.BlockSpec((8, width), lambda i: (0, 0))),
        compiler_params=params(),
        name="in_back",
    )(x, a, b, c, dmid, gain)


def remote(src, dst, send, recv, dp, seq):
    return pltpu.make_async_remote_copy(
        src_ref=src,
        dst_ref=dst,
        send_sem=send,
        recv_sem=recv,
        device_id=(dp, seq),
        device_id_type=pl.DeviceIdType.MESH,
    )


def greet(peers):
    barrier = pltpu.get_barrier_semaphore()
    for dp, seq in peers:
        pl.semaphore_signal(
            barrier, inc=1, device_id=(dp, seq), device_id_type=pl.DeviceIdType.MESH
        )
    pl.semaphore_wait(barrier, len(peers))


class GradSum:
    def __init__(self, part, acc, landx, land, sems, dp, seq):
        self.part, self.landx, self.land, self.sems = part, landx, land, sems
        self.fetched = acc is not None
        self.acc = acc if self.fetched else landx
        self.seq, self.z, self.x = seq, dp // 2, dp % 2

    def cross(self, k):
        return remote(
            self.part.at[2 * k + (1 - self.x)],
            self.landx.at[k],
            self.sems.at[0, k],
            self.sems.at[1, k],
            2 * self.z + (1 - self.x),
            self.seq,
        )

    def fetch(self, k):
        return pltpu.make_async_copy(
            self.part.at[2 * k + self.x], self.acc.at[k], self.sems.at[6, k]
        )

    def right(self, b, first):
        return remote(
            self.acc.at[b] if first else self.land.at[b + 1],
            self.land.at[b + 1],
            self.sems.at[2, b],
            self.sems.at[3, b],
            2 * ((self.z + 1) % 4) + self.x,
            self.seq,
        )

    def left(self, b, first):
        return remote(
            self.acc.at[b] if first else self.land.at[b],
            self.land.at[b],
            self.sems.at[4, b],
            self.sems.at[5, b],
            2 * ((self.z + 3) % 4) + self.x,
            self.seq,
        )

    def start(self):
        for k in (3, 0, 2, 1):
            self.cross(k).start()
        if self.fetched:
            for k in range(4):
                self.fetch(k).start()

    def add_cross(self):
        for k in (3, 0, 2, 1):
            self.cross(k).wait_recv()
            if self.fetched:
                self.fetch(k).wait()
                own = self.acc[k].astype(f32)
            else:
                own = self.part[2 * k + self.x].astype(f32)
            self.acc[k] = (own + self.landx[k].astype(f32)).astype(bf16)

    def stage(self, k):
        @pl.when(self.z == k)
        def _():
            for b in range(3, k, -1):
                if k > 0:
                    self.right(b, False).wait_recv()
                    total = self.land[b + 1].astype(f32) + self.acc[b].astype(f32)
                    self.land[b + 1] = total.astype(bf16)
                self.right(b, k == 0).start()

        @pl.when(self.z == 3 - k)
        def _():
            for b in range(0, 3 - k):
                if k > 0:
                    self.left(b, False).wait_recv()
                    total = self.land[b].astype(f32) + self.acc[b].astype(f32)
                    self.land[b] = total.astype(bf16)
                self.left(b, k == 0).start()

    def finish(self, out):
        z = self.z
        out[...] = self.acc[z].astype(f32)

        @pl.when(z > 0)
        def _():
            self.right(z, False).wait_recv()
            out[...] += self.land[z + 1].astype(f32)

        @pl.when(z < 3)
        def _():
            self.left(z, False).wait_recv()
            out[...] += self.land[z].astype(f32)

    def drain(self):
        for k in range(4):
            self.cross(k).wait_send()
        for k in range(3):

            @pl.when(self.z == k)
            def _(k=k):
                for b in range(3, k, -1):
                    self.right(b, k == 0).wait_send()

            @pl.when(self.z == 3 - k)
            def _(k=k):
                for b in range(0, 3 - k):
                    self.left(b, k == 0).wait_send()

    @staticmethod
    def scratch(m, n, fetched=False):
        own = [pltpu.VMEM((4, m, n), bf16)] if fetched else []
        return own + [
            pltpu.VMEM((4, m, n), bf16),
            pltpu.VMEM((5, m, n), bf16),
            pltpu.SemaphoreType.DMA((7, 4)),
        ]


SMALL_ROWS = 16


class Gather:
    def __init__(self, own, out, sems, dp, seq):
        self.own, self.out, self.sems = own, out, sems
        self.seq, self.z, self.x = seq, dp // 2, dp % 2

    def along(self, k, step, src=None):
        slot = self.out.at[2 * k + self.x]
        return remote(
            slot if src is None else src,
            slot,
            self.sems.at[0 if step > 0 else 1, k],
            self.sems.at[3, k],
            2 * ((self.z + step + 4) % 4) + self.x,
            self.seq,
        )

    def over(self, k, src=None):
        slot = self.out.at[2 * k + self.x]
        return remote(
            slot if src is None else src,
            slot,
            self.sems.at[2, k],
            self.sems.at[4, k],
            2 * self.z + (1 - self.x),
            self.seq,
        )

    def keep(self):
        return pltpu.make_async_copy(
            self.own, self.out.at[2 * self.z + self.x], self.sems.at[5, 0]
        )

    def start(self):
        z = self.z

        @pl.when(z < 3)
        def _():
            self.along(z, 1, self.own).start()

        @pl.when(z > 0)
        def _():
            self.along(z, -1, self.own).start()

        self.over(z, self.own).start()
        self.keep().start()

    def hop(self, dist):
        z = self.z

        @pl.when(z - dist >= 0)
        def _():
            k = z - dist
            self.along(k, 1).wait_recv()

            @pl.when(z < 3)
            def _():
                self.along(k, 1).start()

            self.over(k).start()

        @pl.when(z + dist <= 3)
        def _():
            k = z + dist
            self.along(k, -1).wait_recv()

            @pl.when(z > 0)
            def _():
                self.along(k, -1).start()

            self.over(k).start()

    def finish(self):
        z = self.z
        self.keep().wait()
        for k in range(4):
            self.over(k).wait_recv()
            self.over(k).wait_send()

            @pl.when((z < 3) & (z >= k))
            def _(k=k):
                self.along(k, 1).wait_send()

            @pl.when((z > 0) & (z <= k))
            def _(k=k):
                self.along(k, -1).wait_send()

    @staticmethod
    def scratch():
        return pltpu.SemaphoreType.DMA((6, 4))


class Spread:
    def __init__(self, own, rows, sems, dp, seq):
        mate, across = seq + 1 - 2 * (seq % 2), (seq + 2) % 4
        to = lambda src, r, peer: remote(src, rows.at[r], sems.at[0, r], sems.at[1, r], dp, peer)
        self.near, self.far = to(own, 1, mate), to(own, 2, across)
        self.last = to(rows.at[2], 3, mate)

    def start(self):
        self.far.start()
        self.near.start()

    def forward(self):
        self.far.wait_recv()
        self.last.start()

    def drain(self):
        for copy in (self.near, self.far, self.last):
            copy.wait_send()


def neighbours(seq):
    mate = seq + 1 - 2 * (seq % 2)
    return mate, (seq + 2) % 4, (mate + 2) % 4


def block_at(seq, rel):
    return 2 * ((seq // 2 + rel // 2) % 2) + (seq + rel) % 2


def front_body(
    wq, wo, x, v_up, v_qv, v_g1, v_s1, v_out, v_g2, v_s2, v_down,
    wq_all, wo_all, x_rows, gain1, shift1, bias_qkv, bias_out, gain2, shift2, bias_up, bias_down,
    small, vectors, q_sem, o_sem, x_sem, seq_sem, dp_sem, keep_sem,
):
    dp, seq = lax.axis_index("dp"), lax.axis_index("seq")
    greet([((dp + i) % 8, seq) for i in range(1, 8)] + [(dp, p) for p in neighbours(seq)])
    gather_q = Gather(wq, wq_all, q_sem, dp, seq)
    gather_o = Gather(wo, wo_all, o_sem, dp, seq)
    rows = Spread(x, x_rows, x_sem, dp, seq)
    at = 0
    for ref in (v_up, v_qv, v_g1, v_s1, v_out, v_g2, v_s2, v_down):
        small[:, at : at + ref.shape[1]] = ref[...].astype(f32)
        at += ref.shape[1]
    keep_v = pltpu.make_async_copy(small, vectors.at[dp, seq], keep_sem.at[1])
    keep_v.start()
    group = [
        remote(small, vectors.at[dp, seq], seq_sem.at[0, i], seq_sem.at[1, i], dp, peer)
        for i, peer in enumerate(neighbours(seq))
    ]
    for copy in group:
        copy.start()
    gather_q.start()
    rows.start()
    keep_x = pltpu.make_async_copy(x, x_rows.at[0], keep_sem.at[0])
    keep_x.start()

    def to_dp(i):
        return remote(
            vectors.at[dp], vectors.at[dp], dp_sem.at[0, i], dp_sem.at[1, i], (dp + i) % 8, seq
        )

    keep_v.wait()
    for copy in group:
        copy.wait_recv()
    for i in range(1, 8):
        to_dp(i).start()
    gather_o.start()
    gather_q.hop(1)
    gather_q.hop(2)
    gather_o.hop(1)
    gather_q.hop(3)
    gather_o.hop(2)
    rows.forward()
    gather_o.hop(3)
    for i in range(1, 8):
        to_dp(i).wait_recv()
    for ref, at in (
        (gain1, 192), (shift1, 224), (bias_out, 256), (gain2, 288), (shift2, 320), (bias_down, 352),
    ):
        for d in range(8):
            ref[:, d * LANES : (d + 1) * LANES] = jnp.concatenate(
                [vectors[d, i, :, at : at + 32] for i in range(4)], axis=1
            )
    for part in range(2):
        for half in range(2):
            lane = part * 512 + half * LANES
            bias_qkv[:, lane : lane + LANES] = jnp.concatenate(
                [vectors[4 * part + seq, 2 * half + i, :, 128:192] for i in range(2)], axis=1
            )
    bias_qkv[:, 256:512] = jnp.zeros((1, 256), f32)
    for i in range(8):
        bias_up[:, i * LANES : (i + 1) * LANES] = vectors[2 * seq + i // 4, i % 4, :, 0:LANES]
    gather_q.finish()
    gather_o.finish()
    rows.near.wait_recv()
    rows.last.wait_recv()
    rows.drain()
    keep_x.wait()
    for copy in group:
        copy.wait_send()
    for i in range(1, 8):
        to_dp(i).wait_send()


def front_call(wq, wo, x, small):
    count = sum(v.shape[0] for v in small)
    rows, width = x.shape
    one = lambda n: jax.ShapeDtypeStruct((1, n), f32)
    sem = pltpu.SemaphoreType.DMA
    return pl.pallas_call(
        front_body,
        out_shape=(
            jax.ShapeDtypeStruct((8, *wq.shape), bf16),
            jax.ShapeDtypeStruct((8, *wo.shape), bf16),
            jax.ShapeDtypeStruct((4, rows, width), bf16),
            one(width), one(width), one(wq.shape[1]), one(width), one(width), one(width),
            one(width), one(width),
        ),
        in_specs=[WHOLE] * 11,
        out_specs=(WHOLE,) * 11,
        scratch_shapes=[
            pltpu.VMEM((1, count), f32),
            pltpu.VMEM((8, 4, 1, count), f32),
            Gather.scratch(),
            Gather.scratch(),
            sem((2, 4)),
            sem((2, 3)),
            sem((2, 8)),
            sem((2,)),
        ],
        compiler_params=params(collective_id=4, has_side_effects=True),
        name="front",
    )(wq, wo, x, *(v.reshape(1, -1) for v in small))


def attention_body(
    scal, slopes, x_rows, g, wq, wo, w1, w2, gain1, shift1, bias_qkv, bias_out, gain2, shift2,
    h1, qkv, o, lse, mid, h2, g_rows, w1_all, w2_all,
    bias, vt, flat, part, land_c, sum_y, land_y, g_sem, row_sems, keep_sem, w1_sem, w2_sem,
):
    dp, seq = lax.axis_index("dp"), lax.axis_index("seq")
    mate, across, _ = neighbours(seq)
    greet([((dp + i) % 8, seq) for i in range(1, 8)] + [(dp, mate), (dp, across)])
    rows, width = g.shape
    keys = qkv.shape[0]
    inner = o.shape[1]
    pairs = inner // LANES
    gathers = [Gather(w1, w1_all, w1_sem, dp, seq), Gather(w2, w2_all, w2_sem, dp, seq)]
    for gather in gathers:
        gather.start()
    spread_g = Spread(g, g_rows, g_sem, dp, seq)
    spread_g.start()
    keep = pltpu.make_async_copy(g, g_rows.at[0], keep_sem.at[0])
    keep.start()
    lay_columns(wo, 0, flat)

    def project(r, carry):
        at = pl.ds(pl.multiple_of(block_at(seq, r) * rows, rows), rows)
        unit, _ = normalize(x_rows[r].astype(f32))
        low = (unit * gain1[...] + shift1[...]).astype(bf16)
        h1[at, :] = low
        qkv[at, :] = (mm(low, wq[...]) + bias_qkv[...]).astype(bf16)
        return carry

    lax.fori_loop(0, 4, project, 0)

    def prepare(p, carry):
        pos = lax.broadcasted_iota(jnp.int32, (keys, LANES), 0)
        ramp = pos.astype(f32)
        inside = pos < scal[1]
        for h in range(2):
            bias[2 * p + h] = jnp.where(inside, ramp * slopes[2 * p + h], NEG)
        lane = pl.ds(pl.multiple_of(2 * inner + p * LANES, LANES), LANES)
        vt[p] = qkv[:, lane].T
        return carry

    lax.fori_loop(0, pairs, prepare, 0)
    for gather in gathers:
        gather.hop(1)
    spread_g.forward()

    cores = [
        remote(part.at[r], land_c.at[k], row_sems.at[0, k], row_sems.at[1, k], dp, mate)
        for k, r in ((0, 1), (1, 3))
    ]
    over = remote(sum_y, land_y, row_sems.at[0, 2], row_sems.at[1, 2], dp, across)
    chunk = 128

    def attend(t, carry):
        rel = 3 - t
        c_now = block_at(seq, rel)
        at = pl.ds(pl.multiple_of(c_now * rows, rows), rows)
        for c in range(keys // rows):

            @pl.when(c_now == c)
            def _(c=c):
                length = (c + 1) * rows

                def one_pair(p, carry):
                    lane = pl.ds(pl.multiple_of(p * LANES, LANES), LANES)
                    k_lane = pl.ds(pl.multiple_of(inner + p * LANES, LANES), LANES)
                    scaled = qkv[c * rows : length, lane] * bf16(HEAD_DIM**-0.5)
                    k = qkv[0:length, k_lane]
                    outs, logs = [], []
                    for h in range(2):
                        s = scores(k, head_only(scaled, h), bias[2 * p + h, 0:length, :])
                        top = jnp.max(s, axis=0, keepdims=True)
                        e = jnp.exp(s - top)
                        total = jnp.sum(e, axis=0, keepdims=True)
                        half = vt[p, h * HEAD_DIM : (h + 1) * HEAD_DIM, 0:length]
                        outs.append(mm(half, e.astype(bf16)) / total)
                        logs.append(top + jnp.log(total))
                    o[c * rows : length, lane] = jnp.concatenate(outs, axis=0).T.astype(bf16)
                    lse[p, 0:2, c * rows : length] = jnp.concatenate(logs, axis=0)
                    return carry

                lax.fori_loop(0, pairs, one_pair, 0)

        part[rel] = mm(o[at, :], flat[...]).astype(bf16)

        @pl.when(t == 0)
        def _():
            cores[1].start()

        @pl.when(t == 1)
        def _():
            cores[1].wait_recv()
            for i in range(rows // chunk):
                at = slice(i * chunk, (i + 1) * chunk)
                total = part[2, at, :].astype(f32) + land_c[1, at, :].astype(f32)
                sum_y[at, :] = total.astype(bf16)
            over.start()
            for gather in gathers:
                gather.hop(2)

        @pl.when(t == 2)
        def _():
            cores[0].start()
            for gather in gathers:
                gather.hop(3)

        return carry

    lax.fori_loop(0, 4, attend, 0)
    cores[0].wait_recv()
    over.wait_recv()

    def second_norm(i, carry):
        at = pl.ds(pl.multiple_of(i * chunk, chunk), chunk)
        total = (part[0, at, :].astype(f32) + land_c[0, at, :].astype(f32)) + land_y[
            at, :
        ].astype(f32)
        value = x_rows[0, at, :].astype(f32) + (total + bias_out[...])
        mid[at, :] = value
        unit, _ = normalize(value)
        h2[at, :] = (unit * gain2[...] + shift2[...]).astype(bf16)
        return carry

    lax.fori_loop(0, rows // chunk, second_norm, 0)
    for gather in gathers:
        gather.finish()
    spread_g.near.wait_recv()
    spread_g.last.wait_recv()
    spread_g.drain()
    keep.wait()
    for copy in cores + [over]:
        copy.wait_send()


def scores(k, qm, ramp):
    block = qm.shape[0]
    length = k.shape[0]
    s = mm_t(k, qm) + jnp.concatenate([ramp] * (block // LANES), axis=1)
    key = lax.broadcasted_iota(jnp.int32, (block, block), 0)
    query = lax.broadcasted_iota(jnp.int32, (block, block), 1)
    last = jnp.where(key <= query, s[length - block :], NEG)
    if length == block:
        return last
    return jnp.concatenate([s[: length - block], last], axis=0)


def attention_call(scal, slopes, x_rows, g, wq, wo, w1, w2, *vectors):
    rows, width = g.shape
    keys = 4 * rows
    inner = wo.shape[1]
    pairs = inner // LANES
    sem = pltpu.SemaphoreType.DMA
    return pl.pallas_call(
        attention_body,
        out_shape=(
            jax.ShapeDtypeStruct((keys, width), bf16),
            jax.ShapeDtypeStruct((keys, 3 * inner), bf16),
            jax.ShapeDtypeStruct((keys, inner), bf16),
            jax.ShapeDtypeStruct((pairs, 8, keys), f32),
            jax.ShapeDtypeStruct((rows, width), f32),
            jax.ShapeDtypeStruct((rows, width), bf16),
            jax.ShapeDtypeStruct((4, rows, width), bf16),
            jax.ShapeDtypeStruct((8, *w1.shape), bf16),
            jax.ShapeDtypeStruct((8, *w2.shape), bf16),
        ),
        in_specs=[SCALAR, SCALAR] + [WHOLE] * (6 + len(vectors)),
        out_specs=(WHOLE,) * 9,
        scratch_shapes=[
            pltpu.VMEM((2 * pairs, keys, LANES), f32),
            pltpu.VMEM((pairs, LANES, keys), bf16),
            pltpu.VMEM((inner, width), bf16),
            pltpu.VMEM((4, rows, width), bf16),
            pltpu.VMEM((2, rows, width), bf16),
            pltpu.VMEM((rows, width), bf16),
            pltpu.VMEM((rows, width), bf16),
            sem((2, 4)),
            sem((2, 3)),
            sem((1,)),
            Gather.scratch(),
            Gather.scratch(),
        ],
        compiler_params=params(collective_id=5, has_side_effects=True),
        name="attention",
    )(scal, slopes, x_rows, g, wq, wo, w1, w2, *vectors)


def feed_body(
    h2, g_rows, w1, w2, b1, mid, gain2,
    y_near, y_far, gw1, gw2, dmid, dbr, sums, up_sum,
    h_rows, a_all, du_all, flat, part, land_c, sum_y, land_y, turned, h_sem, row_sems, keep_sem,
):
    dp, seq = lax.axis_index("dp"), lax.axis_index("seq")
    mate, across, _ = neighbours(seq)
    greet([(dp, mate), (dp, across)])
    rows, width = h2.shape
    inner = w1.shape[1]
    spread_h = Spread(h2, h_rows, h_sem, dp, seq)
    spread_h.start()
    keep = pltpu.make_async_copy(h2, h_rows.at[0], keep_sem.at[0])
    keep.start()
    lay_columns(w2, 0, flat)
    up_sum[...] = jnp.zeros_like(up_sum)
    sums[...] = jnp.zeros_like(sums)
    keep.wait()
    cores = [
        remote(part.at[r], land_c.at[k], row_sems.at[0, k], row_sems.at[1, k], dp, mate)
        for k, r in ((0, 1), (1, 3))
    ]
    over = remote(sum_y, land_y, row_sems.at[0, 2], row_sems.at[1, 2], dp, across)
    chunk = 256

    def block(t, carry):
        @pl.when(t == 1)
        def _():
            spread_h.near.wait_recv()

        @pl.when(t == 2)
        def _():
            spread_h.forward()

        @pl.when(t == 3)
        def _():
            spread_h.last.wait_recv()

        at = pl.ds(pl.multiple_of(t * rows, rows), rows)
        for c in range(inner // chunk):
            cols = slice(c * chunk, (c + 1) * chunk)
            u = mm(h_rows[t], w1[:, cols]) + b1[:, cols]
            value, slope = gelu_parts(u)
            a_all[at, cols] = value.astype(bf16)
            du = (mm_t(g_rows[t], flat[cols, :]) * slope).astype(bf16)
            du_all[at, cols] = du
            up_sum[:, cols] += jnp.sum(du.astype(f32), axis=0, keepdims=True)
        y = mm(a_all[at, :], flat[...]).astype(bf16)
        part[t] = mm_t(du_all[at, :], w1[...]).astype(bf16)
        for r, (ref, k) in enumerate(((y_far, 1), (y_near, 0), (y_far, 0), (y_near, 1))):

            @pl.when(t == r)
            def _(ref=ref, k=k):
                ref[k] = y

        @pl.when(t == 1)
        def _():
            cores[0].start()

        @pl.when(t == 3)
        def _():
            cores[1].start()

        return carry

    lax.fori_loop(0, 4, block, 0)

    def turn(load):
        def step(i, carry):
            turned[:, pl.ds(pl.multiple_of(i * rows, rows), rows)] = load(i).T
            return carry

        lax.fori_loop(0, 4, step, 0)

    turn(lambda i: h_rows[i])

    def outer_up(j, carry):
        cols = pl.ds(pl.multiple_of(j * chunk, chunk), chunk)
        gw1[:, cols] = mm(turned[...], du_all[:, cols]).astype(bf16)
        return carry

    lax.fori_loop(0, 1, outer_up, 0)
    cores[1].wait_recv()
    small = 128
    for i in range(rows // small):
        at = slice(i * small, (i + 1) * small)
        total = part[2, at, :].astype(f32) + land_c[1, at, :].astype(f32)
        sum_y[at, :] = total.astype(bf16)
    over.start()
    lax.fori_loop(1, inner // chunk, outer_up, 0)
    turn(lambda i: a_all[pl.ds(pl.multiple_of(i * rows, rows), rows), :])

    def outer_down(j, carry):
        cols = pl.ds(pl.multiple_of(j * chunk, chunk), chunk)
        right = g_rows[:, :, cols].reshape(4 * rows, chunk)
        grad = mm(turned[...], right).astype(bf16)
        gw2[2 * j] = grad[:, :LANES]
        gw2[2 * j + 1] = grad[:, LANES:]
        return carry

    lax.fori_loop(0, width // chunk, outer_down, 0)
    cores[0].wait_recv()
    over.wait_recv()

    def norm_step(i, carry):
        at = pl.ds(pl.multiple_of(i * small, small), small)
        unit, inv = normalize(mid[at, :])
        e = (part[0, at, :].astype(f32) + land_c[0, at, :].astype(f32)) + land_y[at, :].astype(f32)
        grad = g_rows[0, at, :].astype(f32)
        value = grad + norm_back(e, gain2[...], unit, inv)
        dmid[at, :] = value
        low = value.astype(bf16)
        dbr[at, :] = low
        sums[0:1, :] += jnp.sum(e * unit, axis=0, keepdims=True)
        sums[1:2, :] += jnp.sum(e, axis=0, keepdims=True)
        sums[2:3, :] += jnp.sum(low.astype(f32), axis=0, keepdims=True)
        sums[3:4, :] += jnp.sum(grad, axis=0, keepdims=True)
        return carry

    lax.fori_loop(0, rows // small, norm_step, 0)
    spread_h.drain()
    for copy in cores + [over]:
        copy.wait_send()


def feed_call(h2, g_rows, w1, w2, b1, mid, gain2):
    rows, width = h2.shape
    inner = w1.shape[1]
    sem = pltpu.SemaphoreType.DMA
    pair = jax.ShapeDtypeStruct((2, rows, width), bf16)
    return pl.pallas_call(
        feed_body,
        out_shape=(
            pair,
            pair,
            jax.ShapeDtypeStruct((width, inner), bf16),
            jax.ShapeDtypeStruct(w2.shape, bf16),
            jax.ShapeDtypeStruct((rows, width), f32),
            jax.ShapeDtypeStruct((rows, width), bf16),
            jax.ShapeDtypeStruct((8, width), f32),
            jax.ShapeDtypeStruct((1, inner), f32),
        ),
        in_specs=[WHOLE] * 7,
        out_specs=(WHOLE,) * 8,
        scratch_shapes=[
            pltpu.VMEM((4, rows, width), bf16),
            pltpu.VMEM((4 * rows, inner), bf16),
            pltpu.VMEM((4 * rows, inner), bf16),
            pltpu.VMEM((inner, width), bf16),
            pltpu.VMEM((4, rows, width), bf16),
            pltpu.VMEM((2, rows, width), bf16),
            pltpu.VMEM((rows, width), bf16),
            pltpu.VMEM((rows, width), bf16),
            pltpu.VMEM((width, 4 * rows), bf16),
            sem((2, 4)),
            sem((2, 3)),
            sem((1,)),
        ],
        compiler_params=params(collective_id=6, has_side_effects=True),
        name="feed_forward",
    )(h2, g_rows, w1, w2, b1, mid, gain2)


def back_body(
    scal, slopes, dbr, o, wo, qkv, lse, wq, h1, gw1, gw2, y_near, y_far, mid, bias_down, x, dmid,
    gain1, mid_sums, up_sum,
    output, grad, gq_out, go_out, gw1_out, gw2_out, small_out,
    b_rows, flat, do, go_sum, go_part, bias, kt, dk_sum, dv_sum, merged, qkv_sums, h_buf, turned,
    gq_part, land_c, sum_y, land_y, y_land_c, y_sum, y_land_y,
    a_acc, a_x, a_land, a_sem, b_acc, b_x, b_land, b_sem, o_x, o_land, o_sem,
    q0_x, q0_land, q0_sem, q1_x, q1_land, q1_sem, q2_x, q2_land, q2_sem,
    small, small_land, own, seq_land,
    b_row_sem, row_sems, y_sems, h_sem, small_sems, seq_sems,
):
    dp, seq = lax.axis_index("dp"), lax.axis_index("seq")
    mate, across, far_mate = neighbours(seq)
    greet([((dp + i) % 8, seq) for i in range(1, 8)] + [(dp, p) for p in neighbours(seq)])
    rows, width = dbr.shape
    keys, inner = o.shape
    pairs = inner // LANES
    scale = HEAD_DIM**-0.5
    chunk = 128

    spread_b = Spread(dbr, b_rows, b_row_sem, dp, seq)
    spread_b.start()
    sum_a = GradSum(gw2, a_acc, a_x, a_land, a_sem, dp, seq)
    sum_b = GradSum(gw1, b_acc, b_x, b_land, b_sem, dp, seq)
    sum_o = GradSum(go_part, None, o_x, o_land, o_sem, dp, seq)
    sums_q = [
        GradSum(gq_part.at[0], None, q0_x, q0_land, q0_sem, dp, seq),
        GradSum(gq_part.at[1], None, q1_x, q1_land, q1_sem, dp, seq),
        GradSum(gq_part.at[2], None, q2_x, q2_land, q2_sem, dp, seq),
    ]
    sum_a.start()
    sum_b.start()
    y_cores = [
        remote(y_near.at[k], y_land_c.at[k], y_sems.at[0, k], y_sems.at[1, k], dp, mate)
        for k in range(2)
    ]
    y_over = remote(y_sum, y_land_y, y_sems.at[0, 2], y_sems.at[1, 2], dp, across)
    cores = [
        remote(b_rows.at[r], land_c.at[k], row_sems.at[0, k], row_sems.at[1, k], dp, mate)
        for k, r in ((0, 1), (1, 3))
    ]
    over = remote(sum_y, land_y, row_sems.at[0, 2], row_sems.at[1, 2], dp, across)

    def fetch_h(i):
        at = pl.ds(pl.multiple_of(i * rows, rows), rows)
        return pltpu.make_async_copy(h1.at[at], h_buf.at[i % 2], h_sem.at[i % 2])

    fetch_h(0).start()
    fetch_h(1).start()
    lay_columns(wo, 0, flat)
    go_sum[...] = jnp.zeros_like(go_sum)

    def out_back(r, carry):
        if r >= 2:
            spread_b.forward() if r == 2 else spread_b.last.wait_recv()
        if r == 1:
            spread_b.near.wait_recv()
        at = pl.ds(pl.multiple_of(block_at(seq, r) * rows, rows), rows)
        src = dbr if r == 0 else b_rows.at[r]
        do[at, :] = mm_t(src[...], flat[...]).astype(bf16)
        go_sum[...] += mm(o[at, :].T, src[...])
        return carry

    out_back(0, 0)
    y_cores[1].start()
    y_cores[0].start()
    out_back(1, 0)

    def turn(i, carry):
        fetch_h(i).wait()
        turned[:, pl.ds(pl.multiple_of(i * rows, rows), rows)] = h_buf[i % 2].T

        @pl.when(i < 2)
        def _():
            fetch_h(i + 2).start()

        return carry

    lax.fori_loop(0, 4, turn, 0)
    small[...] = jnp.zeros_like(small)
    for d in range(8):
        at = slice(d * LANES, (d + 1) * LANES)
        for row, src in ((4, 2), (5, 0), (6, 1), (11, 3)):
            small[d, row : row + 1, :] = mid_sums[src : src + 1, at]
    for i in range(8):
        at = slice(i * LANES, (i + 1) * LANES)
        small[pl.ds(2 * seq + i // 4, 1), 7 + i % 4, :] = up_sum[:, at]
    out_back(2, 0)
    y_cores[1].wait_recv()
    for i in range(rows // chunk):
        at = slice(i * chunk, (i + 1) * chunk)
        total = y_far[0, at, :].astype(f32) + y_land_c[1, at, :].astype(f32)
        y_sum[at, :] = total.astype(bf16)
    y_over.start()
    out_back(3, 0)
    for d in range(8):
        go_part[d] = go_sum[:, d * LANES : (d + 1) * LANES].astype(bf16)
    sum_o.start()
    sum_a.add_cross()
    sum_a.stage(0)

    def one_pair(p, carry):
        lane = pl.ds(pl.multiple_of(p * LANES, LANES), LANES)
        k_lane = pl.ds(pl.multiple_of(inner + p * LANES, LANES), LANES)
        v_lane = pl.ds(pl.multiple_of(2 * inner + p * LANES, LANES), LANES)
        pos = lax.broadcasted_iota(jnp.int32, (keys, LANES), 0)
        ramp = pos.astype(f32)
        inside = pos < scal[1]
        for h in range(2):
            bias[h] = jnp.where(inside, ramp * slopes[2 * p + h], NEG)
        kt[...] = qkv[:, k_lane].T
        dk_sum[...] = jnp.zeros_like(dk_sum)
        dv_sum[...] = jnp.zeros_like(dv_sum)
        for c in range(keys // rows):
            length = (c + 1) * rows
            at = slice(c * rows, length)
            scaled = qkv[at, lane] * bf16(scale)
            g = do[at, lane]
            both = (g.astype(f32) * o[at, lane].astype(f32)).T
            k = qkv[0:length, k_lane]
            v = qkv[0:length, v_lane]
            outs = []
            for h in range(2):
                half = slice(h * HEAD_DIM, (h + 1) * HEAD_DIM)
                qm = head_only(scaled, h)
                gm = head_only(g, h)
                dot_row = jnp.sum(both[half], axis=0, keepdims=True)
                log = lse[p, h : h + 1, at]
                e = jnp.exp(scores(k, qm, bias[h, 0:length, :]) - log)
                ds = (e * (mm_t(v, gm) - dot_row)).astype(bf16)
                dv_sum[0:length, :] += mm(e.astype(bf16), gm)
                dk_sum[0:length, :] += mm(ds, qm)
                outs.append(mm(kt[half, 0:length], ds))
            merged[at, lane] = (jnp.concatenate(outs, axis=0).T * scale).astype(bf16)
            if c == 2:

                @pl.when(p == 1)
                def _():
                    sum_a.stage(2)

        merged[:, k_lane] = dk_sum[...].astype(bf16)
        merged[:, v_lane] = dv_sum[...].astype(bf16)

        @pl.when(p == 0)
        def _():
            sum_a.stage(1)

        return carry

    lax.fori_loop(0, pairs, one_pair, 0)
    spread_b.drain()
    sum_b.add_cross()
    sum_b.stage(0)
    qkv_sums[...] = jnp.zeros_like(qkv_sums)

    def qkv_back(t, carry):
        rel = 3 - t
        at = pl.ds(pl.multiple_of(block_at(seq, rel) * rows, rows), rows)
        low = merged[at, :]
        b_rows[rel] = mm_t(low, wq[...]).astype(bf16)
        qkv_sums[...] += jnp.sum(low.astype(f32), axis=0, keepdims=True)

        @pl.when(t == 0)
        def _():
            cores[1].start()

        @pl.when(t == 1)
        def _():
            cores[1].wait_recv()
            for i in range(rows // chunk):
                at = slice(i * chunk, (i + 1) * chunk)
                total = b_rows[2, at, :].astype(f32) + land_c[1, at, :].astype(f32)
                sum_y[at, :] = total.astype(bf16)
            over.start()

        @pl.when(t == 2)
        def _():
            cores[0].start()

        return carry

    lax.fori_loop(0, 4, qkv_back, 0)
    for j in range(3):
        cols = slice(j * inner, (j + 1) * inner)
        value = mm(turned[...], merged[:, cols]).astype(bf16)
        gq_part[j] = value.reshape(8, width // 8, inner)
        sums_q[j].start()
        if j == 0:
            sum_o.add_cross()
            sum_o.stage(0)
            sum_b.stage(1)
    for i in range(2):
        at = slice(i * LANES, (i + 1) * LANES)
        small[pl.ds(seq, 1), 2 + i, :] = qkv_sums[:, at]
        at = slice((4 + i) * LANES, (5 + i) * LANES)
        small[pl.ds(4 + seq, 1), 2 + i, :] = qkv_sums[:, at]
    sum_a.finish(gw2_out)
    y_cores[0].wait_recv()
    y_over.wait_recv()

    def out_step(i, carry):
        at = pl.ds(pl.multiple_of(i * chunk, chunk), chunk)
        total = y_far[1, at, :].astype(f32) + y_land_c[0, at, :].astype(f32)
        total = total + y_land_y[at, :].astype(f32)
        output[at, :] = (mid[at, :] + (total + bias_down[...])).astype(bf16)
        return carry

    lax.fori_loop(0, rows // chunk, out_step, 0)
    sums_q[0].add_cross()
    sums_q[0].stage(0)
    sum_b.stage(2)
    sum_o.stage(1)
    cores[0].wait_recv()
    over.wait_recv()
    own[...] = jnp.zeros_like(own)
    qkv_gain = [jnp.zeros((1, width), f32), jnp.zeros((1, width), f32)]
    for i in range(rows // chunk):
        at = slice(i * chunk, (i + 1) * chunk)
        unit, inv = normalize(x[at, :].astype(f32))
        e = (b_rows[0, at, :].astype(f32) + land_c[0, at, :].astype(f32)) + land_y[
            at, :
        ].astype(f32)
        grad[at, :] = (dmid[at, :] + norm_back(e, gain1[...], unit, inv)).astype(bf16)
        qkv_gain[0] += jnp.sum(e * unit, axis=0, keepdims=True)
        qkv_gain[1] += jnp.sum(e, axis=0, keepdims=True)
    for d in range(8):
        at = slice(d * LANES, (d + 1) * LANES)
        small[d, 0:1, :] = qkv_gain[0][:, at]
        small[d, 1:2, :] = qkv_gain[1][:, at]

    def small_to(i):
        peer = (dp + i) % 8
        return remote(
            small.at[peer], small_land.at[i], small_sems.at[0, i], small_sems.at[1, i], peer, seq
        )

    for i in range(1, 8):
        small_to(i).start()
    sums_q[1].add_cross()
    sums_q[1].stage(0)
    sums_q[0].stage(1)
    sum_o.stage(2)
    sums_q[2].add_cross()
    sums_q[2].stage(0)
    sums_q[1].stage(1)
    sums_q[0].stage(2)
    total = small[dp]
    for i in range(1, 8):
        small_to(i).wait_recv()
        total = total + small_land[i]
    own[...] = total

    def seq_to(i, peer):
        return remote(own, seq_land.at[i], seq_sems.at[0, i], seq_sems.at[1, i], dp, peer)

    group = [seq_to(i, peer) for i, peer in enumerate(neighbours(seq))]
    for copy in group:
        copy.start()
    sums_q[2].stage(1)
    sums_q[1].stage(2)
    sums_q[2].stage(2)
    sum_b.finish(gw1_out)
    sum_o.finish(go_out)
    for copy in group:
        copy.wait_recv()
    small_out[...] = (own[...] + seq_land[0]) + (seq_land[1] + seq_land[2])
    for j in range(3):
        sums_q[j].finish(gq_out.at[:, j * inner : (j + 1) * inner])
    for copy in group + cores + y_cores + [over, y_over]:
        copy.wait_send()
    for i in range(1, 8):
        small_to(i).wait_send()
    for part in [sum_a, sum_b, sum_o] + sums_q:
        part.drain()


def back_call(*args):
    dbr, o, wo, qkv, lse, wq, h1, gw1, gw2 = args[2:11]
    rows, width = dbr.shape
    keys, inner = o.shape
    sem = pltpu.SemaphoreType.DMA
    block = lambda dtype: pltpu.VMEM((rows, width), dtype)
    pair_rows = pltpu.VMEM((2, rows, width), bf16)
    any_space = pl.BlockSpec(memory_space=pl.ANY)
    specs = [SCALAR, SCALAR] + [WHOLE] * (len(args) - 2)
    for at in (8, 9, 10, 11):
        specs[at] = any_space
    shape = jax.ShapeDtypeStruct
    return pl.pallas_call(
        back_body,
        out_shape=(
            shape((rows, width), bf16),
            shape((rows, width), bf16),
            shape((width // 8, 3 * inner), f32),
            shape((inner, LANES), f32),
            shape(gw1.shape[1:], f32),
            shape(gw2.shape[1:], f32),
            shape((SMALL_ROWS, LANES), f32),
        ),
        in_specs=specs,
        out_specs=(WHOLE,) * 7,
        scratch_shapes=[
            pltpu.VMEM((4, rows, width), bf16),
            pltpu.VMEM((inner, width), bf16),
            pltpu.VMEM((keys, inner), bf16),
            pltpu.VMEM((inner, width), f32),
            pltpu.VMEM((8, inner, LANES), bf16),
            pltpu.VMEM((2, keys, LANES), f32),
            pltpu.VMEM((LANES, keys), bf16),
            pltpu.VMEM((keys, LANES), f32),
            pltpu.VMEM((keys, LANES), f32),
            pltpu.VMEM((keys, 3 * inner), bf16),
            pltpu.VMEM((1, 3 * inner), f32),
            pair_rows,
            pltpu.VMEM((width, keys), bf16),
            pltpu.VMEM((3, 8, width // 8, inner), bf16),
            pair_rows, block(bf16), block(bf16),
            pair_rows, block(bf16), block(bf16),
            *GradSum.scratch(*gw2.shape[1:], fetched=True),
            *GradSum.scratch(*gw1.shape[1:], fetched=True),
            *GradSum.scratch(inner, LANES),
            *(GradSum.scratch(width // 8, inner) * 3),
            pltpu.VMEM((8, SMALL_ROWS, LANES), f32),
            pltpu.VMEM((8, SMALL_ROWS, LANES), f32),
            pltpu.VMEM((SMALL_ROWS, LANES), f32),
            pltpu.VMEM((3, SMALL_ROWS, LANES), f32),
            sem((2, 4)), sem((2, 3)), sem((2, 3)), sem((2,)), sem((2, 8)), sem((2, 3)),
        ],
        compiler_params=pltpu.CompilerParams(
            vmem_limit_bytes=67043328, collective_id=3, has_side_effects=True
        ),
        name="back",
    )(*args)


def finish_body(
    scal, output, grad, gq, go, gw1, gw2, small,
    output_out, grad_out, gq_out, go_out, gw1_out, gw2_out,
    gain1, shift1, qv, bout, gain2, shift2, up, down,
):
    seq = scal[0]
    output_out[...] = output[...]
    grad_out[...] = grad[...]
    go_out[...] = go[...]
    gw1_out[...] = gw1[...]
    gw2_out[...] = gw2[...]
    cols = gq_out.shape[2]
    for c in range(3):
        gq_out[:, c, :] = gq[:, c * cols : (c + 1) * cols]
    for ref, row in ((gain1, 0), (shift1, 1), (bout, 4), (gain2, 5), (shift2, 6), (down, 11)):
        n = ref.shape[1]
        value = small[row : row + 1, 0:n]
        for i in range(1, 4):
            value = jnp.where(seq == i, small[row : row + 1, i * n : (i + 1) * n], value)
        ref[...] = value
    value = small[2:3, 0:64]
    for i in range(1, 4):
        at = 64 * (i % 2)
        value = jnp.where(seq == i, small[2 + i // 2 : 3 + i // 2, at : at + 64], value)
    qv[...] = value
    up[...] = small[pl.ds(7 + seq, 1), :]


def finish_call(scal, output, grad, gq, go, gw1, gw2, small):
    one = lambda n: jax.ShapeDtypeStruct((1, n), f32)
    like = lambda v: jax.ShapeDtypeStruct(v.shape, v.dtype)
    return pl.pallas_call(
        finish_body,
        out_shape=(
            like(output), like(grad),
            jax.ShapeDtypeStruct((gq.shape[0], 3, gq.shape[1] // 3), f32),
            like(go), like(gw1), like(gw2),
            one(32), one(32), one(64), one(32), one(32), one(32), one(LANES), one(32),
        ),
        in_specs=[SCALAR] + [WHOLE] * 7,
        out_specs=(WHOLE,) * 14,
        compiler_params=params(),
        name="finish",
    )(scal, output, grad, gq, go, gw1, gw2, small)


def after(value, *others):
    return lax.optimization_barrier((value, *others))[0]


def on_device(
    dp_n,
    seq_n,
    tokens,
    lengths,
    cotangent,
    ln1_gain,
    ln1_shift,
    w_qkv,
    b_qv,
    w_out,
    b_out,
    ln2_gain,
    ln2_shift,
    w_fc1,
    b_fc1,
    w_fc2,
    b_fc2,
):
    count = dp_n * seq_n
    rows, width = tokens.shape
    heads = width // HEAD_DIM
    inner = w_out.shape[0]
    ff = w_fc1.shape[1]
    s = lax.axis_index("seq")
    length = lengths[0]

    scal = jnp.stack([s.astype(jnp.int32), length])
    slopes = 2.0 ** (-8.0 * (jnp.arange(heads, dtype=jnp.int32) + 1).astype(f32) / heads)
    slopes = lax.dynamic_slice(slopes, (s * (heads // seq_n),), (heads // seq_n,))
    valid = s * rows + jnp.arange(rows, dtype=jnp.int32) < length
    grad_low = jnp.where(valid[:, None], cotangent, jnp.zeros_like(cotangent))
    wq_own = jnp.concatenate([w_qkv[:, c, :] for c in range(3)], axis=1)
    small = (ln1_gain, ln1_shift, b_qv, b_out, ln2_gain, ln2_shift, b_fc1, b_fc2)
    sizes = [v.shape[0] for v in small]
    ends = [sum(sizes[: i + 1]) for i in range(len(sizes))]
    block = 384
    fast = dp_n == 8 and seq_n == 4 and width == 8 * LANES and ff == width and inner == 2 * LANES
    if fast:
        parts = dp_n
        order = (b_fc1, b_qv, ln1_gain, ln1_shift, b_out, ln2_gain, ln2_shift, b_fc2)
        wq, w_o, x_rows, gain1, shift1, qkv_bias, bias_out, gain2, shift2, own_up, bias_down = (
            front_call(wq_own, w_out, tokens, order)
        )
        wq = wq.reshape(width, 3 * inner)
        h1, qkv, o, lse, mid, h2, g_rows, w1, w_cols = attention_call(
            scal, slopes, x_rows, grad_low, wq, w_o, w_fc1, w_fc2,
            gain1, shift1, qkv_bias, bias_out, gain2, shift2,
        )
        y_near, y_far, grad_up, grad_down, dmid, dbr, mid_sums, up_sum = feed_call(
            h2, g_rows, w1.reshape(width, ff), w_cols, own_up, mid, gain2
        )
        results = back_call(
            scal, slopes, dbr, o, w_o, qkv, lse, wq, h1, grad_up.reshape(8, -1, ff), grad_down,
            y_near, y_far, mid, bias_down, tokens, dmid, gain1, mid_sums, up_sum,
        )
        output, grad_tokens, grad_qkv, grad_out, grad_up, grad_down, *vectors = finish_call(
            scal, *results
        )
        g_gain1, g_shift1, g_qv, g_bout, g_gain2, g_shift2, g_up, g_down = (
            v.reshape(n) for v, n in zip(vectors, sizes)
        )
        return (
            output, grad_tokens, g_gain1, g_shift1, grad_qkv, g_qv, grad_out, g_bout,
            g_gain2, g_shift2, grad_up, g_up, grad_down, g_down,
        )

    wq = lax.all_gather(wq_own, "dp", axis=0, tiled=True)
    col = w_fc2.shape[1]
    both = jnp.concatenate([w_fc2, w_out], axis=0)
    if col % LANES == 0:
        parts = dp_n
        w_cols = lax.all_gather(both, "dp", axis=0, tiled=False)
    else:
        parts = 1
        w_cols = lax.all_gather(both, "dp", axis=1, tiled=True)[None]
    w_o = w_cols
    out_first = ff
    w1 = lax.all_gather(w_fc1, "dp", axis=0, tiled=True)
    packed = small_gather(jnp.concatenate([v.astype(f32) for v in small]), count, seq_n)
    packed = packed.reshape(count, ends[-1])
    gain1, shift1, bias_qv, bias_out, gain2, shift2, bias_up, bias_down = (
        packed[:, e - n : e].reshape(1, count * n) for e, n in zip(ends, sizes)
    )
    own_bias = lambda v, n: lax.dynamic_slice(v, (0, s * n), (1, n))
    own_up = own_bias(bias_up, ff)
    qkv_bias = jnp.concatenate(
        [
            own_bias(bias_qv[:, :width], inner),
            jnp.zeros((1, inner), f32),
            own_bias(bias_qv[:, width:], inner),
        ],
        axis=1,
    )
    x_pieces = spread(tokens)
    g_rows = jnp.stack(spread(after(grad_low, x_pieces[3])))
    h1, qkv = qkv_call(scal, x_pieces, wq, gain1, shift1, qkv_bias)
    o, lse = attend_call(scal, slopes, qkv, block)
    near, far = out_call(scal, o, w_o, out_first)
    got, across = reduce_rows(near, far)
    mid, h2 = mid_call(tokens, far, got, across, bias_out, gain2, shift2)
    h_pieces = spread(h2)
    y_near, y_far, d_near, d_far, a_all, du_all, h_all, g_all, up_sum = mlp_call(
        h_pieces, g_rows, w1, w_cols, own_up
    )
    got, across = reduce_rows(d_near, d_far)
    grad_down = outer_call(a_all, g_all, parts, "grad_fc2")
    grad_up = outer_call(h_all, du_all, 1, "grad_fc1")
    dmid, dbr, mid_sums = mid_back_call(mid, d_far, got, across, grad_low, gain2)

    b_pieces = spread(dbr)

    y_near = after(y_near, b_pieces[3])
    got, across = reduce_rows(y_near, y_far)
    output = (
        mid + ((y_far[1].astype(f32) + got[0].astype(f32)) + across.astype(f32) + bias_down)
    ).astype(bf16)

    do, grad_out = out_back_call(scal, b_pieces, o, w_o, out_first)
    dq, dk, dv = attend_back_call(scal, slopes, qkv, o, do, lse, block)
    near, far, merged, qkv_sums = qkv_back_call(scal, dq, dk, dv, wq)
    grad_qkv = outer_call(h1, merged, 1, "grad_qkv")

    def shared(part):
        if parts > 1:
            return lax.psum_scatter(part, "dp", scatter_dimension=0, tiled=False).astype(f32)
        return lax.psum_scatter(part, "dp", scatter_dimension=1, tiled=True).astype(f32)

    grad_down = shared(grad_down if parts > 1 else grad_down)
    grad_up = lax.psum_scatter(grad_up, "dp", scatter_dimension=0, tiled=True).astype(f32)
    got, across = reduce_rows(near, far)
    grad_tokens, in_sums = in_back_call(tokens, far, got, across, dmid, gain1)
    grad_out = shared(grad_out if parts > 1 else grad_out[0])
    grad_qkv = lax.psum_scatter(grad_qkv, "dp", scatter_dimension=0, tiled=True)
    grad_qkv = grad_qkv.astype(f32).reshape(w_qkv.shape)

    def own_slot(v, total):
        return lax.dynamic_update_slice(jnp.zeros((1, total), f32), v, (0, s * v.shape[1]))

    sums = (
        in_sums[0:1],
        in_sums[1:2],
        jnp.concatenate(
            [own_slot(qkv_sums[:, :inner], width), own_slot(qkv_sums[:, 2 * inner :], width)], axis=1
        ),
        mid_sums[2:3],
        mid_sums[0:1],
        mid_sums[1:2],
        own_slot(up_sum, seq_n * ff),
        mid_sums[3:4],
    )
    grads = jnp.concatenate([v.reshape(count, n) for v, n in zip(sums, sizes)], axis=1)
    grads = small_scatter(grads, count, seq_n).reshape(ends[-1])
    g_gain1, g_shift1, g_qv, g_bout, g_gain2, g_shift2, g_up, g_down = (
        grads[e - n : e] for e, n in zip(ends, sizes)
    )
    return (
        output,
        grad_tokens,
        g_gain1,
        g_shift1,
        grad_qkv,
        g_qv,
        grad_out,
        g_bout,
        g_gain2,
        g_shift2,
        grad_up,
        g_up,
        grad_down,
        g_down,
    )


def solution(mesh):
    rows = P(("dp", "seq"), None)
    vec = P(("dp", "seq"))
    merged = P("dp", None, "seq")
    return jax.shard_map(
        functools.partial(on_device, mesh.shape["dp"], mesh.shape["seq"]),
        mesh=mesh,
        in_specs=(
            rows, P("dp"), rows, vec, vec, merged, vec, P("seq", "dp"), vec, vec, vec,
            P("dp", "seq"), vec, P("seq", "dp"), vec,
        ),
        out_specs=(
            rows, rows, vec, vec, merged, vec, P("seq", "dp"), vec, vec, vec,
            P("dp", "seq"), vec, P("seq", "dp"), vec,
        ),
        check_vma=False,
    )
```

```python
import functools
import math

import jax
import jax.numpy as jnp
from jax import lax
from jax.experimental import pallas as pl
from jax.experimental.pallas import tpu as pltpu
from jax.sharding import PartitionSpec as P

HEAD_DIM = 64
EPS = 1e-05
GELU_COEF = 0.044715
NEG = -1e30
LANES = 128
VMEM_BYTES = 60 * 1024 * 1024

f32 = jnp.float32
bf16 = jnp.bfloat16
WHOLE = pl.BlockSpec(memory_space=pltpu.VMEM)
SCALAR = pl.BlockSpec(memory_space=pltpu.SMEM)


def mm(a, b):
    return jnp.dot(a, b, preferred_element_type=f32)


def mm_t(a, b):
    return lax.dot_general(a, b, (((1,), (1,)), ((), ())), preferred_element_type=f32)


def params(**kw):
    return pltpu.CompilerParams(vmem_limit_bytes=VMEM_BYTES, **kw)


def normalize(v):
    width = v.shape[-1]
    centred = v - jnp.sum(v, axis=-1, keepdims=True) * (1.0 / width)
    inv = lax.rsqrt(jnp.sum(centred * centred, axis=-1, keepdims=True) * (1.0 / width) + EPS)
    return centred * inv, inv


def norm_back(grad_out, gain, unit, inv):
    width = unit.shape[-1]
    scaled = grad_out * gain
    mean_one = jnp.sum(scaled, axis=-1, keepdims=True) * (1.0 / width)
    mean_two = jnp.sum(scaled * unit, axis=-1, keepdims=True) * (1.0 / width)
    return inv * (scaled - mean_one - unit * mean_two)


def device_of(index, seq_n):
    return (index // seq_n, index % seq_n)


def greet_all(me, count, seq_n):
    barrier = pltpu.get_barrier_semaphore()

    def hello(i, carry):
        peer = (me + i) % count
        pl.semaphore_signal(
            barrier, inc=1, device_id=device_of(peer, seq_n), device_id_type=pl.DeviceIdType.MESH
        )
        return carry

    lax.fori_loop(1, count, hello, 0)
    pl.semaphore_wait(barrier, count - 1)


def small_gather_body(count, seq_n, x_ref, out_ref, send_sem, recv_sem):
    me = lax.axis_index("dp") * seq_n + lax.axis_index("seq")
    greet_all(me, count, seq_n)

    def copy_to(i):
        peer = (me + i) % count
        return pltpu.make_async_remote_copy(
            src_ref=x_ref,
            dst_ref=out_ref.at[pl.ds(me, 1)],
            send_sem=send_sem.at[i],
            recv_sem=recv_sem.at[i],
            device_id=device_of(peer, seq_n),
            device_id_type=pl.DeviceIdType.MESH,
        )

    def begin(i, carry):
        copy_to(i).start()
        return carry

    def finish(i, carry):
        copy_to(i).wait()
        return carry

    lax.fori_loop(1, count, begin, 0)
    out_ref[pl.ds(me, 1)] = x_ref[...]
    lax.fori_loop(1, count, finish, 0)


def small_gather(x, count, seq_n):
    width = x.shape[-1]
    return pl.pallas_call(
        functools.partial(small_gather_body, count, seq_n),
        out_shape=jax.ShapeDtypeStruct((count, 1, width), f32),
        in_specs=[WHOLE],
        out_specs=WHOLE,
        scratch_shapes=[pltpu.SemaphoreType.DMA((count,)), pltpu.SemaphoreType.DMA((count,))],
        compiler_params=pltpu.CompilerParams(collective_id=1, has_side_effects=True),
        name="small_gather",
    )(x.reshape(1, 1, width))


def small_scatter_body(count, seq_n, v_ref, out_ref, land, send_sem, recv_sem):
    me = lax.axis_index("dp") * seq_n + lax.axis_index("seq")
    greet_all(me, count, seq_n)

    def copy_to(i):
        peer = (me + i) % count
        return pltpu.make_async_remote_copy(
            src_ref=v_ref.at[pl.ds(peer, 1)],
            dst_ref=land.at[pl.ds(i, 1)],
            send_sem=send_sem.at[i],
            recv_sem=recv_sem.at[i],
            device_id=device_of(peer, seq_n),
            device_id_type=pl.DeviceIdType.MESH,
        )

    def begin(i, carry):
        copy_to(i).start()
        return carry

    def finish(i, total):
        copy_to(i).wait()
        return total + land[pl.ds(i, 1)]

    lax.fori_loop(1, count, begin, 0)
    out_ref[...] = lax.fori_loop(1, count, finish, v_ref[pl.ds(me, 1)])


def small_scatter(v, count, seq_n):
    width = v.shape[-1]
    return pl.pallas_call(
        functools.partial(small_scatter_body, count, seq_n),
        out_shape=jax.ShapeDtypeStruct((1, 1, width), f32),
        in_specs=[WHOLE],
        out_specs=WHOLE,
        scratch_shapes=[
            pltpu.VMEM((count, 1, width), f32),
            pltpu.SemaphoreType.DMA((count,)),
            pltpu.SemaphoreType.DMA((count,)),
        ],
        compiler_params=pltpu.CompilerParams(collective_id=2, has_side_effects=True),
        name="small_scatter",
    )(v.reshape(count, 1, width))


def swap(x, bit):
    return lax.ppermute(x, "seq", [(i, i ^ bit) for i in range(4)])


def spread(own):
    far = swap(own, 2)
    return own, swap(own, 1), far, swap(far, 1)


def reduce_rows(near, far):
    got = swap(near, 1)
    across = swap(far[0] + got[1], 2)
    return got, across


def pick(step, refs, dest):
    for k, ref in enumerate(refs):

        @pl.when(step == k)
        def _(ref=ref):
            dest[...] = ref[...]


ORDER = (1, 3, 2, 0)


def rel_of(t):
    return jnp.where(t == 0, 1, jnp.where(t == 1, 3, jnp.where(t == 2, 2, 0)))


def qkv_body(scal, x0, x1, x2, x3, w, gain, shift, bias, h1, qkv, rows):
    pick(pl.program_id(0), (x0, x1, x2, x3), rows)
    unit, _ = normalize(rows[...].astype(f32))
    low = (unit * gain[...] + shift[...]).astype(bf16)
    h1[...] = low
    qkv[...] = (mm(low, w[...]) + bias[...]).astype(bf16)


def qkv_call(scal, pieces, w, gain, shift, bias):
    rows, width = pieces[0].shape
    cols = w.shape[1]
    out = lambda r, sc: (lax.bitwise_xor(sc[0], r), 0)
    return pl.pallas_call(
        qkv_body,
        out_shape=(
            jax.ShapeDtypeStruct((4 * rows, width), bf16),
            jax.ShapeDtypeStruct((4 * rows, cols), bf16),
        ),
        grid_spec=pltpu.PrefetchScalarGridSpec(
            num_scalar_prefetch=1,
            grid=(4,),
            in_specs=[WHOLE] * 8,
            out_specs=(pl.BlockSpec((rows, width), out), pl.BlockSpec((rows, cols), out)),
            scratch_shapes=[pltpu.VMEM((rows, width), bf16)],
        ),
        compiler_params=params(),
        name="qkv",
    )(scal, *pieces, w, gain, shift, bias)


def make_bias(scal, slopes, pair, bias, keys):
    pos = lax.broadcasted_iota(jnp.int32, (keys, LANES), 0)
    inside = pos < scal[1]
    ramp = pos.astype(f32)
    for h in range(2):
        bias[h] = jnp.where(inside, ramp * slopes[2 * pair + h], NEG)


def head_only(x, h):
    lane = lax.broadcasted_iota(jnp.int32, x.shape, 1)
    return jnp.where((lane >= h * HEAD_DIM) & (lane < (h + 1) * HEAD_DIM), x, jnp.zeros_like(x))


def score_t(k_ref, qm, bias, h, length):
    block = qm.shape[0]
    s = mm_t(k_ref[0:length, :], qm)
    b = bias[h, 0:length, :]
    s = s + jnp.concatenate([b] * (block // LANES), axis=1)
    key = lax.broadcasted_iota(jnp.int32, (block, block), 0)
    query = lax.broadcasted_iota(jnp.int32, (block, block), 1)
    last = jnp.where(key <= query, s[length - block :], NEG)
    if length == block:
        return last
    return jnp.concatenate([s[: length - block], last], axis=0)


def attend_body(scal, q, k, v, slopes, o, lse, bias, vt):
    pair, step = pl.program_id(0), pl.program_id(1)
    block = q.shape[0]
    keys = k.shape[0]

    @pl.when(step == 0)
    def _():
        make_bias(scal, slopes, pair, bias, keys)
        vt[...] = v[...].T

    for c in range(keys // block):

        @pl.when(step == c)
        def _(c=c):
            length = (c + 1) * block
            scaled = q[...] * bf16(HEAD_DIM**-0.5)
            outs, logs = [], []
            for h in range(2):
                s = score_t(k, head_only(scaled, h), bias, h, length)
                top = jnp.max(s, axis=0, keepdims=True)
                e = jnp.exp(s - top)
                total = jnp.sum(e, axis=0, keepdims=True)
                mixed = mm(vt[h * HEAD_DIM : (h + 1) * HEAD_DIM, 0:length], e.astype(bf16))
                outs.append(mixed / total)
                logs.append(top + jnp.log(total))
            o[...] = jnp.concatenate(outs, axis=0).T.astype(bf16)
            lse[0, 0:2, :] = jnp.concatenate(logs, axis=0)


def attend_call(scal, slopes, qkv, block):
    keys, cols = qkv.shape
    width = cols // 3
    pairs = width // LANES
    return pl.pallas_call(
        attend_body,
        out_shape=(
            jax.ShapeDtypeStruct((keys, width), bf16),
            jax.ShapeDtypeStruct((pairs, 8, keys), f32),
        ),
        grid_spec=pltpu.PrefetchScalarGridSpec(
            num_scalar_prefetch=1,
            grid=(pairs, keys // block),
            in_specs=[
                pl.BlockSpec((block, LANES), lambda p, c, sc: (c, p)),
                pl.BlockSpec((keys, LANES), lambda p, c, sc: (0, pairs + p)),
                pl.BlockSpec((keys, LANES), lambda p, c, sc: (0, 2 * pairs + p)),
                SCALAR,
            ],
            out_specs=(
                pl.BlockSpec((block, LANES), lambda p, c, sc: (c, p)),
                pl.BlockSpec((1, 8, block), lambda p, c, sc: (p, 0, c)),
            ),
            scratch_shapes=[
                pltpu.VMEM((2, keys, LANES), f32),
                pltpu.VMEM((LANES, keys), bf16),
            ],
        ),
        compiler_params=params(),
        name="attend",
    )(scal, qkv, qkv, qkv, slopes)


def attend_back_body(scal, q, k, v, o, do, lse, slopes, dq, dk, dv, bias, kt, dk_sum, dv_sum):
    pair, step = pl.program_id(0), pl.program_id(1)
    block = q.shape[0]
    keys = k.shape[0]
    scale = HEAD_DIM**-0.5

    @pl.when(step == 0)
    def _():
        make_bias(scal, slopes, pair, bias, keys)
        kt[...] = k[...].T
        dk_sum[...] = jnp.zeros_like(dk_sum)
        dv_sum[...] = jnp.zeros_like(dv_sum)

    for c in range(keys // block):

        @pl.when(step == c)
        def _(c=c):
            length = (c + 1) * block
            scaled = q[...] * bf16(scale)
            both = (do[...].astype(f32) * o[...].astype(f32)).T
            outs = []
            for h in range(2):
                qm = head_only(scaled, h)
                dom = head_only(do[...], h)
                dot_row = jnp.sum(both[h * HEAD_DIM : (h + 1) * HEAD_DIM], axis=0, keepdims=True)
                p = jnp.exp(score_t(k, qm, bias, h, length) - lse[0, h : h + 1, :])
                dp = mm_t(v[0:length, :], dom)
                ds = (p * (dp - dot_row)).astype(bf16)
                dv_sum[0:length, :] += mm(p.astype(bf16), dom)
                dk_sum[0:length, :] += mm(ds, qm)
                outs.append(mm(kt[h * HEAD_DIM : (h + 1) * HEAD_DIM, 0:length], ds))
            dq[...] = (jnp.concatenate(outs, axis=0).T * scale).astype(bf16)

    @pl.when(step == keys // block - 1)
    def _():
        dk[...] = dk_sum[...].astype(bf16)
        dv[...] = dv_sum[...].astype(bf16)


def attend_back_call(scal, slopes, qkv, o, do, lse, block):
    keys, cols = qkv.shape
    width = cols // 3
    pairs = width // LANES
    some = pl.BlockSpec((block, LANES), lambda p, c, sc: (c, p))
    full = pl.BlockSpec((keys, LANES), lambda p, c, sc: (0, p))
    return pl.pallas_call(
        attend_back_body,
        out_shape=(jax.ShapeDtypeStruct((keys, width), bf16),) * 3,
        grid_spec=pltpu.PrefetchScalarGridSpec(
            num_scalar_prefetch=1,
            grid=(pairs, keys // block),
            in_specs=[
                some,
                pl.BlockSpec((keys, LANES), lambda p, c, sc: (0, pairs + p)),
                pl.BlockSpec((keys, LANES), lambda p, c, sc: (0, 2 * pairs + p)),
                some,
                some,
                pl.BlockSpec((1, 8, block), lambda p, c, sc: (p, 0, c)),
                SCALAR,
            ],
            out_specs=(some, full, full),
            scratch_shapes=[
                pltpu.VMEM((2, keys, LANES), f32),
                pltpu.VMEM((LANES, keys), bf16),
                pltpu.VMEM((keys, LANES), f32),
                pltpu.VMEM((keys, LANES), f32),
            ],
        ),
        compiler_params=params(),
        name="attend_back",
    )(scal, qkv, qkv, qkv, o, do, lse, slopes)


def lay_columns(w_ref, first, dest):
    width = w_ref.shape[2]
    for d in range(w_ref.shape[0]):
        dest[:, d * width : (d + 1) * width] = w_ref[d, first : first + dest.shape[0], :]


def out_body(scal, o, w, near, far, flat, *, first):
    t = pl.program_id(0)

    @pl.when(t == 0)
    def _():
        lay_columns(w, first, flat)

    part = mm(o[...], flat[...]).astype(bf16)

    @pl.when(t < 2)
    def _():
        near[0] = part

    @pl.when(t >= 2)
    def _():
        far[0] = part


def near_map(t, *_):
    return (jnp.minimum(t, 1), 0, 0)


def far_map(t, *_):
    return (jnp.maximum(t - 2, 0), 0, 0)


def out_call(scal, o, w, first):
    keys, inner = o.shape
    rows = keys // 4
    width = w.shape[0] * w.shape[2]
    return pl.pallas_call(
        functools.partial(out_body, first=first),
        out_shape=(jax.ShapeDtypeStruct((2, rows, width), bf16),) * 2,
        grid_spec=pltpu.PrefetchScalarGridSpec(
            num_scalar_prefetch=1,
            grid=(4,),
            in_specs=[
                pl.BlockSpec((rows, inner), lambda t, sc: (lax.bitwise_xor(sc[0], rel_of(t)), 0)),
                WHOLE,
            ],
            out_specs=(
                pl.BlockSpec((1, rows, width), near_map),
                pl.BlockSpec((1, rows, width), far_map),
            ),
            scratch_shapes=[pltpu.VMEM((inner, width), bf16)],
        ),
        compiler_params=params(),
        name="out_proj",
    )(scal, o, w)


def mid_body(x, a, b, c, bias, gain, shift, mid, h2):
    value = x[...].astype(f32) + (
        (a[0].astype(f32) + b[0].astype(f32)) + c[...].astype(f32) + bias[...]
    )
    mid[...] = value
    unit, _ = normalize(value)
    h2[...] = (unit * gain[...] + shift[...]).astype(bf16)


def mid_call(x, a, b, c, bias, gain, shift):
    rows, width = x.shape
    one = pl.BlockSpec((rows // 2, width), lambda i: (i, 0))
    first = pl.BlockSpec((1, rows // 2, width), lambda i: (0, i, 0))
    second = pl.BlockSpec((1, rows // 2, width), lambda i: (1, i, 0))
    row = pl.BlockSpec((1, width), lambda i: (0, 0))
    return pl.pallas_call(
        mid_body,
        out_shape=(
            jax.ShapeDtypeStruct((rows, width), f32),
            jax.ShapeDtypeStruct((rows, width), bf16),
        ),
        grid=(2,),
        in_specs=[one, second, first, one, row, row, row],
        out_specs=(one, one),
        compiler_params=params(),
        name="mid_norm",
    )(x, a, b, c, bias, gain, shift)


def gelu_parts(u):
    root = math.sqrt(2.0 / math.pi)
    sq = u * u
    t = jnp.tanh(root * (u + GELU_COEF * (sq * u)))
    half = 0.5 * (1.0 + t)
    slope = half + 0.5 * u * (1.0 - t * t) * (root * (1.0 + 3.0 * GELU_COEF * sq))
    return u * half, slope


def mlp_body(
    h0, h1, h2, h3, g_rows, w1, w2, b1,
    y_near, y_far, d_near, d_far, a_all, du_all, h_all, g_all, bias_sum,
    flat, hb, gb,
):
    t = pl.program_id(0)

    @pl.when(t == 0)
    def _():
        lay_columns(w2, 0, flat)
        bias_sum[...] = jnp.zeros_like(bias_sum)

    pick(rel_of(t), (h0, h1, h2, h3), hb)
    gb[...] = g_rows[rel_of(t)]
    h_all[...] = hb[...]
    g_all[...] = gb[...]
    inner = w1.shape[1]
    chunk = 256
    for c in range(inner // chunk):
        cols = slice(c * chunk, (c + 1) * chunk)
        u = mm(hb[...], w1[:, cols]) + b1[:, cols]
        value, slope = gelu_parts(u)
        a_all[:, cols] = value.astype(bf16)
        du = (mm_t(gb[...], flat[cols, :]) * slope).astype(bf16)
        du_all[:, cols] = du
        bias_sum[:, cols] += jnp.sum(du.astype(f32), axis=0, keepdims=True)
    y = mm(a_all[...], flat[...]).astype(bf16)
    d = mm_t(du_all[...], w1[...]).astype(bf16)

    @pl.when(t < 2)
    def _():
        y_near[0] = y
        d_near[0] = d

    @pl.when(t >= 2)
    def _():
        y_far[0] = y
        d_far[0] = d


def mlp_call(h_pieces, g_rows, w1, w2, b1):
    rows, width = h_pieces[0].shape
    inner = w1.shape[1]
    pair = jax.ShapeDtypeStruct((2, rows, width), bf16)
    near = pl.BlockSpec((1, rows, width), near_map)
    far = pl.BlockSpec((1, rows, width), far_map)
    block = lambda n: pl.BlockSpec((rows, n), lambda t: (t, 0))
    return pl.pallas_call(
        mlp_body,
        out_shape=(
            pair,
            pair,
            pair,
            pair,
            jax.ShapeDtypeStruct((4 * rows, inner), bf16),
            jax.ShapeDtypeStruct((4 * rows, inner), bf16),
            jax.ShapeDtypeStruct((4 * rows, width), bf16),
            jax.ShapeDtypeStruct((4 * rows, width), bf16),
            jax.ShapeDtypeStruct((1, inner), f32),
        ),
        grid=(4,),
        in_specs=[WHOLE] * 8,
        out_specs=(
            near, far, near, far, block(inner), block(inner), block(width), block(width),
            pl.BlockSpec((1, inner), lambda t: (0, 0)),
        ),
        scratch_shapes=[
            pltpu.VMEM((inner, width), bf16),
            pltpu.VMEM((rows, width), bf16),
            pltpu.VMEM((rows, width), bf16),
        ],
        compiler_params=params(),
        name="mlp",
    )(*h_pieces, g_rows, w1, w2, b1)


def outer_body(left, right, out, turned, *, blocks):
    @pl.when(pl.program_id(0) == 0)
    def _():
        turned[...] = left[...].T

    part = mm(turned[...], right[...]).astype(bf16)
    if blocks:
        width = out.shape[2]
        for d in range(out.shape[0]):
            out[d] = part[:, d * width : (d + 1) * width]
    else:
        out[...] = part


def outer_call(left, right, parts, name):
    rows, m = left.shape
    n = right.shape[1]
    step = 256
    if parts > 1:
        width = n // parts
        out_shape = jax.ShapeDtypeStruct((parts, m, width), bf16)
        out_spec = pl.BlockSpec((step // width, m, width), lambda j: (j, 0, 0))
    else:
        out_shape = jax.ShapeDtypeStruct((m, n), bf16)
        out_spec = pl.BlockSpec((m, step), lambda j: (0, j))
    return pl.pallas_call(
        functools.partial(outer_body, blocks=parts > 1),
        out_shape=out_shape,
        grid=(n // step,),
        in_specs=[WHOLE, pl.BlockSpec((rows, step), lambda j: (0, j))],
        out_specs=out_spec,
        scratch_shapes=[pltpu.VMEM((m, rows), bf16)],
        compiler_params=params(),
        name=name,
    )(left, right)


def mid_back_body(mid, a, b, c, g, gain, dmid, dbr, sums):
    @pl.when(pl.program_id(0) == 0)
    def _():
        sums[...] = jnp.zeros_like(sums)

    unit, inv = normalize(mid[...])
    e = (a[0].astype(f32) + b[0].astype(f32)) + c[...].astype(f32)
    grad = g[...].astype(f32)
    value = grad + norm_back(e, gain[...], unit, inv)
    dmid[...] = value
    low = value.astype(bf16)
    dbr[...] = low
    sums[0:1, :] += jnp.sum(e * unit, axis=0, keepdims=True)
    sums[1:2, :] += jnp.sum(e, axis=0, keepdims=True)
    sums[2:3, :] += jnp.sum(low.astype(f32), axis=0, keepdims=True)
    sums[3:4, :] += jnp.sum(grad, axis=0, keepdims=True)


def mid_back_call(mid, a, b, c, g, gain):
    rows, width = mid.shape
    one = pl.BlockSpec((rows // 2, width), lambda i: (i, 0))
    first = pl.BlockSpec((1, rows // 2, width), lambda i: (0, i, 0))
    second = pl.BlockSpec((1, rows // 2, width), lambda i: (1, i, 0))
    row = pl.BlockSpec((1, width), lambda i: (0, 0))
    return pl.pallas_call(
        mid_back_body,
        out_shape=(
            jax.ShapeDtypeStruct((rows, width), f32),
            jax.ShapeDtypeStruct((rows, width), bf16),
            jax.ShapeDtypeStruct((8, width), f32),
        ),
        grid=(2,),
        in_specs=[one, second, first, one, one, row],
        out_specs=(one, one, pl.BlockSpec((8, width), lambda i: (0, 0))),
        compiler_params=params(),
        name="mid_back",
    )(mid, a, b, c, g, gain)


def out_back_body(scal, b0, b1, b2, b3, o, w, do, grad, flat, rows, total, *, first):
    r = pl.program_id(0)

    @pl.when(r == 0)
    def _():
        lay_columns(w, first, flat)
        total[...] = jnp.zeros_like(total)

    pick(r, (b0, b1, b2, b3), rows)
    do[...] = mm_t(rows[...], flat[...]).astype(bf16)
    total[...] += mm(o[...].T, rows[...])

    @pl.when(r == 3)
    def _():
        width = grad.shape[2]
        for d in range(grad.shape[0]):
            grad[d] = total[:, d * width : (d + 1) * width].astype(bf16)


def out_back_call(scal, pieces, o, w, first):
    rows, width = pieces[0].shape
    inner = o.shape[1]
    at = pl.BlockSpec((rows, inner), lambda r, sc: (lax.bitwise_xor(sc[0], r), 0))
    grad = (w.shape[0], inner, w.shape[2])
    return pl.pallas_call(
        functools.partial(out_back_body, first=first),
        out_shape=(jax.ShapeDtypeStruct(o.shape, bf16), jax.ShapeDtypeStruct(grad, bf16)),
        grid_spec=pltpu.PrefetchScalarGridSpec(
            num_scalar_prefetch=1,
            grid=(4,),
            in_specs=[WHOLE] * 4 + [at, WHOLE],
            out_specs=(at, pl.BlockSpec(grad, lambda r, sc: (0, 0, 0))),
            scratch_shapes=[
                pltpu.VMEM((inner, width), bf16),
                pltpu.VMEM((rows, width), bf16),
                pltpu.VMEM((inner, width), f32),
            ],
        ),
        compiler_params=params(),
        name="out_back",
    )(scal, *pieces, o, w)


def qkv_back_body(scal, dq, dk, dv, w, near, far, merged, sums):
    t = pl.program_id(0)

    @pl.when(t == 0)
    def _():
        sums[...] = jnp.zeros_like(sums)

    low = jnp.concatenate([dq[...], dk[...], dv[...]], axis=1)
    merged[...] = low
    part = mm_t(low, w[...]).astype(bf16)
    sums[...] += jnp.sum(low.astype(f32), axis=0, keepdims=True)

    @pl.when(t < 2)
    def _():
        near[0] = part

    @pl.when(t >= 2)
    def _():
        far[0] = part


def qkv_back_call(scal, dq, dk, dv, w):
    keys, inner = dq.shape
    rows = keys // 4
    width = w.shape[0]
    where = lambda t, sc: (lax.bitwise_xor(sc[0], rel_of(t)), 0)
    at = pl.BlockSpec((rows, inner), where)
    return pl.pallas_call(
        qkv_back_body,
        out_shape=(
            jax.ShapeDtypeStruct((2, rows, width), bf16),
            jax.ShapeDtypeStruct((2, rows, width), bf16),
            jax.ShapeDtypeStruct((keys, 3 * inner), bf16),
            jax.ShapeDtypeStruct((1, 3 * inner), f32),
        ),
        grid_spec=pltpu.PrefetchScalarGridSpec(
            num_scalar_prefetch=1,
            grid=(4,),
            in_specs=[at, at, at, WHOLE],
            out_specs=(
                pl.BlockSpec((1, rows, width), near_map),
                pl.BlockSpec((1, rows, width), far_map),
                pl.BlockSpec((rows, 3 * inner), where),
                pl.BlockSpec((1, 3 * inner), lambda t, sc: (0, 0)),
            ),
        ),
        compiler_params=params(),
        name="qkv_back",
    )(scal, dq, dk, dv, w)


def in_back_body(x, a, b, c, dmid, gain, grad, sums):
    @pl.when(pl.program_id(0) == 0)
    def _():
        sums[...] = jnp.zeros_like(sums)

    unit, inv = normalize(x[...].astype(f32))
    e = (a[0].astype(f32) + b[0].astype(f32)) + c[...].astype(f32)
    grad[...] = (dmid[...] + norm_back(e, gain[...], unit, inv)).astype(bf16)
    sums[0:1, :] += jnp.sum(e * unit, axis=0, keepdims=True)
    sums[1:2, :] += jnp.sum(e, axis=0, keepdims=True)


def in_back_call(x, a, b, c, dmid, gain):
    rows, width = x.shape
    one = pl.BlockSpec((rows // 2, width), lambda i: (i, 0))
    first = pl.BlockSpec((1, rows // 2, width), lambda i: (0, i, 0))
    second = pl.BlockSpec((1, rows // 2, width), lambda i: (1, i, 0))
    row = pl.BlockSpec((1, width), lambda i: (0, 0))
    return pl.pallas_call(
        in_back_body,
        out_shape=(
            jax.ShapeDtypeStruct((rows, width), bf16),
            jax.ShapeDtypeStruct((8, width), f32),
        ),
        grid=(2,),
        in_specs=[one, second, first, one, one, row],
        out_specs=(one, pl.BlockSpec((8, width), lambda i: (0, 0))),
        compiler_params=params(),
        name="in_back",
    )(x, a, b, c, dmid, gain)


def remote(src, dst, send, recv, dp, seq):
    return pltpu.make_async_remote_copy(
        src_ref=src,
        dst_ref=dst,
        send_sem=send,
        recv_sem=recv,
        device_id=(dp, seq),
        device_id_type=pl.DeviceIdType.MESH,
    )


def greet(peers):
    barrier = pltpu.get_barrier_semaphore()
    for dp, seq in peers:
        pl.semaphore_signal(
            barrier, inc=1, device_id=(dp, seq), device_id_type=pl.DeviceIdType.MESH
        )
    pl.semaphore_wait(barrier, len(peers))


class GradSum:
    def __init__(self, part, acc, landx, land, sems, dp, seq):
        self.part, self.landx, self.land, self.sems = part, landx, land, sems
        self.fetched = acc is not None
        self.acc = acc if self.fetched else landx
        self.seq, self.z, self.x = seq, dp // 2, dp % 2

    def cross(self, k):
        return remote(
            self.part.at[2 * k + (1 - self.x)],
            self.landx.at[k],
            self.sems.at[0, k],
            self.sems.at[1, k],
            2 * self.z + (1 - self.x),
            self.seq,
        )

    def fetch(self, k):
        return pltpu.make_async_copy(
            self.part.at[2 * k + self.x], self.acc.at[k], self.sems.at[6, k]
        )

    def right(self, b, first):
        return remote(
            self.acc.at[b] if first else self.land.at[b + 1],
            self.land.at[b + 1],
            self.sems.at[2, b],
            self.sems.at[3, b],
            2 * ((self.z + 1) % 4) + self.x,
            self.seq,
        )

    def left(self, b, first):
        return remote(
            self.acc.at[b] if first else self.land.at[b],
            self.land.at[b],
            self.sems.at[4, b],
            self.sems.at[5, b],
            2 * ((self.z + 3) % 4) + self.x,
            self.seq,
        )

    def start(self):
        for k in (3, 0, 2, 1):
            self.cross(k).start()
        if self.fetched:
            for k in range(4):
                self.fetch(k).start()

    def add_cross(self):
        for k in (3, 0, 2, 1):
            self.cross(k).wait_recv()
            if self.fetched:
                self.fetch(k).wait()
                own = self.acc[k].astype(f32)
            else:
                own = self.part[2 * k + self.x].astype(f32)
            self.acc[k] = (own + self.landx[k].astype(f32)).astype(bf16)

    def stage(self, k):
        @pl.when(self.z == k)
        def _():
            for b in range(3, k, -1):
                if k > 0:
                    self.right(b, False).wait_recv()
                    total = self.land[b + 1].astype(f32) + self.acc[b].astype(f32)
                    self.land[b + 1] = total.astype(bf16)
                self.right(b, k == 0).start()

        @pl.when(self.z == 3 - k)
        def _():
            for b in range(0, 3 - k):
                if k > 0:
                    self.left(b, False).wait_recv()
                    total = self.land[b].astype(f32) + self.acc[b].astype(f32)
                    self.land[b] = total.astype(bf16)
                self.left(b, k == 0).start()

    def finish(self, out):
        z = self.z
        out[...] = self.acc[z].astype(f32)

        @pl.when(z > 0)
        def _():
            self.right(z, False).wait_recv()
            out[...] += self.land[z + 1].astype(f32)

        @pl.when(z < 3)
        def _():
            self.left(z, False).wait_recv()
            out[...] += self.land[z].astype(f32)

    def drain(self):
        for k in range(4):
            self.cross(k).wait_send()
        for k in range(3):

            @pl.when(self.z == k)
            def _(k=k):
                for b in range(3, k, -1):
                    self.right(b, k == 0).wait_send()

            @pl.when(self.z == 3 - k)
            def _(k=k):
                for b in range(0, 3 - k):
                    self.left(b, k == 0).wait_send()

    @staticmethod
    def scratch(m, n, fetched=False):
        own = [pltpu.VMEM((4, m, n), bf16)] if fetched else []
        return own + [
            pltpu.VMEM((4, m, n), bf16),
            pltpu.VMEM((5, m, n), bf16),
            pltpu.SemaphoreType.DMA((7, 4)),
        ]


SMALL_ROWS = 16


class Gather:
    def __init__(self, own, slot, sems, dp, seq):
        self.own, self.slot, self.sems = own, slot, sems
        self.dp, self.seq, self.z, self.x = dp, seq, dp // 2, dp % 2

    def along(self, k, step, src=None):
        slot = self.slot(2 * k + self.x)
        return remote(
            slot if src is None else src,
            slot,
            self.sems.at[0 if step > 0 else 1, k],
            self.sems.at[3, k],
            2 * ((self.z + step + 4) % 4) + self.x,
            self.seq,
        )

    def over(self, k, src=None):
        slot = self.slot(2 * k + self.x)
        return remote(
            slot if src is None else src,
            slot,
            self.sems.at[2, k],
            self.sems.at[4, k],
            2 * self.z + (1 - self.x),
            self.seq,
        )

    def keep(self):
        return pltpu.make_async_copy(self.own, self.slot(self.dp), self.sems.at[5, 0])

    def start(self):
        z = self.z

        @pl.when(z < 3)
        def _():
            self.along(z, 1, self.own).start()

        @pl.when(z > 0)
        def _():
            self.along(z, -1, self.own).start()

        self.over(z, self.own).start()
        self.keep().start()

    def hop(self, dist):
        z = self.z

        @pl.when(z - dist >= 0)
        def _():
            k = z - dist
            self.along(k, 1).wait_recv()

            @pl.when(z < 3)
            def _():
                self.along(k, 1).start()

            self.over(k).start()

        @pl.when(z + dist <= 3)
        def _():
            k = z + dist
            self.along(k, -1).wait_recv()

            @pl.when(z > 0)
            def _():
                self.along(k, -1).start()

            self.over(k).start()

    def arrive(self):
        self.keep().wait()
        for k in range(4):
            self.over(k).wait_recv()

    def drain(self):
        z = self.z
        for k in range(4):
            self.over(k).wait_send()

            @pl.when((z < 3) & (z >= k))
            def _(k=k):
                self.along(k, 1).wait_send()

            @pl.when((z > 0) & (z <= k))
            def _(k=k):
                self.along(k, -1).wait_send()

    @staticmethod
    def scratch():
        return pltpu.SemaphoreType.DMA((6, 4))


class Spread:
    def __init__(self, own, rows, sems, dp, seq):
        mate, across = seq + 1 - 2 * (seq % 2), (seq + 2) % 4
        to = lambda src, r, peer: remote(src, rows.at[r], sems.at[0, r], sems.at[1, r], dp, peer)
        self.near, self.far = to(own, 1, mate), to(own, 2, across)
        self.last = to(rows.at[2], 3, mate)

    def start(self):
        self.far.start()
        self.near.start()

    def forward(self):
        self.far.wait_recv()
        self.last.start()

    def drain(self):
        for copy in (self.near, self.far, self.last):
            copy.wait_send()


def neighbours(seq):
    mate = seq + 1 - 2 * (seq % 2)
    return mate, (seq + 2) % 4, (mate + 2) % 4


def block_at(seq, rel):
    return 2 * ((seq // 2 + rel // 2) % 2) + (seq + rel) % 2


def scores(k, qm, ramp):
    block = qm.shape[0]
    length = k.shape[0]
    s = mm_t(k, qm) + jnp.concatenate([ramp] * (block // LANES), axis=1)
    key = lax.broadcasted_iota(jnp.int32, (block, block), 0)
    query = lax.broadcasted_iota(jnp.int32, (block, block), 1)
    last = jnp.where(key <= query, s[length - block :], NEG)
    if length == block:
        return last
    return jnp.concatenate([s[: length - block], last], axis=0)


def fore_body(
    scal, slopes, wq, wo, x, v_up, v_qv, v_g1, v_s1, v_out, v_g2, v_s2, v_down, g, w1, w2,
    h1, qkv_out, o, lse, wq_all, flat, mid, gain1, bias_down, y_all, gw1, gw2, dmid, dbr, sums,
    up_sum,
    small, vectors, shift1, bias_qkv, bias_out, gain2, shift2, bias_up,
    rows_in, g_rows, h_stage, qkv, ramp, vt, part, land_c, sum_y, land_y, w1_all, w2_flat,
    a_all, du_all, turned, y_stage, up_stage, down_stage,
    q_sem, o_sem, w1_sem, w2_sem, x_sem, g_sem, seq_sem, dp_sem, keep_sem, stage_sem, fwd, mlp, bwd,
):
    dp, seq = lax.axis_index("dp"), lax.axis_index("seq")
    mate, across, _ = neighbours(seq)
    greet([((dp + i) % 8, seq) for i in range(1, 8)] + [(dp, p) for p in neighbours(seq)])
    rows, width = x.shape
    keys = qkv.shape[0]
    inner = o.shape[1]
    pairs = inner // LANES
    ff = du_all.shape[1]
    half_rows = rows // 2
    halves = [slice(0, half_rows), slice(half_rows, rows)]
    column = lambda ref: lambda d: ref.at[:, pl.ds(pl.multiple_of(d * LANES, LANES), LANES)]

    gather_q = Gather(wq, lambda d: wq_all.at[d], q_sem, dp, seq)
    gather_o = Gather(wo, column(flat), o_sem, dp, seq)
    gathers = [
        Gather(w1, lambda d: w1_all.at[d], w1_sem, dp, seq),
        Gather(w2, column(w2_flat), w2_sem, dp, seq),
    ]
    spread_x = Spread(x, rows_in, x_sem, dp, seq)
    spread_g = Spread(g, g_rows, g_sem, dp, seq)
    at = 0
    for ref in (v_up, v_qv, v_g1, v_s1, v_out, v_g2, v_s2, v_down):
        small[:, at : at + ref.shape[1]] = ref[...].astype(f32)
        at += ref.shape[1]
    keep_v = pltpu.make_async_copy(small, vectors.at[dp, seq], keep_sem.at[0])
    keep_v.start()
    group = [
        remote(small, vectors.at[dp, seq], seq_sem.at[0, i], seq_sem.at[1, i], dp, peer)
        for i, peer in enumerate(neighbours(seq))
    ]
    for copy in group:
        copy.start()
    gather_q.start()
    spread_x.start()
    keep_x = pltpu.make_async_copy(x, rows_in.at[0], keep_sem.at[1])
    keep_g = pltpu.make_async_copy(g, g_rows.at[0], keep_sem.at[2])
    keep_x.start()
    keep_g.start()

    def to_dp(i):
        return remote(
            vectors.at[dp], vectors.at[dp], dp_sem.at[0, i], dp_sem.at[1, i], (dp + i) % 8, seq
        )

    keep_v.wait()
    for copy in group:
        copy.wait_recv()
    for i in range(1, 8):
        to_dp(i).start()
    gather_o.start()
    spread_g.start()
    gather_q.hop(1)
    gather_q.hop(2)
    gather_o.hop(1)
    gather_q.hop(3)
    gather_o.hop(2)
    spread_x.forward()
    gather_o.hop(3)
    for gather in gathers:
        gather.start()
    for i in range(1, 8):
        to_dp(i).wait_recv()
    for ref, at in (
        (gain1, 192), (shift1, 224), (bias_out, 256), (gain2, 288), (shift2, 320), (bias_down, 352),
    ):
        for d in range(8):
            ref[:, d * LANES : (d + 1) * LANES] = jnp.concatenate(
                [vectors[d, i, :, at : at + 32] for i in range(4)], axis=1
            )
    for section in range(2):
        for half in range(2):
            lane = section * 512 + half * LANES
            bias_qkv[:, lane : lane + LANES] = jnp.concatenate(
                [vectors[4 * section + seq, 2 * half + i, :, 128:192] for i in range(2)], axis=1
            )
    bias_qkv[:, 256:512] = jnp.zeros((1, 256), f32)
    for i in range(8):
        bias_up[:, i * LANES : (i + 1) * LANES] = vectors[2 * seq + i // 4, i % 4, :, 0:LANES]
    keep_x.wait()
    spread_x.near.wait_recv()
    gather_q.arrive()
    spread_x.last.wait_recv()
    spread_x.drain()

    def h1_copy(r):
        at = pl.ds(pl.multiple_of(block_at(seq, r) * rows, rows), rows)
        return pltpu.make_async_copy(h_stage.at[r % 2], h1.at[at], stage_sem.at[0, r % 2])

    def project(r, carry):
        @pl.when(r >= 2)
        def _():
            h1_copy(r - 2).wait()

        at = pl.ds(pl.multiple_of(block_at(seq, r) * rows, rows), rows)
        unit, _ = normalize(rows_in[r].astype(f32))
        low = (unit * gain1[...] + shift1[...]).astype(bf16)
        h_stage[r % 2] = low
        h1_copy(r).start()
        weight = wq_all[...].reshape(width, 3 * inner)
        qkv[at, :] = (mm(low, weight) + bias_qkv[...]).astype(bf16)
        return carry

    lax.fori_loop(0, 4, project, 0)
    qkv_copy = pltpu.make_async_copy(qkv, qkv_out, keep_sem.at[3])
    qkv_copy.start()
    for gather in gathers:
        gather.hop(1)
    spread_g.forward()
    pos = lax.broadcasted_iota(jnp.int32, (keys, LANES), 0)
    ramp[...] = jnp.where(pos < scal[1], pos.astype(f32), -1e33)
    for p in range(pairs):
        vt[p] = qkv[:, 2 * inner + p * LANES : 2 * inner + (p + 1) * LANES].T
    gather_o.arrive()

    def row_copies(sems):
        rel_one = remote(part.at[1], land_c.at[0], sems.at[0, 0], sems.at[1, 0], dp, mate)
        rel_three = [
            remote(
                part.at[3, at], land_c.at[1, at], sems.at[0, 1 + i], sems.at[1, 1 + i], dp, mate
            )
            for i, at in enumerate(halves)
        ]
        over = [
            remote(sum_y.at[at], land_y.at[at], sems.at[0, 3 + i], sems.at[1, 3 + i], dp, across)
            for i, at in enumerate(halves)
        ]
        return rel_one, rel_three, over

    def send_over(rel_three, over, i):
        rel_three[i].wait_recv()
        at = halves[i]
        total = part[2, at, :].astype(f32) + land_c[1, at, :].astype(f32)
        sum_y[at, :] = total.astype(bf16)
        over[i].start()

    rel_one, rel_three, over = row_copies(fwd)

    def attend(t, carry):
        rel = 3 - t
        c_now = block_at(seq, rel)
        at = pl.ds(pl.multiple_of(c_now * rows, rows), rows)
        for c in range(keys // rows):

            @pl.when(c_now == c)
            def _(c=c):
                length = (c + 1) * rows

                def one_pair(p, carry):
                    lane = pl.ds(pl.multiple_of(p * LANES, LANES), LANES)
                    k_lane = pl.ds(pl.multiple_of(inner + p * LANES, LANES), LANES)
                    scaled = qkv[c * rows : length, lane] * bf16(HEAD_DIM**-0.5)
                    k = qkv[0:length, k_lane]
                    outs, logs = [], []
                    for h in range(2):
                        bias = ramp[0:length, :] * slopes[2 * p + h]
                        s = scores(k, head_only(scaled, h), bias)
                        top = jnp.max(s, axis=0, keepdims=True)
                        e = jnp.exp(s - top)
                        total = jnp.sum(e, axis=0, keepdims=True)
                        half = vt[p, h * HEAD_DIM : (h + 1) * HEAD_DIM, 0:length]
                        outs.append(mm(half, e.astype(bf16)) / total)
                        logs.append(top + jnp.log(total))
                    o[c * rows : length, lane] = jnp.concatenate(outs, axis=0).T.astype(bf16)
                    lse[p, 0:2, c * rows : length] = jnp.concatenate(logs, axis=0)
                    return carry

                lax.fori_loop(0, pairs, one_pair, 0)

        part[rel] = mm(o[at, :], flat[...]).astype(bf16)

        @pl.when(t == 0)
        def _():
            for copy in rel_three:
                copy.start()

        @pl.when(t == 1)
        def _():
            send_over(rel_three, over, 0)
            send_over(rel_three, over, 1)
            for gather in gathers:
                gather.hop(2)

        @pl.when(t == 2)
        def _():
            rel_one.start()
            for gather in gathers:
                gather.hop(3)

        return carry

    lax.fori_loop(0, 4, attend, 0)
    gather_q.drain()
    gather_o.drain()
    rel_one.wait_recv()

    near, far, last = (
        [
            remote(
                rows_in.at[0 if r < 3 else 2, at], rows_in.at[r, at], mlp.at[0, 2 * k + i],
                mlp.at[1, 2 * k + i], dp, across if r == 2 else mate,
            )
            for i, at in enumerate(halves)
        ]
        for k, r in enumerate((1, 2, 3))
    )
    step_rows = 64

    def second_norm(i):
        over[i].wait_recv()

        def step(k, carry):
            at = pl.ds(pl.multiple_of(i * half_rows + k * step_rows, step_rows), step_rows)
            total = (part[0, at, :].astype(f32) + land_c[0, at, :].astype(f32)) + land_y[
                at, :
            ].astype(f32)
            value = rows_in[0, at, :].astype(f32) + (total + bias_out[...])
            mid[at, :] = value
            unit, _ = normalize(value)
            rows_in[0, at, :] = (unit * gain2[...] + shift2[...]).astype(bf16)
            return carry

        lax.fori_loop(0, half_rows // step_rows, step, 0)
        far[i].start()
        near[i].start()

    second_norm(0)
    up_sum[...] = jnp.zeros_like(up_sum)
    sums[...] = jnp.zeros_like(sums)
    keep_g.wait()
    spread_g.near.wait_recv()
    spread_g.last.wait_recv()
    spread_g.drain()
    for gather in gathers:
        gather.arrive()
    for copy in [rel_one] + rel_three:
        copy.wait_send()
    back_one, back_three, back_over = row_copies(bwd)
    chunk = 256

    def y_copy(i):
        rel, half = place(i)
        at = pl.ds(pl.multiple_of(half * half_rows, half_rows), half_rows)
        return pltpu.make_async_copy(y_stage.at[i % 2], y_all.at[rel, at], stage_sem.at[1, i % 2])

    def place(i):
        late = i // 4
        return late * (2 + i % 2) + (1 - late) * (i // 2), late * ((i // 2) % 2) + (1 - late) * (i % 2)

    def block(i, carry):
        rel, half = place(i)

        @pl.when(i == 1)
        def _():
            second_norm(1)

        for k in range(2):

            @pl.when(i == 2 + k)
            def _(k=k):
                near[k].wait_recv()

            @pl.when(i == 4 + 2 * k)
            def _(k=k):
                far[k].wait_recv()
                last[k].start()

            @pl.when(i == 5 + 2 * k)
            def _(k=k):
                last[k].wait_recv()

        @pl.when(i >= 2)
        def _():
            y_copy(i - 2).wait()

        inside = pl.ds(pl.multiple_of(half * half_rows, half_rows), half_rows)
        at = pl.ds(pl.multiple_of(rel * rows + half * half_rows, half_rows), half_rows)
        hidden = rows_in[rel, inside, :]
        grad = g_rows[rel, inside, :]
        up = w1_all[...].reshape(width, ff)
        for c in range(ff // chunk):
            cols = slice(c * chunk, (c + 1) * chunk)
            u = mm(hidden, up[:, cols]) + bias_up[:, cols]
            value, slope = gelu_parts(u)
            a_all[at, cols] = value.astype(bf16)
            du = (mm_t(grad, w2_flat[cols, :]) * slope).astype(bf16)
            du_all[at, cols] = du
            up_sum[:, cols] += jnp.sum(du.astype(f32), axis=0, keepdims=True)
        y_stage[i % 2] = mm(a_all[at, :], w2_flat[...]).astype(bf16)
        y_copy(i).start()
        part[rel, inside, :] = mm_t(du_all[at, :], up).astype(bf16)

        @pl.when(i == 3)
        def _():
            back_one.start()

        @pl.when(i == 5)
        def _():
            back_three[0].start()

        @pl.when(i == 6)
        def _():
            over[0].wait_send()
            over[1].wait_send()
            send_over(back_three, back_over, 0)

        @pl.when(i == 7)
        def _():
            back_three[1].start()

        return carry

    lax.fori_loop(0, 8, block, 0)

    def turn(load):
        def step(i, carry):
            turned[:, pl.ds(pl.multiple_of(i * rows, rows), rows)] = load(i).T
            return carry

        lax.fori_loop(0, 4, step, 0)

    def up_copy(j):
        cols = pl.ds(pl.multiple_of(j * chunk, chunk), chunk)
        return pltpu.make_async_copy(up_stage.at[j % 2], gw1.at[:, :, cols], stage_sem.at[2, j % 2])

    def down_copy(j):
        return pltpu.make_async_copy(
            down_stage.at[j % 2], gw2.at[pl.ds(2 * j, 2)], stage_sem.at[3, j % 2]
        )

    def outer_up(j, carry):
        @pl.when(j >= 2)
        def _():
            up_copy(j - 2).wait()

        cols = pl.ds(pl.multiple_of(j * chunk, chunk), chunk)
        value = mm(turned[...], du_all[:, cols]).astype(bf16)
        up_stage[j % 2] = value.reshape(8, width // 8, chunk)
        up_copy(j).start()
        return carry

    def outer_down(j, carry):
        @pl.when(j >= 2)
        def _():
            down_copy(j - 2).wait()

        cols = pl.ds(pl.multiple_of(j * chunk, chunk), chunk)
        right = g_rows[:, :, cols].reshape(4 * rows, chunk)
        value = mm(turned[...], right).astype(bf16)
        down_stage[j % 2, 0] = value[:, :LANES]
        down_stage[j % 2, 1] = value[:, LANES:]
        down_copy(j).start()
        return carry

    turn(lambda i: rows_in[i])
    send_over(back_three, back_over, 1)
    lax.fori_loop(0, ff // chunk, outer_up, 0)
    turn(lambda i: a_all[pl.ds(pl.multiple_of(i * rows, rows), rows), :])
    lax.fori_loop(0, width // chunk, outer_down, 0)

    back_one.wait_recv()

    def norm_step(k, carry):
        at = pl.ds(pl.multiple_of(k * step_rows, step_rows), step_rows)
        unit, inv = normalize(mid[at, :])
        e = (part[0, at, :].astype(f32) + land_c[0, at, :].astype(f32)) + land_y[at, :].astype(f32)
        grad = g_rows[0, at, :].astype(f32)
        value = grad + norm_back(e, gain2[...], unit, inv)
        dmid[at, :] = value
        low = value.astype(bf16)
        dbr[at, :] = low
        sums[0:1, :] += jnp.sum(e * unit, axis=0, keepdims=True)
        sums[1:2, :] += jnp.sum(e, axis=0, keepdims=True)
        sums[2:3, :] += jnp.sum(low.astype(f32), axis=0, keepdims=True)
        sums[3:4, :] += jnp.sum(grad, axis=0, keepdims=True)
        return carry

    steps = half_rows // step_rows
    back_over[0].wait_recv()
    lax.fori_loop(0, steps, norm_step, 0)
    back_over[1].wait_recv()
    lax.fori_loop(steps, 2 * steps, norm_step, 0)

    for copy in group + near + far + last + [back_one] + back_three + back_over:
        copy.wait_send()
    for i in range(1, 8):
        to_dp(i).wait_send()
    for gather in gathers:
        gather.drain()
    qkv_copy.wait()
    for k in range(2):
        h1_copy(2 + k).wait()
        y_copy(6 + k).wait()
        up_copy(ff // chunk - 2 + k).wait()
        down_copy(width // chunk - 2 + k).wait()


def fore_call(scal, slopes, wq, wo, x, small, g, w1, w2):
    rows, width = x.shape
    keys = 4 * rows
    inner, ff = wo.shape[0], w1.shape[1]
    pairs = inner // LANES
    count = sum(v.shape[0] for v in small)
    sem = pltpu.SemaphoreType.DMA
    shape = jax.ShapeDtypeStruct
    any_space = pl.BlockSpec(memory_space=pl.ANY)
    vec = lambda n: pltpu.VMEM((1, n), f32)
    block = lambda *lead: pltpu.VMEM((*lead, rows, width), bf16)
    return pl.pallas_call(
        fore_body,
        out_shape=(
            shape((keys, width), bf16),
            shape((keys, 3 * inner), bf16),
            shape((keys, inner), bf16),
            shape((pairs, 8, keys), f32),
            shape((8, *wq.shape), bf16),
            shape((inner, width), bf16),
            shape((rows, width), f32),
            shape((1, width), f32),
            shape((1, width), f32),
            shape((4, rows, width), bf16),
            shape((8, width // 8, ff), bf16),
            shape((8, ff, LANES), bf16),
            shape((rows, width), f32),
            shape((rows, width), bf16),
            shape((8, width), f32),
            shape((1, ff), f32),
        ),
        in_specs=[SCALAR, SCALAR] + [any_space] * 3 + [WHOLE] * 8 + [any_space] * 3,
        out_specs=(
            any_space, any_space, WHOLE, WHOLE, WHOLE, WHOLE, WHOLE, WHOLE, WHOLE,
            any_space, any_space, any_space, WHOLE, WHOLE, WHOLE, WHOLE,
        ),
        scratch_shapes=[
            vec(count),
            pltpu.VMEM((8, 4, 1, count), f32),
            vec(width), vec(3 * inner), vec(width), vec(width), vec(width), vec(ff),
            block(4),
            block(4),
            block(2),
            pltpu.VMEM((keys, 3 * inner), bf16),
            pltpu.VMEM((keys, LANES), f32),
            pltpu.VMEM((pairs, LANES, keys), bf16),
            block(4),
            block(2),
            block(),
            block(),
            pltpu.VMEM((8, *w1.shape), bf16),
            pltpu.VMEM((ff, width), bf16),
            pltpu.VMEM((keys, ff), bf16),
            pltpu.VMEM((keys, ff), bf16),
            pltpu.VMEM((width, keys), bf16),
            pltpu.VMEM((2, rows // 2, width), bf16),
            pltpu.VMEM((2, 8, width // 8, 256), bf16),
            pltpu.VMEM((2, 2, ff, LANES), bf16),
            Gather.scratch(), Gather.scratch(), Gather.scratch(), Gather.scratch(),
            sem((2, 4)), sem((2, 4)), sem((2, 3)), sem((2, 8)), sem((4,)), sem((4, 2)),
            sem((2, 5)), sem((2, 6)), sem((2, 5)),
        ],
        compiler_params=pltpu.CompilerParams(
            vmem_limit_bytes=67043328, collective_id=4, has_side_effects=True
        ),
        name="fore",
    )(scal, slopes, wq, wo, x, *(v.reshape(1, -1) for v in small), g, w1, w2)


def back_body(
    scal, slopes, dbr, o, flat, qkv, lse, wq, h1, gw1, gw2, y_all, mid, bias_down, x, dmid,
    gain1, mid_sums, up_sum,
    output, grad, gq_out, go_out, gw1_out, gw2_out, small_out,
    b_rows, y_far, do, go_sum, go_part, bias, kt, dk_sum, dv_sum, merged, qkv_sums, h_buf, turned,
    gq_part, land_c, sum_y, land_y, y_land_c, y_sum, y_land_y,
    a_acc, a_x, a_land, a_sem, b_acc, b_x, b_land, b_sem, o_x, o_land, o_sem,
    q0_x, q0_land, q0_sem, q1_x, q1_land, q1_sem, q2_x, q2_land, q2_sem,
    small, small_land, own, seq_land,
    b_row_sem, row_sems, y_sems, h_sem, small_sems, seq_sems, far_sem,
):
    dp, seq = lax.axis_index("dp"), lax.axis_index("seq")
    mate, across, far_mate = neighbours(seq)
    greet([((dp + i) % 8, seq) for i in range(1, 8)] + [(dp, p) for p in neighbours(seq)])
    rows, width = dbr.shape
    keys, inner = o.shape
    pairs = inner // LANES
    scale = HEAD_DIM**-0.5
    chunk = 128

    spread_b = Spread(dbr, b_rows, b_row_sem, dp, seq)
    spread_b.start()
    sum_a = GradSum(gw2, a_acc, a_x, a_land, a_sem, dp, seq)
    sum_b = GradSum(gw1, b_acc, b_x, b_land, b_sem, dp, seq)
    sum_o = GradSum(go_part, None, o_x, o_land, o_sem, dp, seq)
    sums_q = [
        GradSum(gq_part.at[0], None, q0_x, q0_land, q0_sem, dp, seq),
        GradSum(gq_part.at[1], None, q1_x, q1_land, q1_sem, dp, seq),
        GradSum(gq_part.at[2], None, q2_x, q2_land, q2_sem, dp, seq),
    ]
    sum_a.start()
    sum_b.start()
    y_cores = [
        remote(y_all.at[1 + 2 * k], y_land_c.at[k], y_sems.at[0, k], y_sems.at[1, k], dp, mate)
        for k in range(2)
    ]
    y_over = remote(y_sum, y_land_y, y_sems.at[0, 2], y_sems.at[1, 2], dp, across)
    cores = [
        remote(b_rows.at[r], land_c.at[k], row_sems.at[0, k], row_sems.at[1, k], dp, mate)
        for k, r in ((0, 1), (1, 3))
    ]
    over = remote(sum_y, land_y, row_sems.at[0, 2], row_sems.at[1, 2], dp, across)

    def fetch_h(i):
        at = pl.ds(pl.multiple_of(i * rows, rows), rows)
        return pltpu.make_async_copy(h1.at[at], h_buf.at[i % 2], h_sem.at[i % 2])

    fetch_h(0).start()
    fetch_h(1).start()
    y_fetch = [
        pltpu.make_async_copy(y_all.at[2 - 2 * k], y_far.at[k], far_sem.at[k]) for k in range(2)
    ]
    for copy in y_fetch:
        copy.start()
    go_sum[...] = jnp.zeros_like(go_sum)

    def out_back(r, carry):
        if r >= 2:
            spread_b.forward() if r == 2 else spread_b.last.wait_recv()
        if r == 1:
            spread_b.near.wait_recv()
        at = pl.ds(pl.multiple_of(block_at(seq, r) * rows, rows), rows)
        src = dbr if r == 0 else b_rows.at[r]
        do[at, :] = mm_t(src[...], flat[...]).astype(bf16)
        go_sum[...] += mm(o[at, :].T, src[...])
        return carry

    out_back(0, 0)
    y_cores[1].start()
    y_cores[0].start()
    out_back(1, 0)

    def turn(i, carry):
        fetch_h(i).wait()
        turned[:, pl.ds(pl.multiple_of(i * rows, rows), rows)] = h_buf[i % 2].T

        @pl.when(i < 2)
        def _():
            fetch_h(i + 2).start()

        return carry

    lax.fori_loop(0, 4, turn, 0)
    small[...] = jnp.zeros_like(small)
    for d in range(8):
        at = slice(d * LANES, (d + 1) * LANES)
        for row, src in ((4, 2), (5, 0), (6, 1), (11, 3)):
            small[d, row : row + 1, :] = mid_sums[src : src + 1, at]
    for i in range(8):
        at = slice(i * LANES, (i + 1) * LANES)
        small[pl.ds(2 * seq + i // 4, 1), 7 + i % 4, :] = up_sum[:, at]
    out_back(2, 0)
    y_cores[1].wait_recv()
    for copy in y_fetch:
        copy.wait()
    for i in range(rows // chunk):
        at = slice(i * chunk, (i + 1) * chunk)
        total = y_far[0, at, :].astype(f32) + y_land_c[1, at, :].astype(f32)
        y_sum[at, :] = total.astype(bf16)
    y_over.start()
    out_back(3, 0)
    for d in range(8):
        go_part[d] = go_sum[:, d * LANES : (d + 1) * LANES].astype(bf16)
    sum_o.start()
    sum_a.add_cross()
    sum_a.stage(0)

    def one_pair(p, carry):
        lane = pl.ds(pl.multiple_of(p * LANES, LANES), LANES)
        k_lane = pl.ds(pl.multiple_of(inner + p * LANES, LANES), LANES)
        v_lane = pl.ds(pl.multiple_of(2 * inner + p * LANES, LANES), LANES)
        pos = lax.broadcasted_iota(jnp.int32, (keys, LANES), 0)
        ramp = pos.astype(f32)
        inside = pos < scal[1]
        for h in range(2):
            bias[h] = jnp.where(inside, ramp * slopes[2 * p + h], NEG)
        kt[...] = qkv[:, k_lane].T
        dk_sum[...] = jnp.zeros_like(dk_sum)
        dv_sum[...] = jnp.zeros_like(dv_sum)
        for c in range(keys // rows):
            length = (c + 1) * rows
            at = slice(c * rows, length)
            scaled = qkv[at, lane] * bf16(scale)
            g = do[at, lane]
            both = (g.astype(f32) * o[at, lane].astype(f32)).T
            k = qkv[0:length, k_lane]
            v = qkv[0:length, v_lane]
            outs = []
            for h in range(2):
                half = slice(h * HEAD_DIM, (h + 1) * HEAD_DIM)
                qm = head_only(scaled, h)
                gm = head_only(g, h)
                dot_row = jnp.sum(both[half], axis=0, keepdims=True)
                log = lse[p, h : h + 1, at]
                e = jnp.exp(scores(k, qm, bias[h, 0:length, :]) - log)
                ds = (e * (mm_t(v, gm) - dot_row)).astype(bf16)
                dv_sum[0:length, :] += mm(e.astype(bf16), gm)
                dk_sum[0:length, :] += mm(ds, qm)
                outs.append(mm(kt[half, 0:length], ds))
            merged[at, lane] = (jnp.concatenate(outs, axis=0).T * scale).astype(bf16)
            if c == 2:

                @pl.when(p == 1)
                def _():
                    sum_a.stage(2)

        merged[:, k_lane] = dk_sum[...].astype(bf16)
        merged[:, v_lane] = dv_sum[...].astype(bf16)

        @pl.when(p == 0)
        def _():
            sum_a.stage(1)

        return carry

    lax.fori_loop(0, pairs, one_pair, 0)
    spread_b.drain()
    sum_b.add_cross()
    sum_b.stage(0)
    qkv_sums[...] = jnp.zeros_like(qkv_sums)

    def qkv_back(t, carry):
        rel = 3 - t
        at = pl.ds(pl.multiple_of(block_at(seq, rel) * rows, rows), rows)
        low = merged[at, :]
        b_rows[rel] = mm_t(low, wq[...]).astype(bf16)
        qkv_sums[...] += jnp.sum(low.astype(f32), axis=0, keepdims=True)

        @pl.when(t == 0)
        def _():
            cores[1].start()

        @pl.when(t == 1)
        def _():
            cores[1].wait_recv()
            for i in range(rows // chunk):
                at = slice(i * chunk, (i + 1) * chunk)
                total = b_rows[2, at, :].astype(f32) + land_c[1, at, :].astype(f32)
                sum_y[at, :] = total.astype(bf16)
            over.start()

        @pl.when(t == 2)
        def _():
            cores[0].start()

        return carry

    lax.fori_loop(0, 4, qkv_back, 0)
    for j in range(3):
        cols = slice(j * inner, (j + 1) * inner)
        value = mm(turned[...], merged[:, cols]).astype(bf16)
        gq_part[j] = value.reshape(8, width // 8, inner)
        sums_q[j].start()
        if j == 0:
            sum_o.add_cross()
            sum_o.stage(0)
            sum_b.stage(1)
    for i in range(2):
        at = slice(i * LANES, (i + 1) * LANES)
        small[pl.ds(seq, 1), 2 + i, :] = qkv_sums[:, at]
        at = slice((4 + i) * LANES, (5 + i) * LANES)
        small[pl.ds(4 + seq, 1), 2 + i, :] = qkv_sums[:, at]
    sum_a.finish(gw2_out)
    y_cores[0].wait_recv()
    y_over.wait_recv()

    def out_step(i, carry):
        at = pl.ds(pl.multiple_of(i * chunk, chunk), chunk)
        total = y_far[1, at, :].astype(f32) + y_land_c[0, at, :].astype(f32)
        total = total + y_land_y[at, :].astype(f32)
        output[at, :] = (mid[at, :] + (total + bias_down[...])).astype(bf16)
        return carry

    lax.fori_loop(0, rows // chunk, out_step, 0)
    sums_q[0].add_cross()
    sums_q[0].stage(0)
    sum_b.stage(2)
    sum_o.stage(1)
    cores[0].wait_recv()
    over.wait_recv()
    own[...] = jnp.zeros_like(own)
    qkv_gain = [jnp.zeros((1, width), f32), jnp.zeros((1, width), f32)]
    for i in range(rows // chunk):
        at = slice(i * chunk, (i + 1) * chunk)
        unit, inv = normalize(x[at, :].astype(f32))
        e = (b_rows[0, at, :].astype(f32) + land_c[0, at, :].astype(f32)) + land_y[
            at, :
        ].astype(f32)
        grad[at, :] = (dmid[at, :] + norm_back(e, gain1[...], unit, inv)).astype(bf16)
        qkv_gain[0] += jnp.sum(e * unit, axis=0, keepdims=True)
        qkv_gain[1] += jnp.sum(e, axis=0, keepdims=True)
    for d in range(8):
        at = slice(d * LANES, (d + 1) * LANES)
        small[d, 0:1, :] = qkv_gain[0][:, at]
        small[d, 1:2, :] = qkv_gain[1][:, at]

    def small_to(i):
        peer = (dp + i) % 8
        return remote(
            small.at[peer], small_land.at[i], small_sems.at[0, i], small_sems.at[1, i], peer, seq
        )

    for i in range(1, 8):
        small_to(i).start()
    sums_q[1].add_cross()
    sums_q[1].stage(0)
    sums_q[0].stage(1)
    sum_o.stage(2)
    sums_q[2].add_cross()
    sums_q[2].stage(0)
    sums_q[1].stage(1)
    sums_q[0].stage(2)
    total = small[dp]
    for i in range(1, 8):
        small_to(i).wait_recv()
        total = total + small_land[i]
    own[...] = total

    def seq_to(i, peer):
        return remote(own, seq_land.at[i], seq_sems.at[0, i], seq_sems.at[1, i], dp, peer)

    group = [seq_to(i, peer) for i, peer in enumerate(neighbours(seq))]
    for copy in group:
        copy.start()
    sums_q[2].stage(1)
    sums_q[1].stage(2)
    sums_q[2].stage(2)
    sum_b.finish(gw1_out)
    sum_o.finish(go_out)
    for copy in group:
        copy.wait_recv()
    small_out[...] = (own[...] + seq_land[0]) + (seq_land[1] + seq_land[2])
    for j in range(3):
        sums_q[j].finish(gq_out.at[:, j * inner : (j + 1) * inner])
    for copy in group + cores + y_cores + [over, y_over]:
        copy.wait_send()
    for i in range(1, 8):
        small_to(i).wait_send()
    for part in [sum_a, sum_b, sum_o] + sums_q:
        part.drain()


def back_call(*args):
    dbr, o, wo, qkv, lse, wq, h1, gw1, gw2 = args[2:11]
    rows, width = dbr.shape
    keys, inner = o.shape
    sem = pltpu.SemaphoreType.DMA
    block = lambda dtype: pltpu.VMEM((rows, width), dtype)
    pair_rows = pltpu.VMEM((2, rows, width), bf16)
    any_space = pl.BlockSpec(memory_space=pl.ANY)
    specs = [SCALAR, SCALAR] + [WHOLE] * (len(args) - 2)
    for at in (8, 9, 10, 11):
        specs[at] = any_space
    shape = jax.ShapeDtypeStruct
    return pl.pallas_call(
        back_body,
        out_shape=(
            shape((rows, width), bf16),
            shape((rows, width), bf16),
            shape((width // 8, 3 * inner), f32),
            shape((inner, LANES), f32),
            shape(gw1.shape[1:], f32),
            shape(gw2.shape[1:], f32),
            shape((SMALL_ROWS, LANES), f32),
        ),
        in_specs=specs,
        out_specs=(WHOLE,) * 7,
        scratch_shapes=[
            pltpu.VMEM((4, rows, width), bf16),
            pair_rows,
            pltpu.VMEM((keys, inner), bf16),
            pltpu.VMEM((inner, width), f32),
            pltpu.VMEM((8, inner, LANES), bf16),
            pltpu.VMEM((2, keys, LANES), f32),
            pltpu.VMEM((LANES, keys), bf16),
            pltpu.VMEM((keys, LANES), f32),
            pltpu.VMEM((keys, LANES), f32),
            pltpu.VMEM((keys, 3 * inner), bf16),
            pltpu.VMEM((1, 3 * inner), f32),
            pair_rows,
            pltpu.VMEM((width, keys), bf16),
            pltpu.VMEM((3, 8, width // 8, inner), bf16),
            pair_rows, block(bf16), block(bf16),
            pair_rows, block(bf16), block(bf16),
            *GradSum.scratch(*gw2.shape[1:], fetched=True),
            *GradSum.scratch(*gw1.shape[1:], fetched=True),
            *GradSum.scratch(inner, LANES),
            *(GradSum.scratch(width // 8, inner) * 3),
            pltpu.VMEM((8, SMALL_ROWS, LANES), f32),
            pltpu.VMEM((8, SMALL_ROWS, LANES), f32),
            pltpu.VMEM((SMALL_ROWS, LANES), f32),
            pltpu.VMEM((3, SMALL_ROWS, LANES), f32),
            sem((2, 4)), sem((2, 3)), sem((2, 3)), sem((2,)), sem((2, 8)), sem((2, 3)), sem((2,)),
        ],
        compiler_params=pltpu.CompilerParams(
            vmem_limit_bytes=67043328, collective_id=3, has_side_effects=True
        ),
        name="back",
    )(*args)


def finish_body(
    scal, output, grad, gq, go, gw1, gw2, small,
    output_out, grad_out, gq_out, go_out, gw1_out, gw2_out,
    gain1, shift1, qv, bout, gain2, shift2, up, down,
):
    seq = scal[0]
    output_out[...] = output[...]
    grad_out[...] = grad[...]
    go_out[...] = go[...]
    gw1_out[...] = gw1[...]
    gw2_out[...] = gw2[...]
    cols = gq_out.shape[2]
    for c in range(3):
        gq_out[:, c, :] = gq[:, c * cols : (c + 1) * cols]
    for ref, row in ((gain1, 0), (shift1, 1), (bout, 4), (gain2, 5), (shift2, 6), (down, 11)):
        n = ref.shape[1]
        value = small[row : row + 1, 0:n]
        for i in range(1, 4):
            value = jnp.where(seq == i, small[row : row + 1, i * n : (i + 1) * n], value)
        ref[...] = value
    value = small[2:3, 0:64]
    for i in range(1, 4):
        at = 64 * (i % 2)
        value = jnp.where(seq == i, small[2 + i // 2 : 3 + i // 2, at : at + 64], value)
    qv[...] = value
    up[...] = small[pl.ds(7 + seq, 1), :]


def finish_call(scal, output, grad, gq, go, gw1, gw2, small):
    one = lambda n: jax.ShapeDtypeStruct((1, n), f32)
    like = lambda v: jax.ShapeDtypeStruct(v.shape, v.dtype)
    return pl.pallas_call(
        finish_body,
        out_shape=(
            like(output), like(grad),
            jax.ShapeDtypeStruct((gq.shape[0], 3, gq.shape[1] // 3), f32),
            like(go), like(gw1), like(gw2),
            one(32), one(32), one(64), one(32), one(32), one(32), one(LANES), one(32),
        ),
        in_specs=[SCALAR] + [WHOLE] * 7,
        out_specs=(WHOLE,) * 14,
        compiler_params=params(),
        name="finish",
    )(scal, output, grad, gq, go, gw1, gw2, small)


def after(value, *others):
    return lax.optimization_barrier((value, *others))[0]


def on_device(
    dp_n,
    seq_n,
    tokens,
    lengths,
    cotangent,
    ln1_gain,
    ln1_shift,
    w_qkv,
    b_qv,
    w_out,
    b_out,
    ln2_gain,
    ln2_shift,
    w_fc1,
    b_fc1,
    w_fc2,
    b_fc2,
):
    count = dp_n * seq_n
    rows, width = tokens.shape
    heads = width // HEAD_DIM
    inner = w_out.shape[0]
    ff = w_fc1.shape[1]
    s = lax.axis_index("seq")
    length = lengths[0]

    scal = jnp.stack([s.astype(jnp.int32), length])
    slopes = 2.0 ** (-8.0 * (jnp.arange(heads, dtype=jnp.int32) + 1).astype(f32) / heads)
    slopes = lax.dynamic_slice(slopes, (s * (heads // seq_n),), (heads // seq_n,))
    valid = s * rows + jnp.arange(rows, dtype=jnp.int32) < length
    grad_low = jnp.where(valid[:, None], cotangent, jnp.zeros_like(cotangent))
    wq_own = jnp.concatenate([w_qkv[:, c, :] for c in range(3)], axis=1)
    small = (ln1_gain, ln1_shift, b_qv, b_out, ln2_gain, ln2_shift, b_fc1, b_fc2)
    sizes = [v.shape[0] for v in small]
    ends = [sum(sizes[: i + 1]) for i in range(len(sizes))]
    block = 384
    fast = dp_n == 8 and seq_n == 4 and width == 8 * LANES and ff == width and inner == 2 * LANES
    if fast:
        parts = dp_n
        order = (b_fc1, b_qv, ln1_gain, ln1_shift, b_out, ln2_gain, ln2_shift, b_fc2)
        (
            h1, qkv, o, lse, wq, w_o, mid, gain1, bias_down, y_all, grad_up, grad_down, dmid, dbr,
            mid_sums, up_sum,
        ) = fore_call(scal, slopes, wq_own, w_out, tokens, order, grad_low, w_fc1, w_fc2)
        results = back_call(
            scal, slopes, dbr, o, w_o, qkv, lse, wq.reshape(width, 3 * inner), h1, grad_up,
            grad_down, y_all, mid, bias_down, tokens, dmid, gain1, mid_sums, up_sum,
        )
        output, grad_tokens, grad_qkv, grad_out, grad_up, grad_down, *vectors = finish_call(
            scal, *results
        )
        g_gain1, g_shift1, g_qv, g_bout, g_gain2, g_shift2, g_up, g_down = (
            v.reshape(n) for v, n in zip(vectors, sizes)
        )
        return (
            output, grad_tokens, g_gain1, g_shift1, grad_qkv, g_qv, grad_out, g_bout,
            g_gain2, g_shift2, grad_up, g_up, grad_down, g_down,
        )

    wq = lax.all_gather(wq_own, "dp", axis=0, tiled=True)
    col = w_fc2.shape[1]
    both = jnp.concatenate([w_fc2, w_out], axis=0)
    if col % LANES == 0:
        parts = dp_n
        w_cols = lax.all_gather(both, "dp", axis=0, tiled=False)
    else:
        parts = 1
        w_cols = lax.all_gather(both, "dp", axis=1, tiled=True)[None]
    w_o = w_cols
    out_first = ff
    w1 = lax.all_gather(w_fc1, "dp", axis=0, tiled=True)
    packed = small_gather(jnp.concatenate([v.astype(f32) for v in small]), count, seq_n)
    packed = packed.reshape(count, ends[-1])
    gain1, shift1, bias_qv, bias_out, gain2, shift2, bias_up, bias_down = (
        packed[:, e - n : e].reshape(1, count * n) for e, n in zip(ends, sizes)
    )
    own_bias = lambda v, n: lax.dynamic_slice(v, (0, s * n), (1, n))
    own_up = own_bias(bias_up, ff)
    qkv_bias = jnp.concatenate(
        [
            own_bias(bias_qv[:, :width], inner),
            jnp.zeros((1, inner), f32),
            own_bias(bias_qv[:, width:], inner),
        ],
        axis=1,
    )
    x_pieces = spread(tokens)
    g_rows = jnp.stack(spread(after(grad_low, x_pieces[3])))
    h1, qkv = qkv_call(scal, x_pieces, wq, gain1, shift1, qkv_bias)
    o, lse = attend_call(scal, slopes, qkv, block)
    near, far = out_call(scal, o, w_o, out_first)
    got, across = reduce_rows(near, far)
    mid, h2 = mid_call(tokens, far, got, across, bias_out, gain2, shift2)
    h_pieces = spread(h2)
    y_near, y_far, d_near, d_far, a_all, du_all, h_all, g_all, up_sum = mlp_call(
        h_pieces, g_rows, w1, w_cols, own_up
    )
    got, across = reduce_rows(d_near, d_far)
    grad_down = outer_call(a_all, g_all, parts, "grad_fc2")
    grad_up = outer_call(h_all, du_all, 1, "grad_fc1")
    dmid, dbr, mid_sums = mid_back_call(mid, d_far, got, across, grad_low, gain2)

    b_pieces = spread(dbr)

    y_near = after(y_near, b_pieces[3])
    got, across = reduce_rows(y_near, y_far)
    output = (
        mid + ((y_far[1].astype(f32) + got[0].astype(f32)) + across.astype(f32) + bias_down)
    ).astype(bf16)

    do, grad_out = out_back_call(scal, b_pieces, o, w_o, out_first)
    dq, dk, dv = attend_back_call(scal, slopes, qkv, o, do, lse, block)
    near, far, merged, qkv_sums = qkv_back_call(scal, dq, dk, dv, wq)
    grad_qkv = outer_call(h1, merged, 1, "grad_qkv")

    def shared(part):
        if parts > 1:
            return lax.psum_scatter(part, "dp", scatter_dimension=0, tiled=False).astype(f32)
        return lax.psum_scatter(part, "dp", scatter_dimension=1, tiled=True).astype(f32)

    grad_down = shared(grad_down if parts > 1 else grad_down)
    grad_up = lax.psum_scatter(grad_up, "dp", scatter_dimension=0, tiled=True).astype(f32)
    got, across = reduce_rows(near, far)
    grad_tokens, in_sums = in_back_call(tokens, far, got, across, dmid, gain1)
    grad_out = shared(grad_out if parts > 1 else grad_out[0])
    grad_qkv = lax.psum_scatter(grad_qkv, "dp", scatter_dimension=0, tiled=True)
    grad_qkv = grad_qkv.astype(f32).reshape(w_qkv.shape)

    def own_slot(v, total):
        return lax.dynamic_update_slice(jnp.zeros((1, total), f32), v, (0, s * v.shape[1]))

    sums = (
        in_sums[0:1],
        in_sums[1:2],
        jnp.concatenate(
            [own_slot(qkv_sums[:, :inner], width), own_slot(qkv_sums[:, 2 * inner :], width)], axis=1
        ),
        mid_sums[2:3],
        mid_sums[0:1],
        mid_sums[1:2],
        own_slot(up_sum, seq_n * ff),
        mid_sums[3:4],
    )
    grads = jnp.concatenate([v.reshape(count, n) for v, n in zip(sums, sizes)], axis=1)
    grads = small_scatter(grads, count, seq_n).reshape(ends[-1])
    g_gain1, g_shift1, g_qv, g_bout, g_gain2, g_shift2, g_up, g_down = (
        grads[e - n : e] for e, n in zip(ends, sizes)
    )
    return (
        output,
        grad_tokens,
        g_gain1,
        g_shift1,
        grad_qkv,
        g_qv,
        grad_out,
        g_bout,
        g_gain2,
        g_shift2,
        grad_up,
        g_up,
        grad_down,
        g_down,
    )


def solution(mesh):
    rows = P(("dp", "seq"), None)
    vec = P(("dp", "seq"))
    merged = P("dp", None, "seq")
    return jax.shard_map(
        functools.partial(on_device, mesh.shape["dp"], mesh.shape["seq"]),
        mesh=mesh,
        in_specs=(
            rows, P("dp"), rows, vec, vec, merged, vec, P("seq", "dp"), vec, vec, vec,
            P("dp", "seq"), vec, P("seq", "dp"), vec,
        ),
        out_specs=(
            rows, rows, vec, vec, merged, vec, P("seq", "dp"), vec, vec, vec,
            P("dp", "seq"), vec, P("seq", "dp"), vec,
        ),
        check_vma=False,
    )
```

```python
import functools
import math

import jax
import jax.numpy as jnp
from jax import lax
from jax.experimental import pallas as pl
from jax.experimental.pallas import tpu as pltpu
from jax.sharding import PartitionSpec as P

HEAD_DIM = 64
EPS = 1e-05
GELU_COEF = 0.044715
NEG = -1e30
LANES = 128
VMEM_BYTES = 60 * 1024 * 1024

f32 = jnp.float32
bf16 = jnp.bfloat16
WHOLE = pl.BlockSpec(memory_space=pltpu.VMEM)
SCALAR = pl.BlockSpec(memory_space=pltpu.SMEM)


def mm(a, b):
    return jnp.dot(a, b, preferred_element_type=f32)


def mm_t(a, b):
    return lax.dot_general(a, b, (((1,), (1,)), ((), ())), preferred_element_type=f32)


def params(**kw):
    return pltpu.CompilerParams(vmem_limit_bytes=VMEM_BYTES, **kw)


def normalize(v):
    width = v.shape[-1]
    centred = v - jnp.sum(v, axis=-1, keepdims=True) * (1.0 / width)
    inv = lax.rsqrt(jnp.sum(centred * centred, axis=-1, keepdims=True) * (1.0 / width) + EPS)
    return centred * inv, inv


def norm_back(grad_out, gain, unit, inv):
    width = unit.shape[-1]
    scaled = grad_out * gain
    mean_one = jnp.sum(scaled, axis=-1, keepdims=True) * (1.0 / width)
    mean_two = jnp.sum(scaled * unit, axis=-1, keepdims=True) * (1.0 / width)
    return inv * (scaled - mean_one - unit * mean_two)


def device_of(index, seq_n):
    return (index // seq_n, index % seq_n)


def greet_all(me, count, seq_n):
    barrier = pltpu.get_barrier_semaphore()

    def hello(i, carry):
        peer = (me + i) % count
        pl.semaphore_signal(
            barrier, inc=1, device_id=device_of(peer, seq_n), device_id_type=pl.DeviceIdType.MESH
        )
        return carry

    lax.fori_loop(1, count, hello, 0)
    pl.semaphore_wait(barrier, count - 1)


def small_gather_body(count, seq_n, x_ref, out_ref, send_sem, recv_sem):
    me = lax.axis_index("dp") * seq_n + lax.axis_index("seq")
    greet_all(me, count, seq_n)

    def copy_to(i):
        peer = (me + i) % count
        return pltpu.make_async_remote_copy(
            src_ref=x_ref,
            dst_ref=out_ref.at[pl.ds(me, 1)],
            send_sem=send_sem.at[i],
            recv_sem=recv_sem.at[i],
            device_id=device_of(peer, seq_n),
            device_id_type=pl.DeviceIdType.MESH,
        )

    def begin(i, carry):
        copy_to(i).start()
        return carry

    def finish(i, carry):
        copy_to(i).wait()
        return carry

    lax.fori_loop(1, count, begin, 0)
    out_ref[pl.ds(me, 1)] = x_ref[...]
    lax.fori_loop(1, count, finish, 0)


def small_gather(x, count, seq_n):
    width = x.shape[-1]
    return pl.pallas_call(
        functools.partial(small_gather_body, count, seq_n),
        out_shape=jax.ShapeDtypeStruct((count, 1, width), f32),
        in_specs=[WHOLE],
        out_specs=WHOLE,
        scratch_shapes=[pltpu.SemaphoreType.DMA((count,)), pltpu.SemaphoreType.DMA((count,))],
        compiler_params=pltpu.CompilerParams(collective_id=1, has_side_effects=True),
        name="small_gather",
    )(x.reshape(1, 1, width))


def small_scatter_body(count, seq_n, v_ref, out_ref, land, send_sem, recv_sem):
    me = lax.axis_index("dp") * seq_n + lax.axis_index("seq")
    greet_all(me, count, seq_n)

    def copy_to(i):
        peer = (me + i) % count
        return pltpu.make_async_remote_copy(
            src_ref=v_ref.at[pl.ds(peer, 1)],
            dst_ref=land.at[pl.ds(i, 1)],
            send_sem=send_sem.at[i],
            recv_sem=recv_sem.at[i],
            device_id=device_of(peer, seq_n),
            device_id_type=pl.DeviceIdType.MESH,
        )

    def begin(i, carry):
        copy_to(i).start()
        return carry

    def finish(i, total):
        copy_to(i).wait()
        return total + land[pl.ds(i, 1)]

    lax.fori_loop(1, count, begin, 0)
    out_ref[...] = lax.fori_loop(1, count, finish, v_ref[pl.ds(me, 1)])


def small_scatter(v, count, seq_n):
    width = v.shape[-1]
    return pl.pallas_call(
        functools.partial(small_scatter_body, count, seq_n),
        out_shape=jax.ShapeDtypeStruct((1, 1, width), f32),
        in_specs=[WHOLE],
        out_specs=WHOLE,
        scratch_shapes=[
            pltpu.VMEM((count, 1, width), f32),
            pltpu.SemaphoreType.DMA((count,)),
            pltpu.SemaphoreType.DMA((count,)),
        ],
        compiler_params=pltpu.CompilerParams(collective_id=2, has_side_effects=True),
        name="small_scatter",
    )(v.reshape(count, 1, width))


def swap(x, bit):
    return lax.ppermute(x, "seq", [(i, i ^ bit) for i in range(4)])


def spread(own):
    far = swap(own, 2)
    return own, swap(own, 1), far, swap(far, 1)


def reduce_rows(near, far):
    got = swap(near, 1)
    across = swap(far[0] + got[1], 2)
    return got, across


def pick(step, refs, dest):
    for k, ref in enumerate(refs):

        @pl.when(step == k)
        def _(ref=ref):
            dest[...] = ref[...]


ORDER = (1, 3, 2, 0)


def rel_of(t):
    return jnp.where(t == 0, 1, jnp.where(t == 1, 3, jnp.where(t == 2, 2, 0)))


def qkv_body(scal, x0, x1, x2, x3, w, gain, shift, bias, h1, qkv, rows):
    pick(pl.program_id(0), (x0, x1, x2, x3), rows)
    unit, _ = normalize(rows[...].astype(f32))
    low = (unit * gain[...] + shift[...]).astype(bf16)
    h1[...] = low
    qkv[...] = (mm(low, w[...]) + bias[...]).astype(bf16)


def qkv_call(scal, pieces, w, gain, shift, bias):
    rows, width = pieces[0].shape
    cols = w.shape[1]
    out = lambda r, sc: (lax.bitwise_xor(sc[0], r), 0)
    return pl.pallas_call(
        qkv_body,
        out_shape=(
            jax.ShapeDtypeStruct((4 * rows, width), bf16),
            jax.ShapeDtypeStruct((4 * rows, cols), bf16),
        ),
        grid_spec=pltpu.PrefetchScalarGridSpec(
            num_scalar_prefetch=1,
            grid=(4,),
            in_specs=[WHOLE] * 8,
            out_specs=(pl.BlockSpec((rows, width), out), pl.BlockSpec((rows, cols), out)),
            scratch_shapes=[pltpu.VMEM((rows, width), bf16)],
        ),
        compiler_params=params(),
        name="qkv",
    )(scal, *pieces, w, gain, shift, bias)


def make_bias(scal, slopes, pair, bias, keys):
    pos = lax.broadcasted_iota(jnp.int32, (keys, LANES), 0)
    inside = pos < scal[1]
    ramp = pos.astype(f32)
    for h in range(2):
        bias[h] = jnp.where(inside, ramp * slopes[2 * pair + h], NEG)


def head_only(x, h):
    lane = lax.broadcasted_iota(jnp.int32, x.shape, 1)
    return jnp.where((lane >= h * HEAD_DIM) & (lane < (h + 1) * HEAD_DIM), x, jnp.zeros_like(x))


def score_t(k_ref, qm, bias, h, length):
    block = qm.shape[0]
    s = mm_t(k_ref[0:length, :], qm)
    b = bias[h, 0:length, :]
    s = s + jnp.concatenate([b] * (block // LANES), axis=1)
    key = lax.broadcasted_iota(jnp.int32, (block, block), 0)
    query = lax.broadcasted_iota(jnp.int32, (block, block), 1)
    last = jnp.where(key <= query, s[length - block :], NEG)
    if length == block:
        return last
    return jnp.concatenate([s[: length - block], last], axis=0)


def attend_body(scal, q, k, v, slopes, o, lse, bias, vt):
    pair, step = pl.program_id(0), pl.program_id(1)
    block = q.shape[0]
    keys = k.shape[0]

    @pl.when(step == 0)
    def _():
        make_bias(scal, slopes, pair, bias, keys)
        vt[...] = v[...].T

    for c in range(keys // block):

        @pl.when(step == c)
        def _(c=c):
            length = (c + 1) * block
            scaled = q[...] * bf16(HEAD_DIM**-0.5)
            outs, logs = [], []
            for h in range(2):
                s = score_t(k, head_only(scaled, h), bias, h, length)
                top = jnp.max(s, axis=0, keepdims=True)
                e = jnp.exp(s - top)
                total = jnp.sum(e, axis=0, keepdims=True)
                mixed = mm(vt[h * HEAD_DIM : (h + 1) * HEAD_DIM, 0:length], e.astype(bf16))
                outs.append(mixed / total)
                logs.append(top + jnp.log(total))
            o[...] = jnp.concatenate(outs, axis=0).T.astype(bf16)
            lse[0, 0:2, :] = jnp.concatenate(logs, axis=0)


def attend_call(scal, slopes, qkv, block):
    keys, cols = qkv.shape
    width = cols // 3
    pairs = width // LANES
    return pl.pallas_call(
        attend_body,
        out_shape=(
            jax.ShapeDtypeStruct((keys, width), bf16),
            jax.ShapeDtypeStruct((pairs, 8, keys), f32),
        ),
        grid_spec=pltpu.PrefetchScalarGridSpec(
            num_scalar_prefetch=1,
            grid=(pairs, keys // block),
            in_specs=[
                pl.BlockSpec((block, LANES), lambda p, c, sc: (c, p)),
                pl.BlockSpec((keys, LANES), lambda p, c, sc: (0, pairs + p)),
                pl.BlockSpec((keys, LANES), lambda p, c, sc: (0, 2 * pairs + p)),
                SCALAR,
            ],
            out_specs=(
                pl.BlockSpec((block, LANES), lambda p, c, sc: (c, p)),
                pl.BlockSpec((1, 8, block), lambda p, c, sc: (p, 0, c)),
            ),
            scratch_shapes=[
                pltpu.VMEM((2, keys, LANES), f32),
                pltpu.VMEM((LANES, keys), bf16),
            ],
        ),
        compiler_params=params(),
        name="attend",
    )(scal, qkv, qkv, qkv, slopes)


def attend_back_body(scal, q, k, v, o, do, lse, slopes, dq, dk, dv, bias, kt, dk_sum, dv_sum):
    pair, step = pl.program_id(0), pl.program_id(1)
    block = q.shape[0]
    keys = k.shape[0]
    scale = HEAD_DIM**-0.5

    @pl.when(step == 0)
    def _():
        make_bias(scal, slopes, pair, bias, keys)
        kt[...] = k[...].T
        dk_sum[...] = jnp.zeros_like(dk_sum)
        dv_sum[...] = jnp.zeros_like(dv_sum)

    for c in range(keys // block):

        @pl.when(step == c)
        def _(c=c):
            length = (c + 1) * block
            scaled = q[...] * bf16(scale)
            both = (do[...].astype(f32) * o[...].astype(f32)).T
            outs = []
            for h in range(2):
                qm = head_only(scaled, h)
                dom = head_only(do[...], h)
                dot_row = jnp.sum(both[h * HEAD_DIM : (h + 1) * HEAD_DIM], axis=0, keepdims=True)
                p = jnp.exp(score_t(k, qm, bias, h, length) - lse[0, h : h + 1, :])
                dp = mm_t(v[0:length, :], dom)
                ds = (p * (dp - dot_row)).astype(bf16)
                dv_sum[0:length, :] += mm(p.astype(bf16), dom)
                dk_sum[0:length, :] += mm(ds, qm)
                outs.append(mm(kt[h * HEAD_DIM : (h + 1) * HEAD_DIM, 0:length], ds))
            dq[...] = (jnp.concatenate(outs, axis=0).T * scale).astype(bf16)

    @pl.when(step == keys // block - 1)
    def _():
        dk[...] = dk_sum[...].astype(bf16)
        dv[...] = dv_sum[...].astype(bf16)


def attend_back_call(scal, slopes, qkv, o, do, lse, block):
    keys, cols = qkv.shape
    width = cols // 3
    pairs = width // LANES
    some = pl.BlockSpec((block, LANES), lambda p, c, sc: (c, p))
    full = pl.BlockSpec((keys, LANES), lambda p, c, sc: (0, p))
    return pl.pallas_call(
        attend_back_body,
        out_shape=(jax.ShapeDtypeStruct((keys, width), bf16),) * 3,
        grid_spec=pltpu.PrefetchScalarGridSpec(
            num_scalar_prefetch=1,
            grid=(pairs, keys // block),
            in_specs=[
                some,
                pl.BlockSpec((keys, LANES), lambda p, c, sc: (0, pairs + p)),
                pl.BlockSpec((keys, LANES), lambda p, c, sc: (0, 2 * pairs + p)),
                some,
                some,
                pl.BlockSpec((1, 8, block), lambda p, c, sc: (p, 0, c)),
                SCALAR,
            ],
            out_specs=(some, full, full),
            scratch_shapes=[
                pltpu.VMEM((2, keys, LANES), f32),
                pltpu.VMEM((LANES, keys), bf16),
                pltpu.VMEM((keys, LANES), f32),
                pltpu.VMEM((keys, LANES), f32),
            ],
        ),
        compiler_params=params(),
        name="attend_back",
    )(scal, qkv, qkv, qkv, o, do, lse, slopes)


def lay_columns(w_ref, first, dest):
    width = w_ref.shape[2]
    for d in range(w_ref.shape[0]):
        dest[:, d * width : (d + 1) * width] = w_ref[d, first : first + dest.shape[0], :]


def out_body(scal, o, w, near, far, flat, *, first):
    t = pl.program_id(0)

    @pl.when(t == 0)
    def _():
        lay_columns(w, first, flat)

    part = mm(o[...], flat[...]).astype(bf16)

    @pl.when(t < 2)
    def _():
        near[0] = part

    @pl.when(t >= 2)
    def _():
        far[0] = part


def near_map(t, *_):
    return (jnp.minimum(t, 1), 0, 0)


def far_map(t, *_):
    return (jnp.maximum(t - 2, 0), 0, 0)


def out_call(scal, o, w, first):
    keys, inner = o.shape
    rows = keys // 4
    width = w.shape[0] * w.shape[2]
    return pl.pallas_call(
        functools.partial(out_body, first=first),
        out_shape=(jax.ShapeDtypeStruct((2, rows, width), bf16),) * 2,
        grid_spec=pltpu.PrefetchScalarGridSpec(
            num_scalar_prefetch=1,
            grid=(4,),
            in_specs=[
                pl.BlockSpec((rows, inner), lambda t, sc: (lax.bitwise_xor(sc[0], rel_of(t)), 0)),
                WHOLE,
            ],
            out_specs=(
                pl.BlockSpec((1, rows, width), near_map),
                pl.BlockSpec((1, rows, width), far_map),
            ),
            scratch_shapes=[pltpu.VMEM((inner, width), bf16)],
        ),
        compiler_params=params(),
        name="out_proj",
    )(scal, o, w)


def mid_body(x, a, b, c, bias, gain, shift, mid, h2):
    value = x[...].astype(f32) + (
        (a[0].astype(f32) + b[0].astype(f32)) + c[...].astype(f32) + bias[...]
    )
    mid[...] = value
    unit, _ = normalize(value)
    h2[...] = (unit * gain[...] + shift[...]).astype(bf16)


def mid_call(x, a, b, c, bias, gain, shift):
    rows, width = x.shape
    one = pl.BlockSpec((rows // 2, width), lambda i: (i, 0))
    first = pl.BlockSpec((1, rows // 2, width), lambda i: (0, i, 0))
    second = pl.BlockSpec((1, rows // 2, width), lambda i: (1, i, 0))
    row = pl.BlockSpec((1, width), lambda i: (0, 0))
    return pl.pallas_call(
        mid_body,
        out_shape=(
            jax.ShapeDtypeStruct((rows, width), f32),
            jax.ShapeDtypeStruct((rows, width), bf16),
        ),
        grid=(2,),
        in_specs=[one, second, first, one, row, row, row],
        out_specs=(one, one),
        compiler_params=params(),
        name="mid_norm",
    )(x, a, b, c, bias, gain, shift)


def gelu_parts(u):
    root = math.sqrt(2.0 / math.pi)
    sq = u * u
    t = jnp.tanh(root * (u + GELU_COEF * (sq * u)))
    half = 0.5 * (1.0 + t)
    slope = half + 0.5 * u * (1.0 - t * t) * (root * (1.0 + 3.0 * GELU_COEF * sq))
    return u * half, slope


def mlp_body(
    h0, h1, h2, h3, g_rows, w1, w2, b1,
    y_near, y_far, d_near, d_far, a_all, du_all, h_all, g_all, bias_sum,
    flat, hb, gb,
):
    t = pl.program_id(0)

    @pl.when(t == 0)
    def _():
        lay_columns(w2, 0, flat)
        bias_sum[...] = jnp.zeros_like(bias_sum)

    pick(rel_of(t), (h0, h1, h2, h3), hb)
    gb[...] = g_rows[rel_of(t)]
    h_all[...] = hb[...]
    g_all[...] = gb[...]
    inner = w1.shape[1]
    chunk = 256
    for c in range(inner // chunk):
        cols = slice(c * chunk, (c + 1) * chunk)
        u = mm(hb[...], w1[:, cols]) + b1[:, cols]
        value, slope = gelu_parts(u)
        a_all[:, cols] = value.astype(bf16)
        du = (mm_t(gb[...], flat[cols, :]) * slope).astype(bf16)
        du_all[:, cols] = du
        bias_sum[:, cols] += jnp.sum(du.astype(f32), axis=0, keepdims=True)
    y = mm(a_all[...], flat[...]).astype(bf16)
    d = mm_t(du_all[...], w1[...]).astype(bf16)

    @pl.when(t < 2)
    def _():
        y_near[0] = y
        d_near[0] = d

    @pl.when(t >= 2)
    def _():
        y_far[0] = y
        d_far[0] = d


def mlp_call(h_pieces, g_rows, w1, w2, b1):
    rows, width = h_pieces[0].shape
    inner = w1.shape[1]
    pair = jax.ShapeDtypeStruct((2, rows, width), bf16)
    near = pl.BlockSpec((1, rows, width), near_map)
    far = pl.BlockSpec((1, rows, width), far_map)
    block = lambda n: pl.BlockSpec((rows, n), lambda t: (t, 0))
    return pl.pallas_call(
        mlp_body,
        out_shape=(
            pair,
            pair,
            pair,
            pair,
            jax.ShapeDtypeStruct((4 * rows, inner), bf16),
            jax.ShapeDtypeStruct((4 * rows, inner), bf16),
            jax.ShapeDtypeStruct((4 * rows, width), bf16),
            jax.ShapeDtypeStruct((4 * rows, width), bf16),
            jax.ShapeDtypeStruct((1, inner), f32),
        ),
        grid=(4,),
        in_specs=[WHOLE] * 8,
        out_specs=(
            near, far, near, far, block(inner), block(inner), block(width), block(width),
            pl.BlockSpec((1, inner), lambda t: (0, 0)),
        ),
        scratch_shapes=[
            pltpu.VMEM((inner, width), bf16),
            pltpu.VMEM((rows, width), bf16),
            pltpu.VMEM((rows, width), bf16),
        ],
        compiler_params=params(),
        name="mlp",
    )(*h_pieces, g_rows, w1, w2, b1)


def outer_body(left, right, out, turned, *, blocks):
    @pl.when(pl.program_id(0) == 0)
    def _():
        turned[...] = left[...].T

    part = mm(turned[...], right[...]).astype(bf16)
    if blocks:
        width = out.shape[2]
        for d in range(out.shape[0]):
            out[d] = part[:, d * width : (d + 1) * width]
    else:
        out[...] = part


def outer_call(left, right, parts, name):
    rows, m = left.shape
    n = right.shape[1]
    step = 256
    if parts > 1:
        width = n // parts
        out_shape = jax.ShapeDtypeStruct((parts, m, width), bf16)
        out_spec = pl.BlockSpec((step // width, m, width), lambda j: (j, 0, 0))
    else:
        out_shape = jax.ShapeDtypeStruct((m, n), bf16)
        out_spec = pl.BlockSpec((m, step), lambda j: (0, j))
    return pl.pallas_call(
        functools.partial(outer_body, blocks=parts > 1),
        out_shape=out_shape,
        grid=(n // step,),
        in_specs=[WHOLE, pl.BlockSpec((rows, step), lambda j: (0, j))],
        out_specs=out_spec,
        scratch_shapes=[pltpu.VMEM((m, rows), bf16)],
        compiler_params=params(),
        name=name,
    )(left, right)


def mid_back_body(mid, a, b, c, g, gain, dmid, dbr, sums):
    @pl.when(pl.program_id(0) == 0)
    def _():
        sums[...] = jnp.zeros_like(sums)

    unit, inv = normalize(mid[...])
    e = (a[0].astype(f32) + b[0].astype(f32)) + c[...].astype(f32)
    grad = g[...].astype(f32)
    value = grad + norm_back(e, gain[...], unit, inv)
    dmid[...] = value
    low = value.astype(bf16)
    dbr[...] = low
    sums[0:1, :] += jnp.sum(e * unit, axis=0, keepdims=True)
    sums[1:2, :] += jnp.sum(e, axis=0, keepdims=True)
    sums[2:3, :] += jnp.sum(low.astype(f32), axis=0, keepdims=True)
    sums[3:4, :] += jnp.sum(grad, axis=0, keepdims=True)


def mid_back_call(mid, a, b, c, g, gain):
    rows, width = mid.shape
    one = pl.BlockSpec((rows // 2, width), lambda i: (i, 0))
    first = pl.BlockSpec((1, rows // 2, width), lambda i: (0, i, 0))
    second = pl.BlockSpec((1, rows // 2, width), lambda i: (1, i, 0))
    row = pl.BlockSpec((1, width), lambda i: (0, 0))
    return pl.pallas_call(
        mid_back_body,
        out_shape=(
            jax.ShapeDtypeStruct((rows, width), f32),
            jax.ShapeDtypeStruct((rows, width), bf16),
            jax.ShapeDtypeStruct((8, width), f32),
        ),
        grid=(2,),
        in_specs=[one, second, first, one, one, row],
        out_specs=(one, one, pl.BlockSpec((8, width), lambda i: (0, 0))),
        compiler_params=params(),
        name="mid_back",
    )(mid, a, b, c, g, gain)


def out_back_body(scal, b0, b1, b2, b3, o, w, do, grad, flat, rows, total, *, first):
    r = pl.program_id(0)

    @pl.when(r == 0)
    def _():
        lay_columns(w, first, flat)
        total[...] = jnp.zeros_like(total)

    pick(r, (b0, b1, b2, b3), rows)
    do[...] = mm_t(rows[...], flat[...]).astype(bf16)
    total[...] += mm(o[...].T, rows[...])

    @pl.when(r == 3)
    def _():
        width = grad.shape[2]
        for d in range(grad.shape[0]):
            grad[d] = total[:, d * width : (d + 1) * width].astype(bf16)


def out_back_call(scal, pieces, o, w, first):
    rows, width = pieces[0].shape
    inner = o.shape[1]
    at = pl.BlockSpec((rows, inner), lambda r, sc: (lax.bitwise_xor(sc[0], r), 0))
    grad = (w.shape[0], inner, w.shape[2])
    return pl.pallas_call(
        functools.partial(out_back_body, first=first),
        out_shape=(jax.ShapeDtypeStruct(o.shape, bf16), jax.ShapeDtypeStruct(grad, bf16)),
        grid_spec=pltpu.PrefetchScalarGridSpec(
            num_scalar_prefetch=1,
            grid=(4,),
            in_specs=[WHOLE] * 4 + [at, WHOLE],
            out_specs=(at, pl.BlockSpec(grad, lambda r, sc: (0, 0, 0))),
            scratch_shapes=[
                pltpu.VMEM((inner, width), bf16),
                pltpu.VMEM((rows, width), bf16),
                pltpu.VMEM((inner, width), f32),
            ],
        ),
        compiler_params=params(),
        name="out_back",
    )(scal, *pieces, o, w)


def qkv_back_body(scal, dq, dk, dv, w, near, far, merged, sums):
    t = pl.program_id(0)

    @pl.when(t == 0)
    def _():
        sums[...] = jnp.zeros_like(sums)

    low = jnp.concatenate([dq[...], dk[...], dv[...]], axis=1)
    merged[...] = low
    part = mm_t(low, w[...]).astype(bf16)
    sums[...] += jnp.sum(low.astype(f32), axis=0, keepdims=True)

    @pl.when(t < 2)
    def _():
        near[0] = part

    @pl.when(t >= 2)
    def _():
        far[0] = part


def qkv_back_call(scal, dq, dk, dv, w):
    keys, inner = dq.shape
    rows = keys // 4
    width = w.shape[0]
    where = lambda t, sc: (lax.bitwise_xor(sc[0], rel_of(t)), 0)
    at = pl.BlockSpec((rows, inner), where)
    return pl.pallas_call(
        qkv_back_body,
        out_shape=(
            jax.ShapeDtypeStruct((2, rows, width), bf16),
            jax.ShapeDtypeStruct((2, rows, width), bf16),
            jax.ShapeDtypeStruct((keys, 3 * inner), bf16),
            jax.ShapeDtypeStruct((1, 3 * inner), f32),
        ),
        grid_spec=pltpu.PrefetchScalarGridSpec(
            num_scalar_prefetch=1,
            grid=(4,),
            in_specs=[at, at, at, WHOLE],
            out_specs=(
                pl.BlockSpec((1, rows, width), near_map),
                pl.BlockSpec((1, rows, width), far_map),
                pl.BlockSpec((rows, 3 * inner), where),
                pl.BlockSpec((1, 3 * inner), lambda t, sc: (0, 0)),
            ),
        ),
        compiler_params=params(),
        name="qkv_back",
    )(scal, dq, dk, dv, w)


def in_back_body(x, a, b, c, dmid, gain, grad, sums):
    @pl.when(pl.program_id(0) == 0)
    def _():
        sums[...] = jnp.zeros_like(sums)

    unit, inv = normalize(x[...].astype(f32))
    e = (a[0].astype(f32) + b[0].astype(f32)) + c[...].astype(f32)
    grad[...] = (dmid[...] + norm_back(e, gain[...], unit, inv)).astype(bf16)
    sums[0:1, :] += jnp.sum(e * unit, axis=0, keepdims=True)
    sums[1:2, :] += jnp.sum(e, axis=0, keepdims=True)


def in_back_call(x, a, b, c, dmid, gain):
    rows, width = x.shape
    one = pl.BlockSpec((rows // 2, width), lambda i: (i, 0))
    first = pl.BlockSpec((1, rows // 2, width), lambda i: (0, i, 0))
    second = pl.BlockSpec((1, rows // 2, width), lambda i: (1, i, 0))
    row = pl.BlockSpec((1, width), lambda i: (0, 0))
    return pl.pallas_call(
        in_back_body,
        out_shape=(
            jax.ShapeDtypeStruct((rows, width), bf16),
            jax.ShapeDtypeStruct((8, width), f32),
        ),
        grid=(2,),
        in_specs=[one, second, first, one, one, row],
        out_specs=(one, pl.BlockSpec((8, width), lambda i: (0, 0))),
        compiler_params=params(),
        name="in_back",
    )(x, a, b, c, dmid, gain)


def remote(src, dst, send, recv, dp, seq):
    return pltpu.make_async_remote_copy(
        src_ref=src,
        dst_ref=dst,
        send_sem=send,
        recv_sem=recv,
        device_id=(dp, seq),
        device_id_type=pl.DeviceIdType.MESH,
    )


def greet(peers):
    barrier = pltpu.get_barrier_semaphore()
    for dp, seq in peers:
        pl.semaphore_signal(
            barrier, inc=1, device_id=(dp, seq), device_id_type=pl.DeviceIdType.MESH
        )
    pl.semaphore_wait(barrier, len(peers))


class GradSum:
    def __init__(self, part, acc, landx, land, sems, dp, seq):
        self.part, self.landx, self.land, self.sems = part, landx, land, sems
        self.fetched = acc is not None
        self.acc = acc if self.fetched else landx
        self.seq, self.z, self.x = seq, dp // 2, dp % 2

    def cross(self, k):
        return remote(
            self.part.at[2 * k + (1 - self.x)],
            self.landx.at[k],
            self.sems.at[0, k],
            self.sems.at[1, k],
            2 * self.z + (1 - self.x),
            self.seq,
        )

    def fetch(self, k):
        return pltpu.make_async_copy(
            self.part.at[2 * k + self.x], self.acc.at[k], self.sems.at[6, k]
        )

    def right(self, b, first):
        return remote(
            self.acc.at[b] if first else self.land.at[b + 1],
            self.land.at[b + 1],
            self.sems.at[2, b],
            self.sems.at[3, b],
            2 * ((self.z + 1) % 4) + self.x,
            self.seq,
        )

    def left(self, b, first):
        return remote(
            self.acc.at[b] if first else self.land.at[b],
            self.land.at[b],
            self.sems.at[4, b],
            self.sems.at[5, b],
            2 * ((self.z + 3) % 4) + self.x,
            self.seq,
        )

    def start(self):
        for k in (3, 0, 2, 1):
            self.cross(k).start()
        if self.fetched:
            for k in range(4):
                self.fetch(k).start()

    def add_cross(self):
        for k in (3, 0, 2, 1):
            self.cross(k).wait_recv()
            if self.fetched:
                self.fetch(k).wait()
                own = self.acc[k].astype(f32)
            else:
                own = self.part[2 * k + self.x].astype(f32)
            self.acc[k] = (own + self.landx[k].astype(f32)).astype(bf16)

    def stage(self, k):
        @pl.when(self.z == k)
        def _():
            for b in range(3, k, -1):
                if k > 0:
                    self.right(b, False).wait_recv()
                    total = self.land[b + 1].astype(f32) + self.acc[b].astype(f32)
                    self.land[b + 1] = total.astype(bf16)
                self.right(b, k == 0).start()

        @pl.when(self.z == 3 - k)
        def _():
            for b in range(0, 3 - k):
                if k > 0:
                    self.left(b, False).wait_recv()
                    total = self.land[b].astype(f32) + self.acc[b].astype(f32)
                    self.land[b] = total.astype(bf16)
                self.left(b, k == 0).start()

    def finish(self, out):
        z = self.z
        out[...] = self.acc[z].astype(f32)

        @pl.when(z > 0)
        def _():
            self.right(z, False).wait_recv()
            out[...] += self.land[z + 1].astype(f32)

        @pl.when(z < 3)
        def _():
            self.left(z, False).wait_recv()
            out[...] += self.land[z].astype(f32)

    def drain(self):
        for k in range(4):
            self.cross(k).wait_send()
        for k in range(3):

            @pl.when(self.z == k)
            def _(k=k):
                for b in range(3, k, -1):
                    self.right(b, k == 0).wait_send()

            @pl.when(self.z == 3 - k)
            def _(k=k):
                for b in range(0, 3 - k):
                    self.left(b, k == 0).wait_send()

    @staticmethod
    def scratch(m, n, fetched=False):
        own = [pltpu.VMEM((4, m, n), bf16)] if fetched else []
        return own + [
            pltpu.VMEM((4, m, n), bf16),
            pltpu.VMEM((5, m, n), bf16),
            pltpu.SemaphoreType.DMA((7, 4)),
        ]


SMALL_ROWS = 16


class Gather:
    def __init__(self, own, slot, sems, dp, seq):
        self.own, self.slot, self.sems = own, slot, sems
        self.dp, self.seq, self.z, self.x = dp, seq, dp // 2, dp % 2

    def along(self, k, step, src=None):
        slot = self.slot(2 * k + self.x)
        return remote(
            slot if src is None else src,
            slot,
            self.sems.at[0 if step > 0 else 1, k],
            self.sems.at[3, k],
            2 * ((self.z + step + 4) % 4) + self.x,
            self.seq,
        )

    def over(self, k, src=None):
        slot = self.slot(2 * k + self.x)
        return remote(
            slot if src is None else src,
            slot,
            self.sems.at[2, k],
            self.sems.at[4, k],
            2 * self.z + (1 - self.x),
            self.seq,
        )

    def keep(self):
        return pltpu.make_async_copy(self.own, self.slot(self.dp), self.sems.at[5, 0])

    def start(self):
        z = self.z

        @pl.when(z < 3)
        def _():
            self.along(z, 1, self.own).start()

        @pl.when(z > 0)
        def _():
            self.along(z, -1, self.own).start()

        self.over(z, self.own).start()
        self.keep().start()

    def hop(self, dist):
        z = self.z

        @pl.when(z - dist >= 0)
        def _():
            k = z - dist
            self.along(k, 1).wait_recv()

            @pl.when(z < 3)
            def _():
                self.along(k, 1).start()

            self.over(k).start()

        @pl.when(z + dist <= 3)
        def _():
            k = z + dist
            self.along(k, -1).wait_recv()

            @pl.when(z > 0)
            def _():
                self.along(k, -1).start()

            self.over(k).start()

    def arrive(self):
        self.keep().wait()
        for k in range(4):
            self.over(k).wait_recv()

    def drain(self):
        z = self.z
        for k in range(4):
            self.over(k).wait_send()

            @pl.when((z < 3) & (z >= k))
            def _(k=k):
                self.along(k, 1).wait_send()

            @pl.when((z > 0) & (z <= k))
            def _(k=k):
                self.along(k, -1).wait_send()

    @staticmethod
    def scratch():
        return pltpu.SemaphoreType.DMA((6, 4))


class Spread:
    def __init__(self, own, rows, sems, dp, seq):
        mate, across = seq + 1 - 2 * (seq % 2), (seq + 2) % 4
        to = lambda src, r, peer: remote(src, rows.at[r], sems.at[0, r], sems.at[1, r], dp, peer)
        self.near, self.far = to(own, 1, mate), to(own, 2, across)
        self.last = to(rows.at[2], 3, mate)

    def start(self):
        self.far.start()
        self.near.start()

    def forward(self):
        self.far.wait_recv()
        self.last.start()

    def drain(self):
        for copy in (self.near, self.far, self.last):
            copy.wait_send()


def neighbours(seq):
    mate = seq + 1 - 2 * (seq % 2)
    return mate, (seq + 2) % 4, (mate + 2) % 4


def block_at(seq, rel):
    return 2 * ((seq // 2 + rel // 2) % 2) + (seq + rel) % 2


def scores(k, qm, ramp):
    block = qm.shape[0]
    length = k.shape[0]
    s = mm_t(k, qm) + jnp.concatenate([ramp] * (block // LANES), axis=1)
    key = lax.broadcasted_iota(jnp.int32, (block, block), 0)
    query = lax.broadcasted_iota(jnp.int32, (block, block), 1)
    last = jnp.where(key <= query, s[length - block :], NEG)
    if length == block:
        return last
    return jnp.concatenate([s[: length - block], last], axis=0)


def fore_body(
    lengths, slopes, wq, wo, x, v_up, v_qv, v_g1, v_s1, v_out, v_g2, v_s2, v_down, g, w1, w2,
    h1, qkv_out, o, lse, wq_all, flat, mid, gain1, bias_down, y_all, gw1, gw2, dmid, dbr, sums,
    up_sum,
    small, vectors, shift1, bias_qkv, bias_out, gain2, shift2, bias_up,
    rows_in, g_rows, h_stage, qkv, ramp, vt, part, land_c, sum_y, land_y, w1_all, w2_flat,
    a_all, du_all, turned, y_stage, up_stage, down_stage,
    q_sem, o_sem, w1_sem, w2_sem, x_sem, g_sem, seq_sem, dp_sem, keep_sem, stage_sem, fwd, mlp, bwd,
):
    dp, seq = lax.axis_index("dp"), lax.axis_index("seq")
    mate, across, _ = neighbours(seq)
    greet([((dp + i) % 8, seq) for i in range(1, 8)] + [(dp, p) for p in neighbours(seq)])
    rows, width = x.shape
    keys = qkv.shape[0]
    inner = o.shape[1]
    pairs = inner // LANES
    ff = du_all.shape[1]
    half_rows = rows // 2
    halves = [slice(0, half_rows), slice(half_rows, rows)]
    column = lambda ref: lambda d: ref.at[:, pl.ds(pl.multiple_of(d * LANES, LANES), LANES)]

    gather_q = Gather(wq, lambda d: wq_all.at[:, d], q_sem, dp, seq)
    gather_o = Gather(wo, column(flat), o_sem, dp, seq)
    gathers = [
        Gather(w1, lambda d: w1_all.at[d], w1_sem, dp, seq),
        Gather(w2, column(w2_flat), w2_sem, dp, seq),
    ]
    spread_x = Spread(x, rows_in, x_sem, dp, seq)
    spread_g = Spread(g_rows.at[0], g_rows, g_sem, dp, seq)
    length = lengths[0]
    heads = 2 * pairs * seq
    at = 0
    for ref in (v_up, v_qv, v_g1, v_s1, v_out, v_g2, v_s2, v_down):
        small[:, at : at + ref.shape[1]] = ref[...].astype(f32)
        at += ref.shape[1]
    keep_v = pltpu.make_async_copy(small, vectors.at[dp, seq], keep_sem.at[0])
    keep_v.start()
    group = [
        remote(small, vectors.at[dp, seq], seq_sem.at[0, i], seq_sem.at[1, i], dp, peer)
        for i, peer in enumerate(neighbours(seq))
    ]
    for copy in group:
        copy.start()
    gather_q.start()
    spread_x.start()
    keep_x = pltpu.make_async_copy(x, rows_in.at[0], keep_sem.at[1])
    keep_g = pltpu.make_async_copy(g, g_rows.at[0], keep_sem.at[2])
    keep_x.start()
    keep_g.start()

    def to_dp(i):
        return remote(
            vectors.at[dp], vectors.at[dp], dp_sem.at[0, i], dp_sem.at[1, i], (dp + i) % 8, seq
        )

    keep_v.wait()
    for copy in group:
        copy.wait_recv()
    for i in range(1, 8):
        to_dp(i).start()
    gather_o.start()
    keep_g.wait()
    where = lax.broadcasted_iota(jnp.int32, (rows, width), 0) + seq * rows
    g_rows[0] = jnp.where(where < length, g_rows[0], jnp.zeros((rows, width), bf16))
    spread_g.start()
    gather_q.hop(1)
    gather_q.hop(2)
    gather_o.hop(1)
    gather_q.hop(3)
    gather_o.hop(2)
    spread_x.forward()
    gather_o.hop(3)
    for gather in gathers:
        gather.start()
    for i in range(1, 8):
        to_dp(i).wait_recv()
    for ref, at in (
        (gain1, 192), (shift1, 224), (bias_out, 256), (gain2, 288), (shift2, 320), (bias_down, 352),
    ):
        for d in range(8):
            ref[:, d * LANES : (d + 1) * LANES] = jnp.concatenate(
                [vectors[d, i, :, at : at + 32] for i in range(4)], axis=1
            )
    for section in range(2):
        for half in range(2):
            lane = section * 512 + half * LANES
            bias_qkv[:, lane : lane + LANES] = jnp.concatenate(
                [vectors[4 * section + seq, 2 * half + i, :, 128:192] for i in range(2)], axis=1
            )
    bias_qkv[:, 256:512] = jnp.zeros((1, 256), f32)
    for i in range(8):
        bias_up[:, i * LANES : (i + 1) * LANES] = vectors[2 * seq + i // 4, i % 4, :, 0:LANES]
    keep_x.wait()
    spread_x.near.wait_recv()
    gather_q.arrive()
    spread_x.last.wait_recv()
    spread_x.drain()

    def h1_copy(r):
        at = pl.ds(pl.multiple_of(block_at(seq, r) * rows, rows), rows)
        return pltpu.make_async_copy(h_stage.at[r % 2], h1.at[at], stage_sem.at[0, r % 2])

    def project(r, carry):
        @pl.when(r >= 2)
        def _():
            h1_copy(r - 2).wait()

        at = pl.ds(pl.multiple_of(block_at(seq, r) * rows, rows), rows)
        unit, _ = normalize(rows_in[r].astype(f32))
        low = (unit * gain1[...] + shift1[...]).astype(bf16)
        h_stage[r % 2] = low
        h1_copy(r).start()
        for c in range(3):
            cols = slice(c * inner, (c + 1) * inner)
            value = mm(low, wq_all[c].reshape(width, inner)) + bias_qkv[:, cols]
            qkv[at, cols] = value.astype(bf16)
        return carry

    lax.fori_loop(0, 4, project, 0)
    qkv_copy = pltpu.make_async_copy(qkv, qkv_out, keep_sem.at[3])
    qkv_copy.start()
    for gather in gathers:
        gather.hop(1)
    spread_g.forward()
    pos = lax.broadcasted_iota(jnp.int32, (keys, LANES), 0)
    ramp[...] = jnp.where(pos < length, pos.astype(f32), -1e33)
    for p in range(pairs):
        vt[p] = qkv[:, 2 * inner + p * LANES : 2 * inner + (p + 1) * LANES].T
    gather_o.arrive()

    def row_copies(sems):
        rel_one = remote(part.at[1], land_c.at[0], sems.at[0, 0], sems.at[1, 0], dp, mate)
        rel_three = [
            remote(
                part.at[3, at], land_c.at[1, at], sems.at[0, 1 + i], sems.at[1, 1 + i], dp, mate
            )
            for i, at in enumerate(halves)
        ]
        over = [
            remote(sum_y.at[at], land_y.at[at], sems.at[0, 3 + i], sems.at[1, 3 + i], dp, across)
            for i, at in enumerate(halves)
        ]
        return rel_one, rel_three, over

    def send_over(rel_three, over, i):
        rel_three[i].wait_recv()
        at = halves[i]
        total = part[2, at, :].astype(f32) + land_c[1, at, :].astype(f32)
        sum_y[at, :] = total.astype(bf16)
        over[i].start()

    rel_one, rel_three, over = row_copies(fwd)

    def attend(t, carry):
        rel = 3 - t
        c_now = block_at(seq, rel)
        at = pl.ds(pl.multiple_of(c_now * rows, rows), rows)
        for c in range(keys // rows):

            @pl.when(c_now == c)
            def _(c=c):
                length = (c + 1) * rows

                def one_pair(p, carry):
                    lane = pl.ds(pl.multiple_of(p * LANES, LANES), LANES)
                    k_lane = pl.ds(pl.multiple_of(inner + p * LANES, LANES), LANES)
                    scaled = qkv[c * rows : length, lane] * bf16(HEAD_DIM**-0.5)
                    k = qkv[0:length, k_lane]
                    outs, logs = [], []
                    for h in range(2):
                        bias = ramp[0:length, :] * slopes[heads + 2 * p + h]
                        s = scores(k, head_only(scaled, h), bias)
                        top = jnp.max(s, axis=0, keepdims=True)
                        e = jnp.exp(s - top)
                        total = jnp.sum(e, axis=0, keepdims=True)
                        half = vt[p, h * HEAD_DIM : (h + 1) * HEAD_DIM, 0:length]
                        outs.append(mm(half, e.astype(bf16)) / total)
                        logs.append(top + jnp.log(total))
                    o[c * rows : length, lane] = jnp.concatenate(outs, axis=0).T.astype(bf16)
                    lse[p, 0:2, c * rows : length] = jnp.concatenate(logs, axis=0)
                    return carry

                lax.fori_loop(0, pairs, one_pair, 0)

        part[rel] = mm(o[at, :], flat[...]).astype(bf16)

        @pl.when(t == 0)
        def _():
            for copy in rel_three:
                copy.start()

        @pl.when(t == 1)
        def _():
            send_over(rel_three, over, 0)
            send_over(rel_three, over, 1)
            for gather in gathers:
                gather.hop(2)

        @pl.when(t == 2)
        def _():
            rel_one.start()
            for gather in gathers:
                gather.hop(3)

        return carry

    lax.fori_loop(0, 4, attend, 0)
    gather_q.drain()
    gather_o.drain()
    rel_one.wait_recv()

    near, far, last = (
        [
            remote(
                rows_in.at[0 if r < 3 else 2, at], rows_in.at[r, at], mlp.at[0, 2 * k + i],
                mlp.at[1, 2 * k + i], dp, across if r == 2 else mate,
            )
            for i, at in enumerate(halves)
        ]
        for k, r in enumerate((1, 2, 3))
    )
    step_rows = 64

    def second_norm(i):
        over[i].wait_recv()

        def step(k, carry):
            at = pl.ds(pl.multiple_of(i * half_rows + k * step_rows, step_rows), step_rows)
            total = (part[0, at, :].astype(f32) + land_c[0, at, :].astype(f32)) + land_y[
                at, :
            ].astype(f32)
            value = rows_in[0, at, :].astype(f32) + (total + bias_out[...])
            mid[at, :] = value
            unit, _ = normalize(value)
            rows_in[0, at, :] = (unit * gain2[...] + shift2[...]).astype(bf16)
            return carry

        lax.fori_loop(0, half_rows // step_rows, step, 0)
        far[i].start()
        near[i].start()

    second_norm(0)
    up_sum[...] = jnp.zeros_like(up_sum)
    sums[...] = jnp.zeros_like(sums)
    spread_g.near.wait_recv()
    spread_g.last.wait_recv()
    spread_g.drain()
    for gather in gathers:
        gather.arrive()
    for copy in [rel_one] + rel_three:
        copy.wait_send()
    back_one, back_three, back_over = row_copies(bwd)
    chunk = 256

    def y_copy(i):
        rel, half = place(i)
        at = pl.ds(pl.multiple_of(half * half_rows, half_rows), half_rows)
        return pltpu.make_async_copy(y_stage.at[i % 2], y_all.at[rel, at], stage_sem.at[1, i % 2])

    def place(i):
        late = i // 4
        return late * (2 + i % 2) + (1 - late) * (i // 2), late * ((i // 2) % 2) + (1 - late) * (i % 2)

    def block(i, carry):
        rel, half = place(i)

        @pl.when(i == 1)
        def _():
            second_norm(1)

        for k in range(2):

            @pl.when(i == 2 + k)
            def _(k=k):
                near[k].wait_recv()

            @pl.when(i == 4 + 2 * k)
            def _(k=k):
                far[k].wait_recv()
                last[k].start()

            @pl.when(i == 5 + 2 * k)
            def _(k=k):
                last[k].wait_recv()

        @pl.when(i >= 2)
        def _():
            y_copy(i - 2).wait()

        inside = pl.ds(pl.multiple_of(half * half_rows, half_rows), half_rows)
        at = pl.ds(pl.multiple_of(rel * rows + half * half_rows, half_rows), half_rows)
        hidden = rows_in[rel, inside, :]
        grad = g_rows[rel, inside, :]
        up = w1_all[...].reshape(width, ff)
        for c in range(ff // chunk):
            cols = slice(c * chunk, (c + 1) * chunk)
            u = mm(hidden, up[:, cols]) + bias_up[:, cols]
            value, slope = gelu_parts(u)
            a_all[at, cols] = value.astype(bf16)
            du = (mm_t(grad, w2_flat[cols, :]) * slope).astype(bf16)
            du_all[at, cols] = du
            up_sum[:, cols] += jnp.sum(du.astype(f32), axis=0, keepdims=True)
        y_stage[i % 2] = mm(a_all[at, :], w2_flat[...]).astype(bf16)
        y_copy(i).start()
        part[rel, inside, :] = mm_t(du_all[at, :], up).astype(bf16)

        @pl.when(i == 3)
        def _():
            back_one.start()

        @pl.when(i == 5)
        def _():
            back_three[0].start()

        @pl.when(i == 6)
        def _():
            over[0].wait_send()
            over[1].wait_send()
            send_over(back_three, back_over, 0)

        @pl.when(i == 7)
        def _():
            back_three[1].start()

        return carry

    lax.fori_loop(0, 8, block, 0)

    def turn(load):
        def step(i, carry):
            turned[:, pl.ds(pl.multiple_of(i * rows, rows), rows)] = load(i).T
            return carry

        lax.fori_loop(0, 4, step, 0)

    def up_copy(j):
        cols = pl.ds(pl.multiple_of(j * chunk, chunk), chunk)
        return pltpu.make_async_copy(up_stage.at[j % 2], gw1.at[:, :, cols], stage_sem.at[2, j % 2])

    def down_copy(j):
        return pltpu.make_async_copy(
            down_stage.at[j % 2], gw2.at[pl.ds(2 * j, 2)], stage_sem.at[3, j % 2]
        )

    def outer_up(j, carry):
        @pl.when(j >= 2)
        def _():
            up_copy(j - 2).wait()

        cols = pl.ds(pl.multiple_of(j * chunk, chunk), chunk)
        value = mm(turned[...], du_all[:, cols]).astype(bf16)
        up_stage[j % 2] = value.reshape(8, width // 8, chunk)
        up_copy(j).start()
        return carry

    def outer_down(j, carry):
        @pl.when(j >= 2)
        def _():
            down_copy(j - 2).wait()

        cols = pl.ds(pl.multiple_of(j * chunk, chunk), chunk)
        right = g_rows[:, :, cols].reshape(4 * rows, chunk)
        value = mm(turned[...], right).astype(bf16)
        down_stage[j % 2, 0] = value[:, :LANES]
        down_stage[j % 2, 1] = value[:, LANES:]
        down_copy(j).start()
        return carry

    turn(lambda i: rows_in[i])
    send_over(back_three, back_over, 1)
    lax.fori_loop(0, ff // chunk, outer_up, 0)
    turn(lambda i: a_all[pl.ds(pl.multiple_of(i * rows, rows), rows), :])
    lax.fori_loop(0, width // chunk, outer_down, 0)

    back_one.wait_recv()

    def norm_step(k, carry):
        at = pl.ds(pl.multiple_of(k * step_rows, step_rows), step_rows)
        unit, inv = normalize(mid[at, :])
        e = (part[0, at, :].astype(f32) + land_c[0, at, :].astype(f32)) + land_y[at, :].astype(f32)
        grad = g_rows[0, at, :].astype(f32)
        value = grad + norm_back(e, gain2[...], unit, inv)
        dmid[at, :] = value
        low = value.astype(bf16)
        dbr[at, :] = low
        sums[0:1, :] += jnp.sum(e * unit, axis=0, keepdims=True)
        sums[1:2, :] += jnp.sum(e, axis=0, keepdims=True)
        sums[2:3, :] += jnp.sum(low.astype(f32), axis=0, keepdims=True)
        sums[3:4, :] += jnp.sum(grad, axis=0, keepdims=True)
        return carry

    steps = half_rows // step_rows
    back_over[0].wait_recv()
    lax.fori_loop(0, steps, norm_step, 0)
    back_over[1].wait_recv()
    lax.fori_loop(steps, 2 * steps, norm_step, 0)

    for copy in group + near + far + last + [back_one] + back_three + back_over:
        copy.wait_send()
    for i in range(1, 8):
        to_dp(i).wait_send()
    for gather in gathers:
        gather.drain()
    qkv_copy.wait()
    for k in range(2):
        h1_copy(2 + k).wait()
        y_copy(6 + k).wait()
        up_copy(ff // chunk - 2 + k).wait()
        down_copy(width // chunk - 2 + k).wait()


def fore_call(lengths, slopes, wq, wo, x, small, g, w1, w2):
    rows, width = x.shape
    keys = 4 * rows
    inner, ff = wo.shape[0], w1.shape[1]
    pairs = inner // LANES
    count = sum(v.shape[0] for v in small)
    sem = pltpu.SemaphoreType.DMA
    shape = jax.ShapeDtypeStruct
    any_space = pl.BlockSpec(memory_space=pl.ANY)
    vec = lambda n: pltpu.VMEM((1, n), f32)
    block = lambda *lead: pltpu.VMEM((*lead, rows, width), bf16)
    return pl.pallas_call(
        fore_body,
        out_shape=(
            shape((keys, width), bf16),
            shape((keys, 3 * inner), bf16),
            shape((keys, inner), bf16),
            shape((pairs, 8, keys), f32),
            shape((3, 8, *wq.shape[1:]), bf16),
            shape((inner, width), bf16),
            shape((rows, width), f32),
            shape((1, width), f32),
            shape((1, width), f32),
            shape((4, rows, width), bf16),
            shape((8, width // 8, ff), bf16),
            shape((8, ff, LANES), bf16),
            shape((rows, width), f32),
            shape((rows, width), bf16),
            shape((8, width), f32),
            shape((1, ff), f32),
        ),
        in_specs=[SCALAR, SCALAR] + [any_space] * 3 + [WHOLE] * 8 + [any_space] * 3,
        out_specs=(
            any_space, any_space, WHOLE, WHOLE, WHOLE, WHOLE, WHOLE, WHOLE, WHOLE,
            any_space, any_space, any_space, WHOLE, WHOLE, WHOLE, WHOLE,
        ),
        scratch_shapes=[
            vec(count),
            pltpu.VMEM((8, 4, 1, count), f32),
            vec(width), vec(3 * inner), vec(width), vec(width), vec(width), vec(ff),
            block(4),
            block(4),
            block(2),
            pltpu.VMEM((keys, 3 * inner), bf16),
            pltpu.VMEM((keys, LANES), f32),
            pltpu.VMEM((pairs, LANES, keys), bf16),
            block(4),
            block(2),
            block(),
            block(),
            pltpu.VMEM((8, *w1.shape), bf16),
            pltpu.VMEM((ff, width), bf16),
            pltpu.VMEM((keys, ff), bf16),
            pltpu.VMEM((keys, ff), bf16),
            pltpu.VMEM((width, keys), bf16),
            pltpu.VMEM((2, rows // 2, width), bf16),
            pltpu.VMEM((2, 8, width // 8, 256), bf16),
            pltpu.VMEM((2, 2, ff, LANES), bf16),
            Gather.scratch(), Gather.scratch(), Gather.scratch(), Gather.scratch(),
            sem((2, 4)), sem((2, 4)), sem((2, 3)), sem((2, 8)), sem((4,)), sem((4, 2)),
            sem((2, 5)), sem((2, 6)), sem((2, 5)),
        ],
        compiler_params=pltpu.CompilerParams(
            vmem_limit_bytes=67043328, collective_id=4, has_side_effects=True
        ),
        name="fore",
    )(lengths, slopes, wq, wo, x, *(v.reshape(1, -1) for v in small), g, w1, w2)


def back_body(
    lengths, slopes, dbr, o_in, flat_in, qkv_in, lse, wq_in, h1, gw1, gw2, y_all, mid_in, bias_down,
    x_in, dmid_in, gain1, mid_sums, up_sum,
    output, grad, gq_out, go_out, gw1_out, gw2_out, narrow_out, qv_out, up_out,
    o, flat, qkv, wq, mid, x, dmid,
    b_rows, y_far, do, go_sum, go_part, ramp, kt, dk_sum, dv_sum, merged, qkv_sums, h_buf, turned,
    gq_part, land_c, sum_y, land_y, y_land_c, y_sum, y_land_y,
    a_acc, a_x, a_land, a_sem, b_acc, b_x, b_land, b_sem, o_x, o_land, o_sem,
    q0_x, q0_land, q0_sem, q1_x, q1_land, q1_sem, q2_x, q2_land, q2_sem,
    small, small_land, own, seq_land,
    b_row_sem, row_sems, y_sems, h_sem, small_sems, seq_sems, far_sem, load_sem,
):
    loads = [
        pltpu.make_async_copy(src, dst, load_sem.at[i])
        for i, (src, dst) in enumerate((
            (dbr, b_rows.at[0]), (flat_in, flat), (o_in, o), (qkv_in, qkv), (mid_in, mid),
            (wq_in, wq), (x_in, x), (dmid_in, dmid),
        ))
    ]
    for copy in loads:
        copy.start()
    dp, seq = lax.axis_index("dp"), lax.axis_index("seq")
    mate, across, far_mate = neighbours(seq)
    greet([((dp + i) % 8, seq) for i in range(1, 8)] + [(dp, p) for p in neighbours(seq)])
    rows, width = dbr.shape
    keys, inner = o.shape
    length_all = lengths[0]
    pairs = inner // LANES
    heads = 2 * pairs * seq
    scale = HEAD_DIM**-0.5
    chunk = 128

    spread_b = Spread(dbr, b_rows, b_row_sem, dp, seq)
    spread_b.start()
    sum_a = GradSum(gw2, a_acc, a_x, a_land, a_sem, dp, seq)
    sum_b = GradSum(gw1, b_acc, b_x, b_land, b_sem, dp, seq)
    sum_o = GradSum(go_part, None, o_x, o_land, o_sem, dp, seq)
    sums_q = [
        GradSum(gq_part.at[0], None, q0_x, q0_land, q0_sem, dp, seq),
        GradSum(gq_part.at[1], None, q1_x, q1_land, q1_sem, dp, seq),
        GradSum(gq_part.at[2], None, q2_x, q2_land, q2_sem, dp, seq),
    ]
    sum_a.start()
    sum_b.start()
    y_cores = [
        remote(y_all.at[1 + 2 * k], y_land_c.at[k], y_sems.at[0, k], y_sems.at[1, k], dp, mate)
        for k in range(2)
    ]
    y_over = remote(y_sum, y_land_y, y_sems.at[0, 2], y_sems.at[1, 2], dp, across)
    cores = [
        remote(b_rows.at[r], land_c.at[k], row_sems.at[0, k], row_sems.at[1, k], dp, mate)
        for k, r in ((0, 1), (1, 3))
    ]
    over = remote(sum_y, land_y, row_sems.at[0, 2], row_sems.at[1, 2], dp, across)

    def fetch_h(i):
        at = pl.ds(pl.multiple_of(i * rows, rows), rows)
        return pltpu.make_async_copy(h1.at[at], h_buf.at[i % 2], h_sem.at[i % 2])

    fetch_h(0).start()
    fetch_h(1).start()
    y_fetch = [
        pltpu.make_async_copy(y_all.at[2 - 2 * k], y_far.at[k], far_sem.at[k]) for k in range(2)
    ]
    for copy in y_fetch:
        copy.start()
    go_sum[...] = jnp.zeros_like(go_sum)

    def turn(i, carry):
        fetch_h(i).wait()
        turned[:, pl.ds(pl.multiple_of(i * rows, rows), rows)] = h_buf[i % 2].T

        @pl.when(i < 2)
        def _():
            fetch_h(i + 2).start()

        return carry

    small[...] = jnp.zeros_like(small)
    for d in range(8):
        at = slice(d * LANES, (d + 1) * LANES)
        for row, src in ((4, 2), (5, 0), (6, 1), (11, 3)):
            small[d, row : row + 1, :] = mid_sums[src : src + 1, at]
    for i in range(8):
        at = slice(i * LANES, (i + 1) * LANES)
        small[pl.ds(2 * seq + i // 4, 1), 7 + i % 4, :] = up_sum[:, at]
    dk_sum[...] = jnp.zeros_like(dk_sum)
    dv_sum[...] = jnp.zeros_like(dv_sum)
    pos = lax.broadcasted_iota(jnp.int32, (keys, LANES), 0)
    ramp[...] = jnp.where(pos < length_all, pos.astype(f32), -1e33)
    y_cores[1].start()
    y_cores[0].start()
    for copy in loads[:4]:
        copy.wait()
    for p in range(pairs):
        kt[p] = qkv[:, inner + p * LANES : inner + (p + 1) * LANES].T

    def attend_back(r, carry):
        @pl.when(r == 1)
        def _():
            spread_b.near.wait_recv()

        @pl.when(r == 2)
        def _():
            lax.fori_loop(0, 4, turn, 0)
            spread_b.forward()
            y_cores[1].wait_recv()
            for copy in y_fetch:
                copy.wait()
            for i in range(rows // chunk):
                at = slice(i * chunk, (i + 1) * chunk)
                total = y_far[0, at, :].astype(f32) + y_land_c[1, at, :].astype(f32)
                y_sum[at, :] = total.astype(bf16)
            y_over.start()

        @pl.when(r == 3)
        def _():
            spread_b.last.wait_recv()

        c_now = block_at(seq, r)
        at = pl.ds(pl.multiple_of(c_now * rows, rows), rows)
        do[at, :] = mm_t(b_rows[r], flat[...]).astype(bf16)
        go_sum[...] += mm(o[at, :].T, b_rows[r])
        for c in range(keys // rows):

            @pl.when(c_now == c)
            def _(c=c):
                length = (c + 1) * rows
                at = slice(c * rows, length)

                def one_pair(p, carry):
                    lane = pl.ds(pl.multiple_of(p * LANES, LANES), LANES)
                    k_lane = pl.ds(pl.multiple_of(inner + p * LANES, LANES), LANES)
                    v_lane = pl.ds(pl.multiple_of(2 * inner + p * LANES, LANES), LANES)
                    scaled = qkv[at, lane] * bf16(scale)
                    g = do[at, lane]
                    both = (g.astype(f32) * o[at, lane].astype(f32)).T
                    k = qkv[0:length, k_lane]
                    v = qkv[0:length, v_lane]
                    outs = []
                    for h in range(2):
                        half = slice(h * HEAD_DIM, (h + 1) * HEAD_DIM)
                        qm = head_only(scaled, h)
                        gm = head_only(g, h)
                        dot_row = jnp.sum(both[half], axis=0, keepdims=True)
                        log = lse[p, h : h + 1, at]
                        bias = ramp[0:length, :] * slopes[heads + 2 * p + h]
                        e = jnp.exp(scores(k, qm, bias) - log)
                        ds = (e * (mm_t(v, gm) - dot_row)).astype(bf16)
                        dv_sum[p, 0:length, :] += mm(e.astype(bf16), gm)
                        dk_sum[p, 0:length, :] += mm(ds, qm)
                        outs.append(mm(kt[p, half, 0:length], ds))
                    merged[at, lane] = (jnp.concatenate(outs, axis=0).T * scale).astype(bf16)
                    return carry

                lax.fori_loop(0, pairs, one_pair, 0)

        @pl.when(r == 2)
        def _():
            sum_a.add_cross()
            sum_a.stage(0)

        return carry

    lax.fori_loop(0, 4, attend_back, 0)
    for d in range(8):
        go_part[d] = go_sum[:, d * LANES : (d + 1) * LANES].astype(bf16)
    sum_o.start()
    for p in range(pairs):
        lane = slice(p * LANES, (p + 1) * LANES)
        merged[:, inner + p * LANES : inner + (p + 1) * LANES] = dk_sum[p].astype(bf16)
        merged[:, 2 * inner + p * LANES : 2 * inner + (p + 1) * LANES] = dv_sum[p].astype(bf16)
    spread_b.drain()
    sum_a.stage(1)
    for copy in loads[4:]:
        copy.wait()
    qkv_sums[...] = jnp.zeros_like(qkv_sums)

    def qkv_back(t, carry):
        rel = 3 - t
        at = pl.ds(pl.multiple_of(block_at(seq, rel) * rows, rows), rows)
        low = merged[at, :]
        total = mm_t(low[:, :inner], wq[0].reshape(width, inner))
        for c in range(1, 3):
            total += mm_t(low[:, c * inner : (c + 1) * inner], wq[c].reshape(width, inner))
        b_rows[rel] = total.astype(bf16)
        qkv_sums[...] += jnp.sum(low.astype(f32), axis=0, keepdims=True)

        @pl.when(t == 0)
        def _():
            cores[1].start()

        @pl.when(t == 1)
        def _():
            cores[1].wait_recv()
            for i in range(rows // chunk):
                at = slice(i * chunk, (i + 1) * chunk)
                total = b_rows[2, at, :].astype(f32) + land_c[1, at, :].astype(f32)
                sum_y[at, :] = total.astype(bf16)
            over.start()

        @pl.when(t == 2)
        def _():
            cores[0].start()

        return carry

    lax.fori_loop(0, 4, qkv_back, 0)
    for j in range(3):
        cols = slice(j * inner, (j + 1) * inner)
        value = mm(turned[...], merged[:, cols]).astype(bf16)
        gq_part[j] = value.reshape(8, width // 8, inner)
        sums_q[j].start()
        if j == 0:
            sum_a.stage(2)
    for i in range(2):
        at = slice(i * LANES, (i + 1) * LANES)
        small[pl.ds(seq, 1), 2 + i, :] = qkv_sums[:, at]
        at = slice((4 + i) * LANES, (5 + i) * LANES)
        small[pl.ds(4 + seq, 1), 2 + i, :] = qkv_sums[:, at]
    sum_b.add_cross()
    sum_b.stage(0)
    sum_o.add_cross()
    sum_o.stage(0)
    sum_a.finish(gw2_out)
    y_cores[0].wait_recv()
    y_over.wait_recv()

    def out_step(i, carry):
        at = pl.ds(pl.multiple_of(i * chunk, chunk), chunk)
        total = y_far[1, at, :].astype(f32) + y_land_c[0, at, :].astype(f32)
        total = total + y_land_y[at, :].astype(f32)
        output[at, :] = (mid[at, :] + (total + bias_down[...])).astype(bf16)
        return carry

    lax.fori_loop(0, rows // chunk, out_step, 0)
    sum_b.stage(1)
    sum_o.stage(1)
    sums_q[0].add_cross()
    sums_q[0].stage(0)
    cores[0].wait_recv()
    over.wait_recv()
    qkv_gain = [jnp.zeros((1, width), f32), jnp.zeros((1, width), f32)]
    for i in range(rows // chunk):
        at = slice(i * chunk, (i + 1) * chunk)
        unit, inv = normalize(x[at, :].astype(f32))
        e = (b_rows[0, at, :].astype(f32) + land_c[0, at, :].astype(f32)) + land_y[
            at, :
        ].astype(f32)
        grad[at, :] = (dmid[at, :] + norm_back(e, gain1[...], unit, inv)).astype(bf16)
        qkv_gain[0] += jnp.sum(e * unit, axis=0, keepdims=True)
        qkv_gain[1] += jnp.sum(e, axis=0, keepdims=True)
    for d in range(8):
        at = slice(d * LANES, (d + 1) * LANES)
        small[d, 0:1, :] = qkv_gain[0][:, at]
        small[d, 1:2, :] = qkv_gain[1][:, at]

    def small_to(i):
        peer = (dp + i) % 8
        return remote(
            small.at[peer], small_land.at[i], small_sems.at[0, i], small_sems.at[1, i], peer, seq
        )

    for i in range(1, 8):
        small_to(i).start()
    sum_b.stage(2)
    sums_q[1].add_cross()
    sums_q[1].stage(0)
    sums_q[0].stage(1)
    sum_o.stage(2)
    sums_q[2].add_cross()
    sums_q[2].stage(0)
    sums_q[1].stage(1)
    sums_q[0].stage(2)
    total = small[dp]
    for i in range(1, 8):
        small_to(i).wait_recv()
        total = total + small_land[i]
    own[...] = total

    def seq_to(i, peer):
        return remote(own, seq_land.at[i], seq_sems.at[0, i], seq_sems.at[1, i], dp, peer)

    group = [seq_to(i, peer) for i, peer in enumerate(neighbours(seq))]
    for copy in group:
        copy.start()
    sums_q[2].stage(1)
    sums_q[1].stage(2)
    sums_q[2].stage(2)
    sum_b.finish(gw1_out)
    sum_o.finish(go_out)
    for copy in group:
        copy.wait_recv()
    total = (own[...] + seq_land[0]) + (seq_land[1] + seq_land[2])
    narrow = total[:, 0:32]
    for i in range(1, 4):
        narrow = jnp.where(seq == i, total[:, 32 * i : 32 * (i + 1)], narrow)
    narrow_out[...] = narrow
    value = total[2:3, 0:64]
    for i in range(1, 4):
        at = 64 * (i % 2)
        value = jnp.where(seq == i, total[2 + i // 2 : 3 + i // 2, at : at + 64], value)
    qv_out[...] = value
    value = total[7:8]
    for i in range(1, 4):
        value = jnp.where(seq == i, total[7 + i : 8 + i], value)
    up_out[...] = value
    for j in range(3):
        sums_q[j].finish(gq_out.at[j])
    for copy in group + cores + y_cores + [over, y_over]:
        copy.wait_send()
    for i in range(1, 8):
        small_to(i).wait_send()
    for part in [sum_a, sum_b, sum_o] + sums_q:
        part.drain()


def back_call(*args):
    dbr, o, flat, qkv, lse, wq, h1, gw1, gw2 = args[2:11]
    rows, width = dbr.shape
    keys, inner = o.shape
    pairs = inner // LANES
    sem = pltpu.SemaphoreType.DMA
    block = lambda dtype: pltpu.VMEM((rows, width), dtype)
    pair_rows = pltpu.VMEM((2, rows, width), bf16)
    specs = [SCALAR, SCALAR] + [pl.BlockSpec(memory_space=pl.ANY)] * (len(args) - 2)
    for at in (6, 13, 16, 17, 18):
        specs[at] = WHOLE
    shape = jax.ShapeDtypeStruct
    return pl.pallas_call(
        back_body,
        out_shape=(
            shape((rows, width), bf16),
            shape((rows, width), bf16),
            shape((3, width // 8, inner), f32),
            shape((inner, LANES), f32),
            shape(gw1.shape[1:], f32),
            shape(gw2.shape[1:], f32),
            shape((SMALL_ROWS, 32), f32),
            shape((1, 64), f32),
            shape((1, LANES), f32),
        ),
        in_specs=specs,
        out_specs=(WHOLE,) * 9,
        scratch_shapes=[
            pltpu.VMEM(o.shape, bf16),
            pltpu.VMEM(flat.shape, bf16),
            pltpu.VMEM(qkv.shape, bf16),
            pltpu.VMEM(wq.shape, bf16),
            block(f32),
            block(bf16),
            block(f32),
            pltpu.VMEM((4, rows, width), bf16),
            pair_rows,
            pltpu.VMEM((keys, inner), bf16),
            pltpu.VMEM((inner, width), f32),
            pltpu.VMEM((8, inner, LANES), bf16),
            pltpu.VMEM((keys, LANES), f32),
            pltpu.VMEM((pairs, LANES, keys), bf16),
            pltpu.VMEM((pairs, keys, LANES), f32),
            pltpu.VMEM((pairs, keys, LANES), f32),
            pltpu.VMEM((keys, 3 * inner), bf16),
            pltpu.VMEM((1, 3 * inner), f32),
            pair_rows,
            pltpu.VMEM((width, keys), bf16),
            pltpu.VMEM((3, 8, width // 8, inner), bf16),
            pair_rows, block(bf16), block(bf16),
            pair_rows, block(bf16), block(bf16),
            *GradSum.scratch(*gw2.shape[1:], fetched=True),
            *GradSum.scratch(*gw1.shape[1:], fetched=True),
            *GradSum.scratch(inner, LANES),
            *(GradSum.scratch(width // 8, inner) * 3),
            pltpu.VMEM((8, SMALL_ROWS, LANES), f32),
            pltpu.VMEM((8, SMALL_ROWS, LANES), f32),
            pltpu.VMEM((SMALL_ROWS, LANES), f32),
            pltpu.VMEM((3, SMALL_ROWS, LANES), f32),
            sem((2, 4)), sem((2, 3)), sem((2, 3)), sem((2,)), sem((2, 8)), sem((2, 3)), sem((2,)),
            sem((8,)),
        ],
        compiler_params=pltpu.CompilerParams(
            vmem_limit_bytes=67043328, collective_id=3, has_side_effects=True
        ),
        name="back",
    )(*args)


def finish_body(
    output, grad, gq, go, gw1, gw2, narrow, qv, up,
    output_out, grad_out, gq_out, go_out, gw1_out, gw2_out,
    gain1, shift1, qv_out, bout, gain2, shift2, up_out, down,
):
    for src, dst in (
        (output, output_out), (grad, grad_out), (gq, gq_out), (go, go_out), (gw1, gw1_out),
        (gw2, gw2_out), (qv, qv_out), (up, up_out),
    ):
        dst[...] = src[...]
    for ref, row in ((gain1, 0), (shift1, 1), (bout, 4), (gain2, 5), (shift2, 6), (down, 11)):
        ref[...] = narrow[row : row + 1, :]


def finish_call(output, grad, gq, go, gw1, gw2, narrow, qv, up):
    steps = 4
    like = lambda v: jax.ShapeDtypeStruct(v.shape, v.dtype)
    cut = lambda v: pl.BlockSpec((v.shape[0] // steps, v.shape[1]), lambda i: (i, 0))
    still = lambda v: pl.BlockSpec(v.shape, lambda i: (0, 0))
    deep = pl.BlockSpec((3, gq.shape[1] // steps, gq.shape[2]), lambda i: (0, i, 0))
    one = jax.ShapeDtypeStruct((1, 32), f32)
    specs = [cut(output), cut(grad), deep, cut(go), cut(gw1), cut(gw2)]
    return pl.pallas_call(
        finish_body,
        out_shape=(
            like(output), like(grad), like(gq), like(go), like(gw1), like(gw2),
            one, one, like(qv), one, one, one, like(up), one,
        ),
        grid=(steps,),
        in_specs=specs + [still(narrow), still(qv), still(up)],
        out_specs=specs
        + [still(one), still(one), still(qv), still(one), still(one), still(one), still(up), still(one)],
        compiler_params=params(),
        name="finish",
    )(output, grad, gq, go, gw1, gw2, narrow, qv, up)


def after(value, *others):
    return lax.optimization_barrier((value, *others))[0]


def on_device(
    dp_n,
    seq_n,
    tokens,
    lengths,
    cotangent,
    ln1_gain,
    ln1_shift,
    w_qkv,
    b_qv,
    w_out,
    b_out,
    ln2_gain,
    ln2_shift,
    w_fc1,
    b_fc1,
    w_fc2,
    b_fc2,
):
    count = dp_n * seq_n
    rows, width = tokens.shape
    heads = width // HEAD_DIM
    inner = w_out.shape[0]
    ff = w_fc1.shape[1]
    s = lax.axis_index("seq")
    length = lengths[0]

    scal = jnp.stack([s.astype(jnp.int32), length])
    slopes = 2.0 ** (-8.0 * (jnp.arange(heads, dtype=jnp.int32) + 1).astype(f32) / heads)
    slopes_all = slopes
    slopes = lax.dynamic_slice(slopes, (s * (heads // seq_n),), (heads // seq_n,))
    valid = s * rows + jnp.arange(rows, dtype=jnp.int32) < length
    grad_low = jnp.where(valid[:, None], cotangent, jnp.zeros_like(cotangent))
    wq_own = jnp.concatenate([w_qkv[:, c, :] for c in range(3)], axis=1)
    small = (ln1_gain, ln1_shift, b_qv, b_out, ln2_gain, ln2_shift, b_fc1, b_fc2)
    sizes = [v.shape[0] for v in small]
    ends = [sum(sizes[: i + 1]) for i in range(len(sizes))]
    block = 384
    fast = dp_n == 8 and seq_n == 4 and width == 8 * LANES and ff == width and inner == 2 * LANES
    if fast:
        parts = dp_n
        order = (b_fc1, b_qv, ln1_gain, ln1_shift, b_out, ln2_gain, ln2_shift, b_fc2)
        (
            h1, qkv, o, lse, wq, w_o, mid, gain1, bias_down, y_all, grad_up, grad_down, dmid, dbr,
            mid_sums, up_sum,
        ) = fore_call(
            lengths, slopes_all, jnp.transpose(w_qkv, (1, 0, 2)), w_out, tokens, order, cotangent,
            w_fc1, w_fc2,
        )
        results = back_call(
            lengths, slopes_all, dbr, o, w_o, qkv, lse, wq, h1, grad_up, grad_down, y_all, mid,
            bias_down, tokens, dmid, gain1, mid_sums, up_sum,
        )
        output, grad_tokens, grad_qkv, grad_out, grad_up, grad_down, *vectors = finish_call(*results)
        grad_qkv = jnp.transpose(grad_qkv, (1, 0, 2))
        g_gain1, g_shift1, g_qv, g_bout, g_gain2, g_shift2, g_up, g_down = (
            v.reshape(n) for v, n in zip(vectors, sizes)
        )
        return (
            output, grad_tokens, g_gain1, g_shift1, grad_qkv, g_qv, grad_out, g_bout,
            g_gain2, g_shift2, grad_up, g_up, grad_down, g_down,
        )

    wq = lax.all_gather(wq_own, "dp", axis=0, tiled=True)
    col = w_fc2.shape[1]
    both = jnp.concatenate([w_fc2, w_out], axis=0)
    if col % LANES == 0:
        parts = dp_n
        w_cols = lax.all_gather(both, "dp", axis=0, tiled=False)
    else:
        parts = 1
        w_cols = lax.all_gather(both, "dp", axis=1, tiled=True)[None]
    w_o = w_cols
    out_first = ff
    w1 = lax.all_gather(w_fc1, "dp", axis=0, tiled=True)
    packed = small_gather(jnp.concatenate([v.astype(f32) for v in small]), count, seq_n)
    packed = packed.reshape(count, ends[-1])
    gain1, shift1, bias_qv, bias_out, gain2, shift2, bias_up, bias_down = (
        packed[:, e - n : e].reshape(1, count * n) for e, n in zip(ends, sizes)
    )
    own_bias = lambda v, n: lax.dynamic_slice(v, (0, s * n), (1, n))
    own_up = own_bias(bias_up, ff)
    qkv_bias = jnp.concatenate(
        [
            own_bias(bias_qv[:, :width], inner),
            jnp.zeros((1, inner), f32),
            own_bias(bias_qv[:, width:], inner),
        ],
        axis=1,
    )
    x_pieces = spread(tokens)
    g_rows = jnp.stack(spread(after(grad_low, x_pieces[3])))
    h1, qkv = qkv_call(scal, x_pieces, wq, gain1, shift1, qkv_bias)
    o, lse = attend_call(scal, slopes, qkv, block)
    near, far = out_call(scal, o, w_o, out_first)
    got, across = reduce_rows(near, far)
    mid, h2 = mid_call(tokens, far, got, across, bias_out, gain2, shift2)
    h_pieces = spread(h2)
    y_near, y_far, d_near, d_far, a_all, du_all, h_all, g_all, up_sum = mlp_call(
        h_pieces, g_rows, w1, w_cols, own_up
    )
    got, across = reduce_rows(d_near, d_far)
    grad_down = outer_call(a_all, g_all, parts, "grad_fc2")
    grad_up = outer_call(h_all, du_all, 1, "grad_fc1")
    dmid, dbr, mid_sums = mid_back_call(mid, d_far, got, across, grad_low, gain2)

    b_pieces = spread(dbr)

    y_near = after(y_near, b_pieces[3])
    got, across = reduce_rows(y_near, y_far)
    output = (
        mid + ((y_far[1].astype(f32) + got[0].astype(f32)) + across.astype(f32) + bias_down)
    ).astype(bf16)

    do, grad_out = out_back_call(scal, b_pieces, o, w_o, out_first)
    dq, dk, dv = attend_back_call(scal, slopes, qkv, o, do, lse, block)
    near, far, merged, qkv_sums = qkv_back_call(scal, dq, dk, dv, wq)
    grad_qkv = outer_call(h1, merged, 1, "grad_qkv")

    def shared(part):
        if parts > 1:
            return lax.psum_scatter(part, "dp", scatter_dimension=0, tiled=False).astype(f32)
        return lax.psum_scatter(part, "dp", scatter_dimension=1, tiled=True).astype(f32)

    grad_down = shared(grad_down if parts > 1 else grad_down)
    grad_up = lax.psum_scatter(grad_up, "dp", scatter_dimension=0, tiled=True).astype(f32)
    got, across = reduce_rows(near, far)
    grad_tokens, in_sums = in_back_call(tokens, far, got, across, dmid, gain1)
    grad_out = shared(grad_out if parts > 1 else grad_out[0])
    grad_qkv = lax.psum_scatter(grad_qkv, "dp", scatter_dimension=0, tiled=True)
    grad_qkv = grad_qkv.astype(f32).reshape(w_qkv.shape)

    def own_slot(v, total):
        return lax.dynamic_update_slice(jnp.zeros((1, total), f32), v, (0, s * v.shape[1]))

    sums = (
        in_sums[0:1],
        in_sums[1:2],
        jnp.concatenate(
            [own_slot(qkv_sums[:, :inner], width), own_slot(qkv_sums[:, 2 * inner :], width)], axis=1
        ),
        mid_sums[2:3],
        mid_sums[0:1],
        mid_sums[1:2],
        own_slot(up_sum, seq_n * ff),
        mid_sums[3:4],
    )
    grads = jnp.concatenate([v.reshape(count, n) for v, n in zip(sums, sizes)], axis=1)
    grads = small_scatter(grads, count, seq_n).reshape(ends[-1])
    g_gain1, g_shift1, g_qv, g_bout, g_gain2, g_shift2, g_up, g_down = (
        grads[e - n : e] for e, n in zip(ends, sizes)
    )
    return (
        output,
        grad_tokens,
        g_gain1,
        g_shift1,
        grad_qkv,
        g_qv,
        grad_out,
        g_bout,
        g_gain2,
        g_shift2,
        grad_up,
        g_up,
        grad_down,
        g_down,
    )


def solution(mesh):
    rows = P(("dp", "seq"), None)
    vec = P(("dp", "seq"))
    merged = P("dp", None, "seq")
    return jax.shard_map(
        functools.partial(on_device, mesh.shape["dp"], mesh.shape["seq"]),
        mesh=mesh,
        in_specs=(
            rows, P("dp"), rows, vec, vec, merged, vec, P("seq", "dp"), vec, vec, vec,
            P("dp", "seq"), vec, P("seq", "dp"), vec,
        ),
        out_specs=(
            rows, rows, vec, vec, merged, vec, P("seq", "dp"), vec, vec, vec,
            P("dp", "seq"), vec, P("seq", "dp"), vec,
        ),
        check_vma=False,
    )
```

```python
import functools
import math

import jax
import jax.numpy as jnp
from jax import lax
from jax.experimental import pallas as pl
from jax.experimental.pallas import tpu as pltpu
from jax.sharding import PartitionSpec as P

HEAD_DIM = 64
EPS = 1e-05
GELU_COEF = 0.044715
NEG = -1e30
LANES = 128
VMEM_BYTES = 60 * 1024 * 1024

f32 = jnp.float32
bf16 = jnp.bfloat16
WHOLE = pl.BlockSpec(memory_space=pltpu.VMEM)
SCALAR = pl.BlockSpec(memory_space=pltpu.SMEM)


def mm(a, b):
    return jnp.dot(a, b, preferred_element_type=f32)


def mm_t(a, b):
    return lax.dot_general(a, b, (((1,), (1,)), ((), ())), preferred_element_type=f32)


def params(**kw):
    return pltpu.CompilerParams(vmem_limit_bytes=VMEM_BYTES, **kw)


def normalize(v):
    width = v.shape[-1]
    centred = v - jnp.sum(v, axis=-1, keepdims=True) * (1.0 / width)
    inv = lax.rsqrt(jnp.sum(centred * centred, axis=-1, keepdims=True) * (1.0 / width) + EPS)
    return centred * inv, inv


def norm_back(grad_out, gain, unit, inv):
    width = unit.shape[-1]
    scaled = grad_out * gain
    mean_one = jnp.sum(scaled, axis=-1, keepdims=True) * (1.0 / width)
    mean_two = jnp.sum(scaled * unit, axis=-1, keepdims=True) * (1.0 / width)
    return inv * (scaled - mean_one - unit * mean_two)


def device_of(index, seq_n):
    return (index // seq_n, index % seq_n)


def greet_all(me, count, seq_n):
    barrier = pltpu.get_barrier_semaphore()

    def hello(i, carry):
        peer = (me + i) % count
        pl.semaphore_signal(
            barrier, inc=1, device_id=device_of(peer, seq_n), device_id_type=pl.DeviceIdType.MESH
        )
        return carry

    lax.fori_loop(1, count, hello, 0)
    pl.semaphore_wait(barrier, count - 1)


def small_gather_body(count, seq_n, x_ref, out_ref, send_sem, recv_sem):
    me = lax.axis_index("dp") * seq_n + lax.axis_index("seq")
    greet_all(me, count, seq_n)

    def copy_to(i):
        peer = (me + i) % count
        return pltpu.make_async_remote_copy(
            src_ref=x_ref,
            dst_ref=out_ref.at[pl.ds(me, 1)],
            send_sem=send_sem.at[i],
            recv_sem=recv_sem.at[i],
            device_id=device_of(peer, seq_n),
            device_id_type=pl.DeviceIdType.MESH,
        )

    def begin(i, carry):
        copy_to(i).start()
        return carry

    def finish(i, carry):
        copy_to(i).wait()
        return carry

    lax.fori_loop(1, count, begin, 0)
    out_ref[pl.ds(me, 1)] = x_ref[...]
    lax.fori_loop(1, count, finish, 0)


def small_gather(x, count, seq_n):
    width = x.shape[-1]
    return pl.pallas_call(
        functools.partial(small_gather_body, count, seq_n),
        out_shape=jax.ShapeDtypeStruct((count, 1, width), f32),
        in_specs=[WHOLE],
        out_specs=WHOLE,
        scratch_shapes=[pltpu.SemaphoreType.DMA((count,)), pltpu.SemaphoreType.DMA((count,))],
        compiler_params=pltpu.CompilerParams(collective_id=1, has_side_effects=True),
        name="small_gather",
    )(x.reshape(1, 1, width))


def small_scatter_body(count, seq_n, v_ref, out_ref, land, send_sem, recv_sem):
    me = lax.axis_index("dp") * seq_n + lax.axis_index("seq")
    greet_all(me, count, seq_n)

    def copy_to(i):
        peer = (me + i) % count
        return pltpu.make_async_remote_copy(
            src_ref=v_ref.at[pl.ds(peer, 1)],
            dst_ref=land.at[pl.ds(i, 1)],
            send_sem=send_sem.at[i],
            recv_sem=recv_sem.at[i],
            device_id=device_of(peer, seq_n),
            device_id_type=pl.DeviceIdType.MESH,
        )

    def begin(i, carry):
        copy_to(i).start()
        return carry

    def finish(i, total):
        copy_to(i).wait()
        return total + land[pl.ds(i, 1)]

    lax.fori_loop(1, count, begin, 0)
    out_ref[...] = lax.fori_loop(1, count, finish, v_ref[pl.ds(me, 1)])


def small_scatter(v, count, seq_n):
    width = v.shape[-1]
    return pl.pallas_call(
        functools.partial(small_scatter_body, count, seq_n),
        out_shape=jax.ShapeDtypeStruct((1, 1, width), f32),
        in_specs=[WHOLE],
        out_specs=WHOLE,
        scratch_shapes=[
            pltpu.VMEM((count, 1, width), f32),
            pltpu.SemaphoreType.DMA((count,)),
            pltpu.SemaphoreType.DMA((count,)),
        ],
        compiler_params=pltpu.CompilerParams(collective_id=2, has_side_effects=True),
        name="small_scatter",
    )(v.reshape(count, 1, width))


def swap(x, bit):
    return lax.ppermute(x, "seq", [(i, i ^ bit) for i in range(4)])


def spread(own):
    far = swap(own, 2)
    return own, swap(own, 1), far, swap(far, 1)


def reduce_rows(near, far):
    got = swap(near, 1)
    across = swap(far[0] + got[1], 2)
    return got, across


def pick(step, refs, dest):
    for k, ref in enumerate(refs):

        @pl.when(step == k)
        def _(ref=ref):
            dest[...] = ref[...]


ORDER = (1, 3, 2, 0)


def rel_of(t):
    return jnp.where(t == 0, 1, jnp.where(t == 1, 3, jnp.where(t == 2, 2, 0)))


def qkv_body(scal, x0, x1, x2, x3, w, gain, shift, bias, h1, qkv, rows):
    pick(pl.program_id(0), (x0, x1, x2, x3), rows)
    unit, _ = normalize(rows[...].astype(f32))
    low = (unit * gain[...] + shift[...]).astype(bf16)
    h1[...] = low
    qkv[...] = (mm(low, w[...]) + bias[...]).astype(bf16)


def qkv_call(scal, pieces, w, gain, shift, bias):
    rows, width = pieces[0].shape
    cols = w.shape[1]
    out = lambda r, sc: (lax.bitwise_xor(sc[0], r), 0)
    return pl.pallas_call(
        qkv_body,
        out_shape=(
            jax.ShapeDtypeStruct((4 * rows, width), bf16),
            jax.ShapeDtypeStruct((4 * rows, cols), bf16),
        ),
        grid_spec=pltpu.PrefetchScalarGridSpec(
            num_scalar_prefetch=1,
            grid=(4,),
            in_specs=[WHOLE] * 8,
            out_specs=(pl.BlockSpec((rows, width), out), pl.BlockSpec((rows, cols), out)),
            scratch_shapes=[pltpu.VMEM((rows, width), bf16)],
        ),
        compiler_params=params(),
        name="qkv",
    )(scal, *pieces, w, gain, shift, bias)


def make_bias(scal, slopes, pair, bias, keys):
    pos = lax.broadcasted_iota(jnp.int32, (keys, LANES), 0)
    inside = pos < scal[1]
    ramp = pos.astype(f32)
    for h in range(2):
        bias[h] = jnp.where(inside, ramp * slopes[2 * pair + h], NEG)


def head_only(x, h):
    lane = lax.broadcasted_iota(jnp.int32, x.shape, 1)
    return jnp.where((lane >= h * HEAD_DIM) & (lane < (h + 1) * HEAD_DIM), x, jnp.zeros_like(x))


def score_t(k_ref, qm, bias, h, length):
    block = qm.shape[0]
    s = mm_t(k_ref[0:length, :], qm)
    b = bias[h, 0:length, :]
    s = s + jnp.concatenate([b] * (block // LANES), axis=1)
    key = lax.broadcasted_iota(jnp.int32, (block, block), 0)
    query = lax.broadcasted_iota(jnp.int32, (block, block), 1)
    last = jnp.where(key <= query, s[length - block :], NEG)
    if length == block:
        return last
    return jnp.concatenate([s[: length - block], last], axis=0)


def attend_body(scal, q, k, v, slopes, o, lse, bias, vt):
    pair, step = pl.program_id(0), pl.program_id(1)
    block = q.shape[0]
    keys = k.shape[0]

    @pl.when(step == 0)
    def _():
        make_bias(scal, slopes, pair, bias, keys)
        vt[...] = v[...].T

    for c in range(keys // block):

        @pl.when(step == c)
        def _(c=c):
            length = (c + 1) * block
            scaled = q[...] * bf16(HEAD_DIM**-0.5)
            outs, logs = [], []
            for h in range(2):
                s = score_t(k, head_only(scaled, h), bias, h, length)
                top = jnp.max(s, axis=0, keepdims=True)
                e = jnp.exp(s - top)
                total = jnp.sum(e, axis=0, keepdims=True)
                mixed = mm(vt[h * HEAD_DIM : (h + 1) * HEAD_DIM, 0:length], e.astype(bf16))
                outs.append(mixed / total)
                logs.append(top + jnp.log(total))
            o[...] = jnp.concatenate(outs, axis=0).T.astype(bf16)
            lse[0, 0:2, :] = jnp.concatenate(logs, axis=0)


def attend_call(scal, slopes, qkv, block):
    keys, cols = qkv.shape
    width = cols // 3
    pairs = width // LANES
    return pl.pallas_call(
        attend_body,
        out_shape=(
            jax.ShapeDtypeStruct((keys, width), bf16),
            jax.ShapeDtypeStruct((pairs, 8, keys), f32),
        ),
        grid_spec=pltpu.PrefetchScalarGridSpec(
            num_scalar_prefetch=1,
            grid=(pairs, keys // block),
            in_specs=[
                pl.BlockSpec((block, LANES), lambda p, c, sc: (c, p)),
                pl.BlockSpec((keys, LANES), lambda p, c, sc: (0, pairs + p)),
                pl.BlockSpec((keys, LANES), lambda p, c, sc: (0, 2 * pairs + p)),
                SCALAR,
            ],
            out_specs=(
                pl.BlockSpec((block, LANES), lambda p, c, sc: (c, p)),
                pl.BlockSpec((1, 8, block), lambda p, c, sc: (p, 0, c)),
            ),
            scratch_shapes=[
                pltpu.VMEM((2, keys, LANES), f32),
                pltpu.VMEM((LANES, keys), bf16),
            ],
        ),
        compiler_params=params(),
        name="attend",
    )(scal, qkv, qkv, qkv, slopes)


def attend_back_body(scal, q, k, v, o, do, lse, slopes, dq, dk, dv, bias, kt, dk_sum, dv_sum):
    pair, step = pl.program_id(0), pl.program_id(1)
    block = q.shape[0]
    keys = k.shape[0]
    scale = HEAD_DIM**-0.5

    @pl.when(step == 0)
    def _():
        make_bias(scal, slopes, pair, bias, keys)
        kt[...] = k[...].T
        dk_sum[...] = jnp.zeros_like(dk_sum)
        dv_sum[...] = jnp.zeros_like(dv_sum)

    for c in range(keys // block):

        @pl.when(step == c)
        def _(c=c):
            length = (c + 1) * block
            scaled = q[...] * bf16(scale)
            both = (do[...].astype(f32) * o[...].astype(f32)).T
            outs = []
            for h in range(2):
                qm = head_only(scaled, h)
                dom = head_only(do[...], h)
                dot_row = jnp.sum(both[h * HEAD_DIM : (h + 1) * HEAD_DIM], axis=0, keepdims=True)
                p = jnp.exp(score_t(k, qm, bias, h, length) - lse[0, h : h + 1, :])
                dp = mm_t(v[0:length, :], dom)
                ds = (p * (dp - dot_row)).astype(bf16)
                dv_sum[0:length, :] += mm(p.astype(bf16), dom)
                dk_sum[0:length, :] += mm(ds, qm)
                outs.append(mm(kt[h * HEAD_DIM : (h + 1) * HEAD_DIM, 0:length], ds))
            dq[...] = (jnp.concatenate(outs, axis=0).T * scale).astype(bf16)

    @pl.when(step == keys // block - 1)
    def _():
        dk[...] = dk_sum[...].astype(bf16)
        dv[...] = dv_sum[...].astype(bf16)


def attend_back_call(scal, slopes, qkv, o, do, lse, block):
    keys, cols = qkv.shape
    width = cols // 3
    pairs = width // LANES
    some = pl.BlockSpec((block, LANES), lambda p, c, sc: (c, p))
    full = pl.BlockSpec((keys, LANES), lambda p, c, sc: (0, p))
    return pl.pallas_call(
        attend_back_body,
        out_shape=(jax.ShapeDtypeStruct((keys, width), bf16),) * 3,
        grid_spec=pltpu.PrefetchScalarGridSpec(
            num_scalar_prefetch=1,
            grid=(pairs, keys // block),
            in_specs=[
                some,
                pl.BlockSpec((keys, LANES), lambda p, c, sc: (0, pairs + p)),
                pl.BlockSpec((keys, LANES), lambda p, c, sc: (0, 2 * pairs + p)),
                some,
                some,
                pl.BlockSpec((1, 8, block), lambda p, c, sc: (p, 0, c)),
                SCALAR,
            ],
            out_specs=(some, full, full),
            scratch_shapes=[
                pltpu.VMEM((2, keys, LANES), f32),
                pltpu.VMEM((LANES, keys), bf16),
                pltpu.VMEM((keys, LANES), f32),
                pltpu.VMEM((keys, LANES), f32),
            ],
        ),
        compiler_params=params(),
        name="attend_back",
    )(scal, qkv, qkv, qkv, o, do, lse, slopes)


def lay_columns(w_ref, first, dest):
    width = w_ref.shape[2]
    for d in range(w_ref.shape[0]):
        dest[:, d * width : (d + 1) * width] = w_ref[d, first : first + dest.shape[0], :]


def out_body(scal, o, w, near, far, flat, *, first):
    t = pl.program_id(0)

    @pl.when(t == 0)
    def _():
        lay_columns(w, first, flat)

    part = mm(o[...], flat[...]).astype(bf16)

    @pl.when(t < 2)
    def _():
        near[0] = part

    @pl.when(t >= 2)
    def _():
        far[0] = part


def near_map(t, *_):
    return (jnp.minimum(t, 1), 0, 0)


def far_map(t, *_):
    return (jnp.maximum(t - 2, 0), 0, 0)


def out_call(scal, o, w, first):
    keys, inner = o.shape
    rows = keys // 4
    width = w.shape[0] * w.shape[2]
    return pl.pallas_call(
        functools.partial(out_body, first=first),
        out_shape=(jax.ShapeDtypeStruct((2, rows, width), bf16),) * 2,
        grid_spec=pltpu.PrefetchScalarGridSpec(
            num_scalar_prefetch=1,
            grid=(4,),
            in_specs=[
                pl.BlockSpec((rows, inner), lambda t, sc: (lax.bitwise_xor(sc[0], rel_of(t)), 0)),
                WHOLE,
            ],
            out_specs=(
                pl.BlockSpec((1, rows, width), near_map),
                pl.BlockSpec((1, rows, width), far_map),
            ),
            scratch_shapes=[pltpu.VMEM((inner, width), bf16)],
        ),
        compiler_params=params(),
        name="out_proj",
    )(scal, o, w)


def mid_body(x, a, b, c, bias, gain, shift, mid, h2):
    value = x[...].astype(f32) + (
        (a[0].astype(f32) + b[0].astype(f32)) + c[...].astype(f32) + bias[...]
    )
    mid[...] = value
    unit, _ = normalize(value)
    h2[...] = (unit * gain[...] + shift[...]).astype(bf16)


def mid_call(x, a, b, c, bias, gain, shift):
    rows, width = x.shape
    one = pl.BlockSpec((rows // 2, width), lambda i: (i, 0))
    first = pl.BlockSpec((1, rows // 2, width), lambda i: (0, i, 0))
    second = pl.BlockSpec((1, rows // 2, width), lambda i: (1, i, 0))
    row = pl.BlockSpec((1, width), lambda i: (0, 0))
    return pl.pallas_call(
        mid_body,
        out_shape=(
            jax.ShapeDtypeStruct((rows, width), f32),
            jax.ShapeDtypeStruct((rows, width), bf16),
        ),
        grid=(2,),
        in_specs=[one, second, first, one, row, row, row],
        out_specs=(one, one),
        compiler_params=params(),
        name="mid_norm",
    )(x, a, b, c, bias, gain, shift)


def gelu_parts(u):
    root = math.sqrt(2.0 / math.pi)
    sq = u * u
    t = jnp.tanh(root * (u + GELU_COEF * (sq * u)))
    half = 0.5 * (1.0 + t)
    slope = half + 0.5 * u * (1.0 - t * t) * (root * (1.0 + 3.0 * GELU_COEF * sq))
    return u * half, slope


def mlp_body(
    h0, h1, h2, h3, g_rows, w1, w2, b1,
    y_near, y_far, d_near, d_far, a_all, du_all, h_all, g_all, bias_sum,
    flat, hb, gb,
):
    t = pl.program_id(0)

    @pl.when(t == 0)
    def _():
        lay_columns(w2, 0, flat)
        bias_sum[...] = jnp.zeros_like(bias_sum)

    pick(rel_of(t), (h0, h1, h2, h3), hb)
    gb[...] = g_rows[rel_of(t)]
    h_all[...] = hb[...]
    g_all[...] = gb[...]
    inner = w1.shape[1]
    chunk = 256
    for c in range(inner // chunk):
        cols = slice(c * chunk, (c + 1) * chunk)
        u = mm(hb[...], w1[:, cols]) + b1[:, cols]
        value, slope = gelu_parts(u)
        a_all[:, cols] = value.astype(bf16)
        du = (mm_t(gb[...], flat[cols, :]) * slope).astype(bf16)
        du_all[:, cols] = du
        bias_sum[:, cols] += jnp.sum(du.astype(f32), axis=0, keepdims=True)
    y = mm(a_all[...], flat[...]).astype(bf16)
    d = mm_t(du_all[...], w1[...]).astype(bf16)

    @pl.when(t < 2)
    def _():
        y_near[0] = y
        d_near[0] = d

    @pl.when(t >= 2)
    def _():
        y_far[0] = y
        d_far[0] = d


def mlp_call(h_pieces, g_rows, w1, w2, b1):
    rows, width = h_pieces[0].shape
    inner = w1.shape[1]
    pair = jax.ShapeDtypeStruct((2, rows, width), bf16)
    near = pl.BlockSpec((1, rows, width), near_map)
    far = pl.BlockSpec((1, rows, width), far_map)
    block = lambda n: pl.BlockSpec((rows, n), lambda t: (t, 0))
    return pl.pallas_call(
        mlp_body,
        out_shape=(
            pair,
            pair,
            pair,
            pair,
            jax.ShapeDtypeStruct((4 * rows, inner), bf16),
            jax.ShapeDtypeStruct((4 * rows, inner), bf16),
            jax.ShapeDtypeStruct((4 * rows, width), bf16),
            jax.ShapeDtypeStruct((4 * rows, width), bf16),
            jax.ShapeDtypeStruct((1, inner), f32),
        ),
        grid=(4,),
        in_specs=[WHOLE] * 8,
        out_specs=(
            near, far, near, far, block(inner), block(inner), block(width), block(width),
            pl.BlockSpec((1, inner), lambda t: (0, 0)),
        ),
        scratch_shapes=[
            pltpu.VMEM((inner, width), bf16),
            pltpu.VMEM((rows, width), bf16),
            pltpu.VMEM((rows, width), bf16),
        ],
        compiler_params=params(),
        name="mlp",
    )(*h_pieces, g_rows, w1, w2, b1)


def outer_body(left, right, out, turned, *, blocks):
    @pl.when(pl.program_id(0) == 0)
    def _():
        turned[...] = left[...].T

    part = mm(turned[...], right[...]).astype(bf16)
    if blocks:
        width = out.shape[2]
        for d in range(out.shape[0]):
            out[d] = part[:, d * width : (d + 1) * width]
    else:
        out[...] = part


def outer_call(left, right, parts, name):
    rows, m = left.shape
    n = right.shape[1]
    step = 256
    if parts > 1:
        width = n // parts
        out_shape = jax.ShapeDtypeStruct((parts, m, width), bf16)
        out_spec = pl.BlockSpec((step // width, m, width), lambda j: (j, 0, 0))
    else:
        out_shape = jax.ShapeDtypeStruct((m, n), bf16)
        out_spec = pl.BlockSpec((m, step), lambda j: (0, j))
    return pl.pallas_call(
        functools.partial(outer_body, blocks=parts > 1),
        out_shape=out_shape,
        grid=(n // step,),
        in_specs=[WHOLE, pl.BlockSpec((rows, step), lambda j: (0, j))],
        out_specs=out_spec,
        scratch_shapes=[pltpu.VMEM((m, rows), bf16)],
        compiler_params=params(),
        name=name,
    )(left, right)


def mid_back_body(mid, a, b, c, g, gain, dmid, dbr, sums):
    @pl.when(pl.program_id(0) == 0)
    def _():
        sums[...] = jnp.zeros_like(sums)

    unit, inv = normalize(mid[...])
    e = (a[0].astype(f32) + b[0].astype(f32)) + c[...].astype(f32)
    grad = g[...].astype(f32)
    value = grad + norm_back(e, gain[...], unit, inv)
    dmid[...] = value
    low = value.astype(bf16)
    dbr[...] = low
    sums[0:1, :] += jnp.sum(e * unit, axis=0, keepdims=True)
    sums[1:2, :] += jnp.sum(e, axis=0, keepdims=True)
    sums[2:3, :] += jnp.sum(low.astype(f32), axis=0, keepdims=True)
    sums[3:4, :] += jnp.sum(grad, axis=0, keepdims=True)


def mid_back_call(mid, a, b, c, g, gain):
    rows, width = mid.shape
    one = pl.BlockSpec((rows // 2, width), lambda i: (i, 0))
    first = pl.BlockSpec((1, rows // 2, width), lambda i: (0, i, 0))
    second = pl.BlockSpec((1, rows // 2, width), lambda i: (1, i, 0))
    row = pl.BlockSpec((1, width), lambda i: (0, 0))
    return pl.pallas_call(
        mid_back_body,
        out_shape=(
            jax.ShapeDtypeStruct((rows, width), f32),
            jax.ShapeDtypeStruct((rows, width), bf16),
            jax.ShapeDtypeStruct((8, width), f32),
        ),
        grid=(2,),
        in_specs=[one, second, first, one, one, row],
        out_specs=(one, one, pl.BlockSpec((8, width), lambda i: (0, 0))),
        compiler_params=params(),
        name="mid_back",
    )(mid, a, b, c, g, gain)


def out_back_body(scal, b0, b1, b2, b3, o, w, do, grad, flat, rows, total, *, first):
    r = pl.program_id(0)

    @pl.when(r == 0)
    def _():
        lay_columns(w, first, flat)
        total[...] = jnp.zeros_like(total)

    pick(r, (b0, b1, b2, b3), rows)
    do[...] = mm_t(rows[...], flat[...]).astype(bf16)
    total[...] += mm(o[...].T, rows[...])

    @pl.when(r == 3)
    def _():
        width = grad.shape[2]
        for d in range(grad.shape[0]):
            grad[d] = total[:, d * width : (d + 1) * width].astype(bf16)


def out_back_call(scal, pieces, o, w, first):
    rows, width = pieces[0].shape
    inner = o.shape[1]
    at = pl.BlockSpec((rows, inner), lambda r, sc: (lax.bitwise_xor(sc[0], r), 0))
    grad = (w.shape[0], inner, w.shape[2])
    return pl.pallas_call(
        functools.partial(out_back_body, first=first),
        out_shape=(jax.ShapeDtypeStruct(o.shape, bf16), jax.ShapeDtypeStruct(grad, bf16)),
        grid_spec=pltpu.PrefetchScalarGridSpec(
            num_scalar_prefetch=1,
            grid=(4,),
            in_specs=[WHOLE] * 4 + [at, WHOLE],
            out_specs=(at, pl.BlockSpec(grad, lambda r, sc: (0, 0, 0))),
            scratch_shapes=[
                pltpu.VMEM((inner, width), bf16),
                pltpu.VMEM((rows, width), bf16),
                pltpu.VMEM((inner, width), f32),
            ],
        ),
        compiler_params=params(),
        name="out_back",
    )(scal, *pieces, o, w)


def qkv_back_body(scal, dq, dk, dv, w, near, far, merged, sums):
    t = pl.program_id(0)

    @pl.when(t == 0)
    def _():
        sums[...] = jnp.zeros_like(sums)

    low = jnp.concatenate([dq[...], dk[...], dv[...]], axis=1)
    merged[...] = low
    part = mm_t(low, w[...]).astype(bf16)
    sums[...] += jnp.sum(low.astype(f32), axis=0, keepdims=True)

    @pl.when(t < 2)
    def _():
        near[0] = part

    @pl.when(t >= 2)
    def _():
        far[0] = part


def qkv_back_call(scal, dq, dk, dv, w):
    keys, inner = dq.shape
    rows = keys // 4
    width = w.shape[0]
    where = lambda t, sc: (lax.bitwise_xor(sc[0], rel_of(t)), 0)
    at = pl.BlockSpec((rows, inner), where)
    return pl.pallas_call(
        qkv_back_body,
        out_shape=(
            jax.ShapeDtypeStruct((2, rows, width), bf16),
            jax.ShapeDtypeStruct((2, rows, width), bf16),
            jax.ShapeDtypeStruct((keys, 3 * inner), bf16),
            jax.ShapeDtypeStruct((1, 3 * inner), f32),
        ),
        grid_spec=pltpu.PrefetchScalarGridSpec(
            num_scalar_prefetch=1,
            grid=(4,),
            in_specs=[at, at, at, WHOLE],
            out_specs=(
                pl.BlockSpec((1, rows, width), near_map),
                pl.BlockSpec((1, rows, width), far_map),
                pl.BlockSpec((rows, 3 * inner), where),
                pl.BlockSpec((1, 3 * inner), lambda t, sc: (0, 0)),
            ),
        ),
        compiler_params=params(),
        name="qkv_back",
    )(scal, dq, dk, dv, w)


def in_back_body(x, a, b, c, dmid, gain, grad, sums):
    @pl.when(pl.program_id(0) == 0)
    def _():
        sums[...] = jnp.zeros_like(sums)

    unit, inv = normalize(x[...].astype(f32))
    e = (a[0].astype(f32) + b[0].astype(f32)) + c[...].astype(f32)
    grad[...] = (dmid[...] + norm_back(e, gain[...], unit, inv)).astype(bf16)
    sums[0:1, :] += jnp.sum(e * unit, axis=0, keepdims=True)
    sums[1:2, :] += jnp.sum(e, axis=0, keepdims=True)


def in_back_call(x, a, b, c, dmid, gain):
    rows, width = x.shape
    one = pl.BlockSpec((rows // 2, width), lambda i: (i, 0))
    first = pl.BlockSpec((1, rows // 2, width), lambda i: (0, i, 0))
    second = pl.BlockSpec((1, rows // 2, width), lambda i: (1, i, 0))
    row = pl.BlockSpec((1, width), lambda i: (0, 0))
    return pl.pallas_call(
        in_back_body,
        out_shape=(
            jax.ShapeDtypeStruct((rows, width), bf16),
            jax.ShapeDtypeStruct((8, width), f32),
        ),
        grid=(2,),
        in_specs=[one, second, first, one, one, row],
        out_specs=(one, pl.BlockSpec((8, width), lambda i: (0, 0))),
        compiler_params=params(),
        name="in_back",
    )(x, a, b, c, dmid, gain)


def remote(src, dst, send, recv, dp, seq):
    return pltpu.make_async_remote_copy(
        src_ref=src,
        dst_ref=dst,
        send_sem=send,
        recv_sem=recv,
        device_id=(dp, seq),
        device_id_type=pl.DeviceIdType.MESH,
    )


def greet(peers):
    barrier = pltpu.get_barrier_semaphore()
    for dp, seq in peers:
        pl.semaphore_signal(
            barrier, inc=1, device_id=(dp, seq), device_id_type=pl.DeviceIdType.MESH
        )
    pl.semaphore_wait(barrier, len(peers))


class GradSum:
    def __init__(self, part, acc, landx, land, sems, dp, seq):
        self.part, self.landx, self.land, self.sems = part, landx, land, sems
        self.fetched = acc is not None
        self.acc = acc if self.fetched else landx
        self.seq, self.z, self.x = seq, dp // 2, dp % 2

    def cross(self, k):
        return remote(
            self.part.at[2 * k + (1 - self.x)],
            self.landx.at[k],
            self.sems.at[0, k],
            self.sems.at[1, k],
            2 * self.z + (1 - self.x),
            self.seq,
        )

    def fetch(self, k):
        return pltpu.make_async_copy(
            self.part.at[2 * k + self.x], self.acc.at[k], self.sems.at[6, k]
        )

    def right(self, b, first):
        return remote(
            self.acc.at[b] if first else self.land.at[b + 1],
            self.land.at[b + 1],
            self.sems.at[2, b],
            self.sems.at[3, b],
            2 * ((self.z + 1) % 4) + self.x,
            self.seq,
        )

    def left(self, b, first):
        return remote(
            self.acc.at[b] if first else self.land.at[b],
            self.land.at[b],
            self.sems.at[4, b],
            self.sems.at[5, b],
            2 * ((self.z + 3) % 4) + self.x,
            self.seq,
        )

    def start(self):
        for k in (3, 0, 2, 1):
            self.cross(k).start()
        if self.fetched:
            for k in range(4):
                self.fetch(k).start()

    def add_cross(self):
        for k in (3, 0, 2, 1):
            self.cross(k).wait_recv()
            if self.fetched:
                self.fetch(k).wait()
                own = self.acc[k].astype(f32)
            else:
                own = self.part[2 * k + self.x].astype(f32)
            self.acc[k] = (own + self.landx[k].astype(f32)).astype(bf16)

    def stage(self, k):
        @pl.when(self.z == k)
        def _():
            for b in range(3, k, -1):
                if k > 0:
                    self.right(b, False).wait_recv()
                    total = self.land[b + 1].astype(f32) + self.acc[b].astype(f32)
                    self.land[b + 1] = total.astype(bf16)
                self.right(b, k == 0).start()

        @pl.when(self.z == 3 - k)
        def _():
            for b in range(0, 3 - k):
                if k > 0:
                    self.left(b, False).wait_recv()
                    total = self.land[b].astype(f32) + self.acc[b].astype(f32)
                    self.land[b] = total.astype(bf16)
                self.left(b, k == 0).start()

    def finish(self, out):
        z = self.z
        out[...] = self.acc[z].astype(f32)

        @pl.when(z > 0)
        def _():
            self.right(z, False).wait_recv()
            out[...] += self.land[z + 1].astype(f32)

        @pl.when(z < 3)
        def _():
            self.left(z, False).wait_recv()
            out[...] += self.land[z].astype(f32)

    def drain(self):
        for k in range(4):
            self.cross(k).wait_send()
        for k in range(3):

            @pl.when(self.z == k)
            def _(k=k):
                for b in range(3, k, -1):
                    self.right(b, k == 0).wait_send()

            @pl.when(self.z == 3 - k)
            def _(k=k):
                for b in range(0, 3 - k):
                    self.left(b, k == 0).wait_send()

    @staticmethod
    def scratch(m, n, fetched=False):
        own = [pltpu.VMEM((4, m, n), bf16)] if fetched else []
        return own + [
            pltpu.VMEM((4, m, n), bf16),
            pltpu.VMEM((5, m, n), bf16),
            pltpu.SemaphoreType.DMA((7, 4)),
        ]


class LineSum:
    def __init__(self, part, acc, land, landx, sems, dp, seq):
        self.part, self.acc, self.land, self.landx, self.sems = part, acc, land, landx, sems
        self.seq, self.z, self.x = seq, dp // 2, dp % 2

    def fetch(self, b):
        return pltpu.make_async_copy(
            self.part.at[pl.ds(2 * b, 2)], self.acc.at[b], self.sems.at[4, b]
        )

    def right(self, b, first):
        slot = self.land.at[b + 1]
        return remote(
            self.part.at[pl.ds(2 * b, 2)] if first else slot,
            slot,
            self.sems.at[0, b],
            self.sems.at[1, b],
            2 * ((self.z + 1) % 4) + self.x,
            self.seq,
        )

    def left(self, b, first):
        slot = self.land.at[b]
        return remote(
            self.part.at[pl.ds(2 * b, 2)] if first else slot,
            slot,
            self.sems.at[2, b],
            self.sems.at[3, b],
            2 * ((self.z + 3) % 4) + self.x,
            self.seq,
        )

    def start(self):
        for i in range(3):

            @pl.when(self.z == 0)
            def _(i=i):
                self.right(3 - i, True).start()

            @pl.when(self.z == 3)
            def _(i=i):
                self.left(i, True).start()

        for b in range(4):
            self.fetch(b).start()

    def ready(self):
        for b in range(4):
            self.fetch(b).wait()

    def hop(self, k, b):
        @pl.when(self.z == k)
        def _():
            self.right(b, False).wait_recv()
            total = self.land[b + 1].astype(f32) + self.acc[b].astype(f32)
            self.land[b + 1] = total.astype(bf16)
            self.right(b, False).start()

        c = 3 - b

        @pl.when(self.z == 3 - k)
        def _():
            self.left(c, False).wait_recv()
            total = self.land[c].astype(f32) + self.acc[c].astype(f32)
            self.land[c] = total.astype(bf16)
            self.left(c, False).start()

    def cross(self):
        z = self.z
        return remote(
            self.acc.at[z, 1 - self.x],
            self.landx,
            self.sems.at[5, 0],
            self.sems.at[5, 1],
            2 * z + (1 - self.x),
            self.seq,
        )

    def merge(self):
        z = self.z

        @pl.when(z > 0)
        def _():
            self.right(z, False).wait_recv()
            self.acc[z] = (self.acc[z].astype(f32) + self.land[z + 1].astype(f32)).astype(bf16)

        @pl.when(z < 3)
        def _():
            self.left(z, False).wait_recv()
            self.acc[z] = (self.acc[z].astype(f32) + self.land[z].astype(f32)).astype(bf16)

        self.cross().start()

    def finish(self, out):
        self.cross().wait_recv()
        out[...] = self.acc[self.z, self.x].astype(f32) + self.landx[...].astype(f32)

    def drain(self):
        self.cross().wait_send()
        for k in range(3):

            @pl.when(self.z == k)
            def _(k=k):
                for b in range(3, k, -1):
                    self.right(b, k == 0).wait_send()

            @pl.when(self.z == 3 - k)
            def _(k=k):
                for b in range(0, 3 - k):
                    self.left(b, k == 0).wait_send()

    @staticmethod
    def scratch(m, n):
        return [
            pltpu.VMEM((4, 2, m, n), bf16),
            pltpu.VMEM((5, 2, m, n), bf16),
            pltpu.VMEM((m, n), bf16),
            pltpu.SemaphoreType.DMA((6, 4)),
        ]


SMALL_ROWS = 16


class Gather:
    def __init__(self, own, slot, sems, dp, seq):
        self.own, self.slot, self.sems = own, slot, sems
        self.dp, self.seq, self.z, self.x = dp, seq, dp // 2, dp % 2

    def along(self, k, step, src=None):
        slot = self.slot(2 * k + self.x)
        return remote(
            slot if src is None else src,
            slot,
            self.sems.at[0 if step > 0 else 1, k],
            self.sems.at[3, k],
            2 * ((self.z + step + 4) % 4) + self.x,
            self.seq,
        )

    def over(self, k, src=None):
        slot = self.slot(2 * k + self.x)
        return remote(
            slot if src is None else src,
            slot,
            self.sems.at[2, k],
            self.sems.at[4, k],
            2 * self.z + (1 - self.x),
            self.seq,
        )

    def keep(self):
        return pltpu.make_async_copy(self.own, self.slot(self.dp), self.sems.at[5, 0])

    def start(self):
        z = self.z

        @pl.when(z < 3)
        def _():
            self.along(z, 1, self.own).start()

        @pl.when(z > 0)
        def _():
            self.along(z, -1, self.own).start()

        self.over(z, self.own).start()
        self.keep().start()

    def hop(self, dist):
        z = self.z

        @pl.when(z - dist >= 0)
        def _():
            k = z - dist
            self.along(k, 1).wait_recv()

            @pl.when(z < 3)
            def _():
                self.along(k, 1).start()

            self.over(k).start()

        @pl.when(z + dist <= 3)
        def _():
            k = z + dist
            self.along(k, -1).wait_recv()

            @pl.when(z > 0)
            def _():
                self.along(k, -1).start()

            self.over(k).start()

    def arrive(self):
        self.keep().wait()
        for k in range(4):
            self.over(k).wait_recv()

    def drain(self):
        z = self.z
        for k in range(4):
            self.over(k).wait_send()

            @pl.when((z < 3) & (z >= k))
            def _(k=k):
                self.along(k, 1).wait_send()

            @pl.when((z > 0) & (z <= k))
            def _(k=k):
                self.along(k, -1).wait_send()

    @staticmethod
    def scratch():
        return pltpu.SemaphoreType.DMA((6, 4))


class CrossGather:
    def __init__(self, own, slot, sems, dp, seq):
        self.own, self.slot, self.sems = own, slot, sems
        self.dp, self.seq, self.z, self.x = dp, seq, dp // 2, dp % 2

    def along(self, k, step, side, src=None):
        slot = self.slot(2 * k + (self.x + side) % 2)
        return remote(
            slot if src is None else src,
            slot,
            self.sems.at[side if step > 0 else 2 + side, k],
            self.sems.at[4 + side, k],
            2 * ((self.z + step + 4) % 4) + self.x,
            self.seq,
        )

    def cross(self):
        return remote(
            self.own,
            self.slot(self.dp),
            self.sems.at[6, 0],
            self.sems.at[6, 1],
            2 * self.z + (1 - self.x),
            self.seq,
        )

    def keep(self):
        return pltpu.make_async_copy(self.own, self.slot(self.dp), self.sems.at[6, 2])

    def both_ways(self, side, src=None):
        z = self.z

        @pl.when(z < 3)
        def _():
            self.along(z, 1, side, src).start()

        @pl.when(z > 0)
        def _():
            self.along(z, -1, side, src).start()

    def start(self):
        self.cross().start()
        self.both_ways(0, self.own)
        self.keep().start()

    def turn(self):
        self.cross().wait_recv()
        self.both_ways(1)

    def hop(self, dist, side):
        z = self.z

        @pl.when(z - dist >= 0)
        def _():
            k = z - dist
            self.along(k, 1, side).wait_recv()

            @pl.when(z < 3)
            def _():
                self.along(k, 1, side).start()

        @pl.when(z + dist <= 3)
        def _():
            k = z + dist
            self.along(k, -1, side).wait_recv()

            @pl.when(z > 0)
            def _():
                self.along(k, -1, side).start()

    def arrive(self):
        self.keep().wait()

    def drain(self):
        z = self.z
        self.cross().wait_send()
        for side in range(2):
            for k in range(4):

                @pl.when((z < 3) & (z >= k))
                def _(k=k, side=side):
                    self.along(k, 1, side).wait_send()

                @pl.when((z > 0) & (z <= k))
                def _(k=k, side=side):
                    self.along(k, -1, side).wait_send()

    @staticmethod
    def scratch():
        return pltpu.SemaphoreType.DMA((7, 4))


class Spread:
    def __init__(self, own, rows, sems, dp, seq):
        mate, across = seq + 1 - 2 * (seq % 2), (seq + 2) % 4
        to = lambda src, r, peer: remote(src, rows.at[r], sems.at[0, r], sems.at[1, r], dp, peer)
        self.near, self.far = to(own, 1, mate), to(own, 2, across)
        self.last = to(rows.at[2], 3, mate)

    def start(self):
        self.far.start()
        self.near.start()

    def forward(self):
        self.far.wait_recv()
        self.last.start()

    def drain(self):
        for copy in (self.near, self.far, self.last):
            copy.wait_send()


def neighbours(seq):
    mate = seq + 1 - 2 * (seq % 2)
    return mate, (seq + 2) % 4, (mate + 2) % 4


def block_at(seq, rel):
    return 2 * ((seq // 2 + rel // 2) % 2) + (seq + rel) % 2


def scores(k, qm, ramp):
    block = qm.shape[0]
    length = k.shape[0]
    s = mm_t(k, qm) + jnp.concatenate([ramp] * (block // LANES), axis=1)
    key = lax.broadcasted_iota(jnp.int32, (block, block), 0)
    query = lax.broadcasted_iota(jnp.int32, (block, block), 1)
    last = jnp.where(key <= query, s[length - block :], NEG)
    if length == block:
        return last
    return jnp.concatenate([s[: length - block], last], axis=0)


def fore_body(
    lengths, slopes, wq, wo, x, v_up, v_qv, v_g1, v_s1, v_out, v_g2, v_s2, v_down, g, w1, w2,
    h1, qkv_out, o, lse, wq_all, flat, mid, gain1, bias_down, y_all, gw1, gw2, dmid, dbr, sums,
    up_sum,
    small, vectors, shift1, bias_qkv, bias_out, gain2, shift2, bias_up,
    rows_in, g_rows, h_stage, qkv, ramp, vt, part, land_c, sum_y, land_y, w1_all, w2_flat,
    a_all, du_all, turned, y_stage, up_stage, down_stage,
    q_sem, o_sem, w1_sem, w2_sem, low_sem, x_sem, g_sem, seq_sem, dp_sem, keep_sem, stage_sem, fwd, mlp, bwd,
):
    dp, seq = lax.axis_index("dp"), lax.axis_index("seq")
    mate, across, _ = neighbours(seq)
    greet([((dp + i) % 8, seq) for i in range(1, 8)] + [(dp, p) for p in neighbours(seq)])
    rows, width = x.shape
    keys = qkv.shape[0]
    inner = o.shape[1]
    pairs = inner // LANES
    ff = du_all.shape[1]
    half_rows = rows // 2
    halves = [slice(0, half_rows), slice(half_rows, rows)]
    lanes_of = lambda d: pl.ds(pl.multiple_of(d * LANES, LANES), LANES)
    top, low = pl.ds(0, ff // 2), pl.ds(ff // 2, ff // 2)

    gather_q = Gather(wq, lambda d: wq_all.at[:, d], q_sem, dp, seq)
    gather_o = Gather(wo, lambda d: flat.at[:, lanes_of(d)], o_sem, dp, seq)
    gathers = [
        Gather(w1, lambda d: w1_all.at[d], w1_sem, dp, seq),
        Gather(w2.at[top], lambda d: w2_flat.at[top, lanes_of(d)], w2_sem, dp, seq),
    ]
    gather_low = CrossGather(
        w2.at[low], lambda d: w2_flat.at[low, lanes_of(d)], low_sem, dp, seq
    )
    spread_x = Spread(x, rows_in, x_sem, dp, seq)
    spread_g = Spread(g_rows.at[0], g_rows, g_sem, dp, seq)
    length = lengths[0]
    heads = 2 * pairs * seq
    at = 0
    for ref in (v_up, v_qv, v_g1, v_s1, v_out, v_g2, v_s2, v_down):
        small[:, at : at + ref.shape[1]] = ref[...].astype(f32)
        at += ref.shape[1]
    keep_v = pltpu.make_async_copy(small, vectors.at[dp, seq], keep_sem.at[0])
    keep_v.start()
    group = [
        remote(small, vectors.at[dp, seq], seq_sem.at[0, i], seq_sem.at[1, i], dp, peer)
        for i, peer in enumerate(neighbours(seq))
    ]
    for copy in group:
        copy.start()
    gather_q.start()
    spread_x.start()
    keep_x = pltpu.make_async_copy(x, rows_in.at[0], keep_sem.at[1])
    keep_g = pltpu.make_async_copy(g, g_rows.at[0], keep_sem.at[2])
    keep_x.start()
    keep_g.start()

    def to_dp(i):
        return remote(
            vectors.at[dp], vectors.at[dp], dp_sem.at[0, i], dp_sem.at[1, i], (dp + i) % 8, seq
        )

    keep_v.wait()
    for copy in group:
        copy.wait_recv()
    for i in range(1, 8):
        to_dp(i).start()
    gather_o.start()
    keep_g.wait()
    where = lax.broadcasted_iota(jnp.int32, (rows, width), 0) + seq * rows
    g_rows[0] = jnp.where(where < length, g_rows[0], jnp.zeros((rows, width), bf16))
    spread_g.start()
    gather_q.hop(1)
    gather_q.hop(2)
    gather_o.hop(1)
    gather_q.hop(3)
    gather_low.start()
    gather_o.hop(2)
    spread_x.forward()
    gather_o.hop(3)
    for gather in gathers:
        gather.start()
    for i in range(1, 8):
        to_dp(i).wait_recv()
    for ref, at in (
        (gain1, 192), (shift1, 224), (bias_out, 256), (gain2, 288), (shift2, 320), (bias_down, 352),
    ):
        for d in range(8):
            ref[:, d * LANES : (d + 1) * LANES] = jnp.concatenate(
                [vectors[d, i, :, at : at + 32] for i in range(4)], axis=1
            )
    for section in range(2):
        for half in range(2):
            lane = section * 512 + half * LANES
            bias_qkv[:, lane : lane + LANES] = jnp.concatenate(
                [vectors[4 * section + seq, 2 * half + i, :, 128:192] for i in range(2)], axis=1
            )
    bias_qkv[:, 256:512] = jnp.zeros((1, 256), f32)
    for i in range(8):
        bias_up[:, i * LANES : (i + 1) * LANES] = vectors[2 * seq + i // 4, i % 4, :, 0:LANES]
    keep_x.wait()
    spread_x.near.wait_recv()
    gather_q.arrive()
    spread_x.last.wait_recv()
    spread_x.drain()

    def h1_copy(r):
        at = pl.ds(pl.multiple_of(block_at(seq, r) * rows, rows), rows)
        return pltpu.make_async_copy(h_stage.at[r % 2], h1.at[at], stage_sem.at[0, r % 2])

    def project(r, carry):
        @pl.when(r >= 2)
        def _():
            h1_copy(r - 2).wait()

        @pl.when(r == 2)
        def _():
            gather_low.turn()
            for gather in gathers:
                gather.hop(1)
            gather_low.hop(1, 0)

        at = pl.ds(pl.multiple_of(block_at(seq, r) * rows, rows), rows)
        unit, _ = normalize(rows_in[r].astype(f32))
        low = (unit * gain1[...] + shift1[...]).astype(bf16)
        h_stage[r % 2] = low
        h1_copy(r).start()
        for c in range(3):
            cols = slice(c * inner, (c + 1) * inner)
            value = mm(low, wq_all[c].reshape(width, inner)) + bias_qkv[:, cols]
            qkv[at, cols] = value.astype(bf16)
        return carry

    lax.fori_loop(0, 4, project, 0)
    qkv_copy = pltpu.make_async_copy(qkv, qkv_out, keep_sem.at[3])
    qkv_copy.start()
    gather_low.hop(1, 1)
    spread_g.forward()
    pos = lax.broadcasted_iota(jnp.int32, (keys, LANES), 0)
    ramp[...] = jnp.where(pos < length, pos.astype(f32), -1e33)
    for p in range(pairs):
        vt[p] = qkv[:, 2 * inner + p * LANES : 2 * inner + (p + 1) * LANES].T
    gather_o.arrive()

    def row_copies(sems):
        rel_one = remote(part.at[1], land_c.at[0], sems.at[0, 0], sems.at[1, 0], dp, mate)
        rel_three = [
            remote(
                part.at[3, at], land_c.at[1, at], sems.at[0, 1 + i], sems.at[1, 1 + i], dp, mate
            )
            for i, at in enumerate(halves)
        ]
        over = [
            remote(sum_y.at[at], land_y.at[at], sems.at[0, 3 + i], sems.at[1, 3 + i], dp, across)
            for i, at in enumerate(halves)
        ]
        return rel_one, rel_three, over

    def send_over(rel_three, over, i):
        rel_three[i].wait_recv()
        at = halves[i]
        total = part[2, at, :].astype(f32) + land_c[1, at, :].astype(f32)
        sum_y[at, :] = total.astype(bf16)
        over[i].start()

    rel_one, rel_three, over = row_copies(fwd)

    def attend(t, carry):
        rel = 3 - t
        c_now = block_at(seq, rel)
        at = pl.ds(pl.multiple_of(c_now * rows, rows), rows)
        for c in range(keys // rows):

            @pl.when(c_now == c)
            def _(c=c):
                length = (c + 1) * rows

                def one_pair(p, carry):
                    lane = pl.ds(pl.multiple_of(p * LANES, LANES), LANES)
                    k_lane = pl.ds(pl.multiple_of(inner + p * LANES, LANES), LANES)
                    scaled = qkv[c * rows : length, lane] * bf16(HEAD_DIM**-0.5)
                    k = qkv[0:length, k_lane]
                    outs, logs = [], []
                    for h in range(2):
                        bias = ramp[0:length, :] * slopes[heads + 2 * p + h]
                        s = scores(k, head_only(scaled, h), bias)
                        top = jnp.max(s, axis=0, keepdims=True)
                        e = jnp.exp(s - top)
                        total = jnp.sum(e, axis=0, keepdims=True)
                        half = vt[p, h * HEAD_DIM : (h + 1) * HEAD_DIM, 0:length]
                        outs.append(mm(half, e.astype(bf16)) / total)
                        logs.append(top + jnp.log(total))
                    o[c * rows : length, lane] = jnp.concatenate(outs, axis=0).T.astype(bf16)
                    lse[p, 0:2, c * rows : length] = jnp.concatenate(logs, axis=0)
                    return carry

                lax.fori_loop(0, pairs, one_pair, 0)

        part[rel] = mm(o[at, :], flat[...]).astype(bf16)

        @pl.when(t == 0)
        def _():
            for copy in rel_three:
                copy.start()
            for gather in gathers:
                gather.hop(2)
            gather_low.hop(2, 0)

        @pl.when(t == 1)
        def _():
            send_over(rel_three, over, 0)
            send_over(rel_three, over, 1)
            gather_low.hop(2, 1)

        @pl.when(t == 2)
        def _():
            rel_one.start()
            for gather in gathers:
                gather.hop(3)
            gather_low.hop(3, 0)

        return carry

    lax.fori_loop(0, 4, attend, 0)
    gather_q.drain()
    gather_o.drain()
    gather_low.hop(3, 1)
    rel_one.wait_recv()

    near, far, last = (
        [
            remote(
                rows_in.at[0 if r < 3 else 2, at], rows_in.at[r, at], mlp.at[0, 2 * k + i],
                mlp.at[1, 2 * k + i], dp, across if r == 2 else mate,
            )
            for i, at in enumerate(halves)
        ]
        for k, r in enumerate((1, 2, 3))
    )
    step_rows = 64

    def second_norm(i):
        over[i].wait_recv()

        def step(k, carry):
            at = pl.ds(pl.multiple_of(i * half_rows + k * step_rows, step_rows), step_rows)
            total = (part[0, at, :].astype(f32) + land_c[0, at, :].astype(f32)) + land_y[
                at, :
            ].astype(f32)
            value = rows_in[0, at, :].astype(f32) + (total + bias_out[...])
            mid[at, :] = value
            unit, _ = normalize(value)
            rows_in[0, at, :] = (unit * gain2[...] + shift2[...]).astype(bf16)
            return carry

        lax.fori_loop(0, half_rows // step_rows, step, 0)
        far[i].start()
        near[i].start()

    second_norm(0)
    up_sum[...] = jnp.zeros_like(up_sum)
    sums[...] = jnp.zeros_like(sums)
    spread_g.near.wait_recv()
    spread_g.last.wait_recv()
    spread_g.drain()
    for gather in gathers + [gather_low]:
        gather.arrive()
    for copy in [rel_one] + rel_three:
        copy.wait_send()
    back_one, back_three, back_over = row_copies(bwd)
    chunk = 256

    def y_copy(i):
        rel, half = place(i)
        at = pl.ds(pl.multiple_of(half * half_rows, half_rows), half_rows)
        return pltpu.make_async_copy(y_stage.at[i % 2], y_all.at[rel, at], stage_sem.at[1, i % 2])

    def place(i):
        late = i // 4
        return late * (2 + i % 2) + (1 - late) * (i // 2), late * ((i // 2) % 2) + (1 - late) * (i % 2)

    def block(i, carry):
        rel, half = place(i)

        @pl.when(i == 1)
        def _():
            second_norm(1)

        for k in range(2):

            @pl.when(i == 2 + k)
            def _(k=k):
                near[k].wait_recv()

            @pl.when(i == 4 + 2 * k)
            def _(k=k):
                far[k].wait_recv()
                last[k].start()

            @pl.when(i == 5 + 2 * k)
            def _(k=k):
                last[k].wait_recv()

        @pl.when(i >= 2)
        def _():
            y_copy(i - 2).wait()

        inside = pl.ds(pl.multiple_of(half * half_rows, half_rows), half_rows)
        at = pl.ds(pl.multiple_of(rel * rows + half * half_rows, half_rows), half_rows)
        hidden = rows_in[rel, inside, :]
        grad = g_rows[rel, inside, :]
        up = w1_all[...].reshape(width, ff)
        for c in range(ff // chunk):
            cols = slice(c * chunk, (c + 1) * chunk)
            u = mm(hidden, up[:, cols]) + bias_up[:, cols]
            value, slope = gelu_parts(u)
            a_all[at, cols] = value.astype(bf16)
            du = (mm_t(grad, w2_flat[cols, :]) * slope).astype(bf16)
            du_all[at, cols] = du
            up_sum[:, cols] += jnp.sum(du.astype(f32), axis=0, keepdims=True)
        y_stage[i % 2] = mm(a_all[at, :], w2_flat[...]).astype(bf16)
        y_copy(i).start()
        part[rel, inside, :] = mm_t(du_all[at, :], up).astype(bf16)

        @pl.when(i == 3)
        def _():
            back_one.start()

        @pl.when(i == 5)
        def _():
            back_three[0].start()

        @pl.when(i == 6)
        def _():
            over[0].wait_send()
            over[1].wait_send()
            send_over(back_three, back_over, 0)

        @pl.when(i == 7)
        def _():
            back_three[1].start()

        return carry

    lax.fori_loop(0, 8, block, 0)

    def turn(load):
        def step(i, carry):
            turned[:, pl.ds(pl.multiple_of(i * rows, rows), rows)] = load(i).T
            return carry

        lax.fori_loop(0, 4, step, 0)

    def up_copy(j):
        cols = pl.ds(pl.multiple_of(j * chunk, chunk), chunk)
        return pltpu.make_async_copy(up_stage.at[j % 2], gw1.at[:, :, cols], stage_sem.at[2, j % 2])

    def down_copy(j):
        return pltpu.make_async_copy(
            down_stage.at[j % 2], gw2.at[pl.ds(2 * j, 2)], stage_sem.at[3, j % 2]
        )

    def outer_up(j, carry):
        @pl.when(j >= 2)
        def _():
            up_copy(j - 2).wait()

        cols = pl.ds(pl.multiple_of(j * chunk, chunk), chunk)
        value = mm(turned[...], du_all[:, cols]).astype(bf16)
        up_stage[j % 2] = value.reshape(8, width // 8, chunk)
        up_copy(j).start()
        return carry

    def outer_down(j, carry):
        @pl.when(j >= 2)
        def _():
            down_copy(j - 2).wait()

        cols = pl.ds(pl.multiple_of(j * chunk, chunk), chunk)
        right = g_rows[:, :, cols].reshape(4 * rows, chunk)
        value = mm(turned[...], right).astype(bf16)
        down_stage[j % 2, 0] = value[:, :LANES]
        down_stage[j % 2, 1] = value[:, LANES:]
        down_copy(j).start()
        return carry

    turn(lambda i: rows_in[i])
    send_over(back_three, back_over, 1)
    lax.fori_loop(0, ff // chunk, outer_up, 0)
    turn(lambda i: a_all[pl.ds(pl.multiple_of(i * rows, rows), rows), :])
    lax.fori_loop(0, width // chunk, outer_down, 0)

    back_one.wait_recv()

    def norm_step(k, carry):
        at = pl.ds(pl.multiple_of(k * step_rows, step_rows), step_rows)
        unit, inv = normalize(mid[at, :])
        e = (part[0, at, :].astype(f32) + land_c[0, at, :].astype(f32)) + land_y[at, :].astype(f32)
        grad = g_rows[0, at, :].astype(f32)
        value = grad + norm_back(e, gain2[...], unit, inv)
        dmid[at, :] = value
        low = value.astype(bf16)
        dbr[at, :] = low
        sums[0:1, :] += jnp.sum(e * unit, axis=0, keepdims=True)
        sums[1:2, :] += jnp.sum(e, axis=0, keepdims=True)
        sums[2:3, :] += jnp.sum(low.astype(f32), axis=0, keepdims=True)
        sums[3:4, :] += jnp.sum(grad, axis=0, keepdims=True)
        return carry

    steps = half_rows // step_rows
    back_over[0].wait_recv()
    lax.fori_loop(0, steps, norm_step, 0)
    back_over[1].wait_recv()
    lax.fori_loop(steps, 2 * steps, norm_step, 0)

    for copy in group + near + far + last + [back_one] + back_three + back_over:
        copy.wait_send()
    for i in range(1, 8):
        to_dp(i).wait_send()
    for gather in gathers + [gather_low]:
        gather.drain()
    qkv_copy.wait()
    for k in range(2):
        h1_copy(2 + k).wait()
        y_copy(6 + k).wait()
        up_copy(ff // chunk - 2 + k).wait()
        down_copy(width // chunk - 2 + k).wait()


def fore_call(lengths, slopes, wq, wo, x, small, g, w1, w2):
    rows, width = x.shape
    keys = 4 * rows
    inner, ff = wo.shape[0], w1.shape[1]
    pairs = inner // LANES
    count = sum(v.shape[0] for v in small)
    sem = pltpu.SemaphoreType.DMA
    shape = jax.ShapeDtypeStruct
    any_space = pl.BlockSpec(memory_space=pl.ANY)
    vec = lambda n: pltpu.VMEM((1, n), f32)
    block = lambda *lead: pltpu.VMEM((*lead, rows, width), bf16)
    return pl.pallas_call(
        fore_body,
        out_shape=(
            shape((keys, width), bf16),
            shape((keys, 3 * inner), bf16),
            shape((keys, inner), bf16),
            shape((pairs, 8, keys), f32),
            shape((3, 8, *wq.shape[1:]), bf16),
            shape((inner, width), bf16),
            shape((rows, width), f32),
            shape((1, width), f32),
            shape((1, width), f32),
            shape((4, rows, width), bf16),
            shape((8, width // 8, ff), bf16),
            shape((8, ff, LANES), bf16),
            shape((rows, width), f32),
            shape((rows, width), bf16),
            shape((8, width), f32),
            shape((1, ff), f32),
        ),
        in_specs=[SCALAR, SCALAR] + [any_space] * 3 + [WHOLE] * 8 + [any_space] * 3,
        out_specs=(
            any_space, any_space, WHOLE, WHOLE, WHOLE, WHOLE, WHOLE, WHOLE, WHOLE,
            any_space, any_space, any_space, WHOLE, WHOLE, WHOLE, WHOLE,
        ),
        scratch_shapes=[
            vec(count),
            pltpu.VMEM((8, 4, 1, count), f32),
            vec(width), vec(3 * inner), vec(width), vec(width), vec(width), vec(ff),
            block(4),
            block(4),
            block(2),
            pltpu.VMEM((keys, 3 * inner), bf16),
            pltpu.VMEM((keys, LANES), f32),
            pltpu.VMEM((pairs, LANES, keys), bf16),
            block(4),
            block(2),
            block(),
            block(),
            pltpu.VMEM((8, *w1.shape), bf16),
            pltpu.VMEM((ff, width), bf16),
            pltpu.VMEM((keys, ff), bf16),
            pltpu.VMEM((keys, ff), bf16),
            pltpu.VMEM((width, keys), bf16),
            pltpu.VMEM((2, rows // 2, width), bf16),
            pltpu.VMEM((2, 8, width // 8, 256), bf16),
            pltpu.VMEM((2, 2, ff, LANES), bf16),
            Gather.scratch(), Gather.scratch(), Gather.scratch(), Gather.scratch(),
            CrossGather.scratch(),
            sem((2, 4)), sem((2, 4)), sem((2, 3)), sem((2, 8)), sem((4,)), sem((4, 2)),
            sem((2, 5)), sem((2, 6)), sem((2, 5)),
        ],
        compiler_params=pltpu.CompilerParams(
            vmem_limit_bytes=67043328, collective_id=4, has_side_effects=True
        ),
        name="fore",
    )(lengths, slopes, wq, wo, x, *(v.reshape(1, -1) for v in small), g, w1, w2)


def back_body(
    lengths, slopes, dbr, o_in, flat_in, qkv_in, lse, wq_in, h1, gw1, gw2, y_all, mid_in, bias_down,
    x_in, dmid_in, gain1, mid_sums, up_sum,
    output, grad, gq_out, go_out, gw1_out, gw2_out, narrow_out, qv_out, up_out,
    o, flat, qkv, wq, mid, x, dmid,
    b_rows, y_far, do, go_sum, go_part, ramp, kt, dk_sum, dv_sum, merged, qkv_sums, h_buf, turned,
    gq_part, land_c, sum_y, land_y, y_land_c, y_sum, y_land_y,
    a_acc, a_x, a_land, a_sem, b_acc, b_land, b_x, b_sem, o_x, o_land, o_sem,
    q0_x, q0_land, q0_sem, q1_x, q1_land, q1_sem, q2_x, q2_land, q2_sem,
    small, small_land, own, seq_land,
    b_row_sem, row_sems, y_sems, h_sem, small_sems, seq_sems, far_sem, load_sem,
):
    loads = [
        pltpu.make_async_copy(src, dst, load_sem.at[i])
        for i, (src, dst) in enumerate((
            (dbr, b_rows.at[0]), (flat_in, flat), (o_in, o), (qkv_in, qkv), (mid_in, mid),
            (wq_in, wq), (x_in, x), (dmid_in, dmid),
        ))
    ]
    for copy in loads:
        copy.start()
    dp, seq = lax.axis_index("dp"), lax.axis_index("seq")
    mate, across, far_mate = neighbours(seq)
    greet([((dp + i) % 8, seq) for i in range(1, 8)] + [(dp, p) for p in neighbours(seq)])
    rows, width = dbr.shape
    keys, inner = o.shape
    length_all = lengths[0]
    pairs = inner // LANES
    heads = 2 * pairs * seq
    scale = HEAD_DIM**-0.5
    chunk = 128

    spread_b = Spread(dbr, b_rows, b_row_sem, dp, seq)
    spread_b.start()
    sum_a = GradSum(gw2, a_acc, a_x, a_land, a_sem, dp, seq)
    sum_b = LineSum(gw1, b_acc, b_land, b_x, b_sem, dp, seq)
    sum_o = GradSum(go_part, None, o_x, o_land, o_sem, dp, seq)
    sums_q = [
        GradSum(gq_part.at[0], None, q0_x, q0_land, q0_sem, dp, seq),
        GradSum(gq_part.at[1], None, q1_x, q1_land, q1_sem, dp, seq),
        GradSum(gq_part.at[2], None, q2_x, q2_land, q2_sem, dp, seq),
    ]
    sum_a.start()
    sum_b.start()
    y_cores = [
        remote(y_all.at[1 + 2 * k], y_land_c.at[k], y_sems.at[0, k], y_sems.at[1, k], dp, mate)
        for k in range(2)
    ]
    y_over = remote(y_sum, y_land_y, y_sems.at[0, 2], y_sems.at[1, 2], dp, across)
    cores = [
        remote(b_rows.at[r], land_c.at[k], row_sems.at[0, k], row_sems.at[1, k], dp, mate)
        for k, r in ((0, 1), (1, 3))
    ]
    over = remote(sum_y, land_y, row_sems.at[0, 2], row_sems.at[1, 2], dp, across)

    def fetch_h(i):
        at = pl.ds(pl.multiple_of(i * rows, rows), rows)
        return pltpu.make_async_copy(h1.at[at], h_buf.at[i % 2], h_sem.at[i % 2])

    fetch_h(0).start()
    fetch_h(1).start()
    y_fetch = [
        pltpu.make_async_copy(y_all.at[2 - 2 * k], y_far.at[k], far_sem.at[k]) for k in range(2)
    ]
    for copy in y_fetch:
        copy.start()
    go_sum[...] = jnp.zeros_like(go_sum)

    def turn(i, carry):
        fetch_h(i).wait()
        turned[:, pl.ds(pl.multiple_of(i * rows, rows), rows)] = h_buf[i % 2].T

        @pl.when(i < 2)
        def _():
            fetch_h(i + 2).start()

        return carry

    small[...] = jnp.zeros_like(small)
    for d in range(8):
        at = slice(d * LANES, (d + 1) * LANES)
        for row, src in ((4, 2), (5, 0), (6, 1), (11, 3)):
            small[d, row : row + 1, :] = mid_sums[src : src + 1, at]
    for i in range(8):
        at = slice(i * LANES, (i + 1) * LANES)
        small[pl.ds(2 * seq + i // 4, 1), 7 + i % 4, :] = up_sum[:, at]
    dk_sum[...] = jnp.zeros_like(dk_sum)
    dv_sum[...] = jnp.zeros_like(dv_sum)
    pos = lax.broadcasted_iota(jnp.int32, (keys, LANES), 0)
    ramp[...] = jnp.where(pos < length_all, pos.astype(f32), -1e33)
    y_cores[1].start()
    y_cores[0].start()
    for copy in loads[:4]:
        copy.wait()
    for p in range(pairs):
        kt[p] = qkv[:, inner + p * LANES : inner + (p + 1) * LANES].T

    def attend_back(r, carry):
        @pl.when(r == 1)
        def _():
            spread_b.near.wait_recv()

        @pl.when(r == 2)
        def _():
            lax.fori_loop(0, 4, turn, 0)
            spread_b.forward()
            y_cores[1].wait_recv()
            for copy in y_fetch:
                copy.wait()
            for i in range(rows // chunk):
                at = slice(i * chunk, (i + 1) * chunk)
                total = y_far[0, at, :].astype(f32) + y_land_c[1, at, :].astype(f32)
                y_sum[at, :] = total.astype(bf16)
            y_over.start()

        @pl.when(r == 3)
        def _():
            spread_b.last.wait_recv()

        c_now = block_at(seq, r)
        at = pl.ds(pl.multiple_of(c_now * rows, rows), rows)
        do[at, :] = mm_t(b_rows[r], flat[...]).astype(bf16)
        go_sum[...] += mm(o[at, :].T, b_rows[r])
        for c in range(keys // rows):

            @pl.when(c_now == c)
            def _(c=c):
                length = (c + 1) * rows
                at = slice(c * rows, length)

                def one_pair(p, carry):
                    lane = pl.ds(pl.multiple_of(p * LANES, LANES), LANES)
                    k_lane = pl.ds(pl.multiple_of(inner + p * LANES, LANES), LANES)
                    v_lane = pl.ds(pl.multiple_of(2 * inner + p * LANES, LANES), LANES)
                    scaled = qkv[at, lane] * bf16(scale)
                    g = do[at, lane]
                    both = (g.astype(f32) * o[at, lane].astype(f32)).T
                    k = qkv[0:length, k_lane]
                    v = qkv[0:length, v_lane]
                    outs = []
                    for h in range(2):
                        half = slice(h * HEAD_DIM, (h + 1) * HEAD_DIM)
                        qm = head_only(scaled, h)
                        gm = head_only(g, h)
                        dot_row = jnp.sum(both[half], axis=0, keepdims=True)
                        log = lse[p, h : h + 1, at]
                        bias = ramp[0:length, :] * slopes[heads + 2 * p + h]
                        e = jnp.exp(scores(k, qm, bias) - log)
                        ds = (e * (mm_t(v, gm) - dot_row)).astype(bf16)
                        dv_sum[p, 0:length, :] += mm(e.astype(bf16), gm)
                        dk_sum[p, 0:length, :] += mm(ds, qm)
                        outs.append(mm(kt[p, half, 0:length], ds))
                    merged[at, lane] = (jnp.concatenate(outs, axis=0).T * scale).astype(bf16)
                    return carry

                lax.fori_loop(0, pairs, one_pair, 0)

        @pl.when(r == 1)
        def _():
            sum_b.ready()
            sum_b.hop(1, 3)

        @pl.when(r == 2)
        def _():
            sum_b.hop(1, 2)
            sum_b.hop(2, 3)
            sum_a.add_cross()
            sum_a.stage(0)

        return carry

    lax.fori_loop(0, 4, attend_back, 0)
    for d in range(8):
        go_part[d] = go_sum[:, d * LANES : (d + 1) * LANES].astype(bf16)
    sum_o.start()
    for p in range(pairs):
        lane = slice(p * LANES, (p + 1) * LANES)
        merged[:, inner + p * LANES : inner + (p + 1) * LANES] = dk_sum[p].astype(bf16)
        merged[:, 2 * inner + p * LANES : 2 * inner + (p + 1) * LANES] = dv_sum[p].astype(bf16)
    spread_b.drain()
    for copy in loads[4:]:
        copy.wait()
    qkv_sums[...] = jnp.zeros_like(qkv_sums)

    def qkv_back(t, carry):
        rel = 3 - t
        at = pl.ds(pl.multiple_of(block_at(seq, rel) * rows, rows), rows)
        low = merged[at, :]
        total = mm_t(low[:, :inner], wq[0].reshape(width, inner))
        for c in range(1, 3):
            total += mm_t(low[:, c * inner : (c + 1) * inner], wq[c].reshape(width, inner))
        b_rows[rel] = total.astype(bf16)
        qkv_sums[...] += jnp.sum(low.astype(f32), axis=0, keepdims=True)

        @pl.when(t == 0)
        def _():
            cores[1].start()

        @pl.when(t == 1)
        def _():
            cores[1].wait_recv()
            for i in range(rows // chunk):
                at = slice(i * chunk, (i + 1) * chunk)
                total = b_rows[2, at, :].astype(f32) + land_c[1, at, :].astype(f32)
                sum_y[at, :] = total.astype(bf16)
            over.start()

        @pl.when(t == 2)
        def _():
            cores[0].start()

        return carry

    lax.fori_loop(0, 4, qkv_back, 0)
    sum_b.merge()
    for j in range(3):
        cols = slice(j * inner, (j + 1) * inner)
        value = mm(turned[...], merged[:, cols]).astype(bf16)
        gq_part[j] = value.reshape(8, width // 8, inner)
        sums_q[j].start()
        if j == 0:
            sum_a.stage(1)
    for i in range(2):
        at = slice(i * LANES, (i + 1) * LANES)
        small[pl.ds(seq, 1), 2 + i, :] = qkv_sums[:, at]
        at = slice((4 + i) * LANES, (5 + i) * LANES)
        small[pl.ds(4 + seq, 1), 2 + i, :] = qkv_sums[:, at]
    sum_o.add_cross()
    sum_o.stage(0)
    sum_a.stage(2)
    y_cores[0].wait_recv()
    y_over.wait_recv()

    def out_step(i, carry):
        at = pl.ds(pl.multiple_of(i * chunk, chunk), chunk)
        total = y_far[1, at, :].astype(f32) + y_land_c[0, at, :].astype(f32)
        total = total + y_land_y[at, :].astype(f32)
        output[at, :] = (mid[at, :] + (total + bias_down[...])).astype(bf16)
        return carry

    lax.fori_loop(0, rows // chunk, out_step, 0)
    sum_o.stage(1)
    sums_q[0].add_cross()
    sums_q[0].stage(0)
    cores[0].wait_recv()
    over.wait_recv()
    qkv_gain = [jnp.zeros((1, width), f32), jnp.zeros((1, width), f32)]
    for i in range(rows // chunk):
        at = slice(i * chunk, (i + 1) * chunk)
        unit, inv = normalize(x[at, :].astype(f32))
        e = (b_rows[0, at, :].astype(f32) + land_c[0, at, :].astype(f32)) + land_y[
            at, :
        ].astype(f32)
        grad[at, :] = (dmid[at, :] + norm_back(e, gain1[...], unit, inv)).astype(bf16)
        qkv_gain[0] += jnp.sum(e * unit, axis=0, keepdims=True)
        qkv_gain[1] += jnp.sum(e, axis=0, keepdims=True)
    for d in range(8):
        at = slice(d * LANES, (d + 1) * LANES)
        small[d, 0:1, :] = qkv_gain[0][:, at]
        small[d, 1:2, :] = qkv_gain[1][:, at]

    def small_to(i):
        peer = (dp + i) % 8
        return remote(
            small.at[peer], small_land.at[i], small_sems.at[0, i], small_sems.at[1, i], peer, seq
        )

    for i in range(1, 8):
        small_to(i).start()
    sums_q[1].add_cross()
    sums_q[1].stage(0)
    sums_q[0].stage(1)
    sum_o.stage(2)
    sums_q[2].add_cross()
    sums_q[2].stage(0)
    sums_q[1].stage(1)
    sums_q[0].stage(2)
    total = small[dp]
    for i in range(1, 8):
        small_to(i).wait_recv()
        total = total + small_land[i]
    own[...] = total

    def seq_to(i, peer):
        return remote(own, seq_land.at[i], seq_sems.at[0, i], seq_sems.at[1, i], dp, peer)

    group = [seq_to(i, peer) for i, peer in enumerate(neighbours(seq))]
    for copy in group:
        copy.start()
    sums_q[2].stage(1)
    sums_q[1].stage(2)
    sums_q[2].stage(2)
    sum_a.finish(gw2_out)
    sum_b.finish(gw1_out)
    sum_o.finish(go_out)
    for copy in group:
        copy.wait_recv()
    total = (own[...] + seq_land[0]) + (seq_land[1] + seq_land[2])
    narrow = total[:, 0:32]
    for i in range(1, 4):
        narrow = jnp.where(seq == i, total[:, 32 * i : 32 * (i + 1)], narrow)
    narrow_out[...] = narrow
    value = total[2:3, 0:64]
    for i in range(1, 4):
        at = 64 * (i % 2)
        value = jnp.where(seq == i, total[2 + i // 2 : 3 + i // 2, at : at + 64], value)
    qv_out[...] = value
    value = total[7:8]
    for i in range(1, 4):
        value = jnp.where(seq == i, total[7 + i : 8 + i], value)
    up_out[...] = value
    for j in range(3):
        sums_q[j].finish(gq_out.at[j])
    for copy in group + cores + y_cores + [over, y_over]:
        copy.wait_send()
    for i in range(1, 8):
        small_to(i).wait_send()
    for part in [sum_a, sum_b, sum_o] + sums_q:
        part.drain()


def back_call(*args):
    dbr, o, flat, qkv, lse, wq, h1, gw1, gw2 = args[2:11]
    rows, width = dbr.shape
    keys, inner = o.shape
    pairs = inner // LANES
    sem = pltpu.SemaphoreType.DMA
    block = lambda dtype: pltpu.VMEM((rows, width), dtype)
    pair_rows = pltpu.VMEM((2, rows, width), bf16)
    specs = [SCALAR, SCALAR] + [pl.BlockSpec(memory_space=pl.ANY)] * (len(args) - 2)
    for at in (6, 13, 16, 17, 18):
        specs[at] = WHOLE
    shape = jax.ShapeDtypeStruct
    return pl.pallas_call(
        back_body,
        out_shape=(
            shape((rows, width), bf16),
            shape((rows, width), bf16),
            shape((3, width // 8, inner), f32),
            shape((inner, LANES), f32),
            shape(gw1.shape[1:], f32),
            shape(gw2.shape[1:], f32),
            shape((SMALL_ROWS, 32), f32),
            shape((1, 64), f32),
            shape((1, LANES), f32),
        ),
        in_specs=specs,
        out_specs=(WHOLE,) * 9,
        scratch_shapes=[
            pltpu.VMEM(o.shape, bf16),
            pltpu.VMEM(flat.shape, bf16),
            pltpu.VMEM(qkv.shape, bf16),
            pltpu.VMEM(wq.shape, bf16),
            block(f32),
            block(bf16),
            block(f32),
            pltpu.VMEM((4, rows, width), bf16),
            pair_rows,
            pltpu.VMEM((keys, inner), bf16),
            pltpu.VMEM((inner, width), f32),
            pltpu.VMEM((8, inner, LANES), bf16),
            pltpu.VMEM((keys, LANES), f32),
            pltpu.VMEM((pairs, LANES, keys), bf16),
            pltpu.VMEM((pairs, keys, LANES), f32),
            pltpu.VMEM((pairs, keys, LANES), f32),
            pltpu.VMEM((keys, 3 * inner), bf16),
            pltpu.VMEM((1, 3 * inner), f32),
            pair_rows,
            pltpu.VMEM((width, keys), bf16),
            pltpu.VMEM((3, 8, width // 8, inner), bf16),
            pair_rows, block(bf16), block(bf16),
            pair_rows, block(bf16), block(bf16),
            *GradSum.scratch(*gw2.shape[1:], fetched=True),
            *LineSum.scratch(*gw1.shape[1:]),
            *GradSum.scratch(inner, LANES),
            *(GradSum.scratch(width // 8, inner) * 3),
            pltpu.VMEM((8, SMALL_ROWS, LANES), f32),
            pltpu.VMEM((8, SMALL_ROWS, LANES), f32),
            pltpu.VMEM((SMALL_ROWS, LANES), f32),
            pltpu.VMEM((3, SMALL_ROWS, LANES), f32),
            sem((2, 4)), sem((2, 3)), sem((2, 3)), sem((2,)), sem((2, 8)), sem((2, 3)), sem((2,)),
            sem((8,)),
        ],
        compiler_params=pltpu.CompilerParams(
            vmem_limit_bytes=67043328, collective_id=3, has_side_effects=True
        ),
        name="back",
    )(*args)


def finish_body(
    output, grad, gq, go, gw1, gw2, narrow, qv, up,
    output_out, grad_out, gq_out, go_out, gw1_out, gw2_out,
    gain1, shift1, qv_out, bout, gain2, shift2, up_out, down,
):
    for src, dst in (
        (output, output_out), (grad, grad_out), (gq, gq_out), (go, go_out), (gw1, gw1_out),
        (gw2, gw2_out), (qv, qv_out), (up, up_out),
    ):
        dst[...] = src[...]
    for ref, row in ((gain1, 0), (shift1, 1), (bout, 4), (gain2, 5), (shift2, 6), (down, 11)):
        ref[...] = narrow[row : row + 1, :]


def finish_call(output, grad, gq, go, gw1, gw2, narrow, qv, up):
    steps = 4
    like = lambda v: jax.ShapeDtypeStruct(v.shape, v.dtype)
    cut = lambda v: pl.BlockSpec((v.shape[0] // steps, v.shape[1]), lambda i: (i, 0))
    still = lambda v: pl.BlockSpec(v.shape, lambda i: (0, 0))
    deep = pl.BlockSpec((3, gq.shape[1] // steps, gq.shape[2]), lambda i: (0, i, 0))
    one = jax.ShapeDtypeStruct((1, 32), f32)
    specs = [cut(output), cut(grad), deep, cut(go), cut(gw1), cut(gw2)]
    return pl.pallas_call(
        finish_body,
        out_shape=(
            like(output), like(grad), like(gq), like(go), like(gw1), like(gw2),
            one, one, like(qv), one, one, one, like(up), one,
        ),
        grid=(steps,),
        in_specs=specs + [still(narrow), still(qv), still(up)],
        out_specs=specs
        + [still(one), still(one), still(qv), still(one), still(one), still(one), still(up), still(one)],
        compiler_params=params(),
        name="finish",
    )(output, grad, gq, go, gw1, gw2, narrow, qv, up)


def after(value, *others):
    return lax.optimization_barrier((value, *others))[0]


def on_device(
    dp_n,
    seq_n,
    tokens,
    lengths,
    cotangent,
    ln1_gain,
    ln1_shift,
    w_qkv,
    b_qv,
    w_out,
    b_out,
    ln2_gain,
    ln2_shift,
    w_fc1,
    b_fc1,
    w_fc2,
    b_fc2,
):
    count = dp_n * seq_n
    rows, width = tokens.shape
    heads = width // HEAD_DIM
    inner = w_out.shape[0]
    ff = w_fc1.shape[1]
    s = lax.axis_index("seq")
    length = lengths[0]

    scal = jnp.stack([s.astype(jnp.int32), length])
    slopes = 2.0 ** (-8.0 * (jnp.arange(heads, dtype=jnp.int32) + 1).astype(f32) / heads)
    slopes_all = slopes
    slopes = lax.dynamic_slice(slopes, (s * (heads // seq_n),), (heads // seq_n,))
    valid = s * rows + jnp.arange(rows, dtype=jnp.int32) < length
    grad_low = jnp.where(valid[:, None], cotangent, jnp.zeros_like(cotangent))
    wq_own = jnp.concatenate([w_qkv[:, c, :] for c in range(3)], axis=1)
    small = (ln1_gain, ln1_shift, b_qv, b_out, ln2_gain, ln2_shift, b_fc1, b_fc2)
    sizes = [v.shape[0] for v in small]
    ends = [sum(sizes[: i + 1]) for i in range(len(sizes))]
    block = 384
    fast = dp_n == 8 and seq_n == 4 and width == 8 * LANES and ff == width and inner == 2 * LANES
    if fast:
        parts = dp_n
        order = (b_fc1, b_qv, ln1_gain, ln1_shift, b_out, ln2_gain, ln2_shift, b_fc2)
        (
            h1, qkv, o, lse, wq, w_o, mid, gain1, bias_down, y_all, grad_up, grad_down, dmid, dbr,
            mid_sums, up_sum,
        ) = fore_call(
            lengths, slopes_all, jnp.transpose(w_qkv, (1, 0, 2)), w_out, tokens, order, cotangent,
            w_fc1, w_fc2,
        )
        results = back_call(
            lengths, slopes_all, dbr, o, w_o, qkv, lse, wq, h1, grad_up, grad_down, y_all, mid,
            bias_down, tokens, dmid, gain1, mid_sums, up_sum,
        )
        output, grad_tokens, grad_qkv, grad_out, grad_up, grad_down, *vectors = finish_call(*results)
        grad_qkv = jnp.transpose(grad_qkv, (1, 0, 2))
        g_gain1, g_shift1, g_qv, g_bout, g_gain2, g_shift2, g_up, g_down = (
            v.reshape(n) for v, n in zip(vectors, sizes)
        )
        return (
            output, grad_tokens, g_gain1, g_shift1, grad_qkv, g_qv, grad_out, g_bout,
            g_gain2, g_shift2, grad_up, g_up, grad_down, g_down,
        )

    wq = lax.all_gather(wq_own, "dp", axis=0, tiled=True)
    col = w_fc2.shape[1]
    both = jnp.concatenate([w_fc2, w_out], axis=0)
    if col % LANES == 0:
        parts = dp_n
        w_cols = lax.all_gather(both, "dp", axis=0, tiled=False)
    else:
        parts = 1
        w_cols = lax.all_gather(both, "dp", axis=1, tiled=True)[None]
    w_o = w_cols
    out_first = ff
    w1 = lax.all_gather(w_fc1, "dp", axis=0, tiled=True)
    packed = small_gather(jnp.concatenate([v.astype(f32) for v in small]), count, seq_n)
    packed = packed.reshape(count, ends[-1])
    gain1, shift1, bias_qv, bias_out, gain2, shift2, bias_up, bias_down = (
        packed[:, e - n : e].reshape(1, count * n) for e, n in zip(ends, sizes)
    )
    own_bias = lambda v, n: lax.dynamic_slice(v, (0, s * n), (1, n))
    own_up = own_bias(bias_up, ff)
    qkv_bias = jnp.concatenate(
        [
            own_bias(bias_qv[:, :width], inner),
            jnp.zeros((1, inner), f32),
            own_bias(bias_qv[:, width:], inner),
        ],
        axis=1,
    )
    x_pieces = spread(tokens)
    g_rows = jnp.stack(spread(after(grad_low, x_pieces[3])))
    h1, qkv = qkv_call(scal, x_pieces, wq, gain1, shift1, qkv_bias)
    o, lse = attend_call(scal, slopes, qkv, block)
    near, far = out_call(scal, o, w_o, out_first)
    got, across = reduce_rows(near, far)
    mid, h2 = mid_call(tokens, far, got, across, bias_out, gain2, shift2)
    h_pieces = spread(h2)
    y_near, y_far, d_near, d_far, a_all, du_all, h_all, g_all, up_sum = mlp_call(
        h_pieces, g_rows, w1, w_cols, own_up
    )
    got, across = reduce_rows(d_near, d_far)
    grad_down = outer_call(a_all, g_all, parts, "grad_fc2")
    grad_up = outer_call(h_all, du_all, 1, "grad_fc1")
    dmid, dbr, mid_sums = mid_back_call(mid, d_far, got, across, grad_low, gain2)

    b_pieces = spread(dbr)

    y_near = after(y_near, b_pieces[3])
    got, across = reduce_rows(y_near, y_far)
    output = (
        mid + ((y_far[1].astype(f32) + got[0].astype(f32)) + across.astype(f32) + bias_down)
    ).astype(bf16)

    do, grad_out = out_back_call(scal, b_pieces, o, w_o, out_first)
    dq, dk, dv = attend_back_call(scal, slopes, qkv, o, do, lse, block)
    near, far, merged, qkv_sums = qkv_back_call(scal, dq, dk, dv, wq)
    grad_qkv = outer_call(h1, merged, 1, "grad_qkv")

    def shared(part):
        if parts > 1:
            return lax.psum_scatter(part, "dp", scatter_dimension=0, tiled=False).astype(f32)
        return lax.psum_scatter(part, "dp", scatter_dimension=1, tiled=True).astype(f32)

    grad_down = shared(grad_down if parts > 1 else grad_down)
    grad_up = lax.psum_scatter(grad_up, "dp", scatter_dimension=0, tiled=True).astype(f32)
    got, across = reduce_rows(near, far)
    grad_tokens, in_sums = in_back_call(tokens, far, got, across, dmid, gain1)
    grad_out = shared(grad_out if parts > 1 else grad_out[0])
    grad_qkv = lax.psum_scatter(grad_qkv, "dp", scatter_dimension=0, tiled=True)
    grad_qkv = grad_qkv.astype(f32).reshape(w_qkv.shape)

    def own_slot(v, total):
        return lax.dynamic_update_slice(jnp.zeros((1, total), f32), v, (0, s * v.shape[1]))

    sums = (
        in_sums[0:1],
        in_sums[1:2],
        jnp.concatenate(
            [own_slot(qkv_sums[:, :inner], width), own_slot(qkv_sums[:, 2 * inner :], width)], axis=1
        ),
        mid_sums[2:3],
        mid_sums[0:1],
        mid_sums[1:2],
        own_slot(up_sum, seq_n * ff),
        mid_sums[3:4],
    )
    grads = jnp.concatenate([v.reshape(count, n) for v, n in zip(sums, sizes)], axis=1)
    grads = small_scatter(grads, count, seq_n).reshape(ends[-1])
    g_gain1, g_shift1, g_qv, g_bout, g_gain2, g_shift2, g_up, g_down = (
        grads[e - n : e] for e, n in zip(ends, sizes)
    )
    return (
        output,
        grad_tokens,
        g_gain1,
        g_shift1,
        grad_qkv,
        g_qv,
        grad_out,
        g_bout,
        g_gain2,
        g_shift2,
        grad_up,
        g_up,
        grad_down,
        g_down,
    )


def solution(mesh):
    rows = P(("dp", "seq"), None)
    vec = P(("dp", "seq"))
    merged = P("dp", None, "seq")
    return jax.shard_map(
        functools.partial(on_device, mesh.shape["dp"], mesh.shape["seq"]),
        mesh=mesh,
        in_specs=(
            rows, P("dp"), rows, vec, vec, merged, vec, P("seq", "dp"), vec, vec, vec,
            P("dp", "seq"), vec, P("seq", "dp"), vec,
        ),
        out_specs=(
            rows, rows, vec, vec, merged, vec, P("seq", "dp"), vec, vec, vec,
            P("dp", "seq"), vec, P("seq", "dp"), vec,
        ),
        check_vma=False,
    )
```
